32 devices in a mesh: dp: 8 (over y, x, core), mp: 4 (over z).
Axes of the slice: x: 2, y: 2, z: 4, core: 2. Of those that a mesh axis runs over, the one named last changes fastest.
Arguments:
- inputs: bfloat16 [32768, 768], P(('dp', 'mp')), may hold values from -6 to 6
- lengths: int32 [32], P(('dp', 'mp')), may hold values from 102 to 1024, as said below
- attn_qkv: bfloat16 [1, 768, 2304], P(None, ('dp', 'mp')), may hold values from -0.21875 to 0.21875
- attn_proj: bfloat16 [1, 768, 768], P(None, ('dp', 'mp')), may hold values from -1.75 to 1.75
- mlp_in: bfloat16 [1, 768, 3072], P(None, 'dp', 'mp'), may hold values from -0.21875 to 0.21875
- mlp_out: bfloat16 [1, 3072, 768], P(None, 'mp', 'dp'), may hold values from -0.109375 to 0.109375
- norm_gain: bfloat16 [1, 2, 768], P(None, None, ('dp', 'mp')), may hold values from 0.099609375 to 1.8984375
- norm_bias: bfloat16 [1, 2, 768], P(None, None, ('dp', 'mp')), may hold values from -1.5 to 1.5
- cotangent: bfloat16 [32768, 768], P(('dp', 'mp')), may hold values from -6 to 6
Outputs:
- outputs: bfloat16 [32768, 768], P(('dp', 'mp'))
- input_grad: float32 [32768, 768], P(('dp', 'mp'))
- qkv_grad: float32 [1, 768, 2304], P(None, ('dp', 'mp'))
- proj_grad: float32 [1, 768, 768], P(None, ('dp', 'mp'))
- mlp_in_grad: float32 [1, 768, 3072], P(None, 'dp', 'mp')
- mlp_out_grad: float32 [1, 3072, 768], P(None, 'mp', 'dp')
- gain_grad: float32 [1, 2, 768], P(None, None, ('dp', 'mp'))
- bias_grad: float32 [1, 2, 768], P(None, None, ('dp', 'mp'))
The draws below stay inside these ranges and needn't reach their ends.
Inputs may be any that keep to these rules, and one draw needn't show every extreme that they name: `lengths`: the true patch count of each clip; slots at or beyond it are padding. Some clip has 1024 patches and some has 102.
All inputs are finite; a program needn't handle non-finite values.
Results may differ from the reference program's by a relative error of at most 0.011.
Values may be sent and summed in bfloat16 or wider, within the bound.
A program may use at most 320 MiB of HBM per device.

```python
import math
import jax
import jax.numpy as jnp
from jax import lax

D = 768
HEADS = 12
HEAD_DIM = 64
FF = 3072
LAYERS = 1
SLOTS = 1024
CLIPS = 32
ROWS = 32768


def draw_lengths(key, part):
    key_counts, key_order = jax.random.split(jax.random.fold_in(key, 17))
    counts = jax.random.randint(key_counts, (CLIPS,), SLOTS // 10, SLOTS + 1, dtype=jnp.int32)
    chosen = jax.random.permutation(key_order, CLIPS)
    counts = counts.at[chosen[0]].set(SLOTS)
    counts = counts.at[chosen[1]].set(SLOTS // 10)
    return counts.astype(jnp.int32)


def shard_levels(key, dims, shards, smallest, high):
    loudness, own = 1.0, jax.random.fold_in(key, 6)
    for position, shards_of in shards:
        steps = jnp.exp(jax.random.uniform(jax.random.fold_in(own, position), (shards_of,), jnp.float32, smallest / len(shards), high / len(shards)))
        loudness = loudness * jnp.repeat(steps, dims[position] // shards_of).reshape([-1 if axis == position else 1 for axis in range(len(dims))])
    return loudness


def scatter_about(own_key, extent, width, most, shards=(), kind=jnp.bfloat16):
    values = width * jax.random.normal(own_key, extent, jnp.float32)
    if shards:
        values = values * shard_levels(own_key, extent, shards, -0.22, 0.18)
    return jnp.clip(values, -most, most).astype(kind)


def setup_inputs(seed: int = 0) -> dict:
    seeds = jax.random.split(jax.random.key(seed), 10)
    return {
        "inputs": scatter_about(seeds[0], (ROWS, D), 1.0, 6.0, ((0, 32),)),
        "lengths": draw_lengths(jax.random.fold_in(seeds[9], 71), 0),
        "attn_qkv": scatter_about(seeds[2], (LAYERS, D, 3 * D), D ** -0.5, 0.21875, ((1, 32),)),
        "attn_proj": scatter_about(seeds[3], (LAYERS, D, D), (D // 64) ** -0.5, 1.75, ((1, 32),)),
        "mlp_in": scatter_about(seeds[4], (LAYERS, D, FF), D ** -0.5, 0.21875, ((1, 8), (2, 4))),
        "mlp_out": scatter_about(seeds[5], (LAYERS, FF, D), FF ** -0.5, 0.109375, ((1, 4), (2, 8))),
        "norm_gain": jnp.clip(1.0 + 0.18 * jax.random.normal(seeds[6], (LAYERS, 2, D), jnp.float32), 0.099609375, 1.8984375).astype(jnp.bfloat16),
        "norm_bias": scatter_about(seeds[7], (LAYERS, 2, D), 0.3, 1.5, ((2, 32),)),
        "cotangent": scatter_about(seeds[8], (ROWS, D), 1.0, 6.0, ((0, 32),)),
    }


highest_precision = lax.Precision.HIGHEST

@jax.custom_vjp
def low(v):
    return lax.optimization_barrier(v.astype(jnp.bfloat16)).astype(jnp.float32)

@jax.custom_vjp
def low_back(v):
    return v

def low_keep(v):
    return (low(v), None)

def low_pass(kept, grad):
    return (grad,)

def back_keep(v):
    return (v, None)

def back_low(kept, grad):
    return (low(grad),)
low.defvjp(low_keep, low_pass)
low_back.defvjp(back_keep, back_low)

def layer_norm(values, scales, shifts):
    centre = values - lax.optimization_barrier(jnp.mean(values, axis=-1, keepdims=True))
    spread = lax.optimization_barrier(jnp.mean(centre * centre, axis=-1, keepdims=True))
    return centre * lax.rsqrt(spread + 1e-06) * scales + shifts

def clip_attention(element):
    packed_clip, length = element
    queries = packed_clip[:, :D].reshape(SLOTS, HEADS, HEAD_DIM)
    keys = packed_clip[:, D:2 * D].reshape(SLOTS, HEADS, HEAD_DIM)
    values = packed_clip[:, 2 * D:].reshape(SLOTS, HEADS, HEAD_DIM)
    scores = jnp.einsum('qhd,khd->hqk', queries, keys, precision=highest_precision) * (1.0 / math.sqrt(HEAD_DIM))
    scores = low_back(scores)
    valid = lax.iota(jnp.int32, SLOTS) < length
    scores = jnp.where(valid[None, None, :], scores, -1e+30)
    weights = low(jax.nn.softmax(scores, axis=-1))
    mixed = jnp.einsum('hqk,khd->qhd', weights, values, precision=highest_precision)
    return mixed.reshape(SLOTS, D)

def forward(rows, lengths_group, qkv_w, proj_w, in_w, out_w, gains, shifts):
    hidden = rows
    for layer_index in range(LAYERS):
        normed = low(layer_norm(hidden, gains[layer_index, 0], shifts[layer_index, 0]))
        packed = low(low_back(jnp.dot(normed, qkv_w[layer_index], precision=highest_precision)))
        attended = lax.map(jax.checkpoint(clip_attention), (packed.reshape(-1, SLOTS, 3 * D), lengths_group))
        attended = low(low_back(attended.reshape(-1, D)))
        hidden = hidden + low_back(jnp.dot(attended, proj_w[layer_index], precision=highest_precision))
        second = low(layer_norm(hidden, gains[layer_index, 1], shifts[layer_index, 1]))
        expanded = low_back(jnp.dot(second, in_w[layer_index], precision=highest_precision))
        activated = low(jax.nn.gelu(expanded, approximate=False))
        hidden = hidden + low_back(jnp.dot(activated, out_w[layer_index], precision=highest_precision))
    return hidden

def reference(inputs, lengths, attn_qkv, attn_proj, mlp_in, mlp_out, norm_gain, norm_bias, cotangent):
    params = (attn_qkv.astype(jnp.float32), attn_proj.astype(jnp.float32), mlp_in.astype(jnp.float32), mlp_out.astype(jnp.float32), norm_gain.astype(jnp.float32), norm_bias.astype(jnp.float32))
    group = math.gcd(CLIPS, max(1, 4096 // SLOTS))
    groups = CLIPS // group
    rows_in = inputs.astype(jnp.float32).reshape(groups, group * SLOTS, D)
    lengths_in = lengths.reshape(groups, group)
    valid = (lax.iota(jnp.int32, SLOTS)[None, None, :] < lengths_in[:, :, None]).astype(jnp.float32)
    upstream = cotangent.astype(jnp.float32).reshape(groups, group * SLOTS, D) * valid.reshape(groups, group * SLOTS, 1)

    def one_group(carried, element):
        rows_g, lengths_g, upstream_g = element

        def tied(rows_x, qkv_x, proj_x, in_x, out_x, gain_x, shift_x):
            return forward(rows_x, lengths_g, qkv_x, proj_x, in_x, out_x, gain_x, shift_x)
        result, pull = jax.vjp(tied, rows_g, params[0], params[1], params[2], params[3], params[4], params[5])
        grads = pull(upstream_g)
        carried = jax.tree.map(jnp.add, carried, tuple(grads[1:]))
        return (carried, (result.astype(jnp.bfloat16), grads[0]))
    zeros = jax.tree.map(jnp.zeros_like, params)
    totals, (outputs, input_grad) = lax.scan(one_group, zeros, (rows_in, lengths_in, upstream))
    return (outputs.reshape(ROWS, D), input_grad.reshape(ROWS, D), totals[0], totals[1], totals[2], totals[3], totals[4], totals[5])
```

```python
import functools, math
import jax
import jax.numpy as jnp
from jax.sharding import PartitionSpec as P
from jax import lax
from jax.experimental import pallas as pl
from jax.experimental.pallas import tpu as pltpu
F32=jnp.float32; BF=jnp.bfloat16
HD=64; SCALE=0.125; LOG2E=1.4426950408889634; C=SCALE*LOG2E
NEG=-1e30

def parts3(x):
    hi=x.astype(BF); r=x-hi.astype(F32); mid=r.astype(BF); lo=(r-mid.astype(F32)).astype(BF)
    return hi,mid,lo

def lane_iota(shape): return lax.broadcasted_iota(jnp.int32, shape, len(shape)-1)

def fwd_kernel(len_ref, q_ref, k_ref, v_ref, o_ref, of_ref, lse_ref, *, tq, npair):
    p=pl.program_id(0)
    L=q_ref.shape[0]
    n=len_ref[0]
    lane=lane_iota((L,128))
    k=k_ref[...]; v=v_ref[...]
    kpos=lax.broadcasted_iota(jnp.int32,(L,128),0)
    bias=jnp.where(kpos<n,0.0,NEG).astype(BF)
    zero=jnp.zeros((L,128),BF); one=jnp.ones((L,128),BF)
    @pl.when(p==0)
    def _(): lse_ref[...]=jnp.zeros_like(lse_ref)
    kk=[]; vv=[]
    for h in range(2):
        mine=(lane<64) if h==0 else (lane>=64)
        extra=64*(1-h)
        kk.append(jnp.where(mine,k,jnp.where(lane==extra,bias,zero)))
        vv.append(jnp.where(mine,v,jnp.where(lane==extra,one,zero)))
    lq=lane_iota((tq,128))
    for i in range(L//tq):
        q=q_ref[pl.ds(i*tq,tq),:]
        outs=[]; lses=[]
        for h in range(2):
            mine=(lq<64) if h==0 else (lq>=64)
            extra=64*(1-h)
            qa=jnp.where(mine,q,jnp.where(lq==extra,jnp.ones((tq,128),BF),jnp.zeros((tq,128),BF)))
            s=lax.dot_general(qa,kk[h],(((1,),(1,)),((),())),preferred_element_type=F32)
            m=jnp.max(s,axis=1,keepdims=True)
            e=jnp.exp2(s*C-m*C)
            o=jnp.dot(e.astype(BF),vv[h],preferred_element_type=F32)
            tot=o[:,extra:extra+1]
            outs.append(o/tot); lses.append(m*C+jnp.log2(tot))
        of=jnp.where(lq<64,outs[0],outs[1])
        of_ref[pl.ds(i*tq,tq),:]=of
        o_ref[pl.ds(i*tq,tq),:]=of.astype(BF)
        cur=lse_ref[pl.ds(i*tq,tq),:]
        cur=jnp.where(lq==2*p,lses[0],cur)
        cur=jnp.where(lq==2*p+1,lses[1],cur)
        lse_ref[pl.ds(i*tq,tq),:]=cur

def att_fwd(lengths, packed, tq=256):
    L=packed.shape[0]; D=packed.shape[1]//3; np_=D//128
    spec=lambda off: pl.BlockSpec((L,128),lambda p,off=off:(0,off+p))
    return pl.pallas_call(functools.partial(fwd_kernel,tq=tq,npair=np_),
        grid=(np_,),
        in_specs=[pl.BlockSpec(memory_space=pltpu.SMEM),spec(0),spec(np_),spec(2*np_)],
        out_specs=[pl.BlockSpec((L,128),lambda p:(0,p)),pl.BlockSpec((L,128),lambda p:(0,p)),pl.BlockSpec((L,128),lambda p:(0,0))],
        out_shape=[jax.ShapeDtypeStruct((L,D),BF),jax.ShapeDtypeStruct((L,D),F32),jax.ShapeDtypeStruct((L,128),F32)],
        compiler_params=pltpu.CompilerParams(dimension_semantics=("arbitrary",),vmem_limit_bytes=60*2**20),
    )(lengths,packed,packed,packed)

def bwd_kernel(len_ref, q_ref, k_ref, v_ref, do_ref, of_ref, lse_ref, dq_ref, dk_ref, dv_ref, *, tq):
    p=pl.program_id(0)
    L=q_ref.shape[0]
    n=len_ref[0]
    lane=lane_iota((L,128))
    k=k_ref[...]; v=v_ref[...]
    kpos=lax.broadcasted_iota(jnp.int32,(L,128),0)
    bias=jnp.where(kpos<n,0.0,NEG).astype(BF)
    zero=jnp.zeros((L,128),BF); one=jnp.ones((L,128),BF)
    kk=[]; vv=[]; kz=[]
    for h in range(2):
        mine=(lane<64) if h==0 else (lane>=64)
        b=64*(1-h)
        kk.append(jnp.where(mine,k,jnp.where(lane==b,bias,jnp.where((lane>b)&(lane<b+4),one,zero))))
        vv.append(jnp.where(mine,v,jnp.where((lane>b)&(lane<b+4),one,zero)))
    lq=lane_iota((tq,128))
    dka=[jnp.zeros((L,128),F32)]*2; dva=[jnp.zeros((L,128),F32)]*2
    for i in range(L//tq):
        sl=pl.ds(i*tq,tq)
        q=q_ref[sl,:]; do=do_ref[sl,:]; of=of_ref[sl,:]; lse=lse_ref[sl,:]
        prod=of*do.astype(F32)
        dqs=[]
        for h in range(2):
            mine=(lq<64) if h==0 else (lq>=64)
            b=64*(1-h)
            delta=-jnp.sum(jnp.where(mine,prod,0.0),axis=1,keepdims=True)
            ls=-jnp.sum(jnp.where(lq==2*p+h,lse,0.0),axis=1,keepdims=True)*(1.0/C)
            def aug(x,t,first):
                hi,mid,lo=parts3(jnp.broadcast_to(t,(tq,128)))
                y=jnp.where(lq==b,jnp.full((tq,128),first,BF),jnp.where(lq==b+1,hi,jnp.where(lq==b+2,mid,jnp.where(lq==b+3,lo,jnp.zeros((tq,128),BF)))))
                return jnp.where(mine,x,y)
            qa=aug(q,ls,1.0); da=aug(do,delta,0.0)
            st=lax.dot_general(kk[h],qa,(((1,),(1,)),((),())),preferred_element_type=F32)
            pt=jnp.exp2(st*C)
            dpt=lax.dot_general(vv[h],da,(((1,),(1,)),((),())),preferred_element_type=F32)
            ds=(pt*dpt).astype(BF)
            dva[h]=dva[h]+jnp.dot(pt.astype(BF),do,preferred_element_type=F32)
            dka[h]=dka[h]+jnp.dot(ds,q,preferred_element_type=F32)
            dqs.append(lax.dot_general(ds,k,(((0,),(0,)),((),())),preferred_element_type=F32))
        dq_ref[sl,:]=(jnp.where(lq<64,dqs[0],dqs[1])*SCALE).astype(BF)
    dk_ref[...]=(jnp.where(lane<64,dka[0],dka[1])*SCALE).astype(BF)
    dv_ref[...]=jnp.where(lane<64,dva[0],dva[1]).astype(BF)

def att_bwd(lengths, packed, do, of, lse, tq=256):
    L=packed.shape[0]; D=packed.shape[1]//3; np_=D//128
    spec=lambda off: pl.BlockSpec((L,128),lambda p,off=off:(0,off+p))
    return pl.pallas_call(functools.partial(bwd_kernel,tq=tq),
        grid=(np_,),
        in_specs=[pl.BlockSpec(memory_space=pltpu.SMEM),spec(0),spec(np_),spec(2*np_),spec(0),spec(0),pl.BlockSpec((L,128),lambda p:(0,0))],
        out_specs=[spec(0)]*3,
        out_shape=[jax.ShapeDtypeStruct((L,D),BF)]*3,
        compiler_params=pltpu.CompilerParams(dimension_semantics=("arbitrary",),vmem_limit_bytes=60*2**20),
    )(lengths,packed,packed,packed,do,of,lse)

ISQ2=0.7071067811865476; ISQ2PI=0.3989422804014327
def gelu_both(x):
    phi=0.5+0.5*lax.erf(x*ISQ2)
    g=x*phi
    dg=phi+x*(jnp.exp2((x*x)*(-0.5*LOG2E))*ISQ2PI)
    return g,dg
NN=(((1,),(0,)),((),())); NT=(((1,),(1,)),((),())); TN=(((0,),(0,)),((),()))
def dotf(a,b,dn): return lax.dot_general(a,b,dn,preferred_element_type=F32)
def mlp_kernel(sec_ref, br_ref, win_ref, wout_ref, hid_ref, sg_ref, din_ref, dout_ref, act_s, eg_s, *, tr):
    j=pl.program_id(0)
    L=sec_ref.shape[0]
    win=win_ref[0]; wout=wout_ref[0]
    def row(i,_):
        sl=pl.ds(pl.multiple_of(i*tr,tr),tr)
        e=dotf(sec_ref[sl,:],win,NN)
        ag=dotf(br_ref[sl,:],wout,NN)
        g,dg=gelu_both(e)
        act=g.astype(BF); eg=(ag*dg).astype(BF)
        act_s[sl,:]=act; eg_s[sl,:]=eg
        h=dotf(act,wout,NT); s=dotf(eg,win,NT)
        @pl.when(j==0)
        def _():
            hid_ref[sl,:]=h; sg_ref[sl,:]=s
        @pl.when(j>0)
        def _():
            hid_ref[sl,:]+=h; sg_ref[sl,:]+=s
        return 0
    lax.fori_loop(0,L//tr,row,0)
    din_ref[0]=dotf(sec_ref[...],eg_s[...],TN).astype(din_ref.dtype)
    dout_ref[0]=dotf(br_ref[...],act_s[...],TN).astype(dout_ref.dtype)
def mlp(sec,br,win,wout,tr=256,gdt=BF):
    L,D=sec.shape; M,_,Fb=win.shape
    full=pl.BlockSpec((L,D),lambda j:(0,0)); blk=pl.BlockSpec((1,D,Fb),lambda j:(j,0,0))
    return pl.pallas_call(functools.partial(mlp_kernel,tr=tr),grid=(M,),
        in_specs=[full,full,blk,blk],out_specs=[full,full,blk,blk],
        out_shape=[jax.ShapeDtypeStruct((L,D),F32)]*2+[jax.ShapeDtypeStruct((M,D,Fb),gdt)]*2,
        scratch_shapes=[pltpu.VMEM((L,Fb),BF)]*2,
        compiler_params=pltpu.CompilerParams(dimension_semantics=("arbitrary",),vmem_limit_bytes=60*2**20))(sec,br,win,wout)

ALL = ("dp", "mp")
WIRE = ("mp", "dp")


def norm_stats(v):
    centre = v - jnp.mean(v, axis=-1, keepdims=True)
    r = lax.rsqrt(jnp.mean(centre * centre, axis=-1, keepdims=True) + 1e-06)
    return centre * r, r


def norm_pull(e, xhat, r, g):
    y = e * g
    back = r * (y - jnp.mean(y, axis=-1, keepdims=True) - xhat * jnp.mean(y * xhat, axis=-1, keepdims=True))
    return back, jnp.sum(e * xhat, axis=0), jnp.sum(e, axis=0)


def per_device(inputs, lengths, attn_qkv, attn_proj, mlp_in, mlp_out, norm_gain, norm_bias, cotangent):
    n_dp, n_mp = lax.axis_size("dp"), lax.axis_size("mp")
    n = n_dp * n_mp
    slots, width = inputs.shape
    rows = attn_qkv.shape[1]
    norms = jnp.concatenate([norm_gain[0], norm_bias[0]], axis=0).reshape(1, 4 * rows)
    norms = jnp.pad(norms, ((0, 0), (0, 3 * width - 4 * rows)))
    first = lax.all_gather(jnp.concatenate([attn_qkv[0], norms], axis=0), ALL, axis=0)
    second_part = jnp.concatenate([mlp_in[0].reshape(-1, 256), mlp_out[0].T.reshape(-1, 256)], axis=0)
    rest = lax.all_gather(second_part, WIRE, axis=0)
    proj_w = lax.all_gather(attn_proj[0], ALL, axis=0, tiled=True)
    qkv_w = first[:, :rows].reshape(width, 3 * width)
    params = first[:, rows, : 4 * rows].reshape(n, 4, rows).transpose(1, 0, 2).reshape(4, width).astype(F32)
    block = mlp_in.shape[2]
    win, wout = rest.reshape(n, 2, -1, block).transpose(1, 0, 2, 3).reshape(2, n_mp, width, block)

    hidden = inputs.astype(F32)
    xhat0, r0 = norm_stats(hidden)
    normed = (xhat0 * params[0] + params[2]).astype(BF)
    packed = jnp.dot(normed, qkv_w, preferred_element_type=F32).astype(BF)
    mixed, mixed_wide, logsum = att_fwd(lengths, packed, tq=min(512, slots))
    middle = hidden + jnp.dot(mixed, proj_w, preferred_element_type=F32)
    xhat1, r1 = norm_stats(middle)
    second = (xhat1 * params[1] + params[3]).astype(BF)
    valid = lax.iota(jnp.int32, slots) < lengths[0]
    branch = jnp.where(valid[:, None], cotangent, jnp.zeros_like(cotangent))
    mlp_sum, second_grad, in_grad, out_grad = mlp(second, branch, win, wout, tr=min(512, slots))
    outputs = (middle + mlp_sum).astype(BF)
    both = jnp.stack([in_grad, out_grad]).reshape(2, n, -1, block).transpose(1, 0, 2, 3)
    both = lax.psum_scatter(both, WIRE, scatter_dimension=0, tiled=False)
    part, gain1, bias1 = norm_pull(second_grad, xhat1, r1, params[1])
    middle_grad = branch.astype(F32) + part
    attn_low = middle_grad.astype(BF)
    proj_grad = lax.dot_general(mixed, attn_low, TN, preferred_element_type=F32).astype(BF)
    mixed_grad = lax.dot_general(attn_low, proj_w, NT, preferred_element_type=F32).astype(BF)
    packed_grad = jnp.concatenate(att_bwd(lengths, packed, mixed_grad, mixed_wide, logsum), axis=1)
    qkv_grad = lax.dot_general(normed, packed_grad, TN, preferred_element_type=F32).astype(BF)
    tail = jnp.concatenate([qkv_grad, proj_grad], axis=1).reshape(n, rows, 4 * width)
    tail = lax.psum_scatter(tail, ALL, scatter_dimension=0, tiled=False)
    normed_grad = lax.dot_general(packed_grad, qkv_w, NT, preferred_element_type=F32)
    part, gain0, bias0 = norm_pull(normed_grad, xhat0, r0, params[0])
    input_grad = middle_grad + part
    norm_grads = lax.psum(jnp.stack([gain0, gain1, bias0, bias1]), ALL)
    at = (lax.axis_index("dp") * n_mp + lax.axis_index("mp")) * rows
    mine = lax.dynamic_slice(norm_grads, (0, at), (4, rows))
    return (
        outputs,
        input_grad,
        tail[None, :, : 3 * width].astype(F32),
        tail[None, :, 3 * width :].astype(F32),
        both[0].astype(F32)[None],
        both[1].astype(F32).T[None],
        mine[None, :2],
        mine[None, 2:],
    )


def solution(mesh):
    wide = P(ALL, None)
    return jax.shard_map(
        per_device,
        mesh=mesh,
        in_specs=(wide, P(ALL), P(None, ALL, None), P(None, ALL, None), P(None, "dp", "mp"), P(None, "mp", "dp"),
                  P(None, None, ALL), P(None, None, ALL), wide),
        out_specs=(wide, wide, P(None, ALL, None), P(None, ALL, None), P(None, "dp", "mp"), P(None, "mp", "dp"),
                   P(None, None, ALL), P(None, None, ALL)),
        check_vma=False,
    )
```

```python
import functools

import jax
import jax.numpy as jnp
from jax import lax
from jax.experimental import pallas as pl
from jax.experimental.pallas import tpu as pltpu
from jax.sharding import PartitionSpec as P

F32, BF = jnp.float32, jnp.bfloat16
MESH = pl.DeviceIdType.MESH
HEAD_DIM = 64
SCALE = 0.125
LOG2E = 1.4426950408889634
TO_LOG2 = SCALE * LOG2E
NEG = -1e30
EPS = 1e-06
NN = (((1,), (0,)), ((), ()))
NT = (((1,), (1,)), ((), ()))
TN = (((0,), (0,)), ((), ()))
VMEM_LIMIT = 60 * 2**20
ANY = pl.BlockSpec(memory_space=pl.ANY)
VMEM = pl.BlockSpec(memory_space=pltpu.VMEM)
SMEM = pl.BlockSpec(memory_space=pltpu.SMEM)
DMA = pltpu.SemaphoreType.DMA


def dot(a, b, dims):
    return lax.dot_general(a, b, dims, preferred_element_type=F32)


def params_of(collective_id=None, grid=0):
    extra = {} if collective_id is None else {"collective_id": collective_id, "has_side_effects": True}
    if grid:
        extra["dimension_semantics"] = ("arbitrary",) * grid
    return pltpu.CompilerParams(vmem_limit_bytes=VMEM_LIMIT, **extra)


class Place:
    def __init__(self):
        n_dp, self.M = lax.axis_size("dp"), lax.axis_size("mp")
        self.G = n_dp // 2
        dp = lax.axis_index("dp")
        self.g, self.c, self.z = dp // 2, lax.rem(dp, 2), lax.axis_index("mp")
        self.square = self.G == 4
        if self.square:
            self.chips = [self.g ^ 1, self.g ^ 2]
            self.diag = self.g ^ 3
        else:
            self.chips = [lax.rem(self.g + d, self.G) for d in range(1, self.G)]

    def chip(self, h):
        return (h * 2 + self.c, self.z)

    def core(self):
        return (self.g * 2 + 1 - self.c, self.z)

    def along(self, z):
        return (self.g * 2 + self.c, z)

    def plus(self, d):
        return lax.rem(self.z + d, self.M)

    def minus(self, d):
        return lax.rem(self.z + self.M - d, self.M)

    def greet(self):
        sem = pltpu.get_barrier_semaphore()
        peers = [self.along(self.plus(d)) for d in range(1, self.M)]
        peers += [self.chip(self.chips[i]) for i in self.back()] + [self.core()]
        for dev in peers:
            pl.semaphore_signal(sem, inc=1, device_id=dev, device_id_type=MESH)
        pl.semaphore_wait(sem, len(peers))

    def back(self):
        return range(len(self.chips))


def remote(src, dst, send, recv, dev):
    return pltpu.make_async_remote_copy(src_ref=src, dst_ref=dst, send_sem=send, recv_sem=recv, device_id=dev, device_id_type=MESH)


class GatherUnit:
    def __init__(self, at, own, slot, d, way, sends, recvs):
        self.at, self.own, self.slot, self.d, self.way = at, own, slot, d, way
        self.sends, self.recvs = sends, recvs
        self.src_z = at.plus(d)

    @staticmethod
    def count(G):
        return 2 + (3 if G == 4 else G - 1) + G

    def mine(self, h, c):
        return self.slot(self.src_z, h, c)

    def start_z(self):
        if self.d:
            at = self.at
            remote(self.own, self.slot(at.z, at.g, at.c), self.sends.at[0], self.recvs.at[0], at.along(at.minus(self.d))).start()
        else:
            self._local().start()

    def _local(self):
        at = self.at
        return pltpu.make_async_copy(self.own, self.slot(at.z, at.g, at.c), self.sends.at[0])

    def _z(self):
        at = self.at
        here = self.mine(at.g, at.c)
        return remote(here, here, self.sends.at[0], self.recvs.at[0], at.along(at.minus(self.d)))

    def _to_chip(self, i, src=None):
        at = self.at
        here = self.mine(at.g, at.c)
        return remote(here if src is None else src, here, self.sends.at[1 + i], self.recvs.at[1 + i], at.chip(at.chips[i]))

    def _relay(self):
        at = self.at
        block = self.mine(at.chips[self.way], at.c)
        return remote(block, block, self.sends.at[3], self.recvs.at[3], at.chip(at.chips[1 - self.way]))

    def _to_core(self, i, h, src=None):
        at = self.at
        block = self.mine(h, at.c)
        k = self.count(at.G) - at.G + i
        return remote(block if src is None else src, block, self.sends.at[k], self.recvs.at[k], at.core())

    def spread(self):
        src = None
        if self.d:
            self._z().wait_recv()
        else:
            src = self.own
        for i in range(len(self.at.chips)):
            self._to_chip(i, src).start()
        self._to_core(0, self.at.g, src).start()

    def relay(self):
        at = self.at
        for i in range(len(at.chips)):
            self._to_chip(i).wait_recv()
        if at.square:
            self._relay().start()
        for i, h in enumerate(at.chips):
            self._to_core(1 + i, h).start()

    def last(self):
        at = self.at
        if at.square:
            self._relay().wait_recv()
            self._to_core(3, at.diag).start()

    def finish(self):
        at = self.at
        if self.d:
            self._z().wait_send()
        else:
            self._local().wait()
        for i in range(len(at.chips)):
            self._to_chip(i).wait_send()
        if at.square:
            self._relay().wait_send()
        for i, h in enumerate([at.g] + at.chips + ([at.diag] if at.square else [])):
            self._to_core(i, h).wait()

    STAGES = ("spread", "relay", "last", "finish")


class SumUnit:
    def __init__(self, at, part, own, got, near, diag, out, far, total, d, way, sends, recvs, local=None):
        self.at, self.part, self.own, self.got, self.near, self.diagonal = at, part, own, got, near, diag
        self.out, self.far, self.total, self.d, self.way = out, far, total, d, way
        self.sends, self.recvs, self.local = sends, recvs, local
        self.dest_z = at.plus(d)

    @staticmethod
    def count(G):
        return 3 + (3 if G == 4 else G)

    def _core(self):
        at = self.at
        return remote(self.part(1 - at.c), self.got, self.sends.at[0], self.recvs.at[0], at.core())

    def _local(self):
        return pltpu.make_async_copy(self.part(self.at.c), self.own, self.sends.at[2])

    def _diag(self):
        at = self.at
        return remote(self.got.at[at.diag], self.diagonal, self.sends.at[5], self.recvs.at[5], at.chip(at.chips[1 - self.way]))

    def _chip(self, i):
        at = self.at
        k = 3 + i
        return remote(self.got.at[at.chips[i]], self.near.at[i], self.sends.at[k], self.recvs.at[k], at.chip(at.chips[i]))

    def _z(self):
        at = self.at
        return remote(self.out, self.far, self.sends.at[1], self.recvs.at[1], at.along(self.dest_z))

    def start(self):
        self._core().start()
        if self.local:
            self._local().start()

    def pair(self):
        at = self.at
        self._core().wait_recv()
        if self.local:
            self._local().wait()
            own = self.own
        else:
            own = self.part(at.c)
        self.got[...] = (self.got[...].astype(F32) + own[...].astype(F32)).astype(BF)
        if at.square:
            self._diag().start()
        else:
            for i in range(len(at.chips)):
                self._chip(i).start()

    def cross(self):
        at = self.at
        if at.square:
            self._diag().wait_recv()
            h = at.chips[self.way]
            self.got[h] = (self.got[h].astype(F32) + self.diagonal[...].astype(F32)).astype(BF)
            for i in range(2):
                self._chip(i).start()

    def join(self):
        at = self.at
        value = self.got[at.g].astype(F32)
        for i in range(len(at.chips)):
            self._chip(i).wait_recv()
            value = value + self.near[i].astype(F32)
        if self.d:
            self.out[...] = value.astype(BF)
            self._z().start()
        else:
            self.total[...] = value

    def close(self):
        if self.d:
            self._z().wait_recv()
            self.total[...] += self.far[...].astype(F32)

    def finish(self):
        at = self.at
        self._core().wait_send()
        if self.d:
            self._z().wait_send()
        for i in range(len(at.chips)):
            self._chip(i).wait_send()
        if at.square:
            self._diag().wait_send()

    STAGES = ("start", "pair", "cross", "join", "close", "finish")


class SmallSum:
    def __init__(self, at, have, got, sends, recvs):
        self.at, self.have, self.got, self.sends, self.recvs = at, have, got, sends, recvs
        hops = [[at.along(at.plus(d)) for d in range(1, at.M)]]
        if at.square:
            hops += [[at.chip(h)] for h in at.chips]
        else:
            hops += [[at.chip(h) for h in at.chips]]
        self.hops = hops + [[at.core()]]

    @staticmethod
    def counts(G, M):
        return (5 if G == 4 else 4), (M - 1) + (2 if G == 4 else G - 1) + 1

    def _copies(self, s):
        base = sum(len(h) for h in self.hops[:s])
        return [
            remote(self.have.at[s], self.got.at[base + i], self.sends.at[base + i], self.recvs.at[base + i], dev)
            for i, dev in enumerate(self.hops[s])
        ], base

    def stage(self, s):
        if s:
            copies, base = self._copies(s - 1)
            value = self.have[s - 1]
            for i, cp in enumerate(copies):
                cp.wait_recv()
                value = value + self.got[base + i]
            self.have[s] = value
        if s < len(self.hops):
            for cp in self._copies(s)[0]:
                cp.start()

    def finish(self):
        for s in range(len(self.hops)):
            for cp in self._copies(s)[0]:
                cp.wait_send()


def norm_stats(v):
    centre = v - jnp.mean(v, axis=-1, keepdims=True)
    r = lax.rsqrt(jnp.mean(centre * centre, axis=-1, keepdims=True) + EPS)
    return centre * r, r


def norm_pull(e, xhat, r, g):
    y = e * g
    return r * (y - jnp.mean(y, axis=-1, keepdims=True) - xhat * jnp.mean(y * xhat, axis=-1, keepdims=True))


def order_of(M):
    return sorted(range(M), key=lambda d: (min(d, M - d), d))


def entry_kernel(x_ref, shard_ref, placed_ref, w_ref, normed_ref, params_ref, have, got, sends, recvs, small_sends, small_recvs, *, rows):
    at = Place()
    at.greet()
    slot = lambda z, g, c: w_ref.at[:, g, c, z]
    units = [GatherUnit(at, shard_ref, slot, d, k % 2, sends.at[d], recvs.at[d]) for k, d in enumerate(order_of(at.M))]
    small = SmallSum(at, have, got, small_sends, small_recvs)
    have[0] = placed_ref[...]
    for u in units:
        u.start_z()
    units[0].spread()
    last = len(small.hops)
    small.stage(0)
    pending = 1
    for k in range(1, len(units) + 3):
        if k < len(units):
            units[k].spread()
        if 0 <= k - 1 < len(units):
            units[k - 1].relay()
        if 0 <= k - 2 < len(units):
            units[k - 2].last()
        if pending <= last:
            small.stage(pending)
            pending += 1
    while pending <= last:
        small.stage(pending)
        pending += 1
    params_ref[...] = have[last]
    gain, bias = have[last, 0:1, :], have[last, 2:3, :]

    def norm(i, carry):
        sl = pl.ds(pl.multiple_of(i * rows, rows), rows)
        xhat, _ = norm_stats(x_ref[sl, :].astype(F32))
        normed_ref[sl, :] = (xhat * gain + bias).astype(BF)
        return carry

    lax.fori_loop(0, x_ref.shape[0] // rows, norm, 0)
    for u in units:
        u.finish()
    small.finish()


def entry(x, shard, placed):
    at_G, M = lax.axis_size("dp") // 2, lax.axis_size("mp")
    L, D = x.shape
    n_have, n_got = SmallSum.counts(at_G, M)
    sems = (M, GatherUnit.count(at_G))
    return pl.pallas_call(
        functools.partial(entry_kernel, rows=min(256, L)),
        in_specs=[VMEM, ANY, VMEM],
        out_specs=[ANY, VMEM, VMEM],
        out_shape=[
            jax.ShapeDtypeStruct((3, at_G, 2, M) + shard.shape[1:], BF),
            jax.ShapeDtypeStruct((L, D), BF),
            jax.ShapeDtypeStruct(placed.shape, F32),
        ],
        scratch_shapes=[
            pltpu.VMEM((n_have,) + placed.shape, F32),
            pltpu.VMEM((n_got,) + placed.shape, F32),
            DMA(sems), DMA(sems), DMA((n_got,)), DMA((n_got,)),
        ],
        compiler_params=params_of(0),
    )(x, shard, placed)


def qkv_kernel(x_ref, w_ref, o_ref):
    o_ref[...] = dot(x_ref[...], w_ref[0], NN).astype(BF)


def qkv_matmul(x, w):
    L, D = x.shape
    return pl.pallas_call(
        qkv_kernel,
        grid=(3,),
        in_specs=[pl.BlockSpec((L, D), lambda t: (0, 0)), pl.BlockSpec((1, D, D), lambda t: (t, 0, 0))],
        out_specs=pl.BlockSpec((L, D), lambda t: (0, t)),
        out_shape=jax.ShapeDtypeStruct((L, 3 * D), BF),
        compiler_params=params_of(grid=1),
    )(x, w)


def lanes(shape):
    return lax.broadcasted_iota(jnp.int32, shape, len(shape) - 1)


def three_parts(x):
    hi = x.astype(BF)
    rest = x - hi.astype(F32)
    mid = rest.astype(BF)
    return hi, mid, (rest - mid.astype(F32)).astype(BF)


def mask_bias(shape, length):
    return jnp.where(lax.broadcasted_iota(jnp.int32, shape, 0) < length, 0.0, NEG).astype(BF)


def attend_step(p, len_ref, q_ref, k_ref, v_ref, o_ref, wide_ref, lse_ref, tq, between):
    L = q_ref.shape[0]
    lane = lanes((L, 128))
    k, v = k_ref[...], v_ref[...]
    bias = mask_bias((L, 128), len_ref[0])
    zero, one = jnp.zeros((L, 128), BF), jnp.ones((L, 128), BF)

    @pl.when(p == 0)
    def _():
        lse_ref[...] = jnp.zeros_like(lse_ref)

    keys, values = [], []
    for h in range(2):
        mine = (lane < 64) if h == 0 else (lane >= 64)
        spare = 64 * (1 - h)
        keys.append(jnp.where(mine, k, jnp.where(lane == spare, bias, zero)))
        values.append(jnp.where(mine, v, jnp.where(lane == spare, one, zero)))
    lq = lanes((tq, 128))
    for i in range(L // tq):
        between(i)
        sl = pl.ds(i * tq, tq)
        q = q_ref[sl, :]
        outs, sums = [], []
        for h in range(2):
            mine = (lq < 64) if h == 0 else (lq >= 64)
            spare = 64 * (1 - h)
            q_h = jnp.where(mine, q, jnp.where(lq == spare, jnp.ones((tq, 128), BF), jnp.zeros((tq, 128), BF)))
            s = dot(q_h, keys[h], NT)
            top = jnp.max(s, axis=1, keepdims=True) * TO_LOG2
            e = jnp.exp2(s * TO_LOG2 - top)
            o = dot(e.astype(BF), values[h], NN)
            total = o[:, spare : spare + 1]
            outs.append(o / total)
            sums.append(top + jnp.log2(total))
        out = jnp.where(lq < 64, outs[0], outs[1])
        wide_ref[sl, :] = out
        o_ref[sl, :] = out.astype(BF)
        lse = lse_ref[sl, :]
        lse = jnp.where(lq == 2 * p, sums[0], lse)
        lse_ref[sl, :] = jnp.where(lq == 2 * p + 1, sums[1], lse)


def attend_back_step(p, len_ref, q_ref, k_ref, v_ref, do_ref, wide_ref, lse_ref, dq_ref, dk_ref, dv_ref, tq, between):
    L = q_ref.shape[0]
    lane = lanes((L, 128))
    k, v = k_ref[...], v_ref[...]
    bias = mask_bias((L, 128), len_ref[0])
    zero, one = jnp.zeros((L, 128), BF), jnp.ones((L, 128), BF)
    keys, values = [], []
    for h in range(2):
        mine = (lane < 64) if h == 0 else (lane >= 64)
        b = 64 * (1 - h)
        ones = jnp.where((lane > b) & (lane < b + 4), one, zero)
        keys.append(jnp.where(mine, k, jnp.where(lane == b, bias, ones)))
        values.append(jnp.where(mine, v, ones))
    lq = lanes((tq, 128))
    dk, dv = [jnp.zeros((L, 128), F32)] * 2, [jnp.zeros((L, 128), F32)] * 2
    for i in range(L // tq):
        between(i)
        sl = pl.ds(i * tq, tq)
        q, do, lse = q_ref[sl, :], do_ref[sl, :], lse_ref[sl, :]
        product = wide_ref[sl, :] * do.astype(F32)
        dq = []
        for h in range(2):
            mine = (lq < 64) if h == 0 else (lq >= 64)
            b = 64 * (1 - h)
            minus_delta = -jnp.sum(jnp.where(mine, product, 0.0), axis=1, keepdims=True)
            minus_lse = -jnp.sum(jnp.where(lq == 2 * p + h, lse, 0.0), axis=1, keepdims=True) * (1.0 / TO_LOG2)

            def with_spare(x, term, first):
                hi, mid, lo = three_parts(jnp.broadcast_to(term, (tq, 128)))
                low = jnp.where(lq == b + 2, mid, jnp.where(lq == b + 3, lo, jnp.zeros((tq, 128), BF)))
                low = jnp.where(lq == b, jnp.full((tq, 128), first, BF), jnp.where(lq == b + 1, hi, low))
                return jnp.where(mine, x, low)

            st = dot(keys[h], with_spare(q, minus_lse, 1.0), NT)
            pt = jnp.exp2(st * TO_LOG2)
            dpt = dot(values[h], with_spare(do, minus_delta, 0.0), NT)
            ds = (pt * dpt).astype(BF)
            dv[h] = dv[h] + dot(pt.astype(BF), do, NN)
            dk[h] = dk[h] + dot(ds, q, NN)
            dq.append(dot(ds, k, TN))
        dq_ref[sl, :] = (jnp.where(lq < 64, dq[0], dq[1]) * SCALE).astype(BF)
    dk_ref[...] = (jnp.where(lane < 64, dk[0], dk[1]) * SCALE).astype(BF)
    dv_ref[...] = jnp.where(lane < 64, dv[0], dv[1]).astype(BF)


def at_slots(p, per_step, plan):
    def between(i):
        for slot, actions in sorted(plan.items()):
            if slot % per_step == i:

                @pl.when(p == slot // per_step)
                def _(actions=actions):
                    for action in actions:
                        action()

    return between


def attend_kernel(len_ref, q_ref, k_ref, v_ref, proj_ref, in_ref, out_ref, o_ref, wide_ref, lse_ref, wproj_ref, win_ref, wout_ref,
                  sends, recvs, *, tq):
    p, steps = pl.program_id(0), pl.num_programs(0)
    n_steps = (wide_ref.shape[1] if False else None)
    at = Place()
    parts = q_ref.shape[0] // tq
    units = []
    M = at.M

    def add(own, slot, d, way):
        k = len(units)
        units.append(GatherUnit(at, own, slot, d, way, sends.at[k], recvs.at[k]))

    for k, d in enumerate(order_of(M)):
        add(proj_ref, lambda z, g, c: wproj_ref.at[g, c, z], d, k % 2)
    for d in order_of(M):
        add(in_ref, lambda z, g, c: win_ref.at[z, g, c], d, 0)
        add(out_ref, lambda z, g, c: wout_ref.at[z, g, c], d, 1)

    plan = {}

    def put(slot, action):
        plan.setdefault(slot, []).append(action)

    put(0, at.greet)
    for u in units:
        put(0, u.start_z)
    last_slot = ATTEND_STEPS * parts - 1
    groups = [units[:M]] + [units[M + 2 * i : M + 2 * i + 2] for i in range(M)]
    for n, group in enumerate(groups):
        for s, name in enumerate(("spread", "relay", "last")):
            for u in group:
                put(min((n + s) * GATHER_PACE, last_slot), getattr(u, name))
    attend_step(p, len_ref, q_ref, k_ref, v_ref, o_ref, wide_ref, lse_ref, tq, at_slots(p, parts, plan))

    @pl.when(p == steps - 1)
    def _():
        for u in units:
            u.finish()


ATTEND_STEPS = 6
GATHER_PACE = 2


def attend(lengths, packed, proj, w_in, w_out, tq):
    G, M = lax.axis_size("dp") // 2, lax.axis_size("mp")
    L, D = packed.shape[0], packed.shape[1] // 3
    pairs = D // 128
    column = lambda off: pl.BlockSpec((L, 128), lambda p, off=off: (0, off + p))
    sems = (3 * M, GatherUnit.count(G))
    return pl.pallas_call(
        functools.partial(attend_kernel, tq=tq),
        grid=(pairs,),
        in_specs=[SMEM, column(0), column(pairs), column(2 * pairs), ANY, ANY, ANY],
        out_specs=[column(0), column(0), pl.BlockSpec((L, 128), lambda p: (0, 0)), ANY, ANY, ANY],
        out_shape=[
            jax.ShapeDtypeStruct((L, D), BF),
            jax.ShapeDtypeStruct((L, D), F32),
            jax.ShapeDtypeStruct((L, 128), F32),
            jax.ShapeDtypeStruct((G, 2, M) + proj.shape, BF),
            jax.ShapeDtypeStruct((M, G, 2) + w_in.shape, BF),
            jax.ShapeDtypeStruct((M, G, 2) + w_out.shape, BF),
        ],
        scratch_shapes=[DMA(sems), DMA(sems)],
        compiler_params=params_of(1, grid=1),
    )(lengths, packed, packed, packed, proj, w_in, w_out)


def gelu_and_slope(x):
    phi = 0.5 + 0.5 * lax.erf(x * 0.7071067811865476)
    return x * phi, phi + x * (jnp.exp2((x * x) * (-0.5 * LOG2E)) * 0.3989422804014327)


def mlp_kernel(sec_ref, br_ref, win_ref, wout_ref, hid_ref, sg_ref, din_ref, dout_ref, act_s, eg_s, *, tr):
    j = pl.program_id(0)
    win, wout = win_ref[0], wout_ref[0]

    def row(i, carry):
        sl = pl.ds(pl.multiple_of(i * tr, tr), tr)
        value, slope = gelu_and_slope(dot(sec_ref[sl, :], win, NN))
        act = value.astype(BF)
        eg = (dot(br_ref[sl, :], wout, NN) * slope).astype(BF)
        act_s[sl, :], eg_s[sl, :] = act, eg
        h, s = dot(act, wout, NT), dot(eg, win, NT)

        @pl.when(j == 0)
        def _():
            hid_ref[sl, :], sg_ref[sl, :] = h, s

        @pl.when(j > 0)
        def _():
            hid_ref[sl, :] += h
            sg_ref[sl, :] += s

        return carry

    lax.fori_loop(0, sec_ref.shape[0] // tr, row, 0)
    _, cores, G, R, _ = din_ref.shape
    for ref, a, b in ((din_ref, sec_ref, eg_s), (dout_ref, br_ref, act_s)):
        grad = dot(a[...], b[...], TN)
        for g in range(G):
            for c in range(cores):
                k = (g * cores + c) * R
                ref[0, c, g] = grad[k : k + R, :].astype(BF)


def mlp(sec, br, win, wout, tr):
    G, M = lax.axis_size("dp") // 2, lax.axis_size("mp")
    L, D = sec.shape
    Fb = win.shape[2]
    full = pl.BlockSpec((L, D), lambda j: (0, 0))
    block = pl.BlockSpec((1, D, Fb), lambda j: (j, 0, 0))
    grads = (2, G, D // (2 * G), Fb)
    gblock = pl.BlockSpec((1,) + grads, lambda j: (j, 0, 0, 0, 0))
    return pl.pallas_call(
        functools.partial(mlp_kernel, tr=tr),
        grid=(M,),
        in_specs=[full, full, block, block],
        out_specs=[full, full, gblock, gblock],
        out_shape=[jax.ShapeDtypeStruct((L, D), F32)] * 2 + [jax.ShapeDtypeStruct((M,) + grads, BF)] * 2,
        scratch_shapes=[pltpu.VMEM((L, Fb), BF)] * 2,
        compiler_params=params_of(grid=1),
    )(sec, br, win, wout)


def attend_back_kernel(len_ref, q_ref, k_ref, v_ref, do_ref, wide_ref, lse_ref, pin_ref, pout_ref, pproj_ref,
                       dq_ref, dk_ref, dv_ref, din_ref, dout_ref, dproj_ref,
                       own_m, got_m, near_m, diag_m, send_m, far_m, own_p, got_p, near_p, diag_p, send_p, far_p,
                       sends, recvs, *, tq):
    p, steps = pl.program_id(0), pl.num_programs(0)
    at = Place()
    M = at.M
    parts = q_ref.shape[0] // tq
    units = []

    def add(part, bufs, total, d, way):
        k = len(units)
        own, got, near, diag, out, far = bufs
        units.append(SumUnit(at, part, own, got, near, diag, out, far, total, d, way, sends.at[k], recvs.at[k], local=True))

    groups = []
    order = order_of(M)
    for n, d in enumerate(order):
        j = at.plus(d)
        for a, (ref, total) in enumerate(((pin_ref, din_ref), (pout_ref, dout_ref))):
            k = 2 * n + a
            add(lambda c, ref=ref, j=j: ref.at[j, c], [b.at[k] for b in (own_m, got_m, near_m, diag_m, send_m, far_m)], total, d, a)
        groups.append(units[-2:])
    for n, d in enumerate(order):
        j = at.plus(d)
        add(lambda c, j=j: pproj_ref.at[j, c], [b.at[n] for b in (own_p, got_p, near_p, diag_p, send_p, far_p)], dproj_ref, d, n % 2)
    groups.append(units[-M:])
    plan = {}

    def put(slot, action):
        plan.setdefault(slot, []).append(action)

    last_slot = ATTEND_STEPS * parts - 1
    put(0, at.greet)
    for u in units:
        put(0, u.start)
    for n, group in enumerate(groups):
        for s, name in enumerate(("pair", "cross", "join")):
            for u in group:
                put(min(n * SUM_PACE + 2 + s * SUM_LAG, last_slot), getattr(u, name))
    attend_back_step(p, len_ref, q_ref, k_ref, v_ref, do_ref, wide_ref, lse_ref, dq_ref, dk_ref, dv_ref, tq, at_slots(p, parts, plan))

    @pl.when(p == steps - 1)
    def _():
        for u in units:
            u.close()
        for u in units:
            u.finish()


SUM_PACE = 4
SUM_LAG = 4


def sum_buffers(n, G, shape):
    chips = 2 if G == 4 else G - 1
    return [
        pltpu.VMEM((n, G) + shape, BF), pltpu.VMEM((n, G) + shape, BF), pltpu.VMEM((n, chips) + shape, BF),
        pltpu.VMEM((n,) + shape, BF), pltpu.VMEM((n,) + shape, BF), pltpu.VMEM((n,) + shape, BF),
    ]


def attend_back(lengths, packed, do, wide, lse, p_in, p_out, p_proj, tq):
    G, M = lax.axis_size("dp") // 2, lax.axis_size("mp")
    L, D = do.shape
    pairs = D // 128
    column = lambda off: pl.BlockSpec((L, 128), lambda p, off=off: (0, off + p))
    whole = lambda shape: pl.BlockSpec(shape, lambda p: (0,) * len(shape))
    mshape, pshape = p_in.shape[3:], p_proj.shape[3:]
    sems = (3 * M, SumUnit.count(G))
    return pl.pallas_call(
        functools.partial(attend_back_kernel, tq=tq),
        grid=(pairs,),
        in_specs=[SMEM, column(0), column(pairs), column(2 * pairs), column(0), column(0), whole((L, 128)), ANY, ANY, ANY],
        out_specs=[column(0)] * 3 + [whole(mshape), whole(mshape), whole(pshape)],
        out_shape=[jax.ShapeDtypeStruct((L, D), BF)] * 3
        + [jax.ShapeDtypeStruct(mshape, F32)] * 2 + [jax.ShapeDtypeStruct(pshape, F32)],
        scratch_shapes=sum_buffers(2 * M, G, mshape) + sum_buffers(M, G, pshape) + [DMA(sems), DMA(sems)],
        compiler_params=params_of(2, grid=1),
    )(lengths, packed, packed, packed, do, wide, lse, p_in, p_out, p_proj)


def exit_kernel(x_ref, normed_ref, dq_ref, dk_ref, dv_ref, w_ref, mid_ref, second_ref, params_ref,
                grad_ref, qkv_ref, norms_ref,
                parts_s, got_s, near_s, diag_s, send_s, far_s, have, small_got, sends, recvs, small_sends, small_recvs, *, rows):
    at = Place()
    G, M = at.G, at.M
    R = qkv_ref.shape[1]
    small = SmallSum(at, have, small_got, small_sends, small_recvs)
    thirds = (dq_ref, dk_ref, dv_ref)
    order = order_of(M)
    units = []
    for t in range(3):
        group = []
        for n, d in enumerate(order):
            k = t * M + n
            j = at.plus(d)
            group.append(SumUnit(at, lambda c, t=t, j=j: parts_s.at[t, j, c], None, got_s.at[k], near_s.at[k], diag_s.at[k],
                                 send_s.at[k], far_s.at[k], qkv_ref.at[t], d, n % 2, sends.at[k], recvs.at[k]))
        units.append(group)

    def run(t, name):
        for u in units[t]:
            getattr(u, name)()

    def third(t):
        grad = dot(normed_ref[...], thirds[t][...], TN)
        for g in range(G):
            for c in range(2):
                for z in range(M):
                    k = ((g * 2 + c) * M + z) * R
                    parts_s[t, z, c, g] = grad[k : k + R, :].astype(BF)

    third(0)
    at.greet()
    run(0, "start")
    third(1)
    run(1, "start")
    run(0, "pair")
    third(2)
    run(2, "start")
    run(0, "cross")
    run(1, "pair")
    gain = params_ref[0:1, :]
    have[0] = second_ref[...]
    todo = [(1, "cross"), (2, "pair"), (0, "join"), (2, "cross"), (1, "join")]
    L = x_ref.shape[0]
    for i in range(L // rows):
        sl = pl.ds(i * rows, rows)
        e = sum(dot(thirds[t][sl, :], w_ref[t], NT) for t in range(3))
        xhat, r = norm_stats(x_ref[sl, :].astype(F32))
        grad_ref[sl, :] = mid_ref[sl, :] + norm_pull(e, xhat, r, gain)
        have[0, 0:1, :] += jnp.sum(e * xhat, axis=0, keepdims=True)
        have[0, 2:3, :] += jnp.sum(e, axis=0, keepdims=True)
        if i < len(todo):
            run(*todo[i])
    for item in todo[L // rows :]:
        run(*item)
    small.stage(0)
    run(2, "join")
    small.stage(1)
    for t in range(3):
        run(t, "close")
    for s in range(2, len(small.hops) + 1):
        small.stage(s)
    norms_ref[...] = have[len(small.hops)]
    for t in range(3):
        run(t, "finish")
    small.finish()


def leave(x, normed, dq, dk, dv, w, middle_grad, second_sums, params, R):
    G, M = lax.axis_size("dp") // 2, lax.axis_size("mp")
    L, D = x.shape
    n_have, n_got = SmallSum.counts(G, M)
    sems = (3 * M, SumUnit.count(G))
    return pl.pallas_call(
        functools.partial(exit_kernel, rows=min(256, L)),
        in_specs=[VMEM] * 9,
        out_specs=[VMEM] * 3,
        out_shape=[
            jax.ShapeDtypeStruct((L, D), F32),
            jax.ShapeDtypeStruct((3, R, D), F32),
            jax.ShapeDtypeStruct(params.shape, F32),
        ],
        scratch_shapes=[pltpu.VMEM((3, M, 2, G, R, D), BF)] + sum_buffers(3 * M, G, (R, D))[1:]
        + [pltpu.VMEM((n_have,) + params.shape, F32), pltpu.VMEM((n_got,) + params.shape, F32),
           DMA(sems), DMA(sems), DMA((n_got,)), DMA((n_got,))],
        compiler_params=params_of(3),
    )(x, normed, dq, dk, dv, w, middle_grad, second_sums, params)


def per_device(inputs, lengths, attn_qkv, attn_proj, mlp_in, mlp_out, norm_gain, norm_bias, cotangent):
    n_dp, n_mp = lax.axis_size("dp"), lax.axis_size("mp")
    G = n_dp // 2
    L, D = inputs.shape
    R = attn_qkv.shape[1]
    here = (lax.axis_index("dp") * n_mp + lax.axis_index("mp")) * R
    small = jnp.concatenate([norm_gain[0], norm_bias[0]], axis=0).astype(F32)
    placed = lax.dynamic_update_slice(jnp.zeros((8, D), F32), small, (0, here))
    shard = attn_qkv[0].reshape(R, 3, D).transpose(1, 0, 2)
    wqkv, normed, params = entry(inputs, shard, placed)
    wqkv = wqkv.reshape(3, D, D)
    packed = qkv_matmul(normed, wqkv)
    mixed, wide, lse, wproj, win, wout = attend(lengths, packed, attn_proj[0], mlp_in[0], mlp_out[0].T, min(512, L))
    wproj = wproj.reshape(D, D)
    win, wout = win.reshape(n_mp, D, -1), wout.reshape(n_mp, D, -1)

    middle = inputs.astype(F32) + jnp.dot(mixed, wproj, preferred_element_type=F32)
    xhat1, r1 = norm_stats(middle)
    second = (xhat1 * params[1] + params[3]).astype(BF)
    valid = lax.iota(jnp.int32, L) < lengths[0]
    branch = jnp.where(valid[:, None], cotangent, jnp.zeros_like(cotangent))
    mlp_sum, second_grad, p_in, p_out = mlp(second, branch, win, wout, min(512, L))
    outputs = (middle + mlp_sum).astype(BF)
    middle_grad = branch.astype(F32) + norm_pull(second_grad, xhat1, r1, params[1])
    gain1, bias1 = jnp.sum(second_grad * xhat1, axis=0), jnp.sum(second_grad, axis=0)
    second_sums = jnp.zeros((8, D), F32).at[1].set(gain1).at[3].set(bias1)
    attn_low = middle_grad.astype(BF)
    p_proj = lax.dot_general(mixed, attn_low, TN, preferred_element_type=F32).astype(BF)
    p_proj = p_proj.reshape(G, 2, n_mp, R, D).transpose(2, 1, 0, 3, 4)
    mixed_grad = lax.dot_general(attn_low, wproj, NT, preferred_element_type=F32).astype(BF)
    dq, dk, dv, d_in, d_out, d_proj = attend_back(lengths, packed, mixed_grad, wide, lse, p_in, p_out, p_proj, min(256, L))
    input_grad, d_qkv, norms = leave(inputs, normed, dq, dk, dv, wqkv, middle_grad, second_sums, params, R)
    mine = lax.dynamic_slice(norms, (0, here), (4, R))
    return (
        outputs,
        input_grad,
        d_qkv.transpose(1, 0, 2).reshape(1, R, 3 * D),
        d_proj[None],
        d_in[None],
        d_out.T[None],
        mine[None, :2],
        mine[None, 2:],
    )


def solution(mesh):
    everywhere = ("dp", "mp")
    wide, columns, vector = P(everywhere, None), P(None, everywhere, None), P(None, None, everywhere)
    return jax.shard_map(
        per_device,
        mesh=mesh,
        in_specs=(wide, P(everywhere), columns, columns, P(None, "dp", "mp"), P(None, "mp", "dp"), vector, vector, wide),
        out_specs=(wide, wide, columns, columns, P(None, "dp", "mp"), P(None, "mp", "dp"), vector, vector),
        check_vma=False,
    )
```

```python
import functools

import jax
import jax.numpy as jnp
from jax import lax
from jax.experimental import pallas as pl
from jax.experimental.pallas import tpu as pltpu
from jax.sharding import PartitionSpec as P

F32, BF = jnp.float32, jnp.bfloat16
MESH = pl.DeviceIdType.MESH
HEAD_DIM = 64
SCALE = 0.125
LOG2E = 1.4426950408889634
TO_LOG2 = SCALE * LOG2E
NEG = -1e30
EPS = 1e-06
NN = (((1,), (0,)), ((), ()))
NT = (((1,), (1,)), ((), ()))
TN = (((0,), (0,)), ((), ()))
VMEM_LIMIT = 60 * 2**20
ANY = pl.BlockSpec(memory_space=pl.ANY)
VMEM = pl.BlockSpec(memory_space=pltpu.VMEM)
SMEM = pl.BlockSpec(memory_space=pltpu.SMEM)
DMA = pltpu.SemaphoreType.DMA


def dot(a, b, dims):
    return lax.dot_general(a, b, dims, preferred_element_type=F32)


def params_of(collective_id=None, grid=0):
    extra = {} if collective_id is None else {"collective_id": collective_id, "has_side_effects": True}
    if grid:
        extra["dimension_semantics"] = ("arbitrary",) * grid
    return pltpu.CompilerParams(vmem_limit_bytes=VMEM_LIMIT, **extra)


class Place:
    def __init__(self):
        n_dp, self.M = lax.axis_size("dp"), lax.axis_size("mp")
        self.G = n_dp // 2
        dp = lax.axis_index("dp")
        self.g, self.c, self.z = dp // 2, lax.rem(dp, 2), lax.axis_index("mp")
        self.square = self.G == 4
        if self.square:
            self.chips = [self.g ^ 1, self.g ^ 2]
            self.diag = self.g ^ 3
        else:
            self.chips = [lax.rem(self.g + d, self.G) for d in range(1, self.G)]

    def chip(self, h):
        return (h * 2 + self.c, self.z)

    def core(self):
        return (self.g * 2 + 1 - self.c, self.z)

    def along(self, z):
        return (self.g * 2 + self.c, z)

    def plus(self, d):
        return lax.rem(self.z + d, self.M)

    def minus(self, d):
        return lax.rem(self.z + self.M - d, self.M)

    def peers(self):
        return [self.along(self.plus(d)) for d in range(1, self.M)] + [self.chip(h) for h in self.chips] + [self.core()]

    def greet(self):
        for dev in self.peers():
            pl.semaphore_signal(pltpu.get_barrier_semaphore(), inc=1, device_id=dev, device_id_type=MESH)

    def meet(self):
        pl.semaphore_wait(pltpu.get_barrier_semaphore(), len(self.peers()))


def order_of(M):
    return sorted(range(M), key=lambda d: (min(d, M - d), d))


def remote(src, dst, send, recv, dev):
    return pltpu.make_async_remote_copy(src_ref=src, dst_ref=dst, send_sem=send, recv_sem=recv, device_id=dev, device_id_type=MESH)


class GatherUnit:
    def __init__(self, at, own, slot, d, way, sends, recvs):
        self.at, self.own, self.slot, self.d, self.way = at, own, slot, d, way
        self.sends, self.recvs = sends, recvs
        self.src_z = at.plus(d)

    @staticmethod
    def count(G):
        return 2 + (3 if G == 4 else G - 1) + G

    def mine(self, h, c):
        return self.slot(self.src_z, h, c)

    def start_z(self):
        if self.d:
            at = self.at
            remote(self.own, self.slot(at.z, at.g, at.c), self.sends.at[0], self.recvs.at[0], at.along(at.minus(self.d))).start()
        else:
            self._local().start()

    def _local(self):
        at = self.at
        return pltpu.make_async_copy(self.own, self.slot(at.z, at.g, at.c), self.sends.at[0])

    def _z(self):
        at = self.at
        here = self.mine(at.g, at.c)
        return remote(here, here, self.sends.at[0], self.recvs.at[0], at.along(at.minus(self.d)))

    def _to_chip(self, i, src=None):
        at = self.at
        here = self.mine(at.g, at.c)
        return remote(here if src is None else src, here, self.sends.at[1 + i], self.recvs.at[1 + i], at.chip(at.chips[i]))

    def _relay(self):
        at = self.at
        block = self.mine(at.chips[self.way], at.c)
        return remote(block, block, self.sends.at[3], self.recvs.at[3], at.chip(at.chips[1 - self.way]))

    def _to_core(self, i, h, src=None):
        at = self.at
        block = self.mine(h, at.c)
        k = self.count(at.G) - at.G + i
        return remote(block if src is None else src, block, self.sends.at[k], self.recvs.at[k], at.core())

    def spread(self):
        src = None
        if self.d:
            self._z().wait_recv()
        else:
            src = self.own
        for i in range(len(self.at.chips)):
            self._to_chip(i, src).start()
        self._to_core(0, self.at.g, src).start()

    def relay(self):
        at = self.at
        for i in range(len(at.chips)):
            self._to_chip(i).wait_recv()
        if at.square:
            self._relay().start()
        for i, h in enumerate(at.chips):
            self._to_core(1 + i, h).start()

    def last(self):
        at = self.at
        if at.square:
            self._relay().wait_recv()
            self._to_core(3, at.diag).start()

    def finish(self):
        at = self.at
        if self.d:
            self._z().wait_send()
        else:
            self._local().wait()
        for i in range(len(at.chips)):
            self._to_chip(i).wait_send()
        if at.square:
            self._relay().wait_send()
        for i, h in enumerate([at.g] + at.chips + ([at.diag] if at.square else [])):
            self._to_core(i, h).wait()

    STAGES = ("spread", "relay", "last", "finish")


class SumUnit:
    def __init__(self, at, part, own, got, near, diag, out, far, total, d, way, sends, recvs, local=None):
        self.at, self.part, self.own, self.got, self.near, self.diagonal = at, part, own, got, near, diag
        self.out, self.far, self.total, self.d, self.way = out, far, total, d, way
        self.sends, self.recvs, self.local = sends, recvs, local
        self.dest_z = at.plus(d)

    @staticmethod
    def count(G):
        return 3 + (3 if G == 4 else G)

    def _core(self):
        at = self.at
        return remote(self.part(1 - at.c), self.got, self.sends.at[0], self.recvs.at[0], at.core())

    def _local(self):
        return pltpu.make_async_copy(self.part(self.at.c), self.own, self.sends.at[2])

    def _diag(self):
        at = self.at
        return remote(self.got.at[at.diag], self.diagonal, self.sends.at[5], self.recvs.at[5], at.chip(at.chips[1 - self.way]))

    def _chip(self, i):
        at = self.at
        k = 3 + i
        return remote(self.got.at[at.chips[i]], self.near.at[i], self.sends.at[k], self.recvs.at[k], at.chip(at.chips[i]))

    def _z(self):
        at = self.at
        return remote(self.out, self.far, self.sends.at[1], self.recvs.at[1], at.along(self.dest_z))

    def start(self):
        self._core().start()
        if self.local:
            self._local().start()

    def pair(self):
        at = self.at
        self._core().wait_recv()
        if self.local:
            self._local().wait()
            own = self.own
        else:
            own = self.part(at.c)
        self.got[...] = (self.got[...].astype(F32) + own[...].astype(F32)).astype(BF)
        if at.square:
            self._diag().start()
        else:
            for i in range(len(at.chips)):
                self._chip(i).start()

    def cross(self):
        at = self.at
        if at.square:
            self._diag().wait_recv()
            h = at.chips[self.way]
            self.got[h] = (self.got[h].astype(F32) + self.diagonal[...].astype(F32)).astype(BF)
            for i in range(2):
                self._chip(i).start()

    def join(self):
        at = self.at
        value = self.got[at.g].astype(F32)
        for i in range(len(at.chips)):
            self._chip(i).wait_recv()
            value = value + self.near[i].astype(F32)
        if self.d:
            self.out[...] = value.astype(BF)
            self._z().start()
        else:
            self.total[...] = value

    def close(self):
        if self.d:
            self._z().wait_recv()
            self.total[...] += self.far[...].astype(F32)

    def finish(self):
        at = self.at
        self._core().wait_send()
        if self.d:
            self._z().wait_send()
        for i in range(len(at.chips)):
            self._chip(i).wait_send()
        if at.square:
            self._diag().wait_send()

    STAGES = ("start", "pair", "cross", "join", "close", "finish")


class SmallSum:
    def __init__(self, at, have, got, sends, recvs):
        self.at, self.have, self.got, self.sends, self.recvs = at, have, got, sends, recvs
        hops = [[at.along(at.plus(d)) for d in range(1, at.M)]]
        if at.square:
            hops += [[at.chip(h)] for h in at.chips]
        else:
            hops += [[at.chip(h) for h in at.chips]]
        self.hops = hops + [[at.core()]]

    @staticmethod
    def counts(G, M):
        return (5 if G == 4 else 4), (M - 1) + (2 if G == 4 else G - 1) + 1

    def _copies(self, s):
        base = sum(len(h) for h in self.hops[:s])
        return [
            remote(self.have.at[s], self.got.at[base + i], self.sends.at[base + i], self.recvs.at[base + i], dev)
            for i, dev in enumerate(self.hops[s])
        ], base

    def stage(self, s):
        if s:
            copies, base = self._copies(s - 1)
            value = self.have[s - 1]
            for i, cp in enumerate(copies):
                cp.wait_recv()
                value = value + self.got[base + i]
            self.have[s] = value
        if s < len(self.hops):
            for cp in self._copies(s)[0]:
                cp.start()

    def finish(self):
        for s in range(len(self.hops)):
            for cp in self._copies(s)[0]:
                cp.wait_send()


def norm_stats(v):
    centre = v - jnp.mean(v, axis=-1, keepdims=True)
    r = lax.rsqrt(jnp.mean(centre * centre, axis=-1, keepdims=True) + EPS)
    return centre * r, r


def norm_pull(e, xhat, r, g):
    y = e * g
    return r * (y - jnp.mean(y, axis=-1, keepdims=True) - xhat * jnp.mean(y * xhat, axis=-1, keepdims=True))


def entry_kernel(x_ref, shard_ref, placed_ref, w_ref, normed_ref, params_ref, have, got, sends, recvs, small_sends, small_recvs, *, rows):
    at = Place()
    at.greet()
    at.meet()
    slot = lambda z, g, c: w_ref.at[:, g, c, z]
    units = [GatherUnit(at, shard_ref, slot, d, k % 2, sends.at[d], recvs.at[d]) for k, d in enumerate(order_of(at.M))]
    small = SmallSum(at, have, got, small_sends, small_recvs)
    have[0] = placed_ref[...]
    for u in units:
        u.start_z()
    units[0].spread()
    last = len(small.hops)
    small.stage(0)
    pending = 1
    for k in range(1, len(units) + 3):
        if k < len(units):
            units[k].spread()
        if 0 <= k - 1 < len(units):
            units[k - 1].relay()
        if 0 <= k - 2 < len(units):
            units[k - 2].last()
        if pending <= last:
            small.stage(pending)
            pending += 1
    while pending <= last:
        small.stage(pending)
        pending += 1
    params_ref[...] = have[last]
    gain, bias = have[last, 0:1, :], have[last, 2:3, :]

    def norm(i, carry):
        sl = pl.ds(pl.multiple_of(i * rows, rows), rows)
        xhat, _ = norm_stats(x_ref[sl, :].astype(F32))
        normed_ref[sl, :] = (xhat * gain + bias).astype(BF)
        return carry

    lax.fori_loop(0, x_ref.shape[0] // rows, norm, 0)
    for u in units:
        u.finish()
    small.finish()


def entry(x, shard, placed):
    at_G, M = lax.axis_size("dp") // 2, lax.axis_size("mp")
    L, D = x.shape
    n_have, n_got = SmallSum.counts(at_G, M)
    sems = (M, GatherUnit.count(at_G))
    return pl.pallas_call(
        functools.partial(entry_kernel, rows=min(256, L)),
        in_specs=[VMEM, ANY, VMEM],
        out_specs=[ANY, VMEM, VMEM],
        out_shape=[
            jax.ShapeDtypeStruct((3, at_G, 2, M) + shard.shape[1:], BF),
            jax.ShapeDtypeStruct((L, D), BF),
            jax.ShapeDtypeStruct(placed.shape, F32),
        ],
        scratch_shapes=[
            pltpu.VMEM((n_have,) + placed.shape, F32),
            pltpu.VMEM((n_got,) + placed.shape, F32),
            DMA(sems), DMA(sems), DMA((n_got,)), DMA((n_got,)),
        ],
        compiler_params=params_of(0),
    )(x, shard, placed)


def qkv_kernel(x_ref, w_ref, o_ref):
    o_ref[...] = dot(x_ref[...], w_ref[0], NN).astype(BF)


def qkv_matmul(x, w):
    L, D = x.shape
    return pl.pallas_call(
        qkv_kernel,
        grid=(3,),
        in_specs=[pl.BlockSpec((L, D), lambda t: (0, 0)), pl.BlockSpec((1, D, D), lambda t: (t, 0, 0))],
        out_specs=pl.BlockSpec((L, D), lambda t: (0, t)),
        out_shape=jax.ShapeDtypeStruct((L, 3 * D), BF),
        compiler_params=params_of(grid=1),
    )(x, w)


def lanes(shape):
    return lax.broadcasted_iota(jnp.int32, shape, len(shape) - 1)


def three_parts(x):
    hi = x.astype(BF)
    rest = x - hi.astype(F32)
    mid = rest.astype(BF)
    return hi, mid, (rest - mid.astype(F32)).astype(BF)


def mask_bias(shape, length):
    return jnp.where(lax.broadcasted_iota(jnp.int32, shape, 0) < length, 0.0, NEG).astype(BF)


def attend_step(p, len_ref, q_ref, k_ref, v_ref, o_ref, wide_ref, lse_ref, tq, between):
    L = q_ref.shape[0]
    lane = lanes((L, 128))
    k, v = k_ref[...], v_ref[...]
    bias = mask_bias((L, 128), len_ref[0])
    zero, one = jnp.zeros((L, 128), BF), jnp.ones((L, 128), BF)

    @pl.when(p == 0)
    def _():
        lse_ref[...] = jnp.zeros_like(lse_ref)

    keys, values = [], []
    for h in range(2):
        mine = (lane < 64) if h == 0 else (lane >= 64)
        spare = 64 * (1 - h)
        keys.append(jnp.where(mine, k, jnp.where(lane == spare, bias, zero)))
        values.append(jnp.where(mine, v, jnp.where(lane == spare, one, zero)))
    lq = lanes((tq, 128))
    for i in range(L // tq):
        between(i)
        sl = pl.ds(i * tq, tq)
        q = q_ref[sl, :]
        outs, sums = [], []
        for h in range(2):
            mine = (lq < 64) if h == 0 else (lq >= 64)
            spare = 64 * (1 - h)
            q_h = jnp.where(mine, q, jnp.where(lq == spare, jnp.ones((tq, 128), BF), jnp.zeros((tq, 128), BF)))
            s = dot(q_h, keys[h], NT)
            top = jnp.max(s, axis=1, keepdims=True) * TO_LOG2
            e = jnp.exp2(s * TO_LOG2 - top)
            o = dot(e.astype(BF), values[h], NN)
            total = o[:, spare : spare + 1]
            outs.append(o / total)
            sums.append(top + jnp.log2(total))
        out = jnp.where(lq < 64, outs[0], outs[1])
        wide_ref[sl, :] = out
        o_ref[sl, :] = out.astype(BF)
        lse = lse_ref[sl, :]
        lse = jnp.where(lq == 2 * p, sums[0], lse)
        lse_ref[sl, :] = jnp.where(lq == 2 * p + 1, sums[1], lse)


def attend_back_step(p, len_ref, q_ref, k_ref, v_ref, do_ref, wide_ref, lse_ref, dq_ref, dk_ref, dv_ref, tq, between):
    L = q_ref.shape[0]
    lane = lanes((L, 128))
    k, v = k_ref[...], v_ref[...]
    bias = mask_bias((L, 128), len_ref[0])
    zero, one = jnp.zeros((L, 128), BF), jnp.ones((L, 128), BF)
    keys, values = [], []
    for h in range(2):
        mine = (lane < 64) if h == 0 else (lane >= 64)
        b = 64 * (1 - h)
        ones = jnp.where((lane > b) & (lane < b + 4), one, zero)
        keys.append(jnp.where(mine, k, jnp.where(lane == b, bias, ones)))
        values.append(jnp.where(mine, v, ones))
    lq = lanes((tq, 128))
    dk, dv = [jnp.zeros((L, 128), F32)] * 2, [jnp.zeros((L, 128), F32)] * 2
    for i in range(L // tq):
        between(i)
        sl = pl.ds(i * tq, tq)
        q, do, lse = q_ref[sl, :], do_ref[sl, :], lse_ref[sl, :]
        product = wide_ref[sl, :] * do.astype(F32)
        dq = []
        for h in range(2):
            mine = (lq < 64) if h == 0 else (lq >= 64)
            b = 64 * (1 - h)
            minus_delta = -jnp.sum(jnp.where(mine, product, 0.0), axis=1, keepdims=True)
            minus_lse = -jnp.sum(jnp.where(lq == 2 * p + h, lse, 0.0), axis=1, keepdims=True) * (1.0 / TO_LOG2)

            def with_spare(x, term, first):
                hi, mid, lo = three_parts(jnp.broadcast_to(term, (tq, 128)))
                low = jnp.where(lq == b + 2, mid, jnp.where(lq == b + 3, lo, jnp.zeros((tq, 128), BF)))
                low = jnp.where(lq == b, jnp.full((tq, 128), first, BF), jnp.where(lq == b + 1, hi, low))
                return jnp.where(mine, x, low)

            st = dot(keys[h], with_spare(q, minus_lse, 1.0), NT)
            pt = jnp.exp2(st * TO_LOG2)
            dpt = dot(values[h], with_spare(do, minus_delta, 0.0), NT)
            ds = (pt * dpt).astype(BF)
            dv[h] = dv[h] + dot(pt.astype(BF), do, NN)
            dk[h] = dk[h] + dot(ds, q, NN)
            dq.append(dot(ds, k, TN))
        dq_ref[sl, :] = (jnp.where(lq < 64, dq[0], dq[1]) * SCALE).astype(BF)
    dk_ref[...] = (jnp.where(lane < 64, dk[0], dk[1]) * SCALE).astype(BF)
    dv_ref[...] = jnp.where(lane < 64, dv[0], dv[1]).astype(BF)


def at_slots(p, per_step, plan):
    def between(i):
        for slot, actions in sorted(plan.items()):
            if slot % per_step == i:

                @pl.when(p == slot // per_step)
                def _(actions=actions):
                    for action in actions:
                        action()

    return between


def attend_kernel(len_ref, q_ref, k_ref, v_ref, proj_ref, in_ref, out_ref, o_ref, wide_ref, lse_ref, wproj_ref, win_ref, wout_ref,
                  sends, recvs, *, tq):
    p, steps = pl.program_id(0), pl.num_programs(0)
    at = Place()
    parts = q_ref.shape[0] // tq
    order = order_of(at.M)
    units = []

    def add(own, slot, d, way):
        n = len(units)
        units.append(GatherUnit(at, own, slot, d, way, sends.at[n], recvs.at[n]))
        return units[-1]

    main = []
    for k, d in enumerate(order[: at.M // 2]):
        main.append([
            add(in_ref, lambda z, g, c, k=k: win_ref.at[k, g, c], d, 0),
            add(out_ref, lambda z, g, c, k=k: wout_ref.at[k, g, c], d, 1),
        ])
    proj = [add(proj_ref, lambda z, g, c: wproj_ref.at[g, c, z], d, k % 2) for k, d in enumerate(order)]
    plan = {}

    def put(slot, name, group):
        plan.setdefault(min(slot, ATTEND_STEPS * parts - 1), []).extend(getattr(u, name) for u in group)

    plan[0] = [at.greet, at.meet]
    for group in main + [proj]:
        put(0, "start_z", group)
    put(0, "spread", main[0])
    put(0, "spread", proj[:1])
    put(2, "spread", proj[1:3])
    put(3, "relay", main[0])
    for n, group in enumerate(main[1:]):
        put(4 + 2 * n, "spread", group)
        put(8 + n, "relay", group)
        put(10 + n, "last", group)
    put(5, "last", main[0])
    put(5, "spread", proj[3:])
    put(6, "relay", proj[:1])
    put(7, "relay", proj[1:3])
    put(7, "last", proj[:1])
    put(9, "relay", proj[3:])
    put(9, "last", proj[1:3])
    put(11, "last", proj[3:])
    attend_step(p, len_ref, q_ref, k_ref, v_ref, o_ref, wide_ref, lse_ref, tq, at_slots(p, parts, plan))

    @pl.when(p == steps - 1)
    def _():
        for u in units:
            u.finish()


ATTEND_STEPS = 6


def attend(lengths, packed, proj, w_in, w_out, tq):
    G, M = lax.axis_size("dp") // 2, lax.axis_size("mp")
    L, D = packed.shape[0], packed.shape[1] // 3
    pairs = D // 128
    column = lambda off: pl.BlockSpec((L, 128), lambda p, off=off: (0, off + p))
    sems = (2 * (M // 2) + M, GatherUnit.count(G))
    return pl.pallas_call(
        functools.partial(attend_kernel, tq=tq),
        grid=(pairs,),
        in_specs=[SMEM, column(0), column(pairs), column(2 * pairs), ANY, ANY, ANY],
        out_specs=[column(0), column(0), pl.BlockSpec((L, 128), lambda p: (0, 0)), ANY, ANY, ANY],
        out_shape=[
            jax.ShapeDtypeStruct((L, D), BF),
            jax.ShapeDtypeStruct((L, D), F32),
            jax.ShapeDtypeStruct((L, 128), F32),
            jax.ShapeDtypeStruct((G, 2, M) + proj.shape, BF),
            jax.ShapeDtypeStruct((M // 2, G, 2) + w_in.shape, BF),
            jax.ShapeDtypeStruct((M // 2, G, 2) + w_out.shape, BF),
        ],
        scratch_shapes=[DMA(sems), DMA(sems)],
        compiler_params=params_of(1, grid=1),
    )(lengths, packed, packed, packed, proj, w_in, w_out)


def gelu_and_slope(x):
    phi = 0.5 + 0.5 * lax.erf(x * 0.7071067811865476)
    return x * phi, phi + x * (jnp.exp2((x * x) * (-0.5 * LOG2E)) * 0.3989422804014327)


def mlp_kernel(len_ref, x_ref, mixed_ref, cot_ref, params_ref, wproj_ref, win_ref, wout_ref, own_in_ref, own_out_ref,
               y_ref, mgrad_ref, dmixed_ref, sums_ref, pproj_ref, pin_ref, pout_ref, din_ref, dout_ref,
               w_s, mid_s, hid_s, sg_s, sec_s, br_s, act_s, eg_s, got_s, near_s, diag_s, send_s, far_s,
               load_sems, save_sems, gsends, grecvs, ssends, srecvs, *, tr):
    at = Place()
    G, M = at.G, at.M
    L, D = x_ref.shape
    R, Fb = own_in_ref.shape
    order = order_of(M)
    half = M // 2
    gain, bias = params_ref[1:2, :], params_ref[3:4, :]
    loads = [pltpu.make_async_copy((win_ref, wout_ref)[a].at[k], w_s.at[k, a], load_sems.at[k, a]) for k in range(half) for a in range(2)]
    for cp in loads:
        cp.start()
    at.greet()
    gathers = []
    for n, k in enumerate(range(half, M)):
        gathers.append([
            GatherUnit(at, own, lambda z, g, c, k=k, a=a: w_s.at[k, a, g * 2 + c], order[k], a, gsends.at[n, a], grecvs.at[n, a])
            for a, own in enumerate((own_in_ref, own_out_ref))
        ])
    sums = []
    for k in range(half):
        sums.append([
            SumUnit(at, lambda c, k=k, a=a: w_s.at[k, a, pl.ds(c * G, G)], None, got_s.at[k, a], near_s.at[k, a], diag_s.at[k, a],
                    send_s.at[k, a], far_s.at[k, a], total, order[k], a, ssends.at[k, a], srecvs.at[k, a])
            for a, total in enumerate((din_ref, dout_ref))
        ])

    def rows(i):
        return pl.ds(i * tr, tr)

    def enter(i):
        sl = rows(i)
        mid = x_ref[sl, :].astype(F32) + dot(mixed_ref[sl, :], wproj_ref[...], NN)
        mid_s[sl, :] = mid
        hid_s[sl, :] = mid
        sec_s[sl, :] = (norm_stats(mid)[0] * gain + bias).astype(BF)
        at_row = lax.broadcasted_iota(jnp.int32, (tr, D), 0) + i * tr
        br_s[sl, :] = jnp.where(at_row < len_ref[0], cot_ref[sl, :].astype(F32), 0.0).astype(BF)
        sg_s[sl, :] = jnp.zeros((tr, D), F32)

    n_rows = L // tr
    enter(0)
    at.meet()
    for group in gathers:
        for u in group:
            u.start_z()
    for i in range(1, n_rows):
        enter(i)
    for cp in loads:
        cp.wait()
    per = n_rows + 2
    plan = {}

    def put(k, i, name, group):
        plan.setdefault((min(k, M - 1), min(i, per - 1)), []).extend(getattr(u, name) for u in group)

    for n, group in enumerate(gathers):
        put(n, 1, "spread", group)
        put(n + 1, 0, "relay", group)
        put(n + 1, 2, "last", group)
        put(half + n, 0, "finish", group)
    for k, group in enumerate(sums):
        put(k + 1, 0, "start", group)
        put(k + 1, 1, "pair", group)
        put(k + 1, 3, "cross", group)
        put(k + 2, 1, "join", group)

    def block(k, carry):
        def between(i):
            for (at_k, at_i), actions in sorted(plan.items(), key=lambda item: item[0]):
                if at_i == i:

                    @pl.when(k == at_k)
                    def _(actions=actions):
                        for action in actions:
                            action()

        between(0)
        win, wout = (w_s[k, a].reshape(D, Fb) for a in range(2))
        for i in range(n_rows):
            if i:
                between(i)
            sl = rows(i)
            value, slope = gelu_and_slope(dot(sec_s[sl, :], win, NN))
            act = value.astype(BF)
            eg = (dot(br_s[sl, :], wout, NN) * slope).astype(BF)
            act_s[sl, :], eg_s[sl, :] = act, eg
            hid_s[sl, :] += dot(act, wout, NT)
            sg_s[sl, :] += dot(eg, win, NT)
        for a, (left, right) in enumerate(((sec_s, eg_s), (br_s, act_s))):
            between(n_rows + a)
            grad = dot(left[...], right[...], TN)
            for g in range(G):
                for c in range(2):
                    row = (g * 2 + c) * R
                    w_s[k, a, c * G + g] = grad[row : row + R, :].astype(BF)

        @pl.when(k >= half)
        def _():
            for a, ref in enumerate((pin_ref, pout_ref)):
                pltpu.make_async_copy(w_s.at[k, a], ref.at[k - half], save_sems.at[k - half, a]).start()

        return carry

    lax.fori_loop(0, M, block, 0)
    sums_ref[...] = jnp.zeros_like(sums_ref)
    n_back = L // 256 if L % 256 == 0 else 1
    tb = L // n_back

    def back(i, carry):
        sl = pl.ds(pl.multiple_of(i * tb, tb), tb)
        y_ref[sl, :] = hid_s[sl, :].astype(BF)
        xhat, r = norm_stats(mid_s[sl, :])
        e = sg_s[sl, :]
        sums_ref[1:2, :] += jnp.sum(e * xhat, axis=0, keepdims=True)
        sums_ref[3:4, :] += jnp.sum(e, axis=0, keepdims=True)
        grad = br_s[sl, :].astype(F32) + norm_pull(e, xhat, r, gain)
        mgrad_ref[sl, :] = grad
        low = grad.astype(BF)
        sec_s[sl, :] = low
        dmixed_ref[sl, :] = dot(low, wproj_ref[...], NT).astype(BF)
        return carry

    lax.fori_loop(0, n_back, back, 0)
    for u in sums[-1]:
        u.close()
    grad = dot(mixed_ref[...], sec_s[...], TN)
    R_p = pproj_ref.shape[3]
    for g in range(G):
        for c in range(2):
            for z in range(M):
                row = ((g * 2 + c) * M + z) * R_p
                pproj_ref[z, c, g] = grad[row : row + R_p, :].astype(BF)
    for group in sums[:-1]:
        for u in group:
            u.close()
    for k in range(half, M):
        for a, ref in enumerate((pin_ref, pout_ref)):
            pltpu.make_async_copy(w_s.at[k, a], ref.at[k - half], save_sems.at[k - half, a]).wait()
    for group in sums:
        for u in group:
            u.finish()


def mlp(lengths, x, mixed, cot, params, wproj, win, wout, own_in, own_out, R_p, tr):
    G, M = lax.axis_size("dp") // 2, lax.axis_size("mp")
    half = M // 2
    L, D = x.shape
    R, Fb = own_in.shape
    block = (R, Fb)
    chips = 2 if G == 4 else G - 1
    gsems, ssems = (M - half, 2, GatherUnit.count(G)), (half, 2, SumUnit.count(G))
    pieces = jax.ShapeDtypeStruct((M - half, 2 * G) + block, BF)
    return pl.pallas_call(
        functools.partial(mlp_kernel, tr=tr),
        in_specs=[SMEM, VMEM, VMEM, VMEM, VMEM, VMEM, ANY, ANY, ANY, ANY],
        out_specs=[VMEM] * 5 + [ANY, ANY, VMEM, VMEM],
        out_shape=[
            jax.ShapeDtypeStruct((L, D), BF),
            jax.ShapeDtypeStruct((L, D), F32),
            jax.ShapeDtypeStruct((L, D), BF),
            jax.ShapeDtypeStruct(params.shape, F32),
            jax.ShapeDtypeStruct((M, 2, G, R_p, D), BF),
            pieces, pieces,
            jax.ShapeDtypeStruct(block, F32), jax.ShapeDtypeStruct(block, F32),
        ],
        scratch_shapes=[
            pltpu.VMEM((M, 2, 2 * G) + block, BF),
            pltpu.VMEM((L, D), F32), pltpu.VMEM((L, D), F32), pltpu.VMEM((L, D), F32),
            pltpu.VMEM((L, D), BF), pltpu.VMEM((L, D), BF), pltpu.VMEM((L, Fb), BF), pltpu.VMEM((L, Fb), BF),
            pltpu.VMEM((half, 2, G) + block, BF), pltpu.VMEM((half, 2, chips) + block, BF),
            pltpu.VMEM((half, 2) + block, BF), pltpu.VMEM((half, 2) + block, BF), pltpu.VMEM((half, 2) + block, BF),
            DMA((half, 2)), DMA((M - half, 2)), DMA(gsems), DMA(gsems), DMA(ssems), DMA(ssems),
        ],
        compiler_params=params_of(4),
    )(lengths, x, mixed, cot, params, wproj, win, wout, own_in, own_out)


def attend_back_kernel(len_ref, q_ref, k_ref, v_ref, do_ref, wide_ref, lse_ref, pin_ref, pout_ref, pproj_ref, hin_ref, hout_ref,
                       dq_ref, dk_ref, dv_ref, din_ref, dout_ref, dproj_ref,
                       own_m, got_m, near_m, diag_m, send_m, far_m, own_p, got_p, near_p, diag_p, send_p, far_p,
                       sends, recvs, *, tq):
    p, steps = pl.program_id(0), pl.num_programs(0)
    at = Place()
    G, M = at.G, at.M
    half = M // 2
    parts = q_ref.shape[0] // tq
    order = order_of(M)
    units = []

    def add(part, bufs, total, d, way):
        n = len(units)
        own, got, near, diag, out, far = bufs
        units.append(SumUnit(at, part, own, got, near, diag, out, far, total, d, way, sends.at[n], recvs.at[n], local=True))
        return units[-1]

    main = []
    for n, k in reversed(list(enumerate(range(half, M)))):
        main.append([
            add(lambda c, n=n, ref=ref: ref.at[n, pl.ds(c * G, G)],
                [b.at[2 * n + a] for b in (own_m, got_m, near_m, diag_m, send_m, far_m)], total, order[k], a)
            for a, (ref, total) in enumerate(((pin_ref, din_ref), (pout_ref, dout_ref)))
        ])
    proj = [
        add(lambda c, j=at.plus(d): pproj_ref.at[j, c], [b.at[n] for b in (own_p, got_p, near_p, diag_p, send_p, far_p)], dproj_ref, d, n % 2)
        for n, d in enumerate(order)
    ]
    plan = {}

    def put(slot, name, group):
        plan.setdefault(min(slot, ATTEND_STEPS * parts - 1), []).extend(getattr(u, name) for u in group)

    def begin():
        din_ref[...], dout_ref[...] = hin_ref[...], hout_ref[...]

    plan[0] = [at.greet, begin, at.meet]
    for group in main + [proj]:
        put(0, "start", group)
    for n, group in enumerate(main):
        put(1 + n, "pair", group)
        put(4 + 3 * n, "cross", group)
        put(8 + 4 * n, "join", group)
    n = len(main)
    put(1 + n, "pair", proj)
    put(4 + 3 * n, "cross", proj)
    put(8 + 4 * n, "join", proj)
    for group in main + [proj]:
        put(20, "close", group)
    attend_back_step(p, len_ref, q_ref, k_ref, v_ref, do_ref, wide_ref, lse_ref, dq_ref, dk_ref, dv_ref, tq, at_slots(p, parts, plan))

    @pl.when(p == steps - 1)
    def _():
        for u in units:
            u.finish()


def sum_buffers(n, G, shape):
    chips = 2 if G == 4 else G - 1
    return [
        pltpu.VMEM((n, G) + shape, BF), pltpu.VMEM((n, G) + shape, BF), pltpu.VMEM((n, chips) + shape, BF),
        pltpu.VMEM((n,) + shape, BF), pltpu.VMEM((n,) + shape, BF), pltpu.VMEM((n,) + shape, BF),
    ]


def attend_back(lengths, packed, do, wide, lse, p_in, p_out, p_proj, h_in, h_out, tq):
    G, M = lax.axis_size("dp") // 2, lax.axis_size("mp")
    L, D = do.shape
    pairs = D // 128
    column = lambda off: pl.BlockSpec((L, 128), lambda p, off=off: (0, off + p))
    whole = lambda shape: pl.BlockSpec(shape, lambda p: (0,) * len(shape))
    mshape, pshape = h_in.shape, p_proj.shape[3:]
    rest = 2 * (M - M // 2)
    sems = (rest + M, SumUnit.count(G))
    return pl.pallas_call(
        functools.partial(attend_back_kernel, tq=tq),
        grid=(pairs,),
        in_specs=[SMEM, column(0), column(pairs), column(2 * pairs), column(0), column(0), whole((L, 128)), ANY, ANY, ANY,
                  whole(mshape), whole(mshape)],
        out_specs=[column(0)] * 3 + [whole(mshape), whole(mshape), whole(pshape)],
        out_shape=[jax.ShapeDtypeStruct((L, D), BF)] * 3
        + [jax.ShapeDtypeStruct(mshape, F32)] * 2 + [jax.ShapeDtypeStruct(pshape, F32)],
        scratch_shapes=sum_buffers(rest, G, mshape) + sum_buffers(M, G, pshape) + [DMA(sems), DMA(sems)],
        compiler_params=params_of(2, grid=1),
    )(lengths, packed, packed, packed, do, wide, lse, p_in, p_out, p_proj, h_in, h_out)


def exit_kernel(x_ref, normed_ref, dq_ref, dk_ref, dv_ref, w_ref, mid_ref, second_ref, params_ref,
                grad_ref, qkv_ref, norms_ref,
                parts_s, got_s, near_s, diag_s, send_s, far_s, have, small_got, sends, recvs, small_sends, small_recvs, *, rows):
    at = Place()
    G, M = at.G, at.M
    R = qkv_ref.shape[1]
    small = SmallSum(at, have, small_got, small_sends, small_recvs)
    thirds = (dq_ref, dk_ref, dv_ref)
    order = order_of(M)
    units = []
    for t in range(3):
        group = []
        for n, d in enumerate(order):
            k = t * M + n
            j = at.plus(d)
            group.append(SumUnit(at, lambda c, t=t, j=j: parts_s.at[t, j, c], None, got_s.at[k], near_s.at[k], diag_s.at[k],
                                 send_s.at[k], far_s.at[k], qkv_ref.at[t], d, n % 2, sends.at[k], recvs.at[k]))
        units.append(group)

    def run(t, name):
        for u in units[t]:
            getattr(u, name)()

    def third(t):
        grad = dot(normed_ref[...], thirds[t][...], TN)
        for g in range(G):
            for c in range(2):
                for z in range(M):
                    k = ((g * 2 + c) * M + z) * R
                    parts_s[t, z, c, g] = grad[k : k + R, :].astype(BF)

    L = x_ref.shape[0]

    def norm(i):
        sl = pl.ds(i * rows, rows)
        e = sum(dot(thirds[t][sl, :], w_ref[t], NT) for t in range(3))
        xhat, r = norm_stats(x_ref[sl, :].astype(F32))
        grad_ref[sl, :] = mid_ref[sl, :] + norm_pull(e, xhat, r, gain)
        have[0, 0:1, :] += jnp.sum(e * xhat, axis=0, keepdims=True)
        have[0, 2:3, :] += jnp.sum(e, axis=0, keepdims=True)

    gain = params_ref[0:1, :]
    have[0] = second_ref[...]
    at.greet()
    third(0)
    at.meet()
    run(0, "start")
    third(1)
    run(1, "start")
    run(0, "pair")
    third(2)
    run(2, "start")
    run(0, "cross")
    run(1, "pair")
    todo = [(1, "cross"), (2, "pair"), (0, "join"), (2, "cross"), (1, "join")]
    for i in range(L // rows):
        norm(i)
        if i < len(todo):
            run(*todo[i])
    small.stage(0)
    for item in todo[L // rows :]:
        run(*item)
    small.stage(1)
    run(2, "join")
    small.stage(2)
    for t in range(3):
        run(t, "close")
    for s in range(3, len(small.hops) + 1):
        small.stage(s)
    norms_ref[...] = have[len(small.hops)]
    for t in range(3):
        run(t, "finish")
    small.finish()


def leave(x, normed, dq, dk, dv, w, middle_grad, second_sums, params, R):
    G, M = lax.axis_size("dp") // 2, lax.axis_size("mp")
    L, D = x.shape
    n_have, n_got = SmallSum.counts(G, M)
    sems = (3 * M, SumUnit.count(G))
    return pl.pallas_call(
        functools.partial(exit_kernel, rows=min(256, L)),
        in_specs=[VMEM] * 9,
        out_specs=[VMEM] * 3,
        out_shape=[
            jax.ShapeDtypeStruct((L, D), F32),
            jax.ShapeDtypeStruct((3, R, D), F32),
            jax.ShapeDtypeStruct(params.shape, F32),
        ],
        scratch_shapes=[pltpu.VMEM((3, M, 2, G, R, D), BF)] + sum_buffers(3 * M, G, (R, D))[1:]
        + [pltpu.VMEM((n_have,) + params.shape, F32), pltpu.VMEM((n_got,) + params.shape, F32),
           DMA(sems), DMA(sems), DMA((n_got,)), DMA((n_got,))],
        compiler_params=params_of(3),
    )(x, normed, dq, dk, dv, w, middle_grad, second_sums, params)


def per_device(inputs, lengths, attn_qkv, attn_proj, mlp_in, mlp_out, norm_gain, norm_bias, cotangent):
    n_dp, n_mp = lax.axis_size("dp"), lax.axis_size("mp")
    G = n_dp // 2
    L, D = inputs.shape
    R = attn_qkv.shape[1]
    here = (lax.axis_index("dp") * n_mp + lax.axis_index("mp")) * R
    small = jnp.concatenate([norm_gain[0], norm_bias[0]], axis=0).astype(F32)
    placed = lax.dynamic_update_slice(jnp.zeros((8, D), F32), small, (0, here))
    shard = attn_qkv[0].reshape(R, 3, D).transpose(1, 0, 2)
    wqkv, normed, params = entry(inputs, shard, placed)
    wqkv = wqkv.reshape(3, D, D)
    packed = qkv_matmul(normed, wqkv)
    own_in, own_out = mlp_in[0], mlp_out[0].T
    mixed, wide, lse, wproj, win, wout = attend(lengths, packed, attn_proj[0], own_in, own_out, min(512, L))
    wproj = wproj.reshape(D, D)
    pieces = lambda w: w.reshape((w.shape[0], n_dp) + w.shape[3:])
    outputs, middle_grad, mixed_grad, second_sums, p_proj, p_in, p_out, h_in, h_out = mlp(
        lengths, inputs, mixed, cotangent, params, wproj, pieces(win), pieces(wout), own_in, own_out, R, min(512, L))
    dq, dk, dv, d_in, d_out, d_proj = attend_back(
        lengths, packed, mixed_grad, wide, lse, p_in, p_out, p_proj, h_in, h_out, min(256, L))
    input_grad, d_qkv, norms = leave(inputs, normed, dq, dk, dv, wqkv, middle_grad, second_sums, params, R)
    mine = lax.dynamic_slice(norms, (0, here), (4, R))
    return (
        outputs,
        input_grad,
        d_qkv.transpose(1, 0, 2).reshape(1, R, 3 * D),
        d_proj[None],
        d_in[None],
        d_out.T[None],
        mine[None, :2],
        mine[None, 2:],
    )


def solution(mesh):
    everywhere = ("dp", "mp")
    wide, columns, vector = P(everywhere, None), P(None, everywhere, None), P(None, None, everywhere)
    return jax.shard_map(
        per_device,
        mesh=mesh,
        in_specs=(wide, P(everywhere), columns, columns, P(None, "dp", "mp"), P(None, "mp", "dp"), vector, vector, wide),
        out_specs=(wide, wide, columns, columns, P(None, "dp", "mp"), P(None, "mp", "dp"), vector, vector),
        check_vma=False,
    )
```

```python
import functools

import jax
import jax.numpy as jnp
from jax import lax
from jax.experimental import pallas as pl
from jax.experimental.pallas import tpu as pltpu
from jax.sharding import PartitionSpec as P

F32, BF = jnp.float32, jnp.bfloat16
MESH = pl.DeviceIdType.MESH
HEAD_DIM = 64
SCALE = 0.125
LOG2E = 1.4426950408889634
TO_LOG2 = SCALE * LOG2E
NEG = -1e30
EPS = 1e-06
NN = (((1,), (0,)), ((), ()))
NT = (((1,), (1,)), ((), ()))
TN = (((0,), (0,)), ((), ()))
VMEM_LIMIT = 60 * 2**20
ANY = pl.BlockSpec(memory_space=pl.ANY)
VMEM = pl.BlockSpec(memory_space=pltpu.VMEM)
SMEM = pl.BlockSpec(memory_space=pltpu.SMEM)
DMA = pltpu.SemaphoreType.DMA


def dot(a, b, dims):
    return lax.dot_general(a, b, dims, preferred_element_type=F32)


def params_of(collective_id=None, grid=0):
    extra = {} if collective_id is None else {"collective_id": collective_id, "has_side_effects": True}
    if grid:
        extra["dimension_semantics"] = ("arbitrary",) * grid
    return pltpu.CompilerParams(vmem_limit_bytes=VMEM_LIMIT, **extra)


class Place:
    def __init__(self, everyone=False):
        self.everyone = everyone
        n_dp, self.M = lax.axis_size("dp"), lax.axis_size("mp")
        self.G = n_dp // 2
        dp = lax.axis_index("dp")
        self.g, self.c, self.z = dp // 2, lax.rem(dp, 2), lax.axis_index("mp")
        self.square = self.G == 4
        near = [sorted(range(self.M), key=lambda s: (abs(s - z), s)) for z in range(self.M)]
        self.near = [sum(jnp.where(self.z == z, near[z][n], 0) for z in range(self.M)) for n in range(self.M)]
        if self.square:
            self.chips = [self.g ^ 1, self.g ^ 2]
            self.diag = self.g ^ 3
        else:
            self.chips = [lax.rem(self.g + d, self.G) for d in range(1, self.G)]

    def chip(self, h):
        return (h * 2 + self.c, self.z)

    def core(self):
        return (self.g * 2 + 1 - self.c, self.z)

    def along(self, z):
        return (self.g * 2 + self.c, z)

    def peers(self):
        if self.everyone:
            n = 2 * self.G * self.M
            return [self.device(lax.rem(self.index + d, n)) for d in range(1, n)]
        return [self.along(s) for s in self.near[1:]] + [self.chip(h) for h in self.chips] + [self.core()]

    @property
    def index(self):
        return (self.g * 2 + self.c) * self.M + self.z

    def device(self, i):
        return (i // self.M, lax.rem(i, self.M))

    def greet(self):
        for dev in self.peers():
            pl.semaphore_signal(pltpu.get_barrier_semaphore(), inc=1, device_id=dev, device_id_type=MESH)

    def meet(self):
        pl.semaphore_wait(pltpu.get_barrier_semaphore(), len(self.peers()))


def remote(src, dst, send, recv, dev):
    return pltpu.make_async_remote_copy(src_ref=src, dst_ref=dst, send_sem=send, recv_sem=recv, device_id=dev, device_id_type=MESH)


class Chain:
    def __init__(self, at, own, land, sends, recvs):
        self.at, self.own, self.land, self.sends, self.recvs = at, own, land, sends, recvs
        self.up, self.down = at.z < at.M - 1, at.z > 0

    def _copy(self, k, src, s, z):
        return remote(src, self.land(s), self.sends.at[k], self.recvs.at[s], self.at.along(z))

    def _own(self, act):
        at = self.at
        for k, (ok, z) in enumerate(((self.up, at.z + 1), (self.down, at.z - 1))):
            pl.when(ok)(lambda k=k, z=z: act(self._copy(k, self.own, at.z, z)))

    def _pass(self, n, act):
        at, s = self.at, self.at.near[n]
        block = self.land(s)
        pl.when((s > at.z) & self.down)(lambda: act(self._copy(1 + n, block, s, at.z - 1)))
        pl.when((s < at.z) & self.up)(lambda: act(self._copy(1 + n, block, s, at.z + 1)))

    def start(self):
        self._own(lambda cp: cp.start())

    def arrive(self, n):
        s = self.at.near[n]
        self._copy(1 + n, self.land(s), s, self.at.z).wait_recv()
        if self.at.M > 2:
            self._pass(n, lambda cp: cp.start())

    def finish(self):
        self._own(lambda cp: cp.wait_send())
        if self.at.M > 2:
            for n in range(1, self.at.M):
                self._pass(n, lambda cp: cp.wait_send())


class GatherUnit:
    def __init__(self, at, src, slot, way, sends, recvs, local=True):
        self.at, self.src, self.slot, self.way, self.local = at, src, slot, way, local
        self.sends, self.recvs = sends, recvs

    @staticmethod
    def count(G):
        return 1 + (3 if G == 4 else G - 1) + G

    def _local(self):
        return pltpu.make_async_copy(self.src, self.slot(self.at.g, self.at.c), self.sends.at[0])

    def _to_chip(self, i):
        at = self.at
        return remote(self.src, self.slot(at.g, at.c), self.sends.at[1 + i], self.recvs.at[1 + i], at.chip(at.chips[i]))

    def _relay(self):
        at = self.at
        block = self.slot(at.chips[self.way], at.c)
        return remote(block, block, self.sends.at[3], self.recvs.at[3], at.chip(at.chips[1 - self.way]))

    def _to_core(self, i):
        at = self.at
        h = ([at.g] + at.chips + ([at.diag] if at.square else []))[i]
        k = self.count(at.G) - at.G + i
        block = self.slot(h, at.c)
        return remote(block if i else self.src, block, self.sends.at[k], self.recvs.at[k], at.core())

    def spread(self):
        for i in range(len(self.at.chips)):
            self._to_chip(i).start()
        self._to_core(0).start()
        if self.local:
            self._local().start()

    def relay(self):
        n = len(self.at.chips)
        for i in range(n):
            self._to_chip(i).wait_recv()
        if self.at.square:
            self._relay().start()
        for i in range(n):
            self._to_core(1 + i).start()

    def last(self):
        if self.at.square:
            self._relay().wait_recv()
            self._to_core(3).start()

    def finish(self):
        if self.local:
            self._local().wait()
        for i in range(len(self.at.chips)):
            self._to_chip(i).wait_send()
        if self.at.square:
            self._relay().wait_send()
        for i in range(self.at.G):
            self._to_core(i).wait()


class SumUnit:
    def __init__(self, at, part, own, got, near, diag, out, far, total, n, way, sends, recvs, far_recvs, local=False):
        self.at, self.part, self.own, self.got, self.near, self.diagonal = at, part, own, got, near, diag
        self.out, self.far, self.total, self.n, self.way = out, far, total, n, way
        self.sends, self.recvs, self.far_recvs, self.local = sends, recvs, far_recvs, local
        self.place = at.near[n]

    @staticmethod
    def count(G):
        return 3 + (3 if G == 4 else G)

    def _core(self):
        at = self.at
        return remote(self.part(1 - at.c), self.got, self.sends.at[0], self.recvs.at[0], at.core())

    def _local(self):
        return pltpu.make_async_copy(self.part(self.at.c), self.own, self.sends.at[2])

    def _diag(self):
        at = self.at
        return remote(self.got.at[at.diag], self.diagonal, self.sends.at[5], self.recvs.at[5], at.chip(at.chips[1 - self.way]))

    def _chip(self, i):
        at = self.at
        k = 3 + i
        return remote(self.got.at[at.chips[i]], self.near.at[i], self.sends.at[k], self.recvs.at[k], at.chip(at.chips[i]))

    def _z(self, source):
        return remote(self.out, self.far.at[source], self.sends.at[1], self.far_recvs.at[source], self.at.along(self.place))

    def start(self):
        self._core().start()
        if self.local:
            self._local().start()

    def pair(self):
        at = self.at
        self._core().wait_recv()
        if self.local:
            self._local().wait()
            own = self.own
        else:
            own = self.part(at.c)
        self.got[...] = (self.got[...].astype(F32) + own[...].astype(F32)).astype(BF)
        if at.square:
            self._diag().start()
        else:
            for i in range(len(at.chips)):
                self._chip(i).start()

    def cross(self):
        at = self.at
        if at.square:
            self._diag().wait_recv()
            h = at.chips[self.way]
            self.got[h] = (self.got[h].astype(F32) + self.diagonal[...].astype(F32)).astype(BF)
            for i in range(2):
                self._chip(i).start()

    def join(self):
        at = self.at
        value = self.got[at.g].astype(F32)
        for i in range(len(at.chips)):
            self._chip(i).wait_recv()
            value = value + self.near[i].astype(F32)
        if self.n:
            self.out[...] = value.astype(BF)
            self._z(self.at.z).start()
        else:
            self.total[...] = value

    def close(self):
        if self.n:
            self._z(self.place).wait_recv()
            self.total[...] += self.far[self.place].astype(F32)

    def finish(self):
        at = self.at
        self._core().wait_send()
        if self.n:
            self._z(at.z).wait_send()
        for i in range(len(at.chips)):
            self._chip(i).wait_send()
        if at.square:
            self._diag().wait_send()


def sum_buffers(n, G, shape, own=True, far=0):
    chips = 2 if G == 4 else G - 1
    block = lambda *lead: pltpu.VMEM(lead + shape, BF)
    return ([block(n, G)] if own else []) + [block(n, G), block(n, chips), block(n), block(n), block(max(far, 1))]


class SmallSum:
    def __init__(self, at, have, got, sends, recvs):
        self.at, self.have, self.got, self.sends, self.recvs = at, have, got, sends, recvs
        hops = [[at.along(s) for s in at.near[1:]]]
        if at.square:
            hops += [[at.chip(h)] for h in at.chips]
        else:
            hops += [[at.chip(h) for h in at.chips]]
        self.hops = hops + [[at.core()]]

    @staticmethod
    def counts(G, M):
        return (5 if G == 4 else 4), M + (2 if G == 4 else G - 1) + 1

    def _copies(self, s, back=False):
        at = self.at
        base = at.M + sum(len(h) for h in self.hops[1:s]) if s else 0
        slots = [base + i for i in range(len(self.hops[s]))]
        if s == 0:
            slots = at.near[1:] if back else [at.z] * (at.M - 1)
        return [
            remote(self.have.at[s], self.got.at[k], self.sends.at[base + i], self.recvs.at[k], dev)
            for i, (k, dev) in enumerate(zip(slots, self.hops[s]))
        ], slots

    def stage(self, s):
        if s:
            copies, slots = self._copies(s - 1, True)
            value = self.have[s - 1]
            for k, cp in zip(slots, copies):
                cp.wait_recv()
                value = value + self.got[k]
            self.have[s] = value
        if s < len(self.hops):
            for cp in self._copies(s)[0]:
                cp.start()

    def finish(self):
        for s in range(len(self.hops)):
            for cp in self._copies(s)[0]:
                cp.wait_send()


class SmallScatter:
    def __init__(self, at, parts, got, sends, recvs):
        self.at, self.parts, self.got, self.sends, self.recvs = at, parts, got, sends, recvs
        self.count = 2 * at.G * at.M

    def _copy(self, d, back):
        at = self.at
        to, other = lax.rem(at.index + d, self.count), lax.rem(at.index + self.count - d, self.count)
        return remote(self.parts.at[to], self.got.at[other if back else at.index], self.sends.at[d], self.recvs.at[d], at.device(to))

    def start(self, value, R):
        for i in range(self.count):
            self.parts[i] = (pltpu.roll(value, value.shape[1] - i * R, 1) if i else value)[:, :128]

        def send(d, carry):
            self._copy(d, False).start()
            return carry

        lax.fori_loop(1, self.count, send, 0)

    def collect(self):
        def add(d, value):
            self._copy(d, True).wait_recv()
            return value + self.got[lax.rem(self.at.index + self.count - d, self.count)]

        return lax.fori_loop(1, self.count, add, self.parts[self.at.index])

    def finish(self):
        def wait(d, carry):
            self._copy(d, False).wait_send()
            return carry

        lax.fori_loop(1, self.count, wait, 0)


def norm_stats(v):
    centre = v - jnp.mean(v, axis=-1, keepdims=True)
    r = lax.rsqrt(jnp.mean(centre * centre, axis=-1, keepdims=True) + EPS)
    return centre * r, r


def norm_pull(e, xhat, r, g):
    y = e * g
    return r * (y - jnp.mean(y, axis=-1, keepdims=True) - xhat * jnp.mean(y * xhat, axis=-1, keepdims=True))


def entry_kernel(x_ref, shard_ref, placed_ref, w_ref, normed_ref, params_ref, have, got, chain_sends, chain_recvs, sends, recvs,
                 small_sends, small_recvs, *, rows):
    at = Place()
    at.greet()
    have[0] = placed_ref[...]
    land = lambda s: w_ref.at[:, at.g, at.c, s]
    chain = Chain(at, shard_ref, land, chain_sends, chain_recvs)
    units = [
        GatherUnit(at, land(at.near[n]) if n else shard_ref, lambda g, c, n=n: w_ref.at[:, g, c, at.near[n]], n % 2, sends.at[n], recvs.at[n], n == 0)
        for n in range(at.M)
    ]
    small = SmallSum(at, have, got, small_sends, small_recvs)
    last = len(small.hops)
    at.meet()
    chain.start()
    units[0].spread()
    small.stage(0)
    stage = 1
    for n in range(1, at.M + 2):
        if n < at.M:
            chain.arrive(n)
            units[n].spread()
        if n - 1 < at.M:
            units[n - 1].relay()
        if stage <= last:
            small.stage(stage)
            stage += 1
        if 0 <= n - 2 < at.M:
            units[n - 2].last()
    while stage <= last:
        small.stage(stage)
        stage += 1
    params_ref[...] = have[last]
    gain, bias = have[last, 0:1, :], have[last, 2:3, :]

    def norm(i, carry):
        sl = pl.ds(pl.multiple_of(i * rows, rows), rows)
        xhat, _ = norm_stats(x_ref[sl, :].astype(F32))
        normed_ref[sl, :] = (xhat * gain + bias).astype(BF)
        return carry

    lax.fori_loop(0, x_ref.shape[0] // rows, norm, 0)
    for u in units:
        u.finish()
    chain.finish()
    small.finish()


def entry(x, shard, placed):
    at_G, M = lax.axis_size("dp") // 2, lax.axis_size("mp")
    L, D = x.shape
    n_have, n_got = SmallSum.counts(at_G, M)
    sems = (M, GatherUnit.count(at_G))
    return pl.pallas_call(
        functools.partial(entry_kernel, rows=min(256, L)),
        in_specs=[VMEM, ANY, VMEM],
        out_specs=[ANY, VMEM, VMEM],
        out_shape=[
            jax.ShapeDtypeStruct((3, at_G, 2, M) + shard.shape[1:], BF),
            jax.ShapeDtypeStruct((L, D), BF),
            jax.ShapeDtypeStruct(placed.shape, F32),
        ],
        scratch_shapes=[
            pltpu.VMEM((n_have,) + placed.shape, F32),
            pltpu.VMEM((n_got,) + placed.shape, F32),
            DMA((M + 1,)), DMA((M,)), DMA(sems), DMA(sems), DMA((n_got,)), DMA((n_got,)),
        ],
        compiler_params=params_of(0),
    )(x, shard, placed)


def lanes(shape):
    return lax.broadcasted_iota(jnp.int32, shape, len(shape) - 1)


def three_parts(x):
    hi = x.astype(BF)
    rest = x - hi.astype(F32)
    mid = rest.astype(BF)
    return hi, mid, (rest - mid.astype(F32)).astype(BF)


def mask_bias(shape, length):
    return jnp.where(lax.broadcasted_iota(jnp.int32, shape, 0) < length, 0.0, NEG).astype(BF)


def attend_step(p, len_ref, q_ref, k_ref, v_ref, o_ref, wide_ref, lse_ref, tq, between):
    L = q_ref.shape[0]
    lane = lanes((L, 128))
    k, v = k_ref[...], v_ref[...]
    bias = mask_bias((L, 128), len_ref[0])
    zero, one = jnp.zeros((L, 128), BF), jnp.ones((L, 128), BF)

    @pl.when(p == 0)
    def _():
        lse_ref[...] = jnp.zeros_like(lse_ref)

    keys, values = [], []
    for h in range(2):
        mine = (lane < 64) if h == 0 else (lane >= 64)
        spare = 64 * (1 - h)
        keys.append(jnp.where(mine, k, jnp.where(lane == spare, bias, zero)))
        values.append(jnp.where(mine, v, jnp.where(lane == spare, one, zero)))
    lq = lanes((tq, 128))
    for i in range(L // tq):
        between(i)
        sl = pl.ds(i * tq, tq)
        q = q_ref[sl, :]
        outs, sums = [], []
        for h in range(2):
            mine = (lq < 64) if h == 0 else (lq >= 64)
            spare = 64 * (1 - h)
            q_h = jnp.where(mine, q, jnp.where(lq == spare, jnp.ones((tq, 128), BF), jnp.zeros((tq, 128), BF)))
            s = dot(q_h, keys[h], NT)
            top = jnp.max(s, axis=1, keepdims=True) * TO_LOG2
            e = jnp.exp2(s * TO_LOG2 - top)
            o = dot(e.astype(BF), values[h], NN)
            total = o[:, spare : spare + 1]
            outs.append(o / total)
            sums.append(top + jnp.log2(total))
        out = jnp.where(lq < 64, outs[0], outs[1])
        wide_ref[sl, :] = out
        o_ref[sl, :] = out.astype(BF)
        lse = lse_ref[sl, :]
        lse = jnp.where(lq == 2 * p, sums[0], lse)
        lse_ref[sl, :] = jnp.where(lq == 2 * p + 1, sums[1], lse)


def attend_back_step(p, len_ref, q_ref, k_ref, v_ref, do_ref, wide_ref, lse_ref, dq_ref, dk_ref, dv_ref, tq, between):
    L = q_ref.shape[0]
    lane = lanes((L, 128))
    k, v = k_ref[...], v_ref[...]
    bias = mask_bias((L, 128), len_ref[0])
    zero, one = jnp.zeros((L, 128), BF), jnp.ones((L, 128), BF)
    keys, values = [], []
    for h in range(2):
        mine = (lane < 64) if h == 0 else (lane >= 64)
        b = 64 * (1 - h)
        ones = jnp.where((lane > b) & (lane < b + 4), one, zero)
        keys.append(jnp.where(mine, k, jnp.where(lane == b, bias, ones)))
        values.append(jnp.where(mine, v, ones))
    lq = lanes((tq, 128))
    dk, dv = [jnp.zeros((L, 128), F32)] * 2, [jnp.zeros((L, 128), F32)] * 2
    for i in range(L // tq):
        between(i)
        sl = pl.ds(i * tq, tq)
        q, do, lse = q_ref[sl, :], do_ref[sl, :], lse_ref[sl, :]
        product = wide_ref[sl, :] * do.astype(F32)
        dq = []
        for h in range(2):
            mine = (lq < 64) if h == 0 else (lq >= 64)
            b = 64 * (1 - h)
            minus_delta = -jnp.sum(jnp.where(mine, product, 0.0), axis=1, keepdims=True)
            minus_lse = -jnp.sum(jnp.where(lq == 2 * p + h, lse, 0.0), axis=1, keepdims=True) * (1.0 / TO_LOG2)

            def with_spare(x, term, first):
                hi, mid, lo = three_parts(jnp.broadcast_to(term, (tq, 128)))
                low = jnp.where(lq == b + 2, mid, jnp.where(lq == b + 3, lo, jnp.zeros((tq, 128), BF)))
                low = jnp.where(lq == b, jnp.full((tq, 128), first, BF), jnp.where(lq == b + 1, hi, low))
                return jnp.where(mine, x, low)

            st = dot(keys[h], with_spare(q, minus_lse, 1.0), NT)
            pt = jnp.exp2(st * TO_LOG2)
            dpt = dot(values[h], with_spare(do, minus_delta, 0.0), NT)
            ds = (pt * dpt).astype(BF)
            dv[h] = dv[h] + dot(pt.astype(BF), do, NN)
            dk[h] = dk[h] + dot(ds, q, NN)
            dq.append(dot(ds, k, TN))
        dq_ref[sl, :] = (jnp.where(lq < 64, dq[0], dq[1]) * SCALE).astype(BF)
    dk_ref[...] = (jnp.where(lane < 64, dk[0], dk[1]) * SCALE).astype(BF)
    dv_ref[...] = jnp.where(lane < 64, dv[0], dv[1]).astype(BF)


def at_slots(p, per_step, plan):
    def between(i):
        for slot, actions in sorted(plan.items()):
            if slot % per_step == i:

                @pl.when(p == slot // per_step)
                def _(actions=actions):
                    for action in actions:
                        action()

    return between


def attend_kernel(len_ref, x_ref, w_ref, proj_ref, io_ref, o_ref, wide_ref, lse_ref, packed_ref, wproj_ref, land_ref, win_ref, wout_ref,
                  packed_s, save_sem, pchain_sends, pchain_recvs, chain_sends, chain_recvs, sends, recvs, *, tq):
    p, steps = pl.program_id(0), pl.num_programs(0)
    at = Place()
    M = at.M
    half = M // 2
    D = x_ref.shape[1]
    parts = x_ref.shape[0] // tq
    land = [lambda s, a=a: land_ref.at[s, a] for a in range(2)]
    pland = lambda s: wproj_ref.at[at.g, at.c, s]
    pchain = Chain(at, proj_ref, pland, pchain_sends, pchain_recvs)
    chains = [Chain(at, io_ref.at[a], land[a], chain_sends.at[a], chain_recvs.at[a]) for a in range(2)]
    main = [
        [GatherUnit(at, land[a](at.near[n]) if n else io_ref.at[a], lambda g, c, n=n, ref=ref: ref.at[n, g, c], a, sends.at[2 * n + a], recvs.at[2 * n + a])
         for a, ref in enumerate((win_ref, wout_ref))]
        for n in range(half)
    ]
    proj = [
        GatherUnit(at, pland(at.near[n]) if n else proj_ref, lambda g, c, n=n: wproj_ref.at[g, c, at.near[n]], n % 2,
                   sends.at[2 * half + n], recvs.at[2 * half + n], n == 0)
        for n in range(M)
    ]
    own_land = [pltpu.make_async_copy(io_ref.at[a], land_ref.at[at.z, a], save_sem.at[1 + a]) for a in range(2)]
    save = pltpu.make_async_copy(packed_s, packed_ref, save_sem.at[0])

    def third(t):
        packed_s[:, pl.ds(t * D, D)] = dot(x_ref[...], w_ref[t], NN).astype(BF)

    @pl.when(p == 0)
    def _():
        at.greet()
        third(0)
        at.meet()
        pchain.start()
        for chain in chains:
            chain.start()
        proj[0].spread()
        for u in main[0]:
            u.spread()
        for cp in own_land:
            cp.start()
        third(1)
        third(2)
        save.start()

    plan = {}

    def put(slot, *actions):
        plan.setdefault(min(slot, ATTEND_STEPS * parts - 1), []).extend(actions)

    def arrive(chain, n, unit=None):
        def act():
            chain.arrive(n)
            if unit is not None:
                unit.spread()

        return act

    for n in range(1, M):
        put(2 * n - 2, arrive(pchain, n, proj[n]))
        for a in range(2):
            put(3 * n - 2 + a, arrive(chains[a], n, main[n][a] if n < half else None))
    put(1, main[0][0].relay, main[0][1].relay)
    for n in range(M):
        put(2 + 2 * n, proj[n].relay)
        put(4 + 2 * n, proj[n].last)
    put(4, main[0][0].last, main[0][1].last)
    for n in range(1, half):
        put(4 + 2 * n, main[n][0].relay)
        put(5 + 2 * n, main[n][1].relay)
        put(8 + n, main[n][0].last, main[n][1].last)
    lane = pl.multiple_of(p * 128, 128)
    column = lambda t: packed_s.at[:, pl.ds(t * D + lane, 128)]
    attend_step(p, len_ref, column(0), column(1), column(2), o_ref, wide_ref, lse_ref, tq, at_slots(p, parts, plan))

    @pl.when(p == steps - 1)
    def _():
        for group in main + [proj, chains, [pchain]]:
            for u in group:
                u.finish()
        save.wait()
        for cp in own_land:
            cp.wait()


ATTEND_STEPS = 6


def attend(lengths, x, w, proj, io, tq):
    G, M = lax.axis_size("dp") // 2, lax.axis_size("mp")
    L, D = x.shape
    half = M // 2
    column = pl.BlockSpec((L, 128), lambda p: (0, p))
    whole = lambda shape: pl.BlockSpec(shape, lambda p: (0,) * len(shape), pipeline_mode=pl.Buffered(1))
    sems = (2 * half + M, GatherUnit.count(G))
    weights = jax.ShapeDtypeStruct((half, G, 2) + io.shape[1:], BF)
    return pl.pallas_call(
        functools.partial(attend_kernel, tq=tq),
        grid=(D // 128,),
        in_specs=[SMEM, whole(x.shape), whole(w.shape), ANY, ANY],
        out_specs=[column, column, pl.BlockSpec((L, 128), lambda p: (0, 0)), ANY, ANY, ANY, ANY, ANY],
        out_shape=[
            jax.ShapeDtypeStruct((L, D), BF),
            jax.ShapeDtypeStruct((L, D), F32),
            jax.ShapeDtypeStruct((L, 128), F32),
            jax.ShapeDtypeStruct((L, 3 * D), BF),
            jax.ShapeDtypeStruct((G, 2, M) + proj.shape, BF),
            jax.ShapeDtypeStruct((M,) + io.shape, BF),
            weights, weights,
        ],
        scratch_shapes=[pltpu.VMEM((L, 3 * D), BF), DMA((3,)), DMA((M + 1,)), DMA((M,)), DMA((2, M + 1)), DMA((2, M)), DMA(sems), DMA(sems)],
        compiler_params=params_of(1, grid=1),
    )(lengths, x, w, proj, io)


def gelu_and_slope(x):
    phi = 0.5 + 0.5 * lax.erf(x * 0.7071067811865476)
    return x * phi, phi + x * (jnp.exp2((x * x) * (-0.5 * LOG2E)) * 0.3989422804014327)


def mlp_kernel(len_ref, x_ref, mixed_ref, cot_ref, params_ref, wproj_ref, win_ref, wout_ref, land_ref,
               y_ref, mgrad_ref, dmixed_ref, sums_ref, pproj_ref, pin_ref, pout_ref, din_ref, dout_ref,
               w_s, mid_s, hid_s, sg_s, sec_s, br_s, act_s, eg_s, got_s, near_s, diag_s, send_s, far_s,
               load_sems, save_sems, gsends, grecvs, ssends, srecvs, far_recvs, *, tr):
    at = Place()
    G, M = at.G, at.M
    L, D = x_ref.shape
    R, Fb = land_ref.shape[2:]
    half = M // 2
    gain, bias = params_ref[1:2, :], params_ref[3:4, :]
    loads = [pltpu.make_async_copy((win_ref, wout_ref)[a].at[k], w_s.at[k, a], load_sems.at[k, a]) for k in range(half) for a in range(2)]
    for cp in loads:
        cp.start()
    at.greet()
    gathers = [
        [GatherUnit(at, land_ref.at[at.near[k], a], lambda g, c, k=k, a=a: w_s.at[k, a, g * 2 + c], a, gsends.at[k - half, a], grecvs.at[k - half, a])
         for a in range(2)]
        for k in range(half, M)
    ]
    sums = [
        SumUnit(at, lambda c, a=a: w_s.at[0, a, pl.ds(c * G, G)], None, got_s.at[a], near_s.at[a], diag_s.at[a], send_s.at[a], far_s, total, 0, a,
                ssends.at[a], srecvs.at[a], far_recvs)
        for a, total in enumerate((din_ref, dout_ref))
    ]

    def rows(i):
        return pl.ds(i * tr, tr)

    def enter(i):
        sl = rows(i)
        mid = x_ref[sl, :].astype(F32) + dot(mixed_ref[sl, :], wproj_ref[...], NN)
        mid_s[sl, :] = mid
        hid_s[sl, :] = mid
        sec_s[sl, :] = (norm_stats(mid)[0] * gain + bias).astype(BF)
        at_row = lax.broadcasted_iota(jnp.int32, (tr, D), 0) + i * tr
        br_s[sl, :] = jnp.where(at_row < len_ref[0], cot_ref[sl, :].astype(F32), 0.0).astype(BF)
        sg_s[sl, :] = jnp.zeros((tr, D), F32)

    n_rows = L // tr
    enter(0)
    at.meet()
    for group in gathers:
        for u in group:
            u.spread()
    for i in range(1, n_rows):
        enter(i)
    for cp in loads:
        cp.wait()
    per = n_rows + 2
    plan = {}

    def put(k, i, name, group):
        plan.setdefault((min(k, M - 1), min(i, per - 1)), []).extend(getattr(u, name) for u in group)

    for n, group in enumerate(gathers):
        put(n, 2, "relay", group)
        put(n + 1, 1, "last", group)
        put(half + n, 0, "finish", group)
    put(1, 0, "start", sums)
    put(1, 2, "pair", sums)
    put(2, 1, "cross", sums)
    put(3, 1, "join", sums)

    def block(k, carry):
        def between(i):
            for (at_k, at_i), actions in sorted(plan.items(), key=lambda item: item[0]):
                if at_i == i:

                    @pl.when(k == at_k)
                    def _(actions=actions):
                        for action in actions:
                            action()

        between(0)
        win, wout = (w_s[k, a].reshape(D, Fb) for a in range(2))
        for i in range(n_rows):
            if i:
                between(i)
            sl = rows(i)
            value, slope = gelu_and_slope(dot(sec_s[sl, :], win, NN))
            act = value.astype(BF)
            eg = (dot(br_s[sl, :], wout, NN) * slope).astype(BF)
            act_s[sl, :], eg_s[sl, :] = act, eg
            hid_s[sl, :] += dot(act, wout, NT)
            sg_s[sl, :] += dot(eg, win, NT)
        for a, (left, right) in enumerate(((sec_s, eg_s), (br_s, act_s))):
            between(n_rows + a)
            grad = dot(left[...], right[...], TN)
            for g in range(G):
                for c in range(2):
                    row = (g * 2 + c) * R
                    w_s[k, a, c * G + g] = grad[row : row + R, :].astype(BF)

        @pl.when(k > 0)
        def _():
            for a, ref in enumerate((pin_ref, pout_ref)):
                pltpu.make_async_copy(w_s.at[k, a], ref.at[k - 1], save_sems.at[k - 1, a]).start()

        return carry

    lax.fori_loop(0, M, block, 0)
    sums_ref[...] = jnp.zeros_like(sums_ref)
    n_back = L // 256 if L % 256 == 0 else 1
    tb = L // n_back

    def back(i, carry):
        sl = pl.ds(pl.multiple_of(i * tb, tb), tb)
        y_ref[sl, :] = hid_s[sl, :].astype(BF)
        xhat, r = norm_stats(mid_s[sl, :])
        e = sg_s[sl, :]
        sums_ref[1:2, :] += jnp.sum(e * xhat, axis=0, keepdims=True)
        sums_ref[3:4, :] += jnp.sum(e, axis=0, keepdims=True)
        grad = br_s[sl, :].astype(F32) + norm_pull(e, xhat, r, gain)
        mgrad_ref[sl, :] = grad
        low = grad.astype(BF)
        sec_s[sl, :] = low
        dmixed_ref[sl, :] = dot(low, wproj_ref[...], NT).astype(BF)
        return carry

    lax.fori_loop(0, n_back, back, 0)
    grad = dot(mixed_ref[...], sec_s[...], TN)
    R_p = pproj_ref.shape[3]
    for g in range(G):
        for c in range(2):
            for z in range(M):
                row = ((g * 2 + c) * M + z) * R_p
                pproj_ref[z, c, g] = grad[row : row + R_p, :].astype(BF)
    for k in range(1, M):
        for a, ref in enumerate((pin_ref, pout_ref)):
            pltpu.make_async_copy(w_s.at[k, a], ref.at[k - 1], save_sems.at[k - 1, a]).wait()
    for u in sums:
        u.finish()


def mlp(lengths, x, mixed, cot, params, wproj, win, wout, land, R_p, tr):
    G, M = lax.axis_size("dp") // 2, lax.axis_size("mp")
    half = M // 2
    L, D = x.shape
    R, Fb = block = land.shape[2:]
    gsems, ssems = (M - half, 2, GatherUnit.count(G)), (2, SumUnit.count(G))
    pieces = jax.ShapeDtypeStruct((M - 1, 2 * G) + block, BF)
    return pl.pallas_call(
        functools.partial(mlp_kernel, tr=tr),
        in_specs=[SMEM, VMEM, VMEM, VMEM, VMEM, VMEM, ANY, ANY, ANY],
        out_specs=[VMEM] * 5 + [ANY, ANY, VMEM, VMEM],
        out_shape=[
            jax.ShapeDtypeStruct((L, D), BF),
            jax.ShapeDtypeStruct((L, D), F32),
            jax.ShapeDtypeStruct((L, D), BF),
            jax.ShapeDtypeStruct(params.shape, F32),
            jax.ShapeDtypeStruct((M, 2, G, R_p, D), BF),
            pieces, pieces,
            jax.ShapeDtypeStruct(block, F32), jax.ShapeDtypeStruct(block, F32),
        ],
        scratch_shapes=[
            pltpu.VMEM((M, 2, 2 * G) + block, BF),
            pltpu.VMEM((L, D), F32), pltpu.VMEM((L, D), F32), pltpu.VMEM((L, D), F32),
            pltpu.VMEM((L, D), BF), pltpu.VMEM((L, D), BF), pltpu.VMEM((L, Fb), BF), pltpu.VMEM((L, Fb), BF),
        ] + sum_buffers(2, G, block, own=False) + [DMA((half, 2)), DMA((M - 1, 2)), DMA(gsems), DMA(gsems), DMA(ssems), DMA(ssems), DMA((1,))],
        compiler_params=params_of(4),
    )(lengths, x, mixed, cot, params, wproj, win, wout, land)


def attend_back_kernel(len_ref, q_ref, k_ref, v_ref, do_ref, wide_ref, lse_ref, pin_ref, pout_ref, pproj_ref, hin_ref, hout_ref,
                       dqkv_ref, din_ref, dout_ref, dproj_ref,
                       own_m, got_m, near_m, diag_m, send_m, far_in, own_p, got_p, near_p, diag_p, send_p, far_p, far_out,
                       sends, recvs, far_recvs, *, tq):
    p, steps = pl.program_id(0), pl.num_programs(0)
    at = Place()
    G, M = at.G, at.M
    parts = q_ref.shape[0] // tq
    units = []

    def add(part, bufs, far, total, n, way, kind):
        k = len(units)
        units.append(SumUnit(at, part, *bufs, far, total, n, way, sends.at[k], recvs.at[k], far_recvs.at[kind], local=True))
        return units[-1]

    main = []
    for n in reversed(range(1, M)):
        main.append([
            add(lambda c, n=n, ref=ref: ref.at[n - 1, pl.ds(c * G, G)], [b.at[2 * (n - 1) + a] for b in (own_m, got_m, near_m, diag_m, send_m)],
                far, total, n, a, a)
            for a, (ref, far, total) in enumerate(((pin_ref, far_in, din_ref), (pout_ref, far_out, dout_ref)))
        ])
    proj = [
        add(lambda c, n=n: pproj_ref.at[at.near[n], c], [b.at[n] for b in (own_p, got_p, near_p, diag_p, send_p)], far_p, dproj_ref, n, n % 2, 2)
        for n in reversed(range(M))
    ]
    plan = {}

    def put(slot, name, group):
        plan.setdefault(min(slot, ATTEND_STEPS * parts - 1), []).extend(getattr(u, name) for u in group)

    def begin():
        din_ref[...], dout_ref[...] = hin_ref[...], hout_ref[...]

    plan[0] = [at.greet, begin, at.meet]
    for group in main + [proj]:
        put(0, "start", group)
    for n, group in enumerate(main):
        put(1 + n, "pair", group)
        put(4 + 2 * n, "cross", group)
        put(10 + 3 * n, "join", group)
    put(5, "pair", proj)
    put(11, "cross", proj)
    put(18, "join", proj)
    for group in main + [proj]:
        put(23, "close", group)
    attend_back_step(p, len_ref, q_ref, k_ref, v_ref, do_ref, wide_ref, lse_ref, dqkv_ref.at[0], dqkv_ref.at[1], dqkv_ref.at[2], tq, at_slots(p, parts, plan))

    @pl.when(p == steps - 1)
    def _():
        for u in units:
            u.finish()


def attend_back(lengths, packed, do, wide, lse, p_in, p_out, p_proj, h_in, h_out, tq):
    G, M = lax.axis_size("dp") // 2, lax.axis_size("mp")
    L, D = do.shape
    pairs = D // 128
    column = lambda off: pl.BlockSpec((L, 128), lambda p, off=off: (0, off + p))
    whole = lambda shape: pl.BlockSpec(shape, lambda p: (0,) * len(shape))
    mshape, pshape = h_in.shape, p_proj.shape[3:]
    rest = 2 * (M - 1)
    sems = (rest + M, SumUnit.count(G))
    return pl.pallas_call(
        functools.partial(attend_back_kernel, tq=tq),
        grid=(pairs,),
        in_specs=[SMEM, column(0), column(pairs), column(2 * pairs), column(0), column(0), whole((L, 128)), ANY, ANY, ANY,
                  whole(mshape), whole(mshape)],
        out_specs=[pl.BlockSpec((3, L, 128), lambda p: (0, 0, p)), whole(mshape), whole(mshape), whole(pshape)],
        out_shape=[jax.ShapeDtypeStruct((3, L, D), BF)]
        + [jax.ShapeDtypeStruct(mshape, F32)] * 2 + [jax.ShapeDtypeStruct(pshape, F32)],
        scratch_shapes=sum_buffers(rest, G, mshape, far=M) + sum_buffers(M, G, pshape, far=M)
        + [pltpu.VMEM((M,) + mshape, BF), DMA(sems), DMA(sems), DMA((3, M))],
        compiler_params=params_of(2, grid=1),
    )(lengths, packed, packed, packed, do, wide, lse, p_in, p_out, p_proj, h_in, h_out)


def exit_kernel(x_ref, normed_ref, dqkv_ref, w_ref, mid_ref, second_ref, params_ref, grad_ref, qkv_ref, norms_ref,
                parts_s, got_s, near_s, diag_s, send_s, far_s, norm_s, small_parts, small_got,
                sends, recvs, far_recvs, small_sends, small_recvs, *, rows):
    at = Place(everyone=True)
    G, M = at.G, at.M
    L, D = x_ref.shape
    R = qkv_ref.shape[0]
    small = SmallScatter(at, small_parts, small_got, small_sends, small_recvs)
    units = []
    for t in range(3):
        units.append([
            SumUnit(at, lambda c, t=t, n=n: parts_s.at[t, at.near[n], c], None, *[b.at[t * M + n] for b in (got_s, near_s, diag_s, send_s)],
                    far_s.at[pl.ds(t * M, M)], qkv_ref.at[:, pl.ds(t * D, D)], n, (n + t) % 2, sends.at[t * M + n], recvs.at[t * M + n], far_recvs.at[t])
            for n in reversed(range(M))
        ])

    def run(t, name):
        for u in units[t]:
            getattr(u, name)()

    gain = params_ref[0:1, :]
    n_norm = L // rows
    norm_plan = {0: [(1, "cross")], 1: [(2, "pair"), (0, "join")], 2: [(2, "cross")], 3: [(1, "join")]}
    third_plan = {0: [], 1: [(0, "pair")], 2: [(0, "cross"), (1, "pair")]}

    def third(t, carry):
        grad = dot(normed_ref[...], dqkv_ref[t], TN)
        for g in range(G):
            for c in range(2):
                for z in range(M):
                    k = ((g * 2 + c) * M + z) * R
                    parts_s[t, z, c, g] = grad[k : k + R, :].astype(BF)
        for i, items in third_plan.items():

            @pl.when(t == i)
            def _(i=i, items=items):
                if i == 0:
                    at.meet()
                run(i, "start")
                for item in items:
                    run(*item)

        return carry

    def norm(i, carry):
        sl = pl.ds(pl.multiple_of(i * rows, rows), rows)
        e = sum(dot(dqkv_ref[t, sl, :], w_ref[t], NT) for t in range(3))
        xhat, r = norm_stats(x_ref[sl, :].astype(F32))
        grad_ref[sl, :] = mid_ref[sl, :] + norm_pull(e, xhat, r, gain)
        norm_s[0:1, :] += jnp.sum(e * xhat, axis=0, keepdims=True)
        norm_s[2:3, :] += jnp.sum(e, axis=0, keepdims=True)
        for j, items in norm_plan.items():
            if j < n_norm:

                @pl.when(i == j)
                def _(items=items):
                    for item in items:
                        run(*item)

        return carry

    at.greet()
    norm_s[...] = second_ref[...]
    lax.fori_loop(0, 3, third, 0)
    lax.fori_loop(0, n_norm, norm, 0)
    small.start(norm_s[...], R)
    for j, items in norm_plan.items():
        if j >= n_norm:
            for item in items:
                run(*item)
    run(2, "join")
    run(0, "close")
    run(1, "close")
    norms_ref[...] = small.collect()
    run(2, "close")
    for t in range(3):
        run(t, "finish")
    small.finish()


def leave(x, normed, dqkv, w, middle_grad, second_sums, params, R):
    G, M = lax.axis_size("dp") // 2, lax.axis_size("mp")
    L, D = x.shape
    n = 2 * G * M
    sems = (3 * M, SumUnit.count(G))
    return pl.pallas_call(
        functools.partial(exit_kernel, rows=min(256, L)),
        in_specs=[VMEM] * 7,
        out_specs=[VMEM] * 3,
        out_shape=[
            jax.ShapeDtypeStruct((L, D), F32),
            jax.ShapeDtypeStruct((R, 3 * D), F32),
            jax.ShapeDtypeStruct((8, 128), F32),
        ],
        scratch_shapes=[pltpu.VMEM((3, M, 2, G, R, D), BF)] + sum_buffers(3 * M, G, (R, D), own=False, far=3 * M)
        + [pltpu.VMEM((8, D), F32), pltpu.VMEM((n, 8, 128), F32), pltpu.VMEM((n, 8, 128), F32),
           DMA(sems), DMA(sems), DMA((3, M)), DMA((n,)), DMA((n,))],
        compiler_params=params_of(3),
    )(x, normed, dqkv, w, middle_grad, second_sums, params)


def per_device(inputs, lengths, attn_qkv, attn_proj, mlp_in, mlp_out, norm_gain, norm_bias, cotangent):
    n_dp, n_mp = lax.axis_size("dp"), lax.axis_size("mp")
    G = n_dp // 2
    L, D = inputs.shape
    R = attn_qkv.shape[1]
    here = (lax.axis_index("dp") * n_mp + lax.axis_index("mp")) * R
    small = jnp.concatenate([norm_gain[0], norm_bias[0]], axis=0).astype(F32)
    placed = lax.dynamic_update_slice(jnp.zeros((8, D), F32), small, (0, here))
    shard = attn_qkv[0].reshape(R, 3, D).transpose(1, 0, 2)
    wqkv, normed, params = entry(inputs, shard, placed)
    wqkv = wqkv.reshape(3, D, D)
    io = jnp.stack([mlp_in[0], mlp_out[0].T])
    mixed, wide, lse, packed, wproj, land, win, wout = attend(lengths, normed, wqkv, attn_proj[0], io, min(512, L))
    pieces = lambda w: w.reshape((w.shape[0], n_dp) + w.shape[3:])
    outputs, middle_grad, mixed_grad, second_sums, p_proj, p_in, p_out, h_in, h_out = mlp(
        lengths, inputs, mixed, cotangent, params, wproj.reshape(D, D), pieces(win), pieces(wout), land, R, min(512, L))
    dqkv, d_in, d_out, d_proj = attend_back(
        lengths, packed, mixed_grad, wide, lse, p_in, p_out, p_proj, h_in, h_out, min(256, L))
    input_grad, d_qkv, norms = leave(inputs, normed, dqkv, wqkv, middle_grad, second_sums, params, R)
    return (
        outputs,
        input_grad,
        d_qkv[None],
        d_proj[None],
        d_in[None],
        d_out.T[None],
        norms[None, :2, :R],
        norms[None, 2:4, :R],
    )


def solution(mesh):
    everywhere = ("dp", "mp")
    wide, columns, vector = P(everywhere, None), P(None, everywhere, None), P(None, None, everywhere)
    return jax.shard_map(
        per_device,
        mesh=mesh,
        in_specs=(wide, P(everywhere), columns, columns, P(None, "dp", "mp"), P(None, "mp", "dp"), vector, vector, wide),
        out_specs=(wide, wide, columns, columns, P(None, "dp", "mp"), P(None, "mp", "dp"), vector, vector),
        check_vma=False,
    )
```

```python
import functools

import jax
import jax.numpy as jnp
from jax import lax
from jax.experimental import pallas as pl
from jax.experimental.pallas import tpu as pltpu
from jax.sharding import PartitionSpec as P

F32, BF = jnp.float32, jnp.bfloat16
MESH = pl.DeviceIdType.MESH
HEAD_DIM = 64
SCALE = 0.125
LOG2E = 1.4426950408889634
TO_LOG2 = SCALE * LOG2E
NEG = -1e30
EPS = 1e-06
NN = (((1,), (0,)), ((), ()))
NT = (((1,), (1,)), ((), ()))
TN = (((0,), (0,)), ((), ()))
VMEM_LIMIT = 60 * 2**20
ANY = pl.BlockSpec(memory_space=pl.ANY)
VMEM = pl.BlockSpec(memory_space=pltpu.VMEM)
SMEM = pl.BlockSpec(memory_space=pltpu.SMEM)
DMA = pltpu.SemaphoreType.DMA


def dot(a, b, dims):
    return lax.dot_general(a, b, dims, preferred_element_type=F32)


def params_of(collective_id=None, grid=0):
    extra = {} if collective_id is None else {"collective_id": collective_id, "has_side_effects": True}
    if grid:
        extra["dimension_semantics"] = ("arbitrary",) * grid
    return pltpu.CompilerParams(vmem_limit_bytes=VMEM_LIMIT, **extra)


class Place:
    def __init__(self, everyone=False):
        self.everyone = everyone
        n_dp, self.M = lax.axis_size("dp"), lax.axis_size("mp")
        self.G = n_dp // 2
        dp = lax.axis_index("dp")
        self.g, self.c, self.z = dp // 2, lax.rem(dp, 2), lax.axis_index("mp")
        self.square = self.G == 4
        self.near = [self.z ^ n if self.M & (self.M - 1) == 0 else lax.rem(self.z + n, self.M) for n in range(self.M)]
        if self.square:
            self.chips = [self.g ^ 1, self.g ^ 2]
            self.diag = self.g ^ 3
        else:
            self.chips = [lax.rem(self.g + d, self.G) for d in range(1, self.G)]

    def chip(self, h):
        return (h * 2 + self.c, self.z)

    def core(self):
        return (self.g * 2 + 1 - self.c, self.z)

    def along(self, z):
        return (self.g * 2 + self.c, z)

    def peers(self):
        if self.everyone:
            n = 2 * self.G * self.M
            return [self.device(lax.rem(self.index + d, n)) for d in range(1, n)]
        return [self.along(s) for s in self.near[1:]] + [self.chip(h) for h in self.chips] + [self.core()]

    @property
    def index(self):
        return (self.g * 2 + self.c) * self.M + self.z

    def device(self, i):
        return (i // self.M, lax.rem(i, self.M))

    def greet(self):
        for dev in self.peers():
            pl.semaphore_signal(pltpu.get_barrier_semaphore(), inc=1, device_id=dev, device_id_type=MESH)

    def meet(self):
        pl.semaphore_wait(pltpu.get_barrier_semaphore(), len(self.peers()))


def remote(src, dst, send, recv, dev):
    return pltpu.make_async_remote_copy(src_ref=src, dst_ref=dst, send_sem=send, recv_sem=recv, device_id=dev, device_id_type=MESH)


class Along:
    def __init__(self, at, own, land, sends, recvs):
        self.at, self.own, self.land, self.sends, self.recvs = at, own, land, sends, recvs

    def _copy(self, n, source):
        return remote(self.own, self.land(source), self.sends.at[n], self.recvs.at[source], self.at.along(self.at.near[n]))

    def start(self, *ns):
        for n in ns:
            self._copy(n, self.at.z).start()

    def arrive(self, n):
        self._copy(n, self.at.near[n]).wait_recv()

    def finish(self):
        for n in range(1, self.at.M):
            self._copy(n, self.at.z).wait_send()


class GatherUnit:
    def __init__(self, at, src, slot, way, sends, recvs, local=True):
        self.at, self.src, self.slot, self.way, self.local = at, src, slot, way, local
        self.sends, self.recvs = sends, recvs

    @staticmethod
    def count(G):
        return 1 + (3 if G == 4 else G - 1) + G

    def _local(self):
        return pltpu.make_async_copy(self.src, self.slot(self.at.g, self.at.c), self.sends.at[0])

    def _to_chip(self, i):
        at = self.at
        return remote(self.src, self.slot(at.g, at.c), self.sends.at[1 + i], self.recvs.at[1 + i], at.chip(at.chips[i]))

    def _relay(self):
        at = self.at
        block = self.slot(at.chips[self.way], at.c)
        return remote(block, block, self.sends.at[3], self.recvs.at[3], at.chip(at.chips[1 - self.way]))

    def _to_core(self, i):
        at = self.at
        h = ([at.g] + at.chips + ([at.diag] if at.square else []))[i]
        k = self.count(at.G) - at.G + i
        block = self.slot(h, at.c)
        return remote(block if i else self.src, block, self.sends.at[k], self.recvs.at[k], at.core())

    def spread(self):
        for i in range(len(self.at.chips)):
            self._to_chip(i).start()
        self._to_core(0).start()
        if self.local:
            self._local().start()

    def relay(self):
        n = len(self.at.chips)
        for i in range(n):
            self._to_chip(i).wait_recv()
        if self.at.square:
            self._relay().start()
        for i in range(n):
            self._to_core(1 + i).start()

    def last(self):
        if self.at.square:
            self._relay().wait_recv()
            self._to_core(3).start()

    def finish(self):
        if self.local:
            self._local().wait()
        for i in range(len(self.at.chips)):
            self._to_chip(i).wait_send()
        if self.at.square:
            self._relay().wait_send()
        for i in range(self.at.G):
            self._to_core(i).wait()


class SumUnit:
    def __init__(self, at, part, own, got, near, diag, out, far, total, n, way, sends, recvs, far_recvs, local=False):
        self.at, self.part, self.own, self.got, self.near, self.diagonal = at, part, own, got, near, diag
        self.out, self.far, self.total, self.n, self.way = out, far, total, n, way
        self.sends, self.recvs, self.far_recvs, self.local = sends, recvs, far_recvs, local
        self.place = at.near[n]
        self.passed = at.M == 4 and n == 3
        self.opposite = None

    @staticmethod
    def count(G):
        return 3 + (3 if G == 4 else G)

    def _core(self):
        at = self.at
        return remote(self.part(1 - at.c), self.got, self.sends.at[0], self.recvs.at[0], at.core())

    def _local(self):
        return pltpu.make_async_copy(self.part(self.at.c), self.own, self.sends.at[2])

    def _diag(self):
        at = self.at
        return remote(self.got.at[at.diag], self.diagonal, self.sends.at[5], self.recvs.at[5], at.chip(at.chips[1 - self.way]))

    def _chip(self, i):
        at = self.at
        k = 3 + i
        return remote(self.got.at[at.chips[i]], self.near.at[i], self.sends.at[k], self.recvs.at[k], at.chip(at.chips[i]))

    def _z(self, slot):
        dev = self.at.along(self.at.near[1] if self.passed else self.place)
        return remote(self.out, self.far.at[slot], self.sends.at[1], self.far_recvs.at[slot], dev)

    def send_z(self):
        self._z(self.at.near[2] if self.passed else self.at.z).start()

    def start(self):
        self._core().start()
        if self.local:
            self._local().start()

    def launch(self):
        for i in range(len(self.at.chips)):
            self._chip(i).start()

    def pair(self, hold=False):
        at = self.at
        self._core().wait_recv()
        if self.local:
            self._local().wait()
            own = self.own
        else:
            own = self.part(at.c)

        def add(h, carry):
            self.got[h] = (self.got[h].astype(F32) + own[h].astype(F32)).astype(BF)
            return carry

        lax.fori_loop(0, at.G, add, 0)
        if at.square:
            self._diag().start()
        elif not hold:
            self.launch()

    def cross(self, hold=False):
        at = self.at
        if at.square:
            self._diag().wait_recv()
            h = at.chips[self.way]
            self.got[h] = (self.got[h].astype(F32) + self.diagonal[...].astype(F32)).astype(BF)
            if not hold:
                self.launch()

    def join(self):
        at = self.at
        value = self.got[at.g].astype(F32)
        for i in range(len(at.chips)):
            self._chip(i).wait_recv()
            value = value + self.near[i].astype(F32)
        if self.opposite is not None:
            self._z(at.near[3]).wait_recv()
            value = value + self.far[at.near[3]].astype(F32)
        if self.n:
            self.out[...] = value.astype(BF)
            self.send_z()
        else:
            self.total[...] = value

    def close(self):
        if self.n and not self.passed:
            self._z(self.place).wait_recv()
            self.total[...] += self.far[self.place].astype(F32)

    def finish(self, core=True, rest=True):
        at = self.at
        if core:
            self._core().wait_send()
            if at.square:
                self._diag().wait_send()
        if rest:
            if self.n:
                self._z(at.near[2] if self.passed else at.z).wait_send()
            for i in range(len(at.chips)):
                self._chip(i).wait_send()


def link(units):
    by_n = {u.n: u for u in units}
    if units[0].at.M == 4 and 3 in by_n:
        by_n[2].opposite = by_n[3]
    return units


def sum_buffers(n, G, shape, own=True, far=0):
    chips = 2 if G == 4 else G - 1
    block = lambda *lead: pltpu.VMEM(lead + shape, BF)
    return ([block(n, G)] if own else []) + [block(n, G), block(n, chips), block(n), block(n), block(max(far, 1))]


class SmallGather:
    def __init__(self, at, got, sends, recvs):
        self.at, self.got, self.sends, self.recvs = at, got, sends, recvs
        self.count = 2 * at.G * at.M

    def _copy(self, own, d, back):
        at = self.at
        to, other = lax.rem(at.index + d, self.count), lax.rem(at.index + self.count - d, self.count)
        return remote(own, self.got.at[other if back else at.index], self.sends.at[d], self.recvs.at[d], at.device(to))

    def start(self, own):
        def send(d, carry):
            self._copy(own, d, False).start()
            return carry

        lax.fori_loop(1, self.count, send, 0)

    def collect(self, own, R, width):
        def wait(d, carry):
            self._copy(own, d, True).wait_recv()
            return carry

        lax.fori_loop(1, self.count, wait, 0)
        self.got[self.at.index] = own[...]
        lane = lanes((own.shape[0], width))
        total = jnp.zeros((own.shape[0], width), F32)
        for i in range(self.count):
            wide = jnp.concatenate([self.got[i]] * (width // 128), axis=1)
            total = jnp.where(lane // R == i, pltpu.roll(wide, i * R % width, 1) if i else wide, total)
        return total

    def finish(self, own):
        def wait(d, carry):
            self._copy(own, d, False).wait_send()
            return carry

        lax.fori_loop(1, self.count, wait, 0)


class SmallScatter:
    def __init__(self, at, parts, got, sends, recvs):
        self.at, self.parts, self.got, self.sends, self.recvs = at, parts, got, sends, recvs
        self.count = 2 * at.G * at.M

    def _copy(self, d, back):
        at = self.at
        to, other = lax.rem(at.index + d, self.count), lax.rem(at.index + self.count - d, self.count)
        return remote(self.parts.at[to], self.got.at[other if back else at.index], self.sends.at[d], self.recvs.at[d], at.device(to))

    def start(self, value, R):
        for i in range(self.count):
            self.parts[i] = (pltpu.roll(value, value.shape[1] - i * R, 1) if i else value)[:, :128]

        def send(d, carry):
            self._copy(d, False).start()
            return carry

        lax.fori_loop(1, self.count, send, 0)

    def collect(self):
        def add(d, value):
            self._copy(d, True).wait_recv()
            return value + self.got[lax.rem(self.at.index + self.count - d, self.count)]

        return lax.fori_loop(1, self.count, add, self.parts[self.at.index])

    def finish(self):
        def wait(d, carry):
            self._copy(d, False).wait_send()
            return carry

        lax.fori_loop(1, self.count, wait, 0)


def norm_stats(v):
    centre = v - jnp.mean(v, axis=-1, keepdims=True)
    r = lax.rsqrt(jnp.mean(centre * centre, axis=-1, keepdims=True) + EPS)
    return centre * r, r


def norm_pull(e, xhat, r, g):
    y = e * g
    return r * (y - jnp.mean(y, axis=-1, keepdims=True) - xhat * jnp.mean(y * xhat, axis=-1, keepdims=True))


def entry_kernel(x_ref, shard_ref, own_ref, w_ref, normed_ref, params_ref, got, chain_sends, chain_recvs, sends, recvs,
                 small_sends, small_recvs, *, rows):
    at = Place(everyone=True)
    at.greet()
    land = lambda s: w_ref.at[:, at.g, at.c, s]
    chain = Along(at, shard_ref, land, chain_sends, chain_recvs)
    units = [
        GatherUnit(at, land(at.near[n]) if n else shard_ref, lambda g, c, n=n: w_ref.at[:, g, c, at.near[n]], n % 2, sends.at[n], recvs.at[n], n == 0)
        for n in range(at.M)
    ]
    small = SmallGather(at, got, small_sends, small_recvs)
    L, D = x_ref.shape
    at.meet()
    chain.start(1)
    units[0].spread()
    chain.start(*range(2, at.M))
    small.start(own_ref)

    def norm(i, carry):
        sl = pl.ds(pl.multiple_of(i * rows, rows), rows)
        xhat, _ = norm_stats(x_ref[sl, :].astype(F32))
        normed_ref[sl, :] = (xhat * params_ref[0:1, :] + params_ref[2:3, :]).astype(BF)
        return carry

    steps = L // rows
    for n in range(1, at.M):
        chain.arrive(n)
        units[n].spread()
        units[n - 1].relay()
        if n > 1:
            units[n - 2].last()
    params_ref[...] = small.collect(own_ref, shard_ref.shape[1], D)
    lax.fori_loop(0, steps // 2, norm, 0)
    units[-1].relay()
    if at.M > 1:
        units[-2].last()
    lax.fori_loop(steps // 2, steps, norm, 0)
    units[-1].last()
    for u in units:
        u.finish()
    chain.finish()
    small.finish(own_ref)


def entry(x, shard, own):
    G, M = lax.axis_size("dp") // 2, lax.axis_size("mp")
    L, D = x.shape
    n = 2 * G * M
    sems = (M, GatherUnit.count(G))
    return pl.pallas_call(
        functools.partial(entry_kernel, rows=min(256, L)),
        in_specs=[VMEM, ANY, VMEM],
        out_specs=[ANY, VMEM, VMEM],
        out_shape=[
            jax.ShapeDtypeStruct((3, G, 2, M) + shard.shape[1:], BF),
            jax.ShapeDtypeStruct((L, D), BF),
            jax.ShapeDtypeStruct((8, D), F32),
        ],
        scratch_shapes=[pltpu.VMEM((n,) + own.shape, F32), DMA((M + 1,)), DMA((M,)), DMA(sems), DMA(sems), DMA((n,)), DMA((n,))],
        compiler_params=params_of(0),
    )(x, shard, own)


def lanes(shape):
    return lax.broadcasted_iota(jnp.int32, shape, len(shape) - 1)


def three_parts(x):
    hi = x.astype(BF)
    rest = x - hi.astype(F32)
    mid = rest.astype(BF)
    return hi, mid, (rest - mid.astype(F32)).astype(BF)


def mask_bias(shape, length):
    return jnp.where(lax.broadcasted_iota(jnp.int32, shape, 0) < length, 0.0, NEG).astype(BF)


def attend_step(p, len_ref, q_ref, k_ref, v_ref, o_ref, wide_ref, lse_ref, tq, between):
    L = q_ref.shape[0]
    lane = lanes((L, 128))
    k, v = k_ref[...], v_ref[...]
    bias = mask_bias((L, 128), len_ref[0])
    zero, one = jnp.zeros((L, 128), BF), jnp.ones((L, 128), BF)

    @pl.when(p == 0)
    def _():
        lse_ref[...] = jnp.zeros_like(lse_ref)

    keys, values = [], []
    for h in range(2):
        mine = (lane < 64) if h == 0 else (lane >= 64)
        spare = 64 * (1 - h)
        keys.append(jnp.where(mine, k, jnp.where(lane == spare, bias, zero)))
        values.append(jnp.where(mine, v, jnp.where(lane == spare, one, zero)))
    lq = lanes((tq, 128))
    for i in range(L // tq):
        between(i)
        sl = pl.ds(i * tq, tq)
        q = q_ref[sl, :]
        outs, sums = [], []
        for h in range(2):
            mine = (lq < 64) if h == 0 else (lq >= 64)
            spare = 64 * (1 - h)
            q_h = jnp.where(mine, q, jnp.where(lq == spare, jnp.ones((tq, 128), BF), jnp.zeros((tq, 128), BF)))
            s = dot(q_h, keys[h], NT)
            top = jnp.max(s, axis=1, keepdims=True) * TO_LOG2
            e = jnp.exp2(s * TO_LOG2 - top)
            o = dot(e.astype(BF), values[h], NN)
            total = o[:, spare : spare + 1]
            outs.append(o / total)
            sums.append(top + jnp.log2(total))
        out = jnp.where(lq < 64, outs[0], outs[1])
        wide_ref[sl, :] = out
        o_ref[sl, :] = out.astype(BF)
        lse = lse_ref[sl, :]
        lse = jnp.where(lq == 2 * p, sums[0], lse)
        lse_ref[sl, :] = jnp.where(lq == 2 * p + 1, sums[1], lse)


def attend_back_step(p, len_ref, q_ref, k_ref, v_ref, do_ref, wide_ref, lse_ref, dq_ref, dk_ref, dv_ref, tq, between):
    L = q_ref.shape[0]
    lane = lanes((L, 128))
    k, v = k_ref[...], v_ref[...]
    bias = mask_bias((L, 128), len_ref[0])
    zero, one = jnp.zeros((L, 128), BF), jnp.ones((L, 128), BF)
    keys, values = [], []
    for h in range(2):
        mine = (lane < 64) if h == 0 else (lane >= 64)
        b = 64 * (1 - h)
        ones = jnp.where((lane > b) & (lane < b + 4), one, zero)
        keys.append(jnp.where(mine, k, jnp.where(lane == b, bias, ones)))
        values.append(jnp.where(mine, v, ones))
    lq = lanes((tq, 128))
    dk, dv = [jnp.zeros((L, 128), F32)] * 2, [jnp.zeros((L, 128), F32)] * 2
    for i in range(L // tq):
        between(i)
        sl = pl.ds(i * tq, tq)
        q, do, lse = q_ref[sl, :], do_ref[sl, :], lse_ref[sl, :]
        product = wide_ref[sl, :] * do.astype(F32)
        dq = []
        for h in range(2):
            mine = (lq < 64) if h == 0 else (lq >= 64)
            b = 64 * (1 - h)
            minus_delta = -jnp.sum(jnp.where(mine, product, 0.0), axis=1, keepdims=True)
            minus_lse = -jnp.sum(jnp.where(lq == 2 * p + h, lse, 0.0), axis=1, keepdims=True) * (1.0 / TO_LOG2)

            def with_spare(x, term, first):
                hi, mid, lo = three_parts(jnp.broadcast_to(term, (tq, 128)))
                low = jnp.where(lq == b + 2, mid, jnp.where(lq == b + 3, lo, jnp.zeros((tq, 128), BF)))
                low = jnp.where(lq == b, jnp.full((tq, 128), first, BF), jnp.where(lq == b + 1, hi, low))
                return jnp.where(mine, x, low)

            st = dot(keys[h], with_spare(q, minus_lse, 1.0), NT)
            pt = jnp.exp2(st * TO_LOG2)
            dpt = dot(values[h], with_spare(do, minus_delta, 0.0), NT)
            ds = (pt * dpt).astype(BF)
            dv[h] = dv[h] + dot(pt.astype(BF), do, NN)
            dk[h] = dk[h] + dot(ds, q, NN)
            dq.append(dot(ds, k, TN))
        dq_ref[sl, :] = (jnp.where(lq < 64, dq[0], dq[1]) * SCALE).astype(BF)
    dk_ref[...] = (jnp.where(lane < 64, dk[0], dk[1]) * SCALE).astype(BF)
    dv_ref[...] = jnp.where(lane < 64, dv[0], dv[1]).astype(BF)


def at_slots(p, per_step, plan):
    def between(i):
        for slot, actions in sorted(plan.items()):
            if slot % per_step == i:

                @pl.when(p == slot // per_step)
                def _(actions=actions):
                    for action in actions:
                        action()

    return between


def attend_kernel(len_ref, x_ref, w_ref, proj_ref, io_ref, o_ref, wide_ref, lse_ref, packed_ref, wproj_ref, land_ref, win_ref, wout_ref,
                  packed_s, save_sem, pchain_sends, pchain_recvs, chain_sends, chain_recvs, sends, recvs, *, tq):
    p, steps = pl.program_id(0), pl.num_programs(0)
    at = Place()
    M = at.M
    half = M // 2
    D = x_ref.shape[1]
    parts = x_ref.shape[0] // tq
    land = [lambda s, a=a: land_ref.at[s, a] for a in range(2)]
    pland = lambda s: wproj_ref.at[at.g, at.c, s]
    pchain = Along(at, proj_ref, pland, pchain_sends, pchain_recvs)
    chains = [Along(at, io_ref.at[a], land[a], chain_sends.at[a], chain_recvs.at[a]) for a in range(2)]
    main = [
        [GatherUnit(at, land[a](at.near[n]) if n else io_ref.at[a], lambda g, c, n=n, ref=ref: ref.at[n, g, c], a, sends.at[2 * n + a], recvs.at[2 * n + a])
         for a, ref in enumerate((win_ref, wout_ref))]
        for n in range(half)
    ]
    proj = [
        GatherUnit(at, pland(at.near[n]) if n else proj_ref, lambda g, c, n=n: wproj_ref.at[g, c, at.near[n]], n % 2,
                   sends.at[2 * half + n], recvs.at[2 * half + n], n == 0)
        for n in range(M)
    ]
    own_land = [pltpu.make_async_copy(io_ref.at[a], land_ref.at[at.z, a], save_sem.at[1 + a]) for a in range(2)]
    save = pltpu.make_async_copy(packed_s, packed_ref, save_sem.at[0])

    def third(t):
        packed_s[:, pl.ds(t * D, D)] = dot(x_ref[...], w_ref[t], NN).astype(BF)

    @pl.when(p == 0)
    def _():
        at.greet()
        third(0)
        at.meet()
        pchain.start(*range(1, M))
        for n in range(1, M):
            for chain in chains:
                chain.start(n)
        proj[0].spread()
        for u in main[0]:
            u.spread()
        for cp in own_land:
            cp.start()
        third(1)
        third(2)
        save.start()

    plan = {}

    def put(slot, *actions):
        plan.setdefault(min(slot, ATTEND_STEPS * parts - 1), []).extend(actions)

    def arrive(chain, n, unit=None):
        def act():
            chain.arrive(n)
            if unit is not None:
                unit.spread()

        return act

    for n in range(1, M):
        put((1, 4, 6)[min(n, 3) - 1], arrive(pchain, n, proj[n]))
    put(2, proj[0].relay)
    for n in range(1, half):
        put(1 + 2 * n, arrive(chains[0], n, main[n][0]))
        put(2 + 2 * n, arrive(chains[1], n, main[n][1]))
    put(4, main[0][0].relay, main[0][1].relay)
    put(5, proj[0].last)
    for n in range(1, M):
        put(3 + 2 * n, proj[n].relay)
        put(min(6 + 2 * n, 11), proj[n].last)
    for n in range(1, half):
        put(6 + n, main[n][0].relay)
        put(7 + n, main[n][1].relay)
    put(8, main[0][0].last, main[0][1].last)
    for n in range(1, half):
        put(10 + n, main[n][0].last, main[n][1].last)
    lane = pl.multiple_of(p * 128, 128)
    column = lambda t: packed_s.at[:, pl.ds(t * D + lane, 128)]
    attend_step(p, len_ref, column(0), column(1), column(2), o_ref, wide_ref, lse_ref, tq, at_slots(p, parts, plan))

    @pl.when(p == steps - 1)
    def _():
        for n in range(half, M):
            for chain in chains:
                chain.arrive(n)
        for group in main + [proj, chains, [pchain]]:
            for u in group:
                u.finish()
        save.wait()
        for cp in own_land:
            cp.wait()


ATTEND_STEPS = 6


def attend(lengths, x, w, proj, io, tq):
    G, M = lax.axis_size("dp") // 2, lax.axis_size("mp")
    L, D = x.shape
    half = M // 2
    column = pl.BlockSpec((L, 128), lambda p: (0, p))
    whole = lambda shape: pl.BlockSpec(shape, lambda p: (0,) * len(shape), pipeline_mode=pl.Buffered(1))
    sems = (2 * half + M, GatherUnit.count(G))
    weights = jax.ShapeDtypeStruct((half, G, 2) + io.shape[1:], BF)
    return pl.pallas_call(
        functools.partial(attend_kernel, tq=tq),
        grid=(D // 128,),
        in_specs=[SMEM, whole(x.shape), whole(w.shape), ANY, ANY],
        out_specs=[column, column, pl.BlockSpec((L, 128), lambda p: (0, 0)), ANY, ANY, ANY, ANY, ANY],
        out_shape=[
            jax.ShapeDtypeStruct((L, D), BF),
            jax.ShapeDtypeStruct((L, D), F32),
            jax.ShapeDtypeStruct((L, 128), F32),
            jax.ShapeDtypeStruct((L, 3 * D), BF),
            jax.ShapeDtypeStruct((G, 2, M) + proj.shape, BF),
            jax.ShapeDtypeStruct((M,) + io.shape, BF),
            weights, weights,
        ],
        scratch_shapes=[pltpu.VMEM((L, 3 * D), BF), DMA((3,)), DMA((M + 1,)), DMA((M,)), DMA((2, M + 1)), DMA((2, M)), DMA(sems), DMA(sems)],
        compiler_params=params_of(1, grid=1),
    )(lengths, x, w, proj, io)


def gelu_and_slope(x):
    phi = 0.5 + 0.5 * lax.erf(x * 0.7071067811865476)
    return x * phi, phi + x * (jnp.exp2((x * x) * (-0.5 * LOG2E)) * 0.3989422804014327)


def mlp_kernel(len_ref, x_ref, mixed_ref, cot_ref, params_ref, wproj_ref, win_ref, wout_ref, land_ref,
               y_ref, mgrad_ref, dmixed_ref, sums_ref, pproj_ref, pin_ref, pout_ref, din_ref, dout_ref, half_ref,
               w_s, mid_s, hid_s, sg_s, sec_s, br_s, act_s, eg_s, got_s, near_s, diag_s,
               load_sems, save_sems, gsends, grecvs, ssends, srecvs, *, tr):
    at = Place()
    G, M = at.G, at.M
    L, D = x_ref.shape
    R, Fb = land_ref.shape[2:]
    half = M // 2
    gain, bias = params_ref[1:2, :], params_ref[3:4, :]
    loads = [pltpu.make_async_copy((win_ref, wout_ref)[a].at[k], w_s.at[k, a], load_sems.at[k, a]) for k in range(half) for a in range(2)]
    for cp in loads:
        cp.start()
    at.greet()
    gathers = [
        [GatherUnit(at, land_ref.at[at.near[k], a], lambda g, c, k=k, a=a: w_s.at[k, a, g * 2 + c], a, gsends.at[k - half, a], grecvs.at[k - half, a])
         for a in range(2)]
        for k in range(half, M)
    ]
    sums = [
        [SumUnit(at, lambda c, k=k, a=a: w_s.at[k, a, pl.ds(c * G, G)], None, *[b.at[2 * k + a] for b in (got_s, near_s, diag_s)], None,
                 None, total, k, a, ssends.at[2 * k + a], srecvs.at[2 * k + a], None)
         for a, total in enumerate((din_ref, dout_ref))]
        for k in range(2)
    ]

    def rows(i):
        return pl.ds(i * tr, tr)

    def enter(i):
        sl = rows(i)
        mid = x_ref[sl, :].astype(F32) + dot(mixed_ref[sl, :], wproj_ref[...], NN)
        mid_s[sl, :] = mid
        hid_s[sl, :] = mid
        sec_s[sl, :] = (norm_stats(mid)[0] * gain + bias).astype(BF)
        at_row = lax.broadcasted_iota(jnp.int32, (tr, D), 0) + i * tr
        br_s[sl, :] = jnp.where(at_row < len_ref[0], cot_ref[sl, :].astype(F32), 0.0).astype(BF)
        sg_s[sl, :] = jnp.zeros((tr, D), F32)

    n_rows = L // tr
    enter(0)
    at.meet()
    for group in gathers:
        group[0].spread()
        if group is gathers[0]:
            group[1].spread()
    for i in range(1, n_rows):
        enter(i)
    for cp in loads:
        cp.wait()
    per = n_rows + 2
    plan = {}

    def put(k, i, name, group):
        plan.setdefault((min(k, M - 1), min(i, per - 1)), []).extend(getattr(u, name) for u in group)

    put(0, 3, "relay", gathers[0])
    for n, group in enumerate(gathers):
        if n:
            put(0, 3, "spread", group[1:])
            put(n, 3, "relay", group)
        put(n + 1, 2, "last", group)
        put(half + n, 0, "finish", group)
    put(1, 0, "start", sums[0])
    put(1, 2, "pair", sums[0])
    put(2, 0, "start", sums[1])
    put(2, 1, "cross", sums[0])
    plan.setdefault((2, 3), []).extend(functools.partial(u.pair, True) for u in sums[1])
    put(3, 1, "join", sums[0])

    def block(k, carry):
        def between(i):
            for (at_k, at_i), actions in sorted(plan.items(), key=lambda item: item[0]):
                if at_i == i:

                    @pl.when(k == at_k)
                    def _(actions=actions):
                        for action in actions:
                            action()

        between(0)
        win, wout = (w_s[k, a].reshape(D, Fb) for a in range(2))
        for i in range(n_rows):
            if i:
                between(i)
            sl = rows(i)
            value, slope = gelu_and_slope(dot(sec_s[sl, :], win, NN))
            act = value.astype(BF)
            eg = (dot(br_s[sl, :], wout, NN) * slope).astype(BF)
            act_s[sl, :], eg_s[sl, :] = act, eg
            hid_s[sl, :] += dot(act, wout, NT)
            sg_s[sl, :] += dot(eg, win, NT)
        for a, (left, right) in enumerate(((sec_s, eg_s), (br_s, act_s))):
            between(n_rows + a)
            grad = dot(left[...], right[...], TN)
            for g in range(G):
                for c in range(2):
                    row = (g * 2 + c) * R
                    w_s[k, a, c * G + g] = grad[row : row + R, :].astype(BF)

        @pl.when(k > 1)
        def _():
            for a, ref in enumerate((pin_ref, pout_ref)):
                pltpu.make_async_copy(w_s.at[k, a], ref.at[k - 2], save_sems.at[k - 2, a]).start()

        return carry

    lax.fori_loop(0, M, block, 0)
    sums_ref[...] = jnp.zeros_like(sums_ref)
    n_back = L // 256 if L % 256 == 0 else 1
    tb = L // n_back

    def back(i, carry):
        sl = pl.ds(pl.multiple_of(i * tb, tb), tb)
        y_ref[sl, :] = hid_s[sl, :].astype(BF)
        xhat, r = norm_stats(mid_s[sl, :])
        e = sg_s[sl, :]
        sums_ref[1:2, :] += jnp.sum(e * xhat, axis=0, keepdims=True)
        sums_ref[3:4, :] += jnp.sum(e, axis=0, keepdims=True)
        grad = br_s[sl, :].astype(F32) + norm_pull(e, xhat, r, gain)
        mgrad_ref[sl, :] = grad
        low = grad.astype(BF)
        sec_s[sl, :] = low
        dmixed_ref[sl, :] = dot(low, wproj_ref[...], NT).astype(BF)
        return carry

    lax.fori_loop(0, n_back, back, 0)
    for u in sums[1]:
        u.cross(True)
    save_half = pltpu.make_async_copy(got_s.at[pl.ds(2, 2)], half_ref, load_sems.at[0, 0])
    save_half.start()
    grad = dot(mixed_ref[...], sec_s[...], TN)
    R_p = pproj_ref.shape[3]
    for g in range(G):
        for c in range(2):
            for z in range(M):
                row = ((g * 2 + c) * M + z) * R_p
                pproj_ref[z, c, g] = grad[row : row + R_p, :].astype(BF)
    for k in range(2, M):
        for a, ref in enumerate((pin_ref, pout_ref)):
            pltpu.make_async_copy(w_s.at[k, a], ref.at[k - 2], save_sems.at[k - 2, a]).wait()
    save_half.wait()
    for k, group in enumerate(sums):
        for u in group:
            u.finish(True, k == 0)


def mlp(lengths, x, mixed, cot, params, wproj, win, wout, land, R_p, tr):
    G, M = lax.axis_size("dp") // 2, lax.axis_size("mp")
    half = M // 2
    L, D = x.shape
    R, Fb = block = land.shape[2:]
    gsems, ssems = (M - half, 2, GatherUnit.count(G)), (4, SumUnit.count(G))
    pieces = jax.ShapeDtypeStruct((M - 2, 2 * G) + block, BF)
    return pl.pallas_call(
        functools.partial(mlp_kernel, tr=tr),
        in_specs=[SMEM, VMEM, VMEM, VMEM, VMEM, VMEM, ANY, ANY, ANY],
        out_specs=[VMEM] * 5 + [ANY, ANY, VMEM, VMEM, ANY],
        out_shape=[
            jax.ShapeDtypeStruct((L, D), BF),
            jax.ShapeDtypeStruct((L, D), F32),
            jax.ShapeDtypeStruct((L, D), BF),
            jax.ShapeDtypeStruct(params.shape, F32),
            jax.ShapeDtypeStruct((M, 2, G, R_p, D), BF),
            pieces, pieces,
            jax.ShapeDtypeStruct(block, F32), jax.ShapeDtypeStruct(block, F32), jax.ShapeDtypeStruct((2, G) + block, BF),
        ],
        scratch_shapes=[
            pltpu.VMEM((M, 2, 2 * G) + block, BF),
            pltpu.VMEM((L, D), F32), pltpu.VMEM((L, D), F32), pltpu.VMEM((L, D), F32),
            pltpu.VMEM((L, D), BF), pltpu.VMEM((L, D), BF), pltpu.VMEM((L, Fb), BF), pltpu.VMEM((L, Fb), BF),
        ] + sum_buffers(4, G, block, own=False)[:3] + [DMA((half, 2)), DMA((M - 2, 2)), DMA(gsems), DMA(gsems), DMA(ssems), DMA(ssems)],
        compiler_params=params_of(4),
    )(lengths, x, mixed, cot, params, wproj, win, wout, land)


def attend_back_kernel(len_ref, q_ref, k_ref, v_ref, do_ref, wide_ref, lse_ref, normed_ref, pin_ref, pout_ref, pproj_ref, hin_ref, hout_ref, half_ref,
                       dqkv_ref, din_ref, dout_ref, dproj_ref, sum_ref, rest_ref,
                       own_m, got_m, near_m, diag_m, send_m, far_in, far_out, own_p, got_p, near_p, diag_p, send_p, far_p,
                       parts_s, got_q, near_q, diag_q, send_q, far_q, sends, recvs, far_recvs, far_recvs_q, save_sem, *, tq):
    p, steps = pl.program_id(0), ATTEND_STEPS
    at = Place()
    G, M = at.G, at.M
    parts = q_ref.shape[0] // tq
    R = sum_ref.shape[1]
    units = []

    def add(part, bufs, far, total, n, way, recv, local=True):
        k = len(units)
        units.append(SumUnit(at, part, *bufs, far, total, n, way, sends.at[k], recvs.at[k], recv, local=local))
        return units[-1]

    def block(n):
        made = []
        for a, (ref, far, total) in enumerate(((pin_ref, far_in, din_ref), (pout_ref, far_out, dout_ref))):
            k = 2 * (n - 1) + a
            near, diag, out = [b.at[k] for b in (near_m, diag_m, send_m)]
            own, got = (None, half_ref.at[a]) if n == 1 else (own_m.at[k - 2], got_m.at[k - 2])
            made.append(add(lambda c, ref=ref: ref.at[n - 2, pl.ds(c * G, G)], (own, got, near, diag, out), far, total, n, a, far_recvs.at[a]))
        return made

    main = {n: block(n) for n in range(1, M)}
    for a in range(2):
        link([main[n][a] for n in main])
    proj = {}
    for n in reversed(range(M)):
        proj[n] = add(lambda c, n=n: pproj_ref.at[at.near[n], c], [b.at[n] for b in (own_p, got_p, near_p, diag_p, send_p)],
                      far_p, dproj_ref, n, n % 2, far_recvs.at[2])
    heads = []
    for t in range(steps // 2 - 1):
        heads.append({})
        for n in reversed(range(M)):
            heads[t][n] = add(lambda c, t=t, n=n: parts_s.at[t, at.near[n], c], [None] + [b.at[t * M + n] for b in (got_q, near_q, diag_q, send_q)],
                              far_q.at[pl.ds(t * M, M)], sum_ref.at[t], n, (n + t) % 2, far_recvs_q.at[t], False)
    for group in [proj] + heads:
        link(list(group.values()))
    every = lambda group: list(group.values())
    early = lambda group: [group[n] for n in group if n != 2]
    late = lambda group: [group[n] for n in group if n == 2]
    plan = {}

    def put(slot, name, group):
        slot = slot + 1 if slot % parts == 0 else slot
        plan.setdefault(min(slot, steps * parts - 1), []).extend(getattr(u, name) for u in group)

    def begin():
        din_ref[...], dout_ref[...] = hin_ref[...], hout_ref[...]

    plan[0] = [at.greet, begin]
    plan[1] = [at.meet]
    put(1, "launch", main[1])
    others = [main[n] for n in reversed(range(2, M))]
    for group in others + [every(proj)]:
        put(1, "start", group)
    for n, group in enumerate(others):
        put(5 + n, "pair", group)
        put(13 + 4 * n, "join", group)
    put(7, "pair", every(proj))
    put(7, "join", main[1])
    for group in others[1:]:
        put(9, "cross", group)
    put(10, "pair", every(heads[0]))
    put(11, "cross", every(proj))
    put(17, "cross", every(heads[0]))
    put(18, "pair", every(heads[1]))
    put(19, "join", early(proj))
    put(21, "cross", every(heads[1]))
    put(21, "join", late(proj))
    put(21, "join", early(heads[0]))
    put(23, "join", late(heads[0]))
    grad_to = lambda t: dqkv_ref.at[0, :, pl.ds(pl.multiple_of(t * 256 + lax.rem(p, 2) * 128, 128), 128)]
    attend_back_step(p, len_ref, q_ref, k_ref, v_ref, do_ref, wide_ref, lse_ref, grad_to(0), grad_to(1), grad_to(2), tq, at_slots(p, parts, plan))

    @pl.when(p == 1)
    def _():
        for u in others[0]:
            u.cross()

    @pl.when(p == steps - 1)
    def _():
        for u in early(heads[1]):
            u.join()

    @pl.when(lax.rem(p, 2) == 1)
    def _():
        t = p // 2
        grad = dot(normed_ref[...], dqkv_ref[0], TN)
        for g in range(G):
            for c in range(2):
                for z in range(M):
                    k = ((g * 2 + c) * M + z) * R
                    parts_s[t, z, c, g] = grad[k : k + R, :].astype(BF)

    save = pltpu.make_async_copy(parts_s.at[steps // 2 - 1], rest_ref, save_sem.at[0])
    for t, group in enumerate(heads):

        @pl.when(p == 2 * t + 1)
        def _(group=group):
            for u in every(group):
                u.start()

    @pl.when(p == steps - 1)
    def _():
        save.start()
        for u in late(heads[1]):
            u.join()
        for u in units:
            u.close()
        for u in units:
            u.finish(u not in main[1], True)
        save.wait()


def attend_back(lengths, packed, do, wide, lse, normed, p_in, p_out, p_proj, h_in, h_out, halfway, tq):
    G, M = lax.axis_size("dp") // 2, lax.axis_size("mp")
    L, D = do.shape
    pairs = D // 128
    column = lambda off: pl.BlockSpec((L, 128), lambda p, off=off: (0, off + p))
    whole = lambda shape: pl.BlockSpec(shape, lambda p: (0,) * len(shape), pipeline_mode=pl.Buffered(1))
    out = lambda shape: pl.BlockSpec(shape, lambda p: (0,) * len(shape))
    mshape, pshape = h_in.shape, p_proj.shape[3:]
    groups = pairs // 2
    rest = 2 * (M - 1)
    sems = (rest + groups * M, SumUnit.count(G))
    return pl.pallas_call(
        functools.partial(attend_back_kernel, tq=tq),
        grid=(pairs,),
        in_specs=[SMEM, column(0), column(pairs), column(2 * pairs), column(0), column(0), whole((L, 128)), whole((L, D)), ANY, ANY, ANY,
                  whole(mshape), whole(mshape), whole(halfway.shape)],
        out_specs=[pl.BlockSpec((1, L, 768), lambda p: (p // 2, 0, 0)), out(mshape), out(mshape), out(pshape), out((groups - 1,) + pshape), ANY],
        out_shape=[jax.ShapeDtypeStruct((groups, L, 768), BF)]
        + [jax.ShapeDtypeStruct(mshape, F32)] * 2
        + [jax.ShapeDtypeStruct(pshape, F32), jax.ShapeDtypeStruct((groups - 1,) + pshape, F32), jax.ShapeDtypeStruct((M, 2, G) + pshape, BF)],
        scratch_shapes=sum_buffers(rest - 2, G, mshape)[:2] + sum_buffers(rest, G, mshape, far=M)[2:] + [pltpu.VMEM((M,) + mshape, BF)] + sum_buffers(M, G, pshape, far=M)
        + [pltpu.VMEM((groups, M, 2, G) + pshape, BF)] + sum_buffers((groups - 1) * M, G, pshape, own=False, far=(groups - 1) * M)
        + [DMA(sems), DMA(sems), DMA((3, M)), DMA((groups - 1, M)), DMA((1,))],
        compiler_params=params_of(2, grid=1),
    )(lengths, packed, packed, packed, do, wide, lse, normed, p_in, p_out, p_proj, h_in, h_out, halfway)


def exit_kernel(x_ref, dqkv_ref, w_ref, mid_ref, second_ref, params_ref, parts_ref, sums_ref, grad_ref, qkv_ref, norms_ref,
                got_s, near_s, diag_s, send_s, far_s, sum_s, norm_s, e_s, small_parts, small_got,
                sends, recvs, far_recvs, small_sends, small_recvs, *, rows):
    at = Place(everyone=True)
    M = at.M
    L, D = x_ref.shape
    R = qkv_ref.shape[0]
    groups = dqkv_ref.shape[0]
    small = SmallScatter(at, small_parts, small_got, small_sends, small_recvs)
    units = [
        SumUnit(at, lambda c, n=n: parts_ref.at[at.near[n], c], None, *[b.at[n] for b in (got_s, near_s, diag_s, send_s)], far_s, sum_s, n, n % 2,
                sends.at[n], recvs.at[n], far_recvs)
        for n in reversed(range(M))
    ]
    link(units)

    def run(name, ns=tuple(range(8))):
        for u in units:
            if u.n in ns or u.n > 7:
                getattr(u, name)()

    gain = params_ref[0:1, :]
    plan = {0: "start", 1: "pair", 2: "cross"}

    def matmul(g, carry):
        lane = pl.multiple_of(g * 256, 256)

        def piece(i, carry):
            sl = pl.ds(pl.multiple_of(i * (L // 2), L // 2), L // 2)
            e = sum(dot(dqkv_ref[g, sl, t * 256 : t * 256 + 256], w_ref[t, :, pl.ds(lane, 256)], NT) for t in range(3))
            e_s[sl, :] = e_s[sl, :] + e
            return carry

        lax.fori_loop(0, 2, piece, 0)
        for j, name in plan.items():

            @pl.when(g == j)
            def _(j=j, name=name):
                if j == 0:
                    at.meet()
                run(name)

        return carry

    def norm(i, carry):
        sl = pl.ds(pl.multiple_of(i * rows, rows), rows)
        e = e_s[sl, :]
        xhat, r = norm_stats(x_ref[sl, :].astype(F32))
        grad_ref[sl, :] = mid_ref[sl, :] + norm_pull(e, xhat, r, gain)
        norm_s[0:1, :] += jnp.sum(e * xhat, axis=0, keepdims=True)
        norm_s[2:3, :] += jnp.sum(e, axis=0, keepdims=True)
        return carry

    at.greet()
    norm_s[...] = second_ref[...]
    e_s[...] = jnp.zeros_like(e_s)
    lax.fori_loop(0, groups, matmul, 0)
    lax.fori_loop(0, L // rows, norm, 0)
    small.start(norm_s[...], R)
    run("join", (0, 1, 3, 4, 5, 6, 7))
    for g in range(groups - 1):
        for t in range(3):
            qkv_ref[:, pl.ds(t * D + g * 256, 256)] = sums_ref[g, :, pl.ds(t * 256, 256)]
    run("join", (2,))
    norms_ref[...] = small.collect()
    run("close")
    for t in range(3):
        qkv_ref[:, pl.ds(t * D + (groups - 1) * 256, 256)] = sum_s[:, pl.ds(t * 256, 256)]
    run("finish")
    small.finish()


def leave(x, dqkv, w, middle_grad, second_sums, params, parts, sums):
    G, M = lax.axis_size("dp") // 2, lax.axis_size("mp")
    L, D = x.shape
    R = parts.shape[3]
    n = 2 * G * M
    sems = (M, SumUnit.count(G))
    return pl.pallas_call(
        functools.partial(exit_kernel, rows=min(256, L)),
        in_specs=[VMEM] * 8,
        out_specs=[VMEM] * 3,
        out_shape=[
            jax.ShapeDtypeStruct((L, D), F32),
            jax.ShapeDtypeStruct((R, 3 * D), F32),
            jax.ShapeDtypeStruct((8, 128), F32),
        ],
        scratch_shapes=sum_buffers(M, G, (R, D), own=False, far=M)
        + [pltpu.VMEM((R, D), F32), pltpu.VMEM((8, D), F32), pltpu.VMEM((L, D), F32), pltpu.VMEM((n, 8, 128), F32), pltpu.VMEM((n, 8, 128), F32),
           DMA(sems), DMA(sems), DMA((M,)), DMA((n,)), DMA((n,))],
        compiler_params=params_of(3),
    )(x, dqkv, w, middle_grad, second_sums, params, parts, sums)


def per_device(inputs, lengths, attn_qkv, attn_proj, mlp_in, mlp_out, norm_gain, norm_bias, cotangent):
    n_dp, n_mp = lax.axis_size("dp"), lax.axis_size("mp")
    G = n_dp // 2
    L, D = inputs.shape
    R = attn_qkv.shape[1]
    small = jnp.concatenate([norm_gain[0], norm_bias[0]], axis=0).astype(F32)
    shard = attn_qkv[0].reshape(R, 3, D).transpose(1, 0, 2)
    wqkv, normed, params = entry(inputs, shard, jnp.pad(small, ((0, 4), (0, 128 - R))))
    wqkv = wqkv.reshape(3, D, D)
    io = jnp.stack([mlp_in[0], mlp_out[0].T])
    mixed, wide, lse, packed, wproj, land, win, wout = attend(lengths, normed, wqkv, attn_proj[0], io, min(512, L))
    pieces = lambda w: w.reshape((w.shape[0], n_dp) + w.shape[3:])
    outputs, middle_grad, mixed_grad, second_sums, p_proj, p_in, p_out, h_in, h_out, halfway = mlp(
        lengths, inputs, mixed, cotangent, params, wproj.reshape(D, D), pieces(win), pieces(wout), land, R, min(512, L))
    dqkv, d_in, d_out, d_proj, sums, parts = attend_back(
        lengths, packed, mixed_grad, wide, lse, normed, p_in, p_out, p_proj, h_in, h_out, halfway, min(256, L))
    input_grad, d_qkv, norms = leave(inputs, dqkv, wqkv, middle_grad, second_sums, params, parts, sums)
    return (
        outputs,
        input_grad,
        d_qkv[None],
        d_proj[None],
        d_in[None],
        d_out.T[None],
        norms[None, :2, :R],
        norms[None, 2:4, :R],
    )


def solution(mesh):
    everywhere = ("dp", "mp")
    wide, columns, vector = P(everywhere, None), P(None, everywhere, None), P(None, None, everywhere)
    return jax.shard_map(
        per_device,
        mesh=mesh,
        in_specs=(wide, P(everywhere), columns, columns, P(None, "dp", "mp"), P(None, "mp", "dp"), vector, vector, wide),
        out_specs=(wide, wide, columns, columns, P(None, "dp", "mp"), P(None, "mp", "dp"), vector, vector),
        check_vma=False,
    )
```

```python
import functools

import jax
import jax.numpy as jnp
from jax import lax
from jax.experimental import pallas as pl
from jax.experimental.pallas import tpu as pltpu
from jax.sharding import PartitionSpec as P

F32, BF = jnp.float32, jnp.bfloat16
MESH = pl.DeviceIdType.MESH
HEAD_DIM = 64
SCALE = 0.125
LOG2E = 1.4426950408889634
TO_LOG2 = SCALE * LOG2E
NEG = -1e30
EPS = 1e-06
NN = (((1,), (0,)), ((), ()))
NT = (((1,), (1,)), ((), ()))
TN = (((0,), (0,)), ((), ()))
VMEM_LIMIT = 60 * 2**20
ANY = pl.BlockSpec(memory_space=pl.ANY)
VMEM = pl.BlockSpec(memory_space=pltpu.VMEM)
SMEM = pl.BlockSpec(memory_space=pltpu.SMEM)
DMA = pltpu.SemaphoreType.DMA


def dot(a, b, dims):
    return lax.dot_general(a, b, dims, preferred_element_type=F32)


def params_of(collective_id=None, grid=0):
    extra = {} if collective_id is None else {"collective_id": collective_id, "has_side_effects": True}
    if grid:
        extra["dimension_semantics"] = ("arbitrary",) * grid
    return pltpu.CompilerParams(vmem_limit_bytes=VMEM_LIMIT, **extra)


class Place:
    def __init__(self, everyone=False):
        self.everyone = everyone
        n_dp, self.M = lax.axis_size("dp"), lax.axis_size("mp")
        self.G = n_dp // 2
        dp = lax.axis_index("dp")
        self.g, self.c, self.z = dp // 2, lax.rem(dp, 2), lax.axis_index("mp")
        self.square = self.G == 4
        self.near = [self.z ^ n if self.M & (self.M - 1) == 0 else lax.rem(self.z + n, self.M) for n in range(self.M)]
        if self.square:
            self.chips = [self.g ^ 1, self.g ^ 2]
            self.diag = self.g ^ 3
        else:
            self.chips = [lax.rem(self.g + d, self.G) for d in range(1, self.G)]

    def chip(self, h):
        return (h * 2 + self.c, self.z)

    def core(self):
        return (self.g * 2 + 1 - self.c, self.z)

    def along(self, z):
        return (self.g * 2 + self.c, z)

    def peers(self):
        if self.everyone:
            n = 2 * self.G * self.M
            return [self.device(lax.rem(self.index + d, n)) for d in range(1, n)]
        return [self.along(s) for s in self.near[1:]] + [self.chip(h) for h in self.chips] + [self.core()]

    @property
    def index(self):
        return (self.g * 2 + self.c) * self.M + self.z

    def device(self, i):
        return (i // self.M, lax.rem(i, self.M))

    def greet(self):
        for dev in self.peers():
            pl.semaphore_signal(pltpu.get_barrier_semaphore(), inc=1, device_id=dev, device_id_type=MESH)

    def meet(self):
        pl.semaphore_wait(pltpu.get_barrier_semaphore(), len(self.peers()))


def remote(src, dst, send, recv, dev):
    return pltpu.make_async_remote_copy(src_ref=src, dst_ref=dst, send_sem=send, recv_sem=recv, device_id=dev, device_id_type=MESH)


class Along:
    def __init__(self, at, own, land, sends, recvs):
        self.at, self.own, self.land, self.sends, self.recvs = at, own, land, sends, recvs

    def _copy(self, n, source):
        return remote(self.own, self.land(source), self.sends.at[n], self.recvs.at[source], self.at.along(self.at.near[n]))

    def start(self, *ns):
        for n in ns:
            self._copy(n, self.at.z).start()

    def arrive(self, n):
        self._copy(n, self.at.near[n]).wait_recv()

    def finish(self):
        for n in range(1, self.at.M):
            self._copy(n, self.at.z).wait_send()


class GatherUnit:
    def __init__(self, at, src, slot, way, sends, recvs, local=True):
        self.at, self.src, self.slot, self.way, self.local = at, src, slot, way, local
        self.sends, self.recvs = sends, recvs

    @staticmethod
    def count(G):
        return 1 + (3 if G == 4 else G - 1) + G

    def _local(self):
        return pltpu.make_async_copy(self.src, self.slot(self.at.g, self.at.c), self.sends.at[0])

    def _to_chip(self, i):
        at = self.at
        return remote(self.src, self.slot(at.g, at.c), self.sends.at[1 + i], self.recvs.at[1 + i], at.chip(at.chips[i]))

    def _relay(self):
        at = self.at
        block = self.slot(at.chips[self.way], at.c)
        return remote(block, block, self.sends.at[3], self.recvs.at[3], at.chip(at.chips[1 - self.way]))

    def _to_core(self, i):
        at = self.at
        h = ([at.g] + at.chips + ([at.diag] if at.square else []))[i]
        k = self.count(at.G) - at.G + i
        block = self.slot(h, at.c)
        return remote(block if i else self.src, block, self.sends.at[k], self.recvs.at[k], at.core())

    def spread(self):
        for i in range(len(self.at.chips)):
            self._to_chip(i).start()
        self._to_core(0).start()
        if self.local:
            self._local().start()

    def relay(self):
        n = len(self.at.chips)
        for i in range(n):
            self._to_chip(i).wait_recv()
        if self.at.square:
            self._relay().start()
        for i in range(n):
            self._to_core(1 + i).start()

    def last(self):
        if self.at.square:
            self._relay().wait_recv()
            self._to_core(3).start()

    def finish(self):
        if self.local:
            self._local().wait()
        for i in range(len(self.at.chips)):
            self._to_chip(i).wait_send()
        if self.at.square:
            self._relay().wait_send()
        for i in range(self.at.G):
            self._to_core(i).wait()


class SumUnit:
    def __init__(self, at, part, own, got, near, diag, out, far, total, n, way, sends, recvs, far_recvs, local=False):
        self.at, self.part, self.own, self.got, self.near, self.diagonal = at, part, own, got, near, diag
        self.out, self.far, self.total, self.n, self.way = out, far, total, n, way
        self.sends, self.recvs, self.far_recvs, self.local = sends, recvs, far_recvs, local
        self.place = at.near[n]
        self.passed = at.M == 4 and n == 3
        self.opposite = None

    @staticmethod
    def count(G):
        return 3 + (3 if G == 4 else G)

    def _core(self):
        at = self.at
        return remote(self.part(1 - at.c), self.got, self.sends.at[0], self.recvs.at[0], at.core())

    def _local(self):
        return pltpu.make_async_copy(self.part(self.at.c), self.own, self.sends.at[2])

    def _diag(self):
        at = self.at
        return remote(self.got.at[at.diag], self.diagonal, self.sends.at[5], self.recvs.at[5], at.chip(at.chips[1 - self.way]))

    def _chip(self, i):
        at = self.at
        k = 3 + i
        return remote(self.got.at[at.chips[i]], self.near.at[i], self.sends.at[k], self.recvs.at[k], at.chip(at.chips[i]))

    def _z(self, slot):
        dev = self.at.along(self.at.near[1] if self.passed else self.place)
        return remote(self.out, self.far.at[slot], self.sends.at[1], self.far_recvs.at[slot], dev)

    def send_z(self):
        self._z(self.at.near[2] if self.passed else self.at.z).start()

    def start(self):
        self._core().start()
        if self.local:
            self._local().start()

    def launch(self):
        for i in range(len(self.at.chips)):
            self._chip(i).start()

    def pair(self, hold=False):
        at = self.at
        self._core().wait_recv()
        if self.local:
            self._local().wait()
            own = self.own
        else:
            own = self.part(at.c)

        def add(h, carry):
            self.got[h] = (self.got[h].astype(F32) + own[h].astype(F32)).astype(BF)
            return carry

        lax.fori_loop(0, at.G, add, 0)
        if at.square:
            self._diag().start()
        elif not hold:
            self.launch()

    def cross(self, hold=False):
        at = self.at
        if at.square:
            self._diag().wait_recv()
            h = at.chips[self.way]
            self.got[h] = (self.got[h].astype(F32) + self.diagonal[...].astype(F32)).astype(BF)
            if not hold:
                self.launch()

    def join(self):
        at = self.at
        value = self.got[at.g].astype(F32)
        for i in range(len(at.chips)):
            self._chip(i).wait_recv()
            value = value + self.near[i].astype(F32)
        if self.opposite is not None:
            self._z(at.near[3]).wait_recv()
            value = value + self.far[at.near[3]].astype(F32)
        if self.n:
            self.out[...] = value.astype(BF)
            self.send_z()
        else:
            self.total[...] = value

    def close(self):
        if self.n and not self.passed:
            self._z(self.place).wait_recv()
            self.total[...] += self.far[self.place].astype(F32)

    def finish(self, core=True, rest=True):
        at = self.at
        if core:
            self._core().wait_send()
            if at.square:
                self._diag().wait_send()
        if rest:
            if self.n:
                self._z(at.near[2] if self.passed else at.z).wait_send()
            for i in range(len(at.chips)):
                self._chip(i).wait_send()


def link(units):
    by_n = {u.n: u for u in units}
    if units[0].at.M == 4 and 3 in by_n:
        by_n[2].opposite = by_n[3]
    return units


def sum_buffers(n, G, shape, own=True, far=0):
    chips = 2 if G == 4 else G - 1
    block = lambda *lead: pltpu.VMEM(lead + shape, BF)
    return ([block(n, G)] if own else []) + [block(n, G), block(n, chips), block(n), block(n), block(max(far, 1))]


class SmallGather:
    def __init__(self, at, got, sends, recvs):
        self.at, self.got, self.sends, self.recvs = at, got, sends, recvs
        self.count = 2 * at.G * at.M

    def _copy(self, own, d, back):
        at = self.at
        to, other = lax.rem(at.index + d, self.count), lax.rem(at.index + self.count - d, self.count)
        return remote(own, self.got.at[other if back else at.index], self.sends.at[d], self.recvs.at[d], at.device(to))

    def start(self, own):
        def send(d, carry):
            self._copy(own, d, False).start()
            return carry

        lax.fori_loop(1, self.count, send, 0)

    def collect(self, own, R, width):
        def wait(d, carry):
            self._copy(own, d, True).wait_recv()
            return carry

        lax.fori_loop(1, self.count, wait, 0)
        self.got[self.at.index] = own[...]
        lane = lanes((own.shape[0], width))
        total = jnp.zeros((own.shape[0], width), F32)
        for i in range(self.count):
            wide = jnp.concatenate([self.got[i]] * (width // 128), axis=1)
            total = jnp.where(lane // R == i, pltpu.roll(wide, i * R % width, 1) if i else wide, total)
        return total

    def finish(self, own):
        def wait(d, carry):
            self._copy(own, d, False).wait_send()
            return carry

        lax.fori_loop(1, self.count, wait, 0)


class SmallScatter:
    def __init__(self, at, parts, got, sends, recvs):
        self.at, self.parts, self.got, self.sends, self.recvs = at, parts, got, sends, recvs
        self.count = 2 * at.G * at.M

    def _copy(self, d, back):
        at = self.at
        to, other = lax.rem(at.index + d, self.count), lax.rem(at.index + self.count - d, self.count)
        return remote(self.parts.at[to], self.got.at[other if back else at.index], self.sends.at[d], self.recvs.at[d], at.device(to))

    def start(self, value, R):
        for i in range(self.count):
            self.parts[i] = (pltpu.roll(value, value.shape[1] - i * R, 1) if i else value)[:, :128]

        def send(d, carry):
            self._copy(d, False).start()
            return carry

        lax.fori_loop(1, self.count, send, 0)

    def collect(self):
        def add(d, value):
            self._copy(d, True).wait_recv()
            return value + self.got[lax.rem(self.at.index + self.count - d, self.count)]

        return lax.fori_loop(1, self.count, add, self.parts[self.at.index])

    def finish(self):
        def wait(d, carry):
            self._copy(d, False).wait_send()
            return carry

        lax.fori_loop(1, self.count, wait, 0)


def norm_stats(v):
    centre = v - jnp.mean(v, axis=-1, keepdims=True)
    r = lax.rsqrt(jnp.mean(centre * centre, axis=-1, keepdims=True) + EPS)
    return centre * r, r


def norm_pull(e, xhat, r, g):
    y = e * g
    return r * (y - jnp.mean(y, axis=-1, keepdims=True) - xhat * jnp.mean(y * xhat, axis=-1, keepdims=True))


def entry_kernel(x_ref, block_ref, gain_ref, bias_ref, w_ref, normed_ref, params_ref, shard_ref, own_ref, got, chain_sends, chain_recvs, sends, recvs,
                 small_sends, small_recvs, *, rows):
    at = Place(everyone=True)
    at.greet()
    land = lambda s: w_ref.at[:, at.g, at.c, s]
    chain = Along(at, shard_ref, land, chain_sends, chain_recvs)
    units = [
        GatherUnit(at, land(at.near[n]) if n else shard_ref, lambda g, c, n=n: w_ref.at[:, g, c, at.near[n]], n % 2, sends.at[n], recvs.at[n], n == 0)
        for n in range(at.M)
    ]
    small = SmallGather(at, got, small_sends, small_recvs)
    L, D = x_ref.shape
    R = block_ref.shape[0]
    for t in range(3):
        shard_ref[t] = block_ref[:, pl.ds(t * D, D)]
    own_ref[...] = jnp.zeros_like(own_ref)
    own_ref[0:2, 0:R] = gain_ref[...].astype(F32)
    own_ref[2:4, 0:R] = bias_ref[...].astype(F32)
    at.meet()
    chain.start(1)
    units[0].spread()
    chain.start(*range(2, at.M))
    small.start(own_ref)

    def norm(i, carry):
        sl = pl.ds(pl.multiple_of(i * rows, rows), rows)
        xhat, _ = norm_stats(x_ref[sl, :].astype(F32))
        normed_ref[sl, :] = (xhat * params_ref[0:1, :] + params_ref[2:3, :]).astype(BF)
        return carry

    steps = L // rows
    for n in range(1, at.M):
        chain.arrive(n)
        units[n].spread()
        units[n - 1].relay()
        if n > 1:
            units[n - 2].last()
    params_ref[...] = small.collect(own_ref, R, D)
    lax.fori_loop(0, steps // 2, norm, 0)
    units[-1].relay()
    if at.M > 1:
        units[-2].last()
    lax.fori_loop(steps // 2, steps, norm, 0)
    units[-1].last()
    for u in units:
        u.finish()
    chain.finish()
    small.finish(own_ref)


def entry(x, block, gain, bias):
    G, M = lax.axis_size("dp") // 2, lax.axis_size("mp")
    L, D = x.shape
    R = block.shape[0]
    n = 2 * G * M
    sems = (M, GatherUnit.count(G))
    return pl.pallas_call(
        functools.partial(entry_kernel, rows=min(256, L)),
        in_specs=[VMEM] * 4,
        out_specs=[ANY, VMEM, VMEM],
        out_shape=[
            jax.ShapeDtypeStruct((3, G, 2, M, R, D), BF),
            jax.ShapeDtypeStruct((L, D), BF),
            jax.ShapeDtypeStruct((8, D), F32),
        ],
        scratch_shapes=[pltpu.VMEM((3, R, D), BF), pltpu.VMEM((8, 128), F32), pltpu.VMEM((n, 8, 128), F32), DMA((M + 1,)), DMA((M,)), DMA(sems), DMA(sems), DMA((n,)), DMA((n,))],
        compiler_params=params_of(0),
    )(x, block, gain, bias)


def lanes(shape):
    return lax.broadcasted_iota(jnp.int32, shape, len(shape) - 1)


def three_parts(x):
    hi = x.astype(BF)
    rest = x - hi.astype(F32)
    mid = rest.astype(BF)
    return hi, mid, (rest - mid.astype(F32)).astype(BF)


def mask_bias(shape, length):
    return jnp.where(lax.broadcasted_iota(jnp.int32, shape, 0) < length, 0.0, NEG).astype(BF)


def attend_step(p, len_ref, q_ref, k_ref, v_ref, o_ref, wide_ref, lse_ref, tq, between):
    L = q_ref.shape[0]
    lane = lanes((L, 128))
    k, v = k_ref[...], v_ref[...]
    bias = mask_bias((L, 128), len_ref[0])
    zero, one = jnp.zeros((L, 128), BF), jnp.ones((L, 128), BF)

    @pl.when(p == 0)
    def _():
        lse_ref[...] = jnp.zeros_like(lse_ref)

    keys, values = [], []
    for h in range(2):
        mine = (lane < 64) if h == 0 else (lane >= 64)
        spare = 64 * (1 - h)
        keys.append(jnp.where(mine, k, jnp.where(lane == spare, bias, zero)))
        values.append(jnp.where(mine, v, jnp.where(lane == spare, one, zero)))
    lq = lanes((tq, 128))
    for i in range(L // tq):
        between(i)
        sl = pl.ds(i * tq, tq)
        q = q_ref[sl, :]
        outs, sums = [], []
        for h in range(2):
            mine = (lq < 64) if h == 0 else (lq >= 64)
            spare = 64 * (1 - h)
            q_h = jnp.where(mine, q, jnp.where(lq == spare, jnp.ones((tq, 128), BF), jnp.zeros((tq, 128), BF)))
            s = dot(q_h, keys[h], NT)
            top = jnp.max(s, axis=1, keepdims=True) * TO_LOG2
            e = jnp.exp2(s * TO_LOG2 - top)
            o = dot(e.astype(BF), values[h], NN)
            total = o[:, spare : spare + 1]
            outs.append(o / total)
            sums.append(top + jnp.log2(total))
        out = jnp.where(lq < 64, outs[0], outs[1])
        wide_ref[sl, :] = out
        o_ref[sl, :] = out.astype(BF)
        lse = lse_ref[sl, :]
        lse = jnp.where(lq == 2 * p, sums[0], lse)
        lse_ref[sl, :] = jnp.where(lq == 2 * p + 1, sums[1], lse)


def attend_back_step(p, len_ref, q_ref, k_ref, v_ref, do_ref, wide_ref, lse_ref, dq_ref, dk_ref, dv_ref, tq, between):
    L = q_ref.shape[0]
    lane = lanes((L, 128))
    k, v = k_ref[...], v_ref[...]
    bias = mask_bias((L, 128), len_ref[0])
    zero, one = jnp.zeros((L, 128), BF), jnp.ones((L, 128), BF)
    keys, values = [], []
    for h in range(2):
        mine = (lane < 64) if h == 0 else (lane >= 64)
        b = 64 * (1 - h)
        ones = jnp.where((lane > b) & (lane < b + 4), one, zero)
        keys.append(jnp.where(mine, k, jnp.where(lane == b, bias, ones)))
        values.append(jnp.where(mine, v, ones))
    lq = lanes((tq, 128))
    dk, dv = [jnp.zeros((L, 128), F32)] * 2, [jnp.zeros((L, 128), F32)] * 2
    for i in range(L // tq):
        between(i)
        sl = pl.ds(i * tq, tq)
        q, do, lse = q_ref[sl, :], do_ref[sl, :], lse_ref[sl, :]
        product = wide_ref[sl, :] * do.astype(F32)
        dq = []
        for h in range(2):
            mine = (lq < 64) if h == 0 else (lq >= 64)
            b = 64 * (1 - h)
            minus_delta = -jnp.sum(jnp.where(mine, product, 0.0), axis=1, keepdims=True)
            minus_lse = -jnp.sum(jnp.where(lq == 2 * p + h, lse, 0.0), axis=1, keepdims=True) * (1.0 / TO_LOG2)

            def with_spare(x, term, first):
                hi, mid, lo = three_parts(jnp.broadcast_to(term, (tq, 128)))
                low = jnp.where(lq == b + 2, mid, jnp.where(lq == b + 3, lo, jnp.zeros((tq, 128), BF)))
                low = jnp.where(lq == b, jnp.full((tq, 128), first, BF), jnp.where(lq == b + 1, hi, low))
                return jnp.where(mine, x, low)

            st = dot(keys[h], with_spare(q, minus_lse, 1.0), NT)
            pt = jnp.exp2(st * TO_LOG2)
            dpt = dot(values[h], with_spare(do, minus_delta, 0.0), NT)
            ds = (pt * dpt).astype(BF)
            dv[h] = dv[h] + dot(pt.astype(BF), do, NN)
            dk[h] = dk[h] + dot(ds, q, NN)
            dq.append(dot(ds, k, TN))
        dq_ref[sl, :] = (jnp.where(lq < 64, dq[0], dq[1]) * SCALE).astype(BF)
    dk_ref[...] = (jnp.where(lane < 64, dk[0], dk[1]) * SCALE).astype(BF)
    dv_ref[...] = jnp.where(lane < 64, dv[0], dv[1]).astype(BF)


def at_slots(p, per_step, plan):
    def between(i):
        for slot, actions in sorted(plan.items()):
            if slot % per_step == i:

                @pl.when(p == slot // per_step)
                def _(actions=actions):
                    for action in actions:
                        action()

    return between


def attend_kernel(len_ref, x_ref, w_ref, proj_ref, in_ref, out_ref, o_ref, wide_ref, lse_ref, packed_ref, wproj_ref, land_ref, win_ref, wout_ref,
                  packed_s, save_sem, pchain_sends, pchain_recvs, chain_sends, chain_recvs, sends, recvs, *, tq):
    p, steps = pl.program_id(0), pl.num_programs(0)
    at = Place()
    M = at.M
    half = M // 2
    D = x_ref.shape[1]
    parts = x_ref.shape[0] // tq
    land = [lambda s, a=a: land_ref.at[s, a] for a in range(2)]
    own = (in_ref, out_ref)
    pland = lambda s: wproj_ref.at[at.g, at.c, s]
    pchain = Along(at, proj_ref, pland, pchain_sends, pchain_recvs)
    chains = [Along(at, own[a], land[a], chain_sends.at[a], chain_recvs.at[a]) for a in range(2)]
    main = [
        [GatherUnit(at, land[a](at.near[n]) if n else own[a], lambda g, c, n=n, ref=ref: ref.at[n, g, c], a, sends.at[2 * n + a], recvs.at[2 * n + a])
         for a, ref in enumerate((win_ref, wout_ref))]
        for n in range(half)
    ]
    proj = [
        GatherUnit(at, pland(at.near[n]) if n else proj_ref, lambda g, c, n=n: wproj_ref.at[g, c, at.near[n]], n % 2,
                   sends.at[2 * half + n], recvs.at[2 * half + n], n == 0)
        for n in range(M)
    ]
    own_land = [pltpu.make_async_copy(own[a], land_ref.at[at.z, a], save_sem.at[1 + a]) for a in range(2)]
    save = pltpu.make_async_copy(packed_s, packed_ref, save_sem.at[0])

    def third(t):
        packed_s[:, pl.ds(t * D, D)] = dot(x_ref[...], w_ref[t], NN).astype(BF)

    @pl.when(p == 0)
    def _():
        at.greet()
        third(0)
        at.meet()
        pchain.start(*range(1, M))
        for n in range(1, M):
            for chain in chains:
                chain.start(n)
        proj[0].spread()
        for u in main[0]:
            u.spread()
        for cp in own_land:
            cp.start()
        third(1)
        third(2)
        save.start()

    plan = {}

    def put(slot, *actions):
        plan.setdefault(min(slot, ATTEND_STEPS * parts - 1), []).extend(actions)

    def arrive(chain, n, unit=None):
        def act():
            chain.arrive(n)
            if unit is not None:
                unit.spread()

        return act

    for n in range(M):
        arrives, relays, lasts = ATTEND_PROJ[min(n, 3)]
        put(relays, proj[n].relay)
        put(lasts, proj[n].last)
        if n:
            put(arrives, arrive(pchain, n, proj[n]))
    for n in range(half):
        for a in range(2):
            arrives, relays, lasts = ATTEND_MAIN[min(n, 1)][a]
            if n:
                put(arrives, arrive(chains[a], n, main[n][a]))
            put(relays, main[n][a].relay)
            put(lasts, main[n][a].last)
    lane = pl.multiple_of(p * 128, 128)
    column = lambda t: packed_s.at[:, pl.ds(t * D + lane, 128)]
    attend_step(p, len_ref, column(0), column(1), column(2), o_ref, wide_ref, lse_ref, tq, at_slots(p, parts, plan))

    @pl.when(p == steps - 1)
    def _():
        for n in range(half, M):
            for chain in chains:
                chain.arrive(n)
        for group in main + [proj, chains, [pchain]]:
            for u in group:
                u.finish()
        save.wait()
        for cp in own_land:
            cp.wait()


ATTEND_STEPS = 6
ATTEND_PROJ = [[0, 2, 5], [1, 5, 8], [4, 7, 10], [6, 9, 11]]
ATTEND_MAIN = [[[0, 4, 8], [0, 4, 8]], [[3, 7, 11], [4, 8, 11]]]
BACK = {"pair0": 5, "pair1": 6, "pair_p": 7, "join_1": 7, "cross1": 9, "pair_h0": 10, "cross_p": 11, "join0": 13, "join1": 17, "cross_h0": 17,
        "pair_h1": 18, "join_p": 19, "cross_h1": 21, "late_p": 21, "join_h0": 21, "late_h0": 23}
MLP = {"relay0": (0, 3), "spread1": (0, 3), "relay1": (1, 3), "last0": (1, 2), "last1": (2, 2), "pair0": (1, 2), "cross0": (2, 1), "pair1": (2, 3), "join0": (3, 1)}


def attend(lengths, x, w, proj, w_in, w_out, tq):
    G, M = lax.axis_size("dp") // 2, lax.axis_size("mp")
    L, D = x.shape
    half = M // 2
    column = pl.BlockSpec((L, 128), lambda p: (0, p))
    whole = lambda shape: pl.BlockSpec(shape, lambda p: (0,) * len(shape), pipeline_mode=pl.Buffered(1))
    sems = (2 * half + M, GatherUnit.count(G))
    weights = jax.ShapeDtypeStruct((half, G, 2) + w_in.shape, BF)
    return pl.pallas_call(
        functools.partial(attend_kernel, tq=tq),
        grid=(D // 128,),
        in_specs=[SMEM, whole(x.shape), whole(w.shape), ANY, ANY, ANY],
        out_specs=[column, column, pl.BlockSpec((L, 128), lambda p: (0, 0)), ANY, ANY, ANY, ANY, ANY],
        out_shape=[
            jax.ShapeDtypeStruct((L, D), BF),
            jax.ShapeDtypeStruct((L, D), F32),
            jax.ShapeDtypeStruct((L, 128), F32),
            jax.ShapeDtypeStruct((L, 3 * D), BF),
            jax.ShapeDtypeStruct((G, 2, M) + proj.shape, BF),
            jax.ShapeDtypeStruct((M, 2) + w_in.shape, BF),
            weights, weights,
        ],
        scratch_shapes=[pltpu.VMEM((L, 3 * D), BF), DMA((3,)), DMA((M + 1,)), DMA((M,)), DMA((2, M + 1)), DMA((2, M)), DMA(sems), DMA(sems)],
        compiler_params=params_of(1, grid=1),
    )(lengths, x, w, proj, w_in, w_out)


def gelu_and_slope(x):
    phi = 0.5 + 0.5 * lax.erf(x * 0.7071067811865476)
    return x * phi, phi + x * (jnp.exp2((x * x) * (-0.5 * LOG2E)) * 0.3989422804014327)


def mlp_kernel(len_ref, x_ref, mixed_ref, cot_ref, params_ref, wproj_ref, win_ref, wout_ref, land_ref,
               y_ref, mgrad_ref, dmixed_ref, sums_ref, pproj_ref, pin_ref, pout_ref, din_ref, dout_ref, half_ref,
               w_s, mid_s, hid_s, sg_s, sec_s, br_s, act_s, eg_s, got_s, near_s, diag_s,
               load_sems, save_sems, gsends, grecvs, ssends, srecvs, *, tr):
    at = Place()
    G, M = at.G, at.M
    L, D = x_ref.shape
    R, Fb = land_ref.shape[2:]
    half = M // 2
    gain, bias = params_ref[1:2, :], params_ref[3:4, :]
    loads = [pltpu.make_async_copy((win_ref, wout_ref)[a].at[k], w_s.at[k, a], load_sems.at[k, a]) for k in range(half) for a in range(2)]
    for cp in loads:
        cp.start()
    at.greet()
    gathers = [
        [GatherUnit(at, land_ref.at[at.near[k], a], lambda g, c, k=k, a=a: w_s.at[k, a, g * 2 + c], a, gsends.at[k - half, a], grecvs.at[k - half, a])
         for a in range(2)]
        for k in range(half, M)
    ]
    sums = [
        [SumUnit(at, lambda c, k=k, a=a: w_s.at[k, a, pl.ds(c * G, G)], None, *[b.at[2 * k + a] for b in (got_s, near_s, diag_s)], None,
                 None, total, k, a, ssends.at[2 * k + a], srecvs.at[2 * k + a], None)
         for a, total in enumerate((din_ref, dout_ref))]
        for k in range(2)
    ]

    def rows(i):
        return pl.ds(i * tr, tr)

    def enter(i):
        sl = rows(i)
        mid = x_ref[sl, :].astype(F32) + dot(mixed_ref[sl, :], wproj_ref[...], NN)
        mid_s[sl, :] = mid
        hid_s[sl, :] = mid
        sec_s[sl, :] = (norm_stats(mid)[0] * gain + bias).astype(BF)
        at_row = lax.broadcasted_iota(jnp.int32, (tr, D), 0) + i * tr
        br_s[sl, :] = jnp.where(at_row < len_ref[0], cot_ref[sl, :].astype(F32), 0.0).astype(BF)
        sg_s[sl, :] = jnp.zeros((tr, D), F32)

    n_rows = L // tr
    enter(0)
    at.meet()
    for group in gathers:
        group[0].spread()
        if group is gathers[0]:
            group[1].spread()
    for i in range(1, n_rows):
        enter(i)
    for cp in loads:
        cp.wait()
    per = n_rows + 2
    plan = {}

    def put(k, i, name, group):
        plan.setdefault((min(k, M - 1), min(i, per - 1)), []).extend(getattr(u, name) for u in group)

    for n, group in enumerate(gathers):
        after = lambda name: (MLP[name + "0"] if n == 0 else (MLP[name + "1"][0] + n - 1, MLP[name + "1"][1]))
        put(*after("relay"), "relay", group)
        if n:
            put(*MLP["spread1"], "spread", group[1:])
        put(*after("last"), "last", group)
        put(half + n, 0, "finish", group)
    put(1, 0, "start", sums[0])
    put(*MLP["pair0"], "pair", sums[0])
    put(2, 0, "start", sums[1])
    put(*MLP["cross0"], "cross", sums[0])
    plan.setdefault(MLP["pair1"], []).extend(functools.partial(u.pair, True) for u in sums[1])
    put(*MLP["join0"], "join", sums[0])

    def block(k, carry):
        def between(i):
            for (at_k, at_i), actions in sorted(plan.items(), key=lambda item: item[0]):
                if at_i == i:

                    @pl.when(k == at_k)
                    def _(actions=actions):
                        for action in actions:
                            action()

        between(0)
        win, wout = (w_s[k, a].reshape(D, Fb) for a in range(2))
        for i in range(n_rows):
            if i:
                between(i)
            sl = rows(i)
            value, slope = gelu_and_slope(dot(sec_s[sl, :], win, NN))
            act = value.astype(BF)
            eg = (dot(br_s[sl, :], wout, NN) * slope).astype(BF)
            act_s[sl, :], eg_s[sl, :] = act, eg
            hid_s[sl, :] += dot(act, wout, NT)
            sg_s[sl, :] += dot(eg, win, NT)
        for a, (left, right) in enumerate(((sec_s, eg_s), (br_s, act_s))):
            between(n_rows + a)
            grad = dot(left[...], right[...], TN)
            for g in range(G):
                for c in range(2):
                    row = (g * 2 + c) * R
                    w_s[k, a, c * G + g] = grad[row : row + R, :].astype(BF)

        @pl.when(k > 1)
        def _():
            for a, ref in enumerate((pin_ref, pout_ref)):
                pltpu.make_async_copy(w_s.at[k, a], ref.at[k - 2], save_sems.at[k - 2, a]).start()

        return carry

    lax.fori_loop(0, M, block, 0)
    sums_ref[...] = jnp.zeros_like(sums_ref)
    n_back = L // 256 if L % 256 == 0 else 1
    tb = L // n_back

    def back(i, carry):
        sl = pl.ds(pl.multiple_of(i * tb, tb), tb)
        y_ref[sl, :] = hid_s[sl, :].astype(BF)
        xhat, r = norm_stats(mid_s[sl, :])
        e = sg_s[sl, :]
        sums_ref[1:2, :] += jnp.sum(e * xhat, axis=0, keepdims=True)
        sums_ref[3:4, :] += jnp.sum(e, axis=0, keepdims=True)
        grad = br_s[sl, :].astype(F32) + norm_pull(e, xhat, r, gain)
        mgrad_ref[sl, :] = grad
        low = grad.astype(BF)
        sec_s[sl, :] = low
        dmixed_ref[sl, :] = dot(low, wproj_ref[...], NT).astype(BF)
        return carry

    lax.fori_loop(0, n_back, back, 0)
    for u in sums[1]:
        u.cross(True)
    save_half = pltpu.make_async_copy(got_s.at[pl.ds(2, 2)], half_ref, load_sems.at[0, 0])
    save_half.start()
    grad = dot(mixed_ref[...], sec_s[...], TN)
    R_p = pproj_ref.shape[3]
    for g in range(G):
        for c in range(2):
            for z in range(M):
                row = ((g * 2 + c) * M + z) * R_p
                pproj_ref[z, c, g] = grad[row : row + R_p, :].astype(BF)
    for k in range(2, M):
        for a, ref in enumerate((pin_ref, pout_ref)):
            pltpu.make_async_copy(w_s.at[k, a], ref.at[k - 2], save_sems.at[k - 2, a]).wait()
    save_half.wait()
    for k, group in enumerate(sums):
        for u in group:
            u.finish(True, k == 0)


def mlp(lengths, x, mixed, cot, params, wproj, win, wout, land, R_p, tr):
    G, M = lax.axis_size("dp") // 2, lax.axis_size("mp")
    half = M // 2
    L, D = x.shape
    R, Fb = block = land.shape[2:]
    gsems, ssems = (M - half, 2, GatherUnit.count(G)), (4, SumUnit.count(G))
    pieces = jax.ShapeDtypeStruct((M - 2, 2 * G) + block, BF)
    return pl.pallas_call(
        functools.partial(mlp_kernel, tr=tr),
        in_specs=[SMEM, VMEM, VMEM, VMEM, VMEM, VMEM, ANY, ANY, ANY],
        out_specs=[VMEM] * 5 + [ANY, ANY, VMEM, VMEM, ANY],
        out_shape=[
            jax.ShapeDtypeStruct((L, D), BF),
            jax.ShapeDtypeStruct((L, D), F32),
            jax.ShapeDtypeStruct((L, D), BF),
            jax.ShapeDtypeStruct(params.shape, F32),
            jax.ShapeDtypeStruct((M, 2, G, R_p, D), BF),
            pieces, pieces,
            jax.ShapeDtypeStruct(block, F32), jax.ShapeDtypeStruct(block, F32), jax.ShapeDtypeStruct((2, G) + block, BF),
        ],
        scratch_shapes=[
            pltpu.VMEM((M, 2, 2 * G) + block, BF),
            pltpu.VMEM((L, D), F32), pltpu.VMEM((L, D), F32), pltpu.VMEM((L, D), F32),
            pltpu.VMEM((L, D), BF), pltpu.VMEM((L, D), BF), pltpu.VMEM((L, Fb), BF), pltpu.VMEM((L, Fb), BF),
        ] + sum_buffers(4, G, block, own=False)[:3] + [DMA((half, 2)), DMA((M - 2, 2)), DMA(gsems), DMA(gsems), DMA(ssems), DMA(ssems)],
        compiler_params=params_of(4),
    )(lengths, x, mixed, cot, params, wproj, win, wout, land)


def attend_back_kernel(len_ref, q_ref, k_ref, v_ref, do_ref, wide_ref, lse_ref, normed_ref, pin_ref, pout_ref, pproj_ref, hin_ref, hout_ref, half_ref,
                       dqkv_ref, din_ref, dout_ref, dproj_ref, sum_ref, rest_ref,
                       own_m, got_m, near_m, diag_m, send_m, far_in, far_out, own_p, got_p, near_p, diag_p, send_p, far_p,
                       parts_s, got_q, near_q, diag_q, send_q, far_q, sends, recvs, far_recvs, far_recvs_q, save_sem, *, tq):
    p, steps = pl.program_id(0), ATTEND_STEPS
    at = Place()
    G, M = at.G, at.M
    parts = q_ref.shape[0] // tq
    R = sum_ref.shape[1]
    units = []

    def add(part, bufs, far, total, n, way, recv, local=True):
        k = len(units)
        units.append(SumUnit(at, part, *bufs, far, total, n, way, sends.at[k], recvs.at[k], recv, local=local))
        return units[-1]

    def block(n):
        made = []
        for a, (ref, far, total) in enumerate(((pin_ref, far_in, din_ref), (pout_ref, far_out, dout_ref))):
            k = 2 * (n - 1) + a
            near, diag, out = [b.at[k] for b in (near_m, diag_m, send_m)]
            own, got = (None, half_ref.at[a]) if n == 1 else (own_m.at[k - 2], got_m.at[k - 2])
            made.append(add(lambda c, ref=ref: ref.at[n - 2, pl.ds(c * G, G)], (own, got, near, diag, out), far, total, n, a, far_recvs.at[a]))
        return made

    main = {n: block(n) for n in range(1, M)}
    for a in range(2):
        link([main[n][a] for n in main])
    proj = {}
    for n in reversed(range(M)):
        proj[n] = add(lambda c, n=n: pproj_ref.at[at.near[n], c], [b.at[n] for b in (own_p, got_p, near_p, diag_p, send_p)],
                      far_p, dproj_ref, n, n % 2, far_recvs.at[2])
    heads = []
    for t in range(steps // 2 - 1):
        heads.append({})
        for n in reversed(range(M)):
            heads[t][n] = add(lambda c, t=t, n=n: parts_s.at[t, at.near[n], c], [None] + [b.at[t * M + n] for b in (got_q, near_q, diag_q, send_q)],
                              far_q.at[pl.ds(t * M, M)], sum_ref.at[t], n, (n + t) % 2, far_recvs_q.at[t], False)
    for group in [proj] + heads:
        link(list(group.values()))
    every = lambda group: list(group.values())
    early = lambda group: [group[n] for n in group if n != 2]
    late = lambda group: [group[n] for n in group if n == 2]
    plan = {}

    def put(slot, name, group):
        slot = slot + 1 if slot % parts == 0 else slot
        plan.setdefault(min(slot, steps * parts - 1), []).extend(getattr(u, name) for u in group)

    def begin():
        din_ref[...], dout_ref[...] = hin_ref[...], hout_ref[...]

    plan[0] = [at.greet, begin]
    plan[1] = [at.meet]
    put(1, "launch", main[1])
    others = [main[n] for n in reversed(range(2, M))]
    for group in others + [every(proj)]:
        put(1, "start", group)
    for n, group in enumerate(others):
        put(BACK["pair0"] if n == 0 else BACK["pair1"], "pair", group)
        put(BACK["join0"] if n == 0 else BACK["join1"], "join", group)
    put(BACK["pair_p"], "pair", every(proj))
    put(BACK["join_1"], "join", main[1])
    for group in others[1:]:
        put(BACK["cross1"], "cross", group)
    put(BACK["pair_h0"], "pair", every(heads[0]))
    put(BACK["cross_p"], "cross", every(proj))
    put(BACK["cross_h0"], "cross", every(heads[0]))
    put(BACK["pair_h1"], "pair", every(heads[1]))
    put(BACK["join_p"], "join", early(proj))
    put(BACK["cross_h1"], "cross", every(heads[1]))
    put(BACK["late_p"], "join", late(proj))
    put(BACK["join_h0"], "join", early(heads[0]))
    put(BACK["late_h0"], "join", late(heads[0]))
    grad_to = lambda t: dqkv_ref.at[0, :, pl.ds(pl.multiple_of(t * 256 + lax.rem(p, 2) * 128, 128), 128)]
    attend_back_step(p, len_ref, q_ref, k_ref, v_ref, do_ref, wide_ref, lse_ref, grad_to(0), grad_to(1), grad_to(2), tq, at_slots(p, parts, plan))

    @pl.when(p == 1)
    def _():
        for u in others[0]:
            u.cross()

    @pl.when(p == steps - 1)
    def _():
        for u in early(heads[1]):
            u.join()

    @pl.when(lax.rem(p, 2) == 1)
    def _():
        t = p // 2
        grad = dot(normed_ref[...], dqkv_ref[0], TN)
        for g in range(G):
            for c in range(2):
                for z in range(M):
                    k = ((g * 2 + c) * M + z) * R
                    parts_s[t, z, c, g] = grad[k : k + R, :].astype(BF)

    save = pltpu.make_async_copy(parts_s.at[steps // 2 - 1], rest_ref, save_sem.at[0])
    for t, group in enumerate(heads):

        @pl.when(p == 2 * t + 1)
        def _(group=group):
            for u in every(group):
                u.start()

    @pl.when(p == steps - 1)
    def _():
        save.start()
        for u in late(heads[1]):
            u.join()
        for u in units:
            u.close()
        for u in units:
            u.finish(u not in main[1], True)
        save.wait()


def attend_back(lengths, packed, do, wide, lse, normed, p_in, p_out, p_proj, h_in, h_out, halfway, tq):
    G, M = lax.axis_size("dp") // 2, lax.axis_size("mp")
    L, D = do.shape
    pairs = D // 128
    column = lambda off: pl.BlockSpec((L, 128), lambda p, off=off: (0, off + p))
    whole = lambda shape: pl.BlockSpec(shape, lambda p: (0,) * len(shape), pipeline_mode=pl.Buffered(1))
    out = lambda shape: pl.BlockSpec(shape, lambda p: (0,) * len(shape))
    mshape, pshape = h_in.shape, p_proj.shape[3:]
    groups = pairs // 2
    rest = 2 * (M - 1)
    sems = (rest + groups * M, SumUnit.count(G))
    return pl.pallas_call(
        functools.partial(attend_back_kernel, tq=tq),
        grid=(pairs,),
        in_specs=[SMEM, column(0), column(pairs), column(2 * pairs), column(0), column(0), whole((L, 128)), whole((L, D)), ANY, ANY, ANY,
                  whole(mshape), whole(mshape), whole(halfway.shape)],
        out_specs=[pl.BlockSpec((1, L, 768), lambda p: (p // 2, 0, 0)), out(mshape), out(mshape), out(pshape), out((groups - 1,) + pshape), ANY],
        out_shape=[jax.ShapeDtypeStruct((groups, L, 768), BF)]
        + [jax.ShapeDtypeStruct(mshape, F32)] * 2
        + [jax.ShapeDtypeStruct(pshape, F32), jax.ShapeDtypeStruct((groups - 1,) + pshape, F32), jax.ShapeDtypeStruct((M, 2, G) + pshape, BF)],
        scratch_shapes=sum_buffers(rest - 2, G, mshape)[:2] + sum_buffers(rest, G, mshape, far=M)[2:] + [pltpu.VMEM((M,) + mshape, BF)] + sum_buffers(M, G, pshape, far=M)
        + [pltpu.VMEM((groups, M, 2, G) + pshape, BF)] + sum_buffers((groups - 1) * M, G, pshape, own=False, far=(groups - 1) * M)
        + [DMA(sems), DMA(sems), DMA((3, M)), DMA((groups - 1, M)), DMA((1,))],
        compiler_params=params_of(2, grid=1),
    )(lengths, packed, packed, packed, do, wide, lse, normed, p_in, p_out, p_proj, h_in, h_out, halfway)


def exit_kernel(x_ref, dqkv_ref, w_ref, mid_ref, second_ref, params_ref, parts_ref, sums_ref, grad_ref, qkv_ref, norms_ref,
                got_s, near_s, diag_s, send_s, far_s, sum_s, norm_s, e_s, small_parts, small_got,
                sends, recvs, far_recvs, small_sends, small_recvs, *, rows):
    at = Place(everyone=True)
    M = at.M
    L, D = x_ref.shape
    R = qkv_ref.shape[0]
    groups = dqkv_ref.shape[0]
    small = SmallScatter(at, small_parts, small_got, small_sends, small_recvs)
    units = [
        SumUnit(at, lambda c, n=n: parts_ref.at[at.near[n], c], None, *[b.at[n] for b in (got_s, near_s, diag_s, send_s)], far_s, sum_s, n, n % 2,
                sends.at[n], recvs.at[n], far_recvs)
        for n in reversed(range(M))
    ]
    link(units)

    def run(name, ns=tuple(range(8))):
        for u in units:
            if u.n in ns or u.n > 7:
                getattr(u, name)()

    gain = params_ref[0:1, :]
    plan = {0: "start", 1: "pair", 2: "cross"}

    def matmul(g, carry):
        lane = pl.multiple_of(g * 256, 256)

        def piece(i, carry):
            sl = pl.ds(pl.multiple_of(i * (L // 2), L // 2), L // 2)
            e = sum(dot(dqkv_ref[g, sl, t * 256 : t * 256 + 256], w_ref[t, :, pl.ds(lane, 256)], NT) for t in range(3))
            e_s[sl, :] = e_s[sl, :] + e
            return carry

        lax.fori_loop(0, 2, piece, 0)
        for j, name in plan.items():

            @pl.when(g == j)
            def _(j=j, name=name):
                if j == 0:
                    at.meet()
                run(name)

        return carry

    def norm(i, carry):
        sl = pl.ds(pl.multiple_of(i * rows, rows), rows)
        e = e_s[sl, :]
        xhat, r = norm_stats(x_ref[sl, :].astype(F32))
        grad_ref[sl, :] = mid_ref[sl, :] + norm_pull(e, xhat, r, gain)
        norm_s[0:1, :] += jnp.sum(e * xhat, axis=0, keepdims=True)
        norm_s[2:3, :] += jnp.sum(e, axis=0, keepdims=True)
        return carry

    at.greet()
    norm_s[...] = second_ref[...]
    e_s[...] = jnp.zeros_like(e_s)
    lax.fori_loop(0, groups, matmul, 0)
    lax.fori_loop(0, L // rows, norm, 0)
    small.start(norm_s[...], R)
    run("join", (0, 1, 3, 4, 5, 6, 7))
    for g in range(groups - 1):
        for t in range(3):
            qkv_ref[:, pl.ds(t * D + g * 256, 256)] = sums_ref[g, :, pl.ds(t * 256, 256)]
    run("join", (2,))
    norms_ref[...] = small.collect()
    run("close")
    for t in range(3):
        qkv_ref[:, pl.ds(t * D + (groups - 1) * 256, 256)] = sum_s[:, pl.ds(t * 256, 256)]
    run("finish")
    small.finish()


def leave(x, dqkv, w, middle_grad, second_sums, params, parts, sums):
    G, M = lax.axis_size("dp") // 2, lax.axis_size("mp")
    L, D = x.shape
    R = parts.shape[3]
    n = 2 * G * M
    sems = (M, SumUnit.count(G))
    return pl.pallas_call(
        functools.partial(exit_kernel, rows=min(256, L)),
        in_specs=[VMEM] * 8,
        out_specs=[VMEM] * 3,
        out_shape=[
            jax.ShapeDtypeStruct((L, D), F32),
            jax.ShapeDtypeStruct((R, 3 * D), F32),
            jax.ShapeDtypeStruct((8, 128), F32),
        ],
        scratch_shapes=sum_buffers(M, G, (R, D), own=False, far=M)
        + [pltpu.VMEM((R, D), F32), pltpu.VMEM((8, D), F32), pltpu.VMEM((L, D), F32), pltpu.VMEM((n, 8, 128), F32), pltpu.VMEM((n, 8, 128), F32),
           DMA(sems), DMA(sems), DMA((M,)), DMA((n,)), DMA((n,))],
        compiler_params=params_of(3),
    )(x, dqkv, w, middle_grad, second_sums, params, parts, sums)


def per_device(inputs, lengths, attn_qkv, attn_proj, mlp_in, mlp_out, norm_gain, norm_bias, cotangent):
    n_dp, n_mp = lax.axis_size("dp"), lax.axis_size("mp")
    G = n_dp // 2
    L, D = inputs.shape
    R = attn_qkv.shape[1]
    wqkv, normed, params = entry(inputs, attn_qkv[0], norm_gain[0], norm_bias[0])
    wqkv = wqkv.reshape(3, D, D)
    mixed, wide, lse, packed, wproj, land, win, wout = attend(lengths, normed, wqkv, attn_proj[0], mlp_in[0], mlp_out[0].T, min(512, L))
    pieces = lambda w: w.reshape((w.shape[0], n_dp) + w.shape[3:])
    outputs, middle_grad, mixed_grad, second_sums, p_proj, p_in, p_out, h_in, h_out, halfway = mlp(
        lengths, inputs, mixed, cotangent, params, wproj.reshape(D, D), pieces(win), pieces(wout), land, R, min(512, L))
    dqkv, d_in, d_out, d_proj, sums, parts = attend_back(
        lengths, packed, mixed_grad, wide, lse, normed, p_in, p_out, p_proj, h_in, h_out, halfway, min(256, L))
    input_grad, d_qkv, norms = leave(inputs, dqkv, wqkv, middle_grad, second_sums, params, parts, sums)
    return (
        outputs,
        input_grad,
        d_qkv[None],
        d_proj[None],
        d_in[None],
        d_out.T[None],
        norms[None, :2, :R],
        norms[None, 2:4, :R],
    )


def solution(mesh):
    everywhere = ("dp", "mp")
    wide, columns, vector = P(everywhere, None), P(None, everywhere, None), P(None, None, everywhere)
    return jax.shard_map(
        per_device,
        mesh=mesh,
        in_specs=(wide, P(everywhere), columns, columns, P(None, "dp", "mp"), P(None, "mp", "dp"), vector, vector, wide),
        out_specs=(wide, wide, columns, columns, P(None, "dp", "mp"), P(None, "mp", "dp"), vector, vector),
        check_vma=False,
    )
```

```python
import functools

import jax
import jax.numpy as jnp
from jax import lax
from jax.experimental import pallas as pl
from jax.experimental.pallas import tpu as pltpu
from jax.sharding import PartitionSpec as P

F32, BF = jnp.float32, jnp.bfloat16
MESH = pl.DeviceIdType.MESH
HEAD_DIM = 64
SCALE = 0.125
LOG2E = 1.4426950408889634
TO_LOG2 = SCALE * LOG2E
NEG = -1e30
EPS = 1e-06
NN = (((1,), (0,)), ((), ()))
NT = (((1,), (1,)), ((), ()))
TN = (((0,), (0,)), ((), ()))
VMEM_LIMIT = 60 * 2**20
ANY = pl.BlockSpec(memory_space=pl.ANY)
VMEM = pl.BlockSpec(memory_space=pltpu.VMEM)
SMEM = pl.BlockSpec(memory_space=pltpu.SMEM)
DMA = pltpu.SemaphoreType.DMA


def dot(a, b, dims):
    return lax.dot_general(a, b, dims, preferred_element_type=F32)


def params_of(collective_id=None, grid=0):
    extra = {} if collective_id is None else {"collective_id": collective_id, "has_side_effects": True}
    if grid:
        extra["dimension_semantics"] = ("arbitrary",) * grid
    return pltpu.CompilerParams(vmem_limit_bytes=VMEM_LIMIT, **extra)


class Place:
    def __init__(self, everyone=False):
        self.everyone = everyone
        n_dp, self.M = lax.axis_size("dp"), lax.axis_size("mp")
        self.G = n_dp // 2
        dp = lax.axis_index("dp")
        self.g, self.c, self.z = dp // 2, lax.rem(dp, 2), lax.axis_index("mp")
        self.square = self.G == 4
        self.near = [self.z ^ n if self.M & (self.M - 1) == 0 else lax.rem(self.z + n, self.M) for n in range(self.M)]
        if self.square:
            self.chips = [self.g ^ 1, self.g ^ 2]
            self.diag = self.g ^ 3
        else:
            self.chips = [lax.rem(self.g + d, self.G) for d in range(1, self.G)]

    def chip(self, h):
        return (h * 2 + self.c, self.z)

    def core(self):
        return (self.g * 2 + 1 - self.c, self.z)

    def along(self, z):
        return (self.g * 2 + self.c, z)

    def peers(self):
        if self.everyone:
            n = 2 * self.G * self.M
            return [self.device(lax.rem(self.index + d, n)) for d in range(1, n)]
        return [self.along(s) for s in self.near[1:]] + [self.chip(h) for h in self.chips] + [self.core()]

    @property
    def index(self):
        return (self.g * 2 + self.c) * self.M + self.z

    def device(self, i):
        return (i // self.M, lax.rem(i, self.M))

    def greet(self):
        for dev in self.peers():
            pl.semaphore_signal(pltpu.get_barrier_semaphore(), inc=1, device_id=dev, device_id_type=MESH)

    def meet(self):
        pl.semaphore_wait(pltpu.get_barrier_semaphore(), len(self.peers()))


def remote(src, dst, send, recv, dev):
    return pltpu.make_async_remote_copy(src_ref=src, dst_ref=dst, send_sem=send, recv_sem=recv, device_id=dev, device_id_type=MESH)


class Along:
    def __init__(self, at, own, land, sends, recvs):
        self.at, self.own, self.land, self.sends, self.recvs = at, own, land, sends, recvs

    def _copy(self, n, source):
        return remote(self.own, self.land(source), self.sends.at[n], self.recvs.at[source], self.at.along(self.at.near[n]))

    def start(self, *ns):
        for n in ns:
            self._copy(n, self.at.z).start()

    def pass_on(self):
        block = self.land(self.at.near[2])
        remote(block, block, self.sends.at[3], self.recvs.at[self.at.near[2]], self.at.along(self.at.near[1])).start()

    def arrive(self, n):
        self._copy(n, self.at.near[n]).wait_recv()

    def finish(self):
        for n in range(1, self.at.M):
            self._copy(n, self.at.z).wait_send()


class GatherUnit:
    def __init__(self, at, src, slot, way, sends, recvs, local=True):
        self.at, self.src, self.slot, self.way, self.local = at, src, slot, way, local
        self.sends, self.recvs = sends, recvs

    @staticmethod
    def count(G):
        return 1 + (3 if G == 4 else G - 1) + G

    def _local(self):
        return pltpu.make_async_copy(self.src, self.slot(self.at.g, self.at.c), self.sends.at[0])

    def _to_chip(self, i):
        at = self.at
        return remote(self.src, self.slot(at.g, at.c), self.sends.at[1 + i], self.recvs.at[1 + i], at.chip(at.chips[i]))

    def _relay(self):
        at = self.at
        block = self.slot(at.chips[self.way], at.c)
        return remote(block, block, self.sends.at[3], self.recvs.at[3], at.chip(at.chips[1 - self.way]))

    def _to_core(self, i):
        at = self.at
        h = ([at.g] + at.chips + ([at.diag] if at.square else []))[i]
        k = self.count(at.G) - at.G + i
        block = self.slot(h, at.c)
        return remote(block if i else self.src, block, self.sends.at[k], self.recvs.at[k], at.core())

    def spread(self):
        for i in range(len(self.at.chips)):
            self._to_chip(i).start()
        self._to_core(0).start()
        if self.local:
            self._local().start()

    def relay(self):
        n = len(self.at.chips)
        for i in range(n):
            self._to_chip(i).wait_recv()
        if self.at.square:
            self._relay().start()
        for i in range(n):
            self._to_core(1 + i).start()

    def last(self):
        if self.at.square:
            self._relay().wait_recv()
            self._to_core(3).start()

    def finish(self):
        if self.local:
            self._local().wait()
        for i in range(len(self.at.chips)):
            self._to_chip(i).wait_send()
        if self.at.square:
            self._relay().wait_send()
        for i in range(self.at.G):
            self._to_core(i).wait()


class SumUnit:
    def __init__(self, at, part, own, got, near, diag, out, far, total, n, way, sends, recvs, far_recvs, local=False):
        self.at, self.part, self.own, self.got, self.near, self.diagonal = at, part, own, got, near, diag
        self.out, self.far, self.total, self.n, self.way = out, far, total, n, way
        self.sends, self.recvs, self.far_recvs, self.local = sends, recvs, far_recvs, local
        self.place = at.near[n]
        self.passed = False
        self.opposite = None

    @staticmethod
    def count(G):
        return 3 + (3 if G == 4 else G)

    def _core(self):
        at = self.at
        return remote(self.part(1 - at.c), self.got, self.sends.at[0], self.recvs.at[0], at.core())

    def _local(self):
        return pltpu.make_async_copy(self.part(self.at.c), self.own, self.sends.at[2])

    def _diag(self):
        at = self.at
        return remote(self.got.at[at.diag], self.diagonal, self.sends.at[5], self.recvs.at[5], at.chip(at.chips[1 - self.way]))

    def _chip(self, i):
        at = self.at
        k = 3 + i
        return remote(self.got.at[at.chips[i]], self.near.at[i], self.sends.at[k], self.recvs.at[k], at.chip(at.chips[i]))

    def _z(self, slot):
        dev = self.at.along(self.at.near[1] if self.passed else self.place)
        return remote(self.out, self.far.at[slot], self.sends.at[1], self.far_recvs.at[slot], dev)

    def send_z(self):
        self._z(self.at.near[2] if self.passed else self.at.z).start()

    def start(self):
        self._core().start()
        if self.local:
            self._local().start()

    def launch(self):
        for i in range(len(self.at.chips)):
            self._chip(i).start()

    def pair(self, hold=False):
        at = self.at
        self._core().wait_recv()
        if self.local:
            self._local().wait()
            own = self.own
        else:
            own = self.part(at.c)

        def add(h, carry):
            self.got[h] = (self.got[h].astype(F32) + own[h].astype(F32)).astype(BF)
            return carry

        lax.fori_loop(0, at.G, add, 0)
        if at.square:
            self._diag().start()
        elif not hold:
            self.launch()

    def cross(self, hold=False):
        at = self.at
        if at.square:
            self._diag().wait_recv()
            h = at.chips[self.way]
            self.got[h] = (self.got[h].astype(F32) + self.diagonal[...].astype(F32)).astype(BF)
            if not hold:
                self.launch()

    def join(self):
        at = self.at
        value = self.got[at.g].astype(F32)
        for i in range(len(at.chips)):
            self._chip(i).wait_recv()
            value = value + self.near[i].astype(F32)
        if self.opposite is not None:
            self._z(at.near[3]).wait_recv()
            value = value + self.far[at.near[3]].astype(F32)
        if self.n:
            self.out[...] = value.astype(BF)
            self.send_z()
        else:
            self.total[...] = value

    def close(self):
        if self.n and not self.passed:
            self._z(self.place).wait_recv()
            self.total[...] += self.far[self.place].astype(F32)

    def finish(self, core=True, rest=True):
        at = self.at
        if core:
            self._core().wait_send()
            if at.square:
                self._diag().wait_send()
        if rest:
            if self.n:
                self._z(at.near[2] if self.passed else at.z).wait_send()
            for i in range(len(at.chips)):
                self._chip(i).wait_send()


def link(units):
    by_n = {u.n: u for u in units}
    if units[0].at.M == 4 and 3 in by_n:
        by_n[2].opposite = by_n[3]
        by_n[3].passed = True
    return units


def sum_buffers(n, G, shape, own=True, far=0):
    chips = 2 if G == 4 else G - 1
    block = lambda *lead: pltpu.VMEM(lead + shape, BF)
    return ([block(n, G)] if own else []) + [block(n, G), block(n, chips), block(n), block(n), block(max(far, 1))]


class SmallGather:
    def __init__(self, at, got, sends, recvs):
        self.at, self.got, self.sends, self.recvs = at, got, sends, recvs
        self.count = 2 * at.G * at.M

    def _copy(self, own, d, back):
        at = self.at
        to, other = lax.rem(at.index + d, self.count), lax.rem(at.index + self.count - d, self.count)
        return remote(own, self.got.at[other if back else at.index], self.sends.at[d], self.recvs.at[d], at.device(to))

    def start(self, own):
        def send(d, carry):
            self._copy(own, d, False).start()
            return carry

        lax.fori_loop(1, self.count, send, 0)

    def collect(self, own, R, width):
        def wait(d, carry):
            self._copy(own, d, True).wait_recv()
            return carry

        lax.fori_loop(1, self.count, wait, 0)
        self.got[self.at.index] = own[...]
        lane = lanes((own.shape[0], width))
        total = jnp.zeros((own.shape[0], width), F32)
        for i in range(self.count):
            wide = jnp.concatenate([self.got[i]] * (width // 128), axis=1)
            total = jnp.where(lane // R == i, pltpu.roll(wide, i * R % width, 1) if i else wide, total)
        return total

    def finish(self, own):
        def wait(d, carry):
            self._copy(own, d, False).wait_send()
            return carry

        lax.fori_loop(1, self.count, wait, 0)


class SmallScatter:
    def __init__(self, at, parts, got, sends, recvs):
        self.at, self.parts, self.got, self.sends, self.recvs = at, parts, got, sends, recvs
        self.count = 2 * at.G * at.M

    def _copy(self, d, back):
        at = self.at
        to, other = lax.rem(at.index + d, self.count), lax.rem(at.index + self.count - d, self.count)
        return remote(self.parts.at[to], self.got.at[other if back else at.index], self.sends.at[d], self.recvs.at[d], at.device(to))

    def start(self, value, R):
        for i in range(self.count):
            self.parts[i] = (pltpu.roll(value, value.shape[1] - i * R, 1) if i else value)[:, :128]

        def send(d, carry):
            self._copy(d, False).start()
            return carry

        lax.fori_loop(1, self.count, send, 0)

    def collect(self):
        def add(d, value):
            self._copy(d, True).wait_recv()
            return value + self.got[lax.rem(self.at.index + self.count - d, self.count)]

        return lax.fori_loop(1, self.count, add, self.parts[self.at.index])

    def finish(self):
        def wait(d, carry):
            self._copy(d, False).wait_send()
            return carry

        lax.fori_loop(1, self.count, wait, 0)


def norm_stats(v):
    centre = v - jnp.mean(v, axis=-1, keepdims=True)
    r = lax.rsqrt(jnp.mean(centre * centre, axis=-1, keepdims=True) + EPS)
    return centre * r, r


def norm_pull(e, xhat, r, g):
    y = e * g
    return r * (y - jnp.mean(y, axis=-1, keepdims=True) - xhat * jnp.mean(y * xhat, axis=-1, keepdims=True))


def entry_kernel(x_ref, block_ref, gain_ref, bias_ref, w_ref, normed_ref, params_ref, shard_ref, own_ref, got, chain_sends, chain_recvs, sends, recvs,
                 small_sends, small_recvs, *, rows):
    at = Place(everyone=True)
    at.greet()
    land = lambda s: w_ref.at[:, at.g, at.c, s]
    chain = Along(at, shard_ref, land, chain_sends, chain_recvs)
    units = [
        GatherUnit(at, land(at.near[n]) if n else shard_ref, lambda g, c, n=n: w_ref.at[:, g, c, at.near[n]], n % 2, sends.at[n], recvs.at[n], n == 0)
        for n in range(at.M)
    ]
    small = SmallGather(at, got, small_sends, small_recvs)
    L, D = x_ref.shape
    R = block_ref.shape[0]
    for t in range(3):
        shard_ref[t] = block_ref[:, pl.ds(t * D, D)]
    own_ref[...] = jnp.zeros_like(own_ref)
    own_ref[0:2, 0:R] = gain_ref[...].astype(F32)
    own_ref[2:4, 0:R] = bias_ref[...].astype(F32)
    at.meet()
    chain.start(1)
    units[0].spread()
    chain.start(*range(2, 3 if at.M == 4 else at.M))
    small.start(own_ref)

    def norm(i, carry):
        sl = pl.ds(pl.multiple_of(i * rows, rows), rows)
        xhat, _ = norm_stats(x_ref[sl, :].astype(F32))
        normed_ref[sl, :] = (xhat * params_ref[0:1, :] + params_ref[2:3, :]).astype(BF)
        return carry

    steps = L // rows
    for n in range(1, at.M):
        chain.arrive(n)
        if at.M == 4 and n == 2:
            chain.pass_on()
        units[n].spread()
        units[n - 1].relay()
        if n > 1:
            units[n - 2].last()
    params_ref[...] = small.collect(own_ref, R, D)
    lax.fori_loop(0, steps // 2, norm, 0)
    units[-1].relay()
    if at.M > 1:
        units[-2].last()
    lax.fori_loop(steps // 2, steps, norm, 0)
    units[-1].last()
    for u in units:
        u.finish()
    chain.finish()
    small.finish(own_ref)


def entry(x, block, gain, bias):
    G, M = lax.axis_size("dp") // 2, lax.axis_size("mp")
    L, D = x.shape
    R = block.shape[0]
    n = 2 * G * M
    sems = (M, GatherUnit.count(G))
    return pl.pallas_call(
        functools.partial(entry_kernel, rows=min(256, L)),
        in_specs=[VMEM] * 4,
        out_specs=[ANY, VMEM, VMEM],
        out_shape=[
            jax.ShapeDtypeStruct((3, G, 2, M, R, D), BF),
            jax.ShapeDtypeStruct((L, D), BF),
            jax.ShapeDtypeStruct((8, D), F32),
        ],
        scratch_shapes=[pltpu.VMEM((3, R, D), BF), pltpu.VMEM((8, 128), F32), pltpu.VMEM((n, 8, 128), F32), DMA((M + 1,)), DMA((M,)), DMA(sems), DMA(sems), DMA((n,)), DMA((n,))],
        compiler_params=params_of(0),
    )(x, block, gain, bias)


def lanes(shape):
    return lax.broadcasted_iota(jnp.int32, shape, len(shape) - 1)


def three_parts(x):
    hi = x.astype(BF)
    rest = x - hi.astype(F32)
    mid = rest.astype(BF)
    return hi, mid, (rest - mid.astype(F32)).astype(BF)


def mask_bias(shape, length):
    return jnp.where(lax.broadcasted_iota(jnp.int32, shape, 0) < length, 0.0, NEG).astype(BF)


def attend_step(p, len_ref, q_ref, k_ref, v_ref, o_ref, wide_ref, lse_ref, tq, between):
    L = q_ref.shape[0]
    lane = lanes((L, 128))
    k, v = k_ref[...], v_ref[...]
    bias = mask_bias((L, 128), len_ref[0])
    zero, one = jnp.zeros((L, 128), BF), jnp.ones((L, 128), BF)

    @pl.when(p == 0)
    def _():
        lse_ref[...] = jnp.zeros_like(lse_ref)

    keys, values = [], []
    for h in range(2):
        mine = (lane < 64) if h == 0 else (lane >= 64)
        spare = 64 * (1 - h)
        keys.append(jnp.where(mine, k, jnp.where(lane == spare, bias, zero)))
        values.append(jnp.where(mine, v, jnp.where(lane == spare, one, zero)))
    lq = lanes((tq, 128))
    for i in range(L // tq):
        between(i)
        sl = pl.ds(i * tq, tq)
        q = q_ref[sl, :]
        outs, sums = [], []
        for h in range(2):
            mine = (lq < 64) if h == 0 else (lq >= 64)
            spare = 64 * (1 - h)
            q_h = jnp.where(mine, q, jnp.where(lq == spare, jnp.ones((tq, 128), BF), jnp.zeros((tq, 128), BF)))
            s = dot(q_h, keys[h], NT)
            top = jnp.max(s, axis=1, keepdims=True) * TO_LOG2
            e = jnp.exp2(s * TO_LOG2 - top)
            o = dot(e.astype(BF), values[h], NN)
            total = o[:, spare : spare + 1]
            outs.append(o / total)
            sums.append(top + jnp.log2(total))
        out = jnp.where(lq < 64, outs[0], outs[1])
        wide_ref[sl, :] = out
        o_ref[sl, :] = out.astype(BF)
        lse = lse_ref[sl, :]
        lse = jnp.where(lq == 2 * p, sums[0], lse)
        lse_ref[sl, :] = jnp.where(lq == 2 * p + 1, sums[1], lse)


def attend_back_step(p, len_ref, q_ref, k_ref, v_ref, do_ref, wide_ref, lse_ref, dq_ref, dk_ref, dv_ref, tq, between):
    L = q_ref.shape[0]
    lane = lanes((L, 128))
    k, v = k_ref[...], v_ref[...]
    bias = mask_bias((L, 128), len_ref[0])
    zero, one = jnp.zeros((L, 128), BF), jnp.ones((L, 128), BF)
    keys, values = [], []
    for h in range(2):
        mine = (lane < 64) if h == 0 else (lane >= 64)
        b = 64 * (1 - h)
        ones = jnp.where((lane > b) & (lane < b + 4), one, zero)
        keys.append(jnp.where(mine, k, jnp.where(lane == b, bias, ones)))
        values.append(jnp.where(mine, v, ones))
    lq = lanes((tq, 128))
    dk, dv = [jnp.zeros((L, 128), F32)] * 2, [jnp.zeros((L, 128), F32)] * 2
    for i in range(L // tq):
        between(i)
        sl = pl.ds(i * tq, tq)
        q, do, lse = q_ref[sl, :], do_ref[sl, :], lse_ref[sl, :]
        product = wide_ref[sl, :] * do.astype(F32)
        dq = []
        for h in range(2):
            mine = (lq < 64) if h == 0 else (lq >= 64)
            b = 64 * (1 - h)
            minus_delta = -jnp.sum(jnp.where(mine, product, 0.0), axis=1, keepdims=True)
            minus_lse = -jnp.sum(jnp.where(lq == 2 * p + h, lse, 0.0), axis=1, keepdims=True) * (1.0 / TO_LOG2)

            def with_spare(x, term, first):
                hi, mid, lo = three_parts(jnp.broadcast_to(term, (tq, 128)))
                low = jnp.where(lq == b + 2, mid, jnp.where(lq == b + 3, lo, jnp.zeros((tq, 128), BF)))
                low = jnp.where(lq == b, jnp.full((tq, 128), first, BF), jnp.where(lq == b + 1, hi, low))
                return jnp.where(mine, x, low)

            st = dot(keys[h], with_spare(q, minus_lse, 1.0), NT)
            pt = jnp.exp2(st * TO_LOG2)
            dpt = dot(values[h], with_spare(do, minus_delta, 0.0), NT)
            ds = (pt * dpt).astype(BF)
            dv[h] = dv[h] + dot(pt.astype(BF), do, NN)
            dk[h] = dk[h] + dot(ds, q, NN)
            dq.append(dot(ds, k, TN))
        dq_ref[sl, :] = (jnp.where(lq < 64, dq[0], dq[1]) * SCALE).astype(BF)
    dk_ref[...] = (jnp.where(lane < 64, dk[0], dk[1]) * SCALE).astype(BF)
    dv_ref[...] = jnp.where(lane < 64, dv[0], dv[1]).astype(BF)


def at_slots(p, per_step, plan):
    def between(i):
        for slot, actions in sorted(plan.items()):
            if slot % per_step == i:

                @pl.when(p == slot // per_step)
                def _(actions=actions):
                    for action in actions:
                        action()

    return between


def attend_kernel(len_ref, x_ref, w_ref, proj_ref, in_ref, out_ref, o_ref, wide_ref, lse_ref, packed_ref, wproj_ref, land_ref, win_ref, wout_ref,
                  w_s, w_sem, packed_s, save_sem, pchain_sends, pchain_recvs, chain_sends, chain_recvs, sends, recvs, *, tq):
    p, steps = pl.program_id(0), pl.num_programs(0)
    at = Place()
    M = at.M
    half = M // 2
    D = x_ref.shape[1]
    parts = x_ref.shape[0] // tq
    land = [lambda s, a=a: land_ref.at[s, a] for a in range(2)]
    own = (in_ref, out_ref)
    pland = lambda s: wproj_ref.at[at.g, at.c, s]
    pchain = Along(at, proj_ref, pland, pchain_sends, pchain_recvs)
    chains = [Along(at, own[a], land[a], chain_sends.at[a], chain_recvs.at[a]) for a in range(2)]
    main = [
        [GatherUnit(at, land[a](at.near[n]) if n else own[a], lambda g, c, n=n, ref=ref: ref.at[n, g, c], a, sends.at[2 * n + a], recvs.at[2 * n + a])
         for a, ref in enumerate((win_ref, wout_ref))]
        for n in range(half)
    ]
    proj = [
        GatherUnit(at, pland(at.near[n]) if n else proj_ref, lambda g, c, n=n: wproj_ref.at[g, c, at.near[n]], n % 2,
                   sends.at[2 * half + n], recvs.at[2 * half + n], n == 0)
        for n in range(M)
    ]
    own_land = [pltpu.make_async_copy(own[a], land_ref.at[at.z, a], save_sem.at[1 + a]) for a in range(2)]
    save = pltpu.make_async_copy(packed_s, packed_ref, save_sem.at[0])

    loads = [pltpu.make_async_copy(w_ref.at[t], w_s.at[t], w_sem.at[t]) for t in range(3)]

    def third(t):
        loads[t].wait()
        packed_s[:, pl.ds(t * D, D)] = dot(x_ref[...], w_s[t], NN).astype(BF)

    @pl.when(p == 0)
    def _():
        for cp in loads:
            cp.start()
        at.greet()
        third(0)
        at.meet()
        pchain.start(*range(1, M))
        for n in range(1, M):
            for chain in chains:
                chain.start(n)
        proj[0].spread()
        for u in main[0]:
            u.spread()
        for cp in own_land:
            cp.start()
        third(1)
        third(2)
        save.start()

    plan = {}

    def put(slot, *actions):
        plan.setdefault(min(slot, ATTEND_STEPS * parts - 1), []).extend(actions)

    def arrive(chain, n, unit=None):
        def act():
            chain.arrive(n)
            if unit is not None:
                unit.spread()

        return act

    for n in range(M):
        arrives, relays, lasts = ATTEND_PROJ[min(n, 3)]
        put(relays, proj[n].relay)
        put(lasts, proj[n].last)
        if n:
            put(arrives, arrive(pchain, n, proj[n]))
    for n in range(half):
        for a in range(2):
            arrives, relays, lasts = ATTEND_MAIN[min(n, 1)][a]
            if n:
                put(arrives, arrive(chains[a], n, main[n][a]))
            put(relays, main[n][a].relay)
            put(lasts, main[n][a].last)
    lane = pl.multiple_of(p * 128, 128)
    column = lambda t: packed_s.at[:, pl.ds(t * D + lane, 128)]
    attend_step(p, len_ref, column(0), column(1), column(2), o_ref, wide_ref, lse_ref, tq, at_slots(p, parts, plan))

    @pl.when(p == steps - 1)
    def _():
        for n in range(half, M):
            for chain in chains:
                chain.arrive(n)
        for group in main + [proj, chains, [pchain]]:
            for u in group:
                u.finish()
        save.wait()
        for cp in own_land:
            cp.wait()


ATTEND_STEPS = 6
ATTEND_PROJ = [[0, 2, 5], [1, 5, 8], [4, 7, 10], [6, 9, 11]]
ATTEND_MAIN = [[[0, 4, 8], [0, 4, 8]], [[3, 7, 11], [4, 8, 11]]]
BACK = {"pair0": 5, "pair1": 6, "pair_p": 7, "join_1": 7, "cross1": 9, "pair_h0": 10, "cross_p": 11, "join0": 13, "cross_h0": 17,
        "pair_h1": 17, "join_p": 19, "cross_h1": 19, "late_p": 21, "join_h0": 21, "late_h0": 23, "join_h1": 23}
MLP = {"relay0": (0, 3), "spread1": (0, 3), "relay1": (1, 3), "last0": (1, 2), "last1": (2, 2), "pair0": (1, 2), "cross0": (2, 1), "pair1": (2, 3), "join0": (3, 1)}


def attend(lengths, x, w, proj, w_in, w_out, tq):
    G, M = lax.axis_size("dp") // 2, lax.axis_size("mp")
    L, D = x.shape
    half = M // 2
    column = pl.BlockSpec((L, 128), lambda p: (0, p))
    whole = lambda shape: pl.BlockSpec(shape, lambda p: (0,) * len(shape), pipeline_mode=pl.Buffered(1))
    sems = (2 * half + M, GatherUnit.count(G))
    weights = jax.ShapeDtypeStruct((half, G, 2) + w_in.shape, BF)
    return pl.pallas_call(
        functools.partial(attend_kernel, tq=tq),
        grid=(D // 128,),
        in_specs=[SMEM, whole(x.shape), ANY, ANY, ANY, ANY],
        out_specs=[column, column, pl.BlockSpec((L, 128), lambda p: (0, 0)), ANY, ANY, ANY, ANY, ANY],
        out_shape=[
            jax.ShapeDtypeStruct((L, D), BF),
            jax.ShapeDtypeStruct((L, D), F32),
            jax.ShapeDtypeStruct((L, 128), F32),
            jax.ShapeDtypeStruct((L, 3 * D), BF),
            jax.ShapeDtypeStruct((G, 2, M) + proj.shape, BF),
            jax.ShapeDtypeStruct((M, 2) + w_in.shape, BF),
            weights, weights,
        ],
        scratch_shapes=[pltpu.VMEM(w.shape, BF), DMA((3,)), pltpu.VMEM((L, 3 * D), BF), DMA((3,)), DMA((M + 1,)), DMA((M,)), DMA((2, M + 1)), DMA((2, M)), DMA(sems), DMA(sems)],
        compiler_params=params_of(1, grid=1),
    )(lengths, x, w, proj, w_in, w_out)


def gelu_and_slope(x):
    phi = 0.5 + 0.5 * lax.erf(x * 0.7071067811865476)
    return x * phi, phi + x * (jnp.exp2((x * x) * (-0.5 * LOG2E)) * 0.3989422804014327)


def mlp_kernel(len_ref, x_hbm, mixed_hbm, cot_hbm, params_ref, wproj_hbm, win_ref, wout_ref, land_ref,
               y_hbm, mgrad_hbm, dmixed_hbm, sums_ref, pproj_ref, pin_ref, pout_ref, din_ref, dout_ref, half_ref,
               x_ref, mixed_ref, cot_ref, wproj_ref, in_sems, out_sems, w_s, mid_s, hid_s, sg_s, sec_s, br_s, act_s, eg_s, got_s, near_s, diag_s,
               load_sems, save_sems, gsends, grecvs, ssends, srecvs, *, tr):
    at = Place()
    G, M = at.G, at.M
    L, D = x_ref.shape
    n_rows = L // tr
    enter_loads = [
        [pltpu.make_async_copy(src.at[pl.ds(i * tr, tr)], dst.at[pl.ds(i * tr, tr)], in_sems.at[i, j])
         for j, (src, dst) in enumerate(((mixed_hbm, mixed_ref), (x_hbm, x_ref), (cot_hbm, cot_ref)))]
        for i in range(n_rows)
    ]
    proj_load = pltpu.make_async_copy(wproj_hbm, wproj_ref, in_sems.at[0, 3])
    proj_load.start()
    for group in enter_loads:
        for cp in group:
            cp.start()
    R, Fb = land_ref.shape[2:]
    half = M // 2
    gain, bias = params_ref[1:2, :], params_ref[3:4, :]
    loads = [pltpu.make_async_copy((win_ref, wout_ref)[a].at[k], w_s.at[k, a], load_sems.at[k, a]) for k in range(half) for a in range(2)]
    for cp in loads:
        cp.start()
    at.greet()
    gathers = [
        [GatherUnit(at, land_ref.at[at.near[k], a], lambda g, c, k=k, a=a: w_s.at[k, a, g * 2 + c], a, gsends.at[k - half, a], grecvs.at[k - half, a])
         for a in range(2)]
        for k in range(half, M)
    ]
    sums = [
        [SumUnit(at, lambda c, k=k, a=a: w_s.at[k, a, pl.ds(c * G, G)], None, *[b.at[2 * k + a] for b in (got_s, near_s, diag_s)], None,
                 None, total, k, a, ssends.at[2 * k + a], srecvs.at[2 * k + a], None)
         for a, total in enumerate((din_ref, dout_ref))]
        for k in range(2)
    ]

    def rows(i):
        return pl.ds(i * tr, tr)

    def enter(i):
        if i == 0:
            proj_load.wait()
        for cp in enter_loads[i]:
            cp.wait()
        sl = rows(i)
        mid = x_ref[sl, :].astype(F32) + dot(mixed_ref[sl, :], wproj_ref[...], NN)
        mid_s[sl, :] = mid
        hid_s[sl, :] = mid
        sec_s[sl, :] = (norm_stats(mid)[0] * gain + bias).astype(BF)
        at_row = lax.broadcasted_iota(jnp.int32, (tr, D), 0) + i * tr
        br_s[sl, :] = jnp.where(at_row < len_ref[0], cot_ref[sl, :].astype(F32), 0.0).astype(BF)
        sg_s[sl, :] = jnp.zeros((tr, D), F32)

    enter(0)
    at.meet()
    for group in gathers:
        group[0].spread()
        if group is gathers[0]:
            group[1].spread()
    for i in range(1, n_rows):
        enter(i)
    for cp in loads:
        cp.wait()
    per = n_rows + 2
    plan = {}

    def put(k, i, name, group):
        plan.setdefault((min(k, M - 1), min(i, per - 1)), []).extend(getattr(u, name) for u in group)

    for n, group in enumerate(gathers):
        after = lambda name: (MLP[name + "0"] if n == 0 else (MLP[name + "1"][0] + n - 1, MLP[name + "1"][1]))
        put(*after("relay"), "relay", group)
        if n:
            put(*MLP["spread1"], "spread", group[1:])
        put(*after("last"), "last", group)
        put(half + n, 0, "finish", group)
    put(1, 0, "start", sums[0])
    put(*MLP["pair0"], "pair", sums[0])
    put(2, 0, "start", sums[1])
    put(*MLP["cross0"], "cross", sums[0])
    plan.setdefault(MLP["pair1"], []).extend(functools.partial(u.pair, True) for u in sums[1])
    put(*MLP["join0"], "join", sums[0])

    def block(k, carry):
        def between(i):
            for (at_k, at_i), actions in sorted(plan.items(), key=lambda item: item[0]):
                if at_i == i:

                    @pl.when(k == at_k)
                    def _(actions=actions):
                        for action in actions:
                            action()

        between(0)
        win, wout = (w_s[k, a].reshape(D, Fb) for a in range(2))
        for i in range(n_rows):
            if i:
                between(i)
            sl = rows(i)
            value, slope = gelu_and_slope(dot(sec_s[sl, :], win, NN))
            act = value.astype(BF)
            eg = (dot(br_s[sl, :], wout, NN) * slope).astype(BF)
            act_s[sl, :], eg_s[sl, :] = act, eg
            hid_s[sl, :] += dot(act, wout, NT)
            sg_s[sl, :] += dot(eg, win, NT)
        for a, (left, right) in enumerate(((sec_s, eg_s), (br_s, act_s))):
            between(n_rows + a)
            grad = dot(left[...], right[...], TN)
            for g in range(G):
                for c in range(2):
                    row = (g * 2 + c) * R
                    w_s[k, a, c * G + g] = grad[row : row + R, :].astype(BF)

        @pl.when(k > 1)
        def _():
            for a, ref in enumerate((pin_ref, pout_ref)):
                pltpu.make_async_copy(w_s.at[k, a], ref.at[k - 2], save_sems.at[k - 2, a]).start()

        return carry

    lax.fori_loop(0, M, block, 0)
    sums_ref[...] = jnp.zeros_like(sums_ref)
    n_back = L // 256 if L % 256 == 0 else 1
    tb = L // n_back

    def saves(i):
        sl = pl.ds(pl.multiple_of(i * tb, tb), tb)
        return [pltpu.make_async_copy(src.at[sl], dst.at[sl], out_sems.at[i, j])
                for j, (src, dst) in enumerate(((x_ref, y_hbm), (mid_s, mgrad_hbm), (cot_ref, dmixed_hbm)))]

    def back(i, carry):
        sl = pl.ds(pl.multiple_of(i * tb, tb), tb)
        x_ref[sl, :] = hid_s[sl, :].astype(BF)
        xhat, r = norm_stats(mid_s[sl, :])
        e = sg_s[sl, :]
        sums_ref[1:2, :] += jnp.sum(e * xhat, axis=0, keepdims=True)
        sums_ref[3:4, :] += jnp.sum(e, axis=0, keepdims=True)
        grad = br_s[sl, :].astype(F32) + norm_pull(e, xhat, r, gain)
        mid_s[sl, :] = grad
        low = grad.astype(BF)
        sec_s[sl, :] = low
        cot_ref[sl, :] = dot(low, wproj_ref[...], NT).astype(BF)
        for cp in saves(i):
            cp.start()
        return carry

    lax.fori_loop(0, n_back, back, 0)
    for u in sums[1]:
        u.cross(True)
    save_half = pltpu.make_async_copy(got_s.at[pl.ds(2, 2)], half_ref, load_sems.at[0, 0])
    save_half.start()
    grad = dot(mixed_ref[...], sec_s[...], TN)
    R_p = pproj_ref.shape[3]
    for g in range(G):
        for c in range(2):
            for z in range(M):
                row = ((g * 2 + c) * M + z) * R_p
                pproj_ref[z, c, g] = grad[row : row + R_p, :].astype(BF)
    for k in range(2, M):
        for a, ref in enumerate((pin_ref, pout_ref)):
            pltpu.make_async_copy(w_s.at[k, a], ref.at[k - 2], save_sems.at[k - 2, a]).wait()
    save_half.wait()

    def saved(i, carry):
        for cp in saves(i):
            cp.wait()
        return carry

    lax.fori_loop(0, n_back, saved, 0)
    for k, group in enumerate(sums):
        for u in group:
            u.finish(True, k == 0)


def mlp(lengths, x, mixed, cot, params, wproj, win, wout, land, R_p, tr):
    G, M = lax.axis_size("dp") // 2, lax.axis_size("mp")
    half = M // 2
    L, D = x.shape
    R, Fb = block = land.shape[2:]
    gsems, ssems = (M - half, 2, GatherUnit.count(G)), (4, SumUnit.count(G))
    pieces = jax.ShapeDtypeStruct((M - 2, 2 * G) + block, BF)
    return pl.pallas_call(
        functools.partial(mlp_kernel, tr=tr),
        in_specs=[SMEM, ANY, ANY, ANY, VMEM, ANY, ANY, ANY, ANY],
        out_specs=[ANY] * 3 + [VMEM] * 2 + [ANY, ANY, VMEM, VMEM, ANY],
        out_shape=[
            jax.ShapeDtypeStruct((L, D), BF),
            jax.ShapeDtypeStruct((L, D), F32),
            jax.ShapeDtypeStruct((L, D), BF),
            jax.ShapeDtypeStruct(params.shape, F32),
            jax.ShapeDtypeStruct((M, 2, G, R_p, D), BF),
            pieces, pieces,
            jax.ShapeDtypeStruct(block, F32), jax.ShapeDtypeStruct(block, F32), jax.ShapeDtypeStruct((2, G) + block, BF),
        ],
        scratch_shapes=[
            pltpu.VMEM((L, D), BF), pltpu.VMEM((L, D), BF), pltpu.VMEM((L, D), BF), pltpu.VMEM((D, D), BF),
            DMA((L // tr, 4)), DMA((L // 256 if L % 256 == 0 else 1, 3)),
            pltpu.VMEM((M, 2, 2 * G) + block, BF),
            pltpu.VMEM((L, D), F32), pltpu.VMEM((L, D), F32), pltpu.VMEM((L, D), F32),
            pltpu.VMEM((L, D), BF), pltpu.VMEM((L, D), BF), pltpu.VMEM((L, Fb), BF), pltpu.VMEM((L, Fb), BF),
        ] + sum_buffers(4, G, block, own=False)[:3] + [DMA((half, 2)), DMA((M - 2, 2)), DMA(gsems), DMA(gsems), DMA(ssems), DMA(ssems)],
        compiler_params=params_of(4),
    )(lengths, x, mixed, cot, params, wproj, win, wout, land)


def attend_back_kernel(len_ref, q_ref, k_ref, v_ref, do_ref, wide_ref, lse_ref, normed_hbm, pin_ref, pout_ref, pproj_ref, hin_ref, hout_ref, half_ref,
                       dqkv_ref, din_ref, dout_ref, dproj_ref, sum_ref, rest_ref,
                       own_m, got_m, near_m, diag_m, send_m, far_in, far_out, own_p, got_p, near_p, diag_p, send_p, far_p,
                       parts_s, got_q, near_q, diag_q, send_q, far_q, sends, recvs, far_recvs, far_recvs_q, save_sem, normed_ref, *, tq):
    p, steps = pl.program_id(0), ATTEND_STEPS
    at = Place()
    G, M = at.G, at.M
    parts = q_ref.shape[0] // tq
    R = sum_ref.shape[1]
    units = []

    def add(part, bufs, far, total, n, way, recv, local=True):
        k = len(units)
        units.append(SumUnit(at, part, *bufs, far, total, n, way, sends.at[k], recvs.at[k], recv, local=local))
        return units[-1]

    def block(n):
        made = []
        for a, (ref, far, total) in enumerate(((pin_ref, far_in, din_ref), (pout_ref, far_out, dout_ref))):
            k = 2 * (n - 1) + a
            near, diag, out = [b.at[k] for b in (near_m, diag_m, send_m)]
            own, got = (None, half_ref.at[a]) if n == 1 else (own_m.at[k - 2], got_m.at[k - 2])
            made.append(add(lambda c, ref=ref: ref.at[n - 2, pl.ds(c * G, G)], (own, got, near, diag, out), far, total, n, a, far_recvs.at[a]))
        return made

    main = {n: block(n) for n in range(1, M)}
    for a in range(2):
        link([main[n][a] for n in main])
    proj = {}
    for n in reversed(range(M)):
        proj[n] = add(lambda c, n=n: pproj_ref.at[at.near[n], c], [b.at[n] for b in (own_p, got_p, near_p, diag_p, send_p)],
                      far_p, dproj_ref, n, n % 2, far_recvs.at[2])
    heads = []
    for t in range(steps // 2 - 1):
        heads.append({})
        for n in reversed(range(M)):
            heads[t][n] = add(lambda c, t=t, n=n: parts_s.at[t, at.near[n], c], [None] + [b.at[t * M + n] for b in (got_q, near_q, diag_q, send_q)],
                              far_q.at[pl.ds(t * M, M)], sum_ref.at[t], n, (n + t) % 2, far_recvs_q.at[t], False)
    for group in [proj] + heads:
        link(list(group.values()))
    every = lambda group: list(group.values())
    early = lambda group: [group[n] for n in group if n != 2]
    late = lambda group: [group[n] for n in group if n == 2]
    plan = {}

    def put(slot, name, group):
        slot = slot + 1 if slot % parts == 0 else slot
        plan.setdefault(min(slot, steps * parts - 1), []).extend(getattr(u, name) for u in group)

    load = pltpu.make_async_copy(normed_hbm, normed_ref, save_sem.at[1])
    pl.when(p == 0)(load.start)
    pl.when(p == 1)(load.wait)

    def begin():
        din_ref[...], dout_ref[...] = hin_ref[...], hout_ref[...]

    plan[0] = [at.greet, begin]
    plan[1] = [at.meet]
    put(1, "launch", main[1])
    others = [main[n] for n in reversed(range(2, M))]
    for group in others + [every(proj)]:
        put(1, "start", group)
    for n, group in enumerate(others):
        put(BACK["pair0"] if n == 0 else BACK["pair1"], "pair", group)
        if n != 1:
            put(BACK["join0"], "join", group)
    put(BACK["pair_p"], "pair", every(proj))
    put(BACK["join_1"], "join", main[1])
    for group in others[1:]:
        put(BACK["cross1"], "cross", group)
    put(BACK["pair_h0"], "pair", every(heads[0]))
    put(BACK["cross_p"], "cross", every(proj))
    put(BACK["pair_h1"], "pair", every(heads[1]))
    put(BACK["cross_h0"], "cross", every(heads[0]))
    put(BACK["join_p"], "join", early(proj))
    put(BACK["cross_h1"], "cross", every(heads[1]))
    put(BACK["late_p"], "join", late(proj))
    put(BACK["join_h0"], "join", early(heads[0]))
    put(BACK["late_h0"], "join", late(heads[0]))
    put(BACK["join_h1"], "join", early(heads[1]))
    grad_to = lambda t: dqkv_ref.at[0, :, pl.ds(pl.multiple_of(t * 256 + lax.rem(p, 2) * 128, 128), 128)]
    attend_back_step(p, len_ref, q_ref, k_ref, v_ref, do_ref, wide_ref, lse_ref, grad_to(0), grad_to(1), grad_to(2), tq, at_slots(p, parts, plan))

    @pl.when(p == 1)
    def _():
        for u in others[0]:
            u.cross()

    @pl.when(p == steps - 1)
    def _():
        for u in late(heads[1]):
            u.join()

    @pl.when(lax.rem(p, 2) == 1)
    def _():
        t = p // 2
        grad = dot(normed_ref[...], dqkv_ref[0], TN)
        for g in range(G):
            for c in range(2):
                for z in range(M):
                    k = ((g * 2 + c) * M + z) * R
                    parts_s[t, z, c, g] = grad[k : k + R, :].astype(BF)

    save = pltpu.make_async_copy(parts_s.at[steps // 2 - 1], rest_ref, save_sem.at[0])
    for t, group in enumerate(heads):

        @pl.when(p == 2 * t + 1)
        def _(group=group):
            for u in every(group):
                u.start()

    @pl.when(p == 3)
    def _():
        for u in others[1] if len(others) > 1 else []:
            u.join()

    @pl.when(p == steps - 1)
    def _():
        save.start()
        for u in units:
            u.close()
        for u in units:
            u.finish(u not in main[1], True)
        save.wait()


def attend_back(lengths, packed, do, wide, lse, normed, p_in, p_out, p_proj, h_in, h_out, halfway, tq):
    G, M = lax.axis_size("dp") // 2, lax.axis_size("mp")
    L, D = do.shape
    pairs = D // 128
    column = lambda off: pl.BlockSpec((L, 128), lambda p, off=off: (0, off + p))
    whole = lambda shape: pl.BlockSpec(shape, lambda p: (0,) * len(shape), pipeline_mode=pl.Buffered(1))
    out = lambda shape: pl.BlockSpec(shape, lambda p: (0,) * len(shape))
    mshape, pshape = h_in.shape, p_proj.shape[3:]
    groups = pairs // 2
    rest = 2 * (M - 1)
    sems = (rest + groups * M, SumUnit.count(G))
    return pl.pallas_call(
        functools.partial(attend_back_kernel, tq=tq),
        grid=(pairs,),
        in_specs=[SMEM, column(0), column(pairs), column(2 * pairs), column(0), column(0), whole((L, 128)), ANY, ANY, ANY, ANY,
                  whole(mshape), whole(mshape), whole(halfway.shape)],
        out_specs=[pl.BlockSpec((1, L, 768), lambda p: (p // 2, 0, 0)), out(mshape), out(mshape), out(pshape), out((groups - 1,) + pshape), ANY],
        out_shape=[jax.ShapeDtypeStruct((groups, L, 768), BF)]
        + [jax.ShapeDtypeStruct(mshape, F32)] * 2
        + [jax.ShapeDtypeStruct(pshape, F32), jax.ShapeDtypeStruct((groups - 1,) + pshape, F32), jax.ShapeDtypeStruct((M, 2, G) + pshape, BF)],
        scratch_shapes=sum_buffers(rest - 2, G, mshape)[:2] + sum_buffers(rest, G, mshape, far=M)[2:] + [pltpu.VMEM((M,) + mshape, BF)] + sum_buffers(M, G, pshape, far=M)
        + [pltpu.VMEM((groups, M, 2, G) + pshape, BF)] + sum_buffers((groups - 1) * M, G, pshape, own=False, far=(groups - 1) * M)
        + [DMA(sems), DMA(sems), DMA((3, M)), DMA((groups - 1, M)), DMA((2,)), pltpu.VMEM((L, D), BF)],
        compiler_params=params_of(2, grid=1),
    )(lengths, packed, packed, packed, do, wide, lse, normed, p_in, p_out, p_proj, h_in, h_out, halfway)


def exit_kernel(x_hbm, dqkv_hbm, w_hbm, mid_hbm, second_ref, params_ref, parts_hbm, sums_ref, grad_hbm, qkv_ref, norms_ref,
                x_ref, dqkv_ref, w_ref, mid_ref, parts_ref, load_sems, save_sems,
                got_s, near_s, diag_s, send_s, far_s, sum_s, norm_s, e_s, small_parts, small_got,
                sends, recvs, far_recvs, small_sends, small_recvs, *, rows):
    at = Place(everyone=True)
    M = at.M
    L, D = x_ref.shape
    R = qkv_ref.shape[0]
    groups = dqkv_ref.shape[0]
    loads = [
        [pltpu.make_async_copy(dqkv_hbm.at[g], dqkv_ref.at[g], load_sems.at[g, 0]),
         pltpu.make_async_copy(w_hbm.at[:, :, pl.ds(g * 256, 256)], w_ref.at[g], load_sems.at[g, 1])]
        for g in range(groups)
    ]
    later = [pltpu.make_async_copy(parts_hbm, parts_ref, load_sems.at[0, 2]), pltpu.make_async_copy(x_hbm, x_ref, load_sems.at[1, 2]),
             pltpu.make_async_copy(mid_hbm, mid_ref, load_sems.at[2, 2])]
    for cp in loads[0] + later[:1] + [cp for group in loads[1:] for cp in group] + later[1:]:
        cp.start()
    small = SmallScatter(at, small_parts, small_got, small_sends, small_recvs)
    units = [
        SumUnit(at, lambda c, n=n: parts_ref.at[at.near[n], c], None, *[b.at[n] for b in (got_s, near_s, diag_s, send_s)], far_s, sum_s, n, n % 2,
                sends.at[n], recvs.at[n], far_recvs)
        for n in reversed(range(M))
    ]

    def run(name):
        for u in units:
            getattr(u, name)()

    gain = params_ref[0:1, :]
    plan = {0: "start", 2: "pair", 5: "cross"}

    def matmul(step, carry):
        g, i = step // 2, lax.rem(step, 2)
        for j, group in enumerate(loads):

            @pl.when(step == 2 * j)
            def _(group=group):
                for cp in group:
                    cp.wait()

        sl = pl.ds(pl.multiple_of(i * (L // 2), L // 2), L // 2)
        e = sum(dot(dqkv_ref[g, sl, t * 256 : t * 256 + 256], w_ref[g, t], NT) for t in range(3))
        e_s[sl, :] = e_s[sl, :] + e
        for j, name in plan.items():

            @pl.when(step == j)
            def _(j=j, name=name):
                if j == 0:
                    later[0].wait()
                    at.meet()
                run(name)

        return carry

    def saves(i):
        sl = pl.ds(pl.multiple_of(i * rows, rows), rows)
        return pltpu.make_async_copy(mid_ref.at[sl], grad_hbm.at[sl], save_sems.at[i])

    def norm(i, carry):
        sl = pl.ds(pl.multiple_of(i * rows, rows), rows)
        e = e_s[sl, :]
        xhat, r = norm_stats(x_ref[sl, :].astype(F32))
        mid_ref[sl, :] = mid_ref[sl, :] + norm_pull(e, xhat, r, gain)
        saves(i).start()
        norm_s[0:1, :] += jnp.sum(e * xhat, axis=0, keepdims=True)
        norm_s[2:3, :] += jnp.sum(e, axis=0, keepdims=True)
        return carry

    at.greet()
    norm_s[...] = second_ref[...]
    e_s[...] = jnp.zeros_like(e_s)
    lax.fori_loop(0, 2 * groups, matmul, 0)
    for cp in later[1:]:
        cp.wait()
    lax.fori_loop(0, L // rows, norm, 0)
    small.start(norm_s[...], R)
    run("join")
    for g in range(groups - 1):
        for t in range(3):
            qkv_ref[:, pl.ds(t * D + g * 256, 256)] = sums_ref[g, :, pl.ds(t * 256, 256)]
    norms_ref[...] = small.collect()
    run("close")
    for t in range(3):
        qkv_ref[:, pl.ds(t * D + (groups - 1) * 256, 256)] = sum_s[:, pl.ds(t * 256, 256)]
    run("finish")
    small.finish()

    def saved(i, carry):
        saves(i).wait()
        return carry

    lax.fori_loop(0, L // rows, saved, 0)


def leave(x, dqkv, w, middle_grad, second_sums, params, parts, sums):
    G, M = lax.axis_size("dp") // 2, lax.axis_size("mp")
    L, D = x.shape
    R = parts.shape[3]
    n = 2 * G * M
    sems = (M, SumUnit.count(G))
    return pl.pallas_call(
        functools.partial(exit_kernel, rows=min(256, L)),
        in_specs=[ANY] * 4 + [VMEM, VMEM, ANY, VMEM],
        out_specs=[ANY, VMEM, VMEM],
        out_shape=[
            jax.ShapeDtypeStruct((L, D), F32),
            jax.ShapeDtypeStruct((R, 3 * D), F32),
            jax.ShapeDtypeStruct((8, 128), F32),
        ],
        scratch_shapes=[
            pltpu.VMEM((L, D), BF), pltpu.VMEM(dqkv.shape, BF), pltpu.VMEM((dqkv.shape[0], 3, D, 256), BF), pltpu.VMEM((L, D), F32),
            pltpu.VMEM(parts.shape, BF), DMA((3, 3)), DMA((L // min(256, L),)),
        ] + sum_buffers(M, G, (R, D), own=False, far=M)
        + [pltpu.VMEM((R, D), F32), pltpu.VMEM((8, D), F32), pltpu.VMEM((L, D), F32), pltpu.VMEM((n, 8, 128), F32), pltpu.VMEM((n, 8, 128), F32),
           DMA(sems), DMA(sems), DMA((M,)), DMA((n,)), DMA((n,))],
        compiler_params=params_of(3),
    )(x, dqkv, w, middle_grad, second_sums, params, parts, sums)


def per_device(inputs, lengths, attn_qkv, attn_proj, mlp_in, mlp_out, norm_gain, norm_bias, cotangent):
    n_dp, n_mp = lax.axis_size("dp"), lax.axis_size("mp")
    G = n_dp // 2
    L, D = inputs.shape
    R = attn_qkv.shape[1]
    wqkv, normed, params = entry(inputs, attn_qkv[0], norm_gain[0], norm_bias[0])
    wqkv = wqkv.reshape(3, D, D)
    mixed, wide, lse, packed, wproj, land, win, wout = attend(lengths, normed, wqkv, attn_proj[0], mlp_in[0], mlp_out[0].T, min(512, L))
    pieces = lambda w: w.reshape((w.shape[0], n_dp) + w.shape[3:])
    outputs, middle_grad, mixed_grad, second_sums, p_proj, p_in, p_out, h_in, h_out, halfway = mlp(
        lengths, inputs, mixed, cotangent, params, wproj.reshape(D, D), pieces(win), pieces(wout), land, R, min(512, L))
    dqkv, d_in, d_out, d_proj, sums, parts = attend_back(
        lengths, packed, mixed_grad, wide, lse, normed, p_in, p_out, p_proj, h_in, h_out, halfway, min(256, L))
    input_grad, d_qkv, norms = leave(inputs, dqkv, wqkv, middle_grad, second_sums, params, parts, sums)
    return (
        outputs,
        input_grad,
        d_qkv[None],
        d_proj[None],
        d_in[None],
        d_out.T[None],
        norms[None, :2, :R],
        norms[None, 2:4, :R],
    )


def solution(mesh):
    everywhere = ("dp", "mp")
    wide, columns, vector = P(everywhere, None), P(None, everywhere, None), P(None, None, everywhere)
    return jax.shard_map(
        per_device,
        mesh=mesh,
        in_specs=(wide, P(everywhere), columns, columns, P(None, "dp", "mp"), P(None, "mp", "dp"), vector, vector, wide),
        out_specs=(wide, wide, columns, columns, P(None, "dp", "mp"), P(None, "mp", "dp"), vector, vector),
        check_vma=False,
    )
```

```python
import functools

import jax
import jax.numpy as jnp
from jax import lax
from jax.experimental import pallas as pl
from jax.experimental.pallas import tpu as pltpu
from jax.sharding import PartitionSpec as P

F32, BF = jnp.float32, jnp.bfloat16
MESH = pl.DeviceIdType.MESH
HEAD_DIM = 64
SCALE = 0.125
LOG2E = 1.4426950408889634
TO_LOG2 = SCALE * LOG2E
NEG = -1e30
EPS = 1e-06
NN = (((1,), (0,)), ((), ()))
NT = (((1,), (1,)), ((), ()))
TN = (((0,), (0,)), ((), ()))
VMEM_LIMIT = 60 * 2**20
ANY = pl.BlockSpec(memory_space=pl.ANY)
VMEM = pl.BlockSpec(memory_space=pltpu.VMEM)
SMEM = pl.BlockSpec(memory_space=pltpu.SMEM)
DMA = pltpu.SemaphoreType.DMA


def dot(a, b, dims):
    return lax.dot_general(a, b, dims, preferred_element_type=F32)


def params_of(collective_id=None, grid=0):
    extra = {} if collective_id is None else {"collective_id": collective_id, "has_side_effects": True}
    if grid:
        extra["dimension_semantics"] = ("arbitrary",) * grid
    return pltpu.CompilerParams(vmem_limit_bytes=VMEM_LIMIT, **extra)


class Place:
    def __init__(self, everyone=False):
        self.everyone = everyone
        n_dp, self.M = lax.axis_size("dp"), lax.axis_size("mp")
        self.G = n_dp // 2
        dp = lax.axis_index("dp")
        self.g, self.c, self.z = dp // 2, lax.rem(dp, 2), lax.axis_index("mp")
        self.square = self.G == 4
        self.near = [self.z ^ n if self.M & (self.M - 1) == 0 else lax.rem(self.z + n, self.M) for n in range(self.M)]
        if self.square:
            self.chips = [self.g ^ 1, self.g ^ 2]
            self.diag = self.g ^ 3
        else:
            self.chips = [lax.rem(self.g + d, self.G) for d in range(1, self.G)]

    def chip(self, h):
        return (h * 2 + self.c, self.z)

    def core(self):
        return (self.g * 2 + 1 - self.c, self.z)

    def along(self, z):
        return (self.g * 2 + self.c, z)

    def peers(self):
        if self.everyone:
            n = 2 * self.G * self.M
            return [self.device(lax.rem(self.index + d, n)) for d in range(1, n)]
        return [self.along(s) for s in self.near[1:]] + [self.chip(h) for h in self.chips] + [self.core()]

    @property
    def index(self):
        return (self.g * 2 + self.c) * self.M + self.z

    def device(self, i):
        return (i // self.M, lax.rem(i, self.M))

    def greet(self):
        for dev in self.peers():
            pl.semaphore_signal(pltpu.get_barrier_semaphore(), inc=1, device_id=dev, device_id_type=MESH)

    def meet(self):
        pl.semaphore_wait(pltpu.get_barrier_semaphore(), len(self.peers()))


def remote(src, dst, send, recv, dev):
    return pltpu.make_async_remote_copy(src_ref=src, dst_ref=dst, send_sem=send, recv_sem=recv, device_id=dev, device_id_type=MESH)


class Along:
    def __init__(self, at, own, land, sends, recvs):
        self.at, self.own, self.land, self.sends, self.recvs = at, own, land, sends, recvs

    def _copy(self, n, source):
        return remote(self.own, self.land(source), self.sends.at[n], self.recvs.at[source], self.at.along(self.at.near[n]))

    def start(self, *ns):
        for n in ns:
            self._copy(n, self.at.z).start()

    def pass_on(self):
        block = self.land(self.at.near[2])
        remote(block, block, self.sends.at[3], self.recvs.at[self.at.near[2]], self.at.along(self.at.near[1])).start()

    def arrive(self, n):
        self._copy(n, self.at.near[n]).wait_recv()

    def finish(self):
        for n in range(1, self.at.M):
            self._copy(n, self.at.z).wait_send()


class GatherUnit:
    def __init__(self, at, src, slot, way, sends, recvs, local=True):
        self.at, self.src, self.slot, self.way, self.local = at, src, slot, way, local
        self.sends, self.recvs = sends, recvs

    @staticmethod
    def count(G):
        return 1 + (3 if G == 4 else G - 1) + G

    def _local(self):
        return pltpu.make_async_copy(self.src, self.slot(self.at.g, self.at.c), self.sends.at[0])

    def _to_chip(self, i):
        at = self.at
        return remote(self.src, self.slot(at.g, at.c), self.sends.at[1 + i], self.recvs.at[1 + i], at.chip(at.chips[i]))

    def _relay(self):
        at = self.at
        block = self.slot(at.chips[self.way], at.c)
        return remote(block, block, self.sends.at[3], self.recvs.at[3], at.chip(at.chips[1 - self.way]))

    def _to_core(self, i):
        at = self.at
        h = ([at.g] + at.chips + ([at.diag] if at.square else []))[i]
        k = self.count(at.G) - at.G + i
        block = self.slot(h, at.c)
        return remote(block if i else self.src, block, self.sends.at[k], self.recvs.at[k], at.core())

    def spread(self):
        for i in range(len(self.at.chips)):
            self._to_chip(i).start()
        self._to_core(0).start()
        if self.local:
            self._local().start()

    def relay(self):
        n = len(self.at.chips)
        for i in range(n):
            self._to_chip(i).wait_recv()
        if self.at.square:
            self._relay().start()
        for i in range(n):
            self._to_core(1 + i).start()

    def last(self):
        if self.at.square:
            self._relay().wait_recv()
            self._to_core(3).start()

    def finish(self):
        if self.local:
            self._local().wait()
        for i in range(len(self.at.chips)):
            self._to_chip(i).wait_send()
        if self.at.square:
            self._relay().wait_send()
        for i in range(self.at.G):
            self._to_core(i).wait()


class SumUnit:
    def __init__(self, at, part, own, got, near, diag, out, far, total, n, way, sends, recvs, far_recvs, local=False):
        self.at, self.part, self.own, self.got, self.near, self.diagonal = at, part, own, got, near, diag
        self.out, self.far, self.total, self.n, self.way = out, far, total, n, way
        self.sends, self.recvs, self.far_recvs, self.local = sends, recvs, far_recvs, local
        self.place = at.near[n]
        self.passed = False
        self.opposite = None

    @staticmethod
    def count(G):
        return 3 + (3 if G == 4 else G)

    def _core(self):
        at = self.at
        return remote(self.part(1 - at.c), self.got, self.sends.at[0], self.recvs.at[0], at.core())

    def _local(self):
        return pltpu.make_async_copy(self.part(self.at.c), self.own, self.sends.at[2])

    def _diag(self):
        at = self.at
        return remote(self.got.at[at.diag], self.diagonal, self.sends.at[5], self.recvs.at[5], at.chip(at.chips[1 - self.way]))

    def _chip(self, i):
        at = self.at
        k = 3 + i
        return remote(self.got.at[at.chips[i]], self.near.at[i], self.sends.at[k], self.recvs.at[k], at.chip(at.chips[i]))

    def _z(self, slot):
        dev = self.at.along(self.at.near[1] if self.passed else self.place)
        return remote(self.out, self.far.at[slot], self.sends.at[1], self.far_recvs.at[slot], dev)

    def send_z(self):
        self._z(self.at.near[2] if self.passed else self.at.z).start()

    def start(self):
        self._core().start()
        if self.local:
            self._local().start()

    def launch(self):
        for i in range(len(self.at.chips)):
            self._chip(i).start()

    def pair(self, hold=False):
        at = self.at
        self._core().wait_recv()
        if self.local:
            self._local().wait()
            own = self.own
        else:
            own = self.part(at.c)

        def add(h, carry):
            self.got[h] = (self.got[h].astype(F32) + own[h].astype(F32)).astype(BF)
            return carry

        lax.fori_loop(0, at.G, add, 0)
        if at.square:
            self._diag().start()
        elif not hold:
            self.launch()

    def cross(self, hold=False):
        at = self.at
        if at.square:
            self._diag().wait_recv()
            h = at.chips[self.way]
            self.got[h] = (self.got[h].astype(F32) + self.diagonal[...].astype(F32)).astype(BF)
            if not hold:
                self.launch()

    def join(self):
        at = self.at
        value = self.got[at.g].astype(F32)
        for i in range(len(at.chips)):
            self._chip(i).wait_recv()
            value = value + self.near[i].astype(F32)
        if self.opposite is not None:
            self._z(at.near[3]).wait_recv()
            value = value + self.far[at.near[3]].astype(F32)
        if self.n:
            self.out[...] = value.astype(BF)
            self.send_z()
        else:
            self.total[...] = value

    def close(self):
        if self.n and not self.passed:
            self._z(self.place).wait_recv()
            self.total[...] += self.far[self.place].astype(F32)

    def finish(self, core=True, rest=True):
        at = self.at
        if core:
            self._core().wait_send()
            if at.square:
                self._diag().wait_send()
        if rest:
            if self.n:
                self._z(at.near[2] if self.passed else at.z).wait_send()
            for i in range(len(at.chips)):
                self._chip(i).wait_send()


def link(units):
    by_n = {u.n: u for u in units}
    if units[0].at.M == 4 and 3 in by_n:
        by_n[2].opposite = by_n[3]
        by_n[3].passed = True
    return units


def sum_buffers(n, G, shape, own=True, far=0):
    chips = 2 if G == 4 else G - 1
    block = lambda *lead: pltpu.VMEM(lead + shape, BF)
    return ([block(n, G)] if own else []) + [block(n, G), block(n, chips), block(n), block(n), block(max(far, 1))]


class SmallGather:
    def __init__(self, at, got, sends, recvs):
        self.at, self.got, self.sends, self.recvs = at, got, sends, recvs
        self.count = 2 * at.G * at.M

    def _copy(self, own, d, back):
        at = self.at
        to, other = lax.rem(at.index + d, self.count), lax.rem(at.index + self.count - d, self.count)
        return remote(own, self.got.at[other if back else at.index], self.sends.at[d], self.recvs.at[d], at.device(to))

    def start(self, own):
        def send(d, carry):
            self._copy(own, d, False).start()
            return carry

        lax.fori_loop(1, self.count, send, 0)

    def collect(self, own, R, width):
        def wait(d, carry):
            self._copy(own, d, True).wait_recv()
            return carry

        lax.fori_loop(1, self.count, wait, 0)
        self.got[self.at.index] = own[...]
        lane = lanes((own.shape[0], width))
        total = jnp.zeros((own.shape[0], width), F32)
        for i in range(self.count):
            wide = jnp.concatenate([self.got[i]] * (width // 128), axis=1)
            total = jnp.where(lane // R == i, pltpu.roll(wide, i * R % width, 1) if i else wide, total)
        return total

    def finish(self, own):
        def wait(d, carry):
            self._copy(own, d, False).wait_send()
            return carry

        lax.fori_loop(1, self.count, wait, 0)


class SmallScatter:
    def __init__(self, at, parts, got, sends, recvs):
        self.at, self.parts, self.got, self.sends, self.recvs = at, parts, got, sends, recvs
        self.count = 2 * at.G * at.M

    def _copy(self, d, back):
        at = self.at
        to, other = lax.rem(at.index + d, self.count), lax.rem(at.index + self.count - d, self.count)
        return remote(self.parts.at[to], self.got.at[other if back else at.index], self.sends.at[d], self.recvs.at[d], at.device(to))

    def start(self, value, R):
        for i in range(self.count):
            self.parts[i] = (pltpu.roll(value, value.shape[1] - i * R, 1) if i else value)[:, :128]

        def send(d, carry):
            self._copy(d, False).start()
            return carry

        lax.fori_loop(1, self.count, send, 0)

    def collect(self):
        def add(d, value):
            self._copy(d, True).wait_recv()
            return value + self.got[lax.rem(self.at.index + self.count - d, self.count)]

        return lax.fori_loop(1, self.count, add, self.parts[self.at.index])

    def finish(self):
        def wait(d, carry):
            self._copy(d, False).wait_send()
            return carry

        lax.fori_loop(1, self.count, wait, 0)


def norm_stats(v):
    centre = v - jnp.mean(v, axis=-1, keepdims=True)
    r = lax.rsqrt(jnp.mean(centre * centre, axis=-1, keepdims=True) + EPS)
    return centre * r, r


def norm_pull(e, xhat, r, g):
    y = e * g
    return r * (y - jnp.mean(y, axis=-1, keepdims=True) - xhat * jnp.mean(y * xhat, axis=-1, keepdims=True))


def entry_kernel(x_ref, block_ref, gain_ref, bias_ref, w_ref, normed_ref, params_ref, shard_ref, own_ref, got, chain_sends, chain_recvs, sends, recvs,
                 small_sends, small_recvs, *, rows):
    at = Place(everyone=True)
    at.greet()
    land = lambda s: w_ref.at[:, at.g, at.c, s]
    chain = Along(at, shard_ref, land, chain_sends, chain_recvs)
    units = [
        GatherUnit(at, land(at.near[n]) if n else shard_ref, lambda g, c, n=n: w_ref.at[:, g, c, at.near[n]], n % 2, sends.at[n], recvs.at[n], n == 0)
        for n in range(at.M)
    ]
    small = SmallGather(at, got, small_sends, small_recvs)
    L, D = x_ref.shape
    R = block_ref.shape[0]
    for t in range(3):
        shard_ref[t] = block_ref[:, pl.ds(t * D, D)]
    own_ref[...] = jnp.zeros_like(own_ref)
    own_ref[0:2, 0:R] = gain_ref[...].astype(F32)
    own_ref[2:4, 0:R] = bias_ref[...].astype(F32)
    at.meet()
    chain.start(1)
    units[0].spread()
    chain.start(*range(2, 3 if at.M == 4 else at.M))
    small.start(own_ref)

    def norm(i, carry):
        sl = pl.ds(pl.multiple_of(i * rows, rows), rows)
        xhat, _ = norm_stats(x_ref[sl, :].astype(F32))
        normed_ref[sl, :] = (xhat * params_ref[0:1, :] + params_ref[2:3, :]).astype(BF)
        return carry

    steps = L // rows
    for n in range(1, at.M):
        chain.arrive(n)
        if at.M == 4 and n == 2:
            chain.pass_on()
        units[n].spread()
        units[n - 1].relay()
        if n > 1:
            units[n - 2].last()
    params_ref[...] = small.collect(own_ref, R, D)
    lax.fori_loop(0, steps // 2, norm, 0)
    units[-1].relay()
    if at.M > 1:
        units[-2].last()
    lax.fori_loop(steps // 2, steps, norm, 0)
    units[-1].last()
    for u in units:
        u.finish()
    chain.finish()
    small.finish(own_ref)


def entry(x, block, gain, bias):
    G, M = lax.axis_size("dp") // 2, lax.axis_size("mp")
    L, D = x.shape
    R = block.shape[0]
    n = 2 * G * M
    sems = (M, GatherUnit.count(G))
    return pl.pallas_call(
        functools.partial(entry_kernel, rows=min(256, L)),
        in_specs=[VMEM] * 4,
        out_specs=[ANY, VMEM, VMEM],
        out_shape=[
            jax.ShapeDtypeStruct((3, G, 2, M, R, D), BF),
            jax.ShapeDtypeStruct((L, D), BF),
            jax.ShapeDtypeStruct((8, D), F32),
        ],
        scratch_shapes=[pltpu.VMEM((3, R, D), BF), pltpu.VMEM((8, 128), F32), pltpu.VMEM((n, 8, 128), F32), DMA((M + 1,)), DMA((M,)), DMA(sems), DMA(sems), DMA((n,)), DMA((n,))],
        compiler_params=params_of(0),
    )(x, block, gain, bias)


def lanes(shape):
    return lax.broadcasted_iota(jnp.int32, shape, len(shape) - 1)


def three_parts(x):
    hi = x.astype(BF)
    rest = x - hi.astype(F32)
    mid = rest.astype(BF)
    return hi, mid, (rest - mid.astype(F32)).astype(BF)


def mask_bias(shape, length):
    return jnp.where(lax.broadcasted_iota(jnp.int32, shape, 0) < length, 0.0, NEG).astype(BF)


def attend_step(p, len_ref, q_ref, k_ref, v_ref, o_ref, wide_ref, lse_ref, tq, between):
    L = q_ref.shape[0]
    lane = lanes((L, 128))
    k, v = k_ref[...], v_ref[...]
    bias = mask_bias((L, 128), len_ref[0])
    zero, one = jnp.zeros((L, 128), BF), jnp.ones((L, 128), BF)

    @pl.when(p == 0)
    def _():
        lse_ref[...] = jnp.zeros_like(lse_ref)

    keys, values = [], []
    for h in range(2):
        mine = (lane < 64) if h == 0 else (lane >= 64)
        spare = 64 * (1 - h)
        keys.append(jnp.where(mine, k, jnp.where(lane == spare, bias, zero)))
        values.append(jnp.where(mine, v, jnp.where(lane == spare, one, zero)))
    lq = lanes((tq, 128))
    for i in range(L // tq):
        between(i)
        sl = pl.ds(i * tq, tq)
        q = q_ref[sl, :]
        outs, sums = [], []
        for h in range(2):
            mine = (lq < 64) if h == 0 else (lq >= 64)
            spare = 64 * (1 - h)
            q_h = jnp.where(mine, q, jnp.where(lq == spare, jnp.ones((tq, 128), BF), jnp.zeros((tq, 128), BF)))
            s = dot(q_h, keys[h], NT)
            top = jnp.max(s, axis=1, keepdims=True) * TO_LOG2
            e = jnp.exp2(s * TO_LOG2 - top)
            o = dot(e.astype(BF), values[h], NN)
            total = o[:, spare : spare + 1]
            outs.append(o / total)
            sums.append(top + jnp.log2(total))
        out = jnp.where(lq < 64, outs[0], outs[1])
        wide_ref[sl, :] = out
        o_ref[sl, :] = out.astype(BF)
        lse = lse_ref[sl, :]
        lse = jnp.where(lq == 2 * p, sums[0], lse)
        lse_ref[sl, :] = jnp.where(lq == 2 * p + 1, sums[1], lse)


def attend_back_step(p, len_ref, q_ref, k_ref, v_ref, do_ref, wide_ref, lse_ref, dq_ref, dk_ref, dv_ref, tq, between):
    L = q_ref.shape[0]
    lane = lanes((L, 128))
    k, v = k_ref[...], v_ref[...]
    bias = mask_bias((L, 128), len_ref[0])
    zero, one = jnp.zeros((L, 128), BF), jnp.ones((L, 128), BF)
    keys, values = [], []
    for h in range(2):
        mine = (lane < 64) if h == 0 else (lane >= 64)
        b = 64 * (1 - h)
        ones = jnp.where((lane > b) & (lane < b + 4), one, zero)
        keys.append(jnp.where(mine, k, jnp.where(lane == b, bias, ones)))
        values.append(jnp.where(mine, v, ones))
    lq = lanes((tq, 128))
    dk, dv = [jnp.zeros((L, 128), F32)] * 2, [jnp.zeros((L, 128), F32)] * 2
    for i in range(L // tq):
        between(i)
        sl = pl.ds(i * tq, tq)
        q, do, lse = q_ref[sl, :], do_ref[sl, :], lse_ref[sl, :]
        product = wide_ref[sl, :] * do.astype(F32)
        dq = []
        for h in range(2):
            mine = (lq < 64) if h == 0 else (lq >= 64)
            b = 64 * (1 - h)
            minus_delta = -jnp.sum(jnp.where(mine, product, 0.0), axis=1, keepdims=True)
            minus_lse = -jnp.sum(jnp.where(lq == 2 * p + h, lse, 0.0), axis=1, keepdims=True) * (1.0 / TO_LOG2)

            def with_spare(x, term, first):
                hi, mid, lo = three_parts(jnp.broadcast_to(term, (tq, 128)))
                low = jnp.where(lq == b + 2, mid, jnp.where(lq == b + 3, lo, jnp.zeros((tq, 128), BF)))
                low = jnp.where(lq == b, jnp.full((tq, 128), first, BF), jnp.where(lq == b + 1, hi, low))
                return jnp.where(mine, x, low)

            st = dot(keys[h], with_spare(q, minus_lse, 1.0), NT)
            pt = jnp.exp2(st * TO_LOG2)
            dpt = dot(values[h], with_spare(do, minus_delta, 0.0), NT)
            ds = (pt * dpt).astype(BF)
            dv[h] = dv[h] + dot(pt.astype(BF), do, NN)
            dk[h] = dk[h] + dot(ds, q, NN)
            dq.append(dot(ds, k, TN))
        dq_ref[sl, :] = (jnp.where(lq < 64, dq[0], dq[1]) * SCALE).astype(BF)
    dk_ref[...] = (jnp.where(lane < 64, dk[0], dk[1]) * SCALE).astype(BF)
    dv_ref[...] = jnp.where(lane < 64, dv[0], dv[1]).astype(BF)


def at_slots(p, per_step, plan):
    def between(i):
        for slot, actions in sorted(plan.items()):
            if slot % per_step == i:

                @pl.when(p == slot // per_step)
                def _(actions=actions):
                    for action in actions:
                        action()

    return between


def attend_kernel(len_ref, x_ref, w_ref, proj_ref, in_ref, out_ref, o_ref, wide_ref, lse_ref, packed_ref, wproj_ref, land_ref, win_ref, wout_ref,
                  w_s, w_sem, packed_s, save_sem, pchain_sends, pchain_recvs, chain_sends, chain_recvs, sends, recvs, *, tq):
    p, steps = pl.program_id(0), pl.num_programs(0)
    at = Place()
    M = at.M
    half = M // 2
    D = x_ref.shape[1]
    parts = x_ref.shape[0] // tq
    land = [lambda s, a=a: land_ref.at[s, a] for a in range(2)]
    own = (in_ref, out_ref)
    pland = lambda s: wproj_ref.at[at.g, at.c, s]
    pchain = Along(at, proj_ref, pland, pchain_sends, pchain_recvs)
    chains = [Along(at, own[a], land[a], chain_sends.at[a], chain_recvs.at[a]) for a in range(2)]
    main = [
        [GatherUnit(at, land[a](at.near[n]) if n else own[a], lambda g, c, n=n, ref=ref: ref.at[n, g, c], a, sends.at[2 * n + a], recvs.at[2 * n + a])
         for a, ref in enumerate((win_ref, wout_ref))]
        for n in range(half)
    ]
    proj = [
        GatherUnit(at, pland(at.near[n]) if n else proj_ref, lambda g, c, n=n: wproj_ref.at[g, c, at.near[n]], n % 2,
                   sends.at[2 * half + n], recvs.at[2 * half + n], n == 0)
        for n in range(M)
    ]
    own_land = [pltpu.make_async_copy(own[a], land_ref.at[at.z, a], save_sem.at[1 + a]) for a in range(2)]
    save = pltpu.make_async_copy(packed_s, packed_ref, save_sem.at[0])

    loads = [pltpu.make_async_copy(w_ref.at[t], w_s.at[t], w_sem.at[t]) for t in range(3)]

    def third(t):
        loads[t].wait()
        packed_s[:, pl.ds(t * D, D)] = dot(x_ref[...], w_s[t], NN).astype(BF)

    @pl.when(p == 0)
    def _():
        for cp in loads:
            cp.start()
        at.greet()
        third(0)
        at.meet()
        pchain.start(*range(1, M))
        for n in range(1, M):
            for chain in chains:
                chain.start(n)
        proj[0].spread()
        for u in main[0]:
            u.spread()
        for cp in own_land:
            cp.start()
        third(1)
        third(2)
        save.start()

    plan = {}

    def put(slot, *actions):
        plan.setdefault(min(slot, ATTEND_STEPS * parts - 1), []).extend(actions)

    def arrive(chain, n, unit=None):
        def act():
            chain.arrive(n)
            if unit is not None:
                unit.spread()

        return act

    for n in range(M):
        arrives, relays, lasts = ATTEND_PROJ[min(n, 3)]
        put(relays, proj[n].relay)
        put(lasts, proj[n].last)
        if n:
            put(arrives, arrive(pchain, n, proj[n]))
    for n in range(half):
        for a in range(2):
            arrives, relays, lasts = ATTEND_MAIN[min(n, 1)][a]
            if n:
                put(arrives, arrive(chains[a], n, main[n][a]))
            put(relays, main[n][a].relay)
            put(lasts, main[n][a].last)
    lane = pl.multiple_of(p * 128, 128)
    column = lambda t: packed_s.at[:, pl.ds(t * D + lane, 128)]
    attend_step(p, len_ref, column(0), column(1), column(2), o_ref, wide_ref, lse_ref, tq, at_slots(p, parts, plan))

    @pl.when(p == steps - 1)
    def _():
        for n in range(half, M):
            for chain in chains:
                chain.arrive(n)
        for group in main + [proj, chains, [pchain]]:
            for u in group:
                u.finish()
        save.wait()
        for cp in own_land:
            cp.wait()


ATTEND_STEPS = 6
ATTEND_PROJ = [[0, 0, 4], [0, 4, 6], [4, 6, 8], [6, 8, 10]]
ATTEND_MAIN = [[[0, 4, 8], [0, 4, 8]], [[2, 8, 10], [4, 8, 10]]]
BACK = {"pair0": 1, "pair1": 1, "pair_p": 1, "cross1": 2, "pair_h0": 3, "cross_p": 3, "join0": 3, "pair_h1": 4, "join_p": 4, "cross_h1": 5, "late_p": 5, "join_h0": 5}
MLP = {"relay0": (0, 2), "spread1": (0, 2), "relay1": (2, 0), "last0": (1, 2), "last1": (2, 2), "pair0": (1, 2), "cross0": (2, 2), "pair1": (3, 0), "join0": (3, 2)}


def attend(lengths, x, w, proj, w_in, w_out, tq):
    G, M = lax.axis_size("dp") // 2, lax.axis_size("mp")
    L, D = x.shape
    half = M // 2
    column = pl.BlockSpec((L, 128), lambda p: (0, p))
    whole = lambda shape: pl.BlockSpec(shape, lambda p: (0,) * len(shape), pipeline_mode=pl.Buffered(1))
    sems = (2 * half + M, GatherUnit.count(G))
    weights = jax.ShapeDtypeStruct((half, G, 2) + w_in.shape, BF)
    return pl.pallas_call(
        functools.partial(attend_kernel, tq=tq),
        grid=(D // 128,),
        in_specs=[SMEM, whole(x.shape), ANY, ANY, ANY, ANY],
        out_specs=[column, column, pl.BlockSpec((L, 128), lambda p: (0, 0)), ANY, ANY, ANY, ANY, ANY],
        out_shape=[
            jax.ShapeDtypeStruct((L, D), BF),
            jax.ShapeDtypeStruct((L, D), F32),
            jax.ShapeDtypeStruct((L, 128), F32),
            jax.ShapeDtypeStruct((L, 3 * D), BF),
            jax.ShapeDtypeStruct((G, 2, M) + proj.shape, BF),
            jax.ShapeDtypeStruct((M, 2) + w_in.shape, BF),
            weights, weights,
        ],
        scratch_shapes=[pltpu.VMEM(w.shape, BF), DMA((3,)), pltpu.VMEM((L, 3 * D), BF), DMA((3,)), DMA((M + 1,)), DMA((M,)), DMA((2, M + 1)), DMA((2, M)), DMA(sems), DMA(sems)],
        compiler_params=params_of(1, grid=1),
    )(lengths, x, w, proj, w_in, w_out)


def gelu_and_slope(x):
    phi = 0.5 + 0.5 * lax.erf(x * 0.7071067811865476)
    return x * phi, phi + x * (jnp.exp2((x * x) * (-0.5 * LOG2E)) * 0.3989422804014327)


def mlp_kernel(len_ref, x_hbm, mixed_hbm, cot_hbm, params_ref, wproj_hbm, win_ref, wout_ref, land_ref,
               y_hbm, mgrad_hbm, dmixed_hbm, sums_ref, pproj_ref, pin_ref, pout_ref, din_ref, dout_ref, half_ref,
               x_ref, mixed_ref, cot_ref, wproj_ref, in_sems, out_sems, w_s, mid_s, hid_s, sg_s, sec_s, br_s, act_s, eg_s, got_s, near_s, diag_s,
               load_sems, save_sems, gsends, grecvs, ssends, srecvs, *, tr):
    at = Place()
    G, M = at.G, at.M
    L, D = x_ref.shape
    n_rows = L // tr
    enter_loads = [
        [pltpu.make_async_copy(src.at[pl.ds(i * tr, tr)], dst.at[pl.ds(i * tr, tr)], in_sems.at[i, j])
         for j, (src, dst) in enumerate(((mixed_hbm, mixed_ref), (x_hbm, x_ref), (cot_hbm, cot_ref)))]
        for i in range(n_rows)
    ]
    proj_load = pltpu.make_async_copy(wproj_hbm, wproj_ref, in_sems.at[0, 3])
    proj_load.start()
    for group in enter_loads:
        for cp in group:
            cp.start()
    R, Fb = land_ref.shape[2:]
    half = M // 2
    gain, bias = params_ref[1:2, :], params_ref[3:4, :]
    loads = [pltpu.make_async_copy((win_ref, wout_ref)[a].at[k], w_s.at[k, a], load_sems.at[k, a]) for k in range(half) for a in range(2)]
    for cp in loads:
        cp.start()
    at.greet()
    gathers = [
        [GatherUnit(at, land_ref.at[at.near[k], a], lambda g, c, k=k, a=a: w_s.at[k, a, g * 2 + c], a, gsends.at[k - half, a], grecvs.at[k - half, a])
         for a in range(2)]
        for k in range(half, M)
    ]
    sums = [
        [SumUnit(at, lambda c, k=k, a=a: w_s.at[k, a, pl.ds(c * G, G)], None, *[b.at[2 * k + a] for b in (got_s, near_s, diag_s)], None,
                 None, total, k, a, ssends.at[2 * k + a], srecvs.at[2 * k + a], None)
         for a, total in enumerate((din_ref, dout_ref))]
        for k in range(2)
    ]

    def rows(i):
        return pl.ds(i * tr, tr)

    def enter(i):
        if i == 0:
            proj_load.wait()
        for cp in enter_loads[i]:
            cp.wait()
        sl = rows(i)
        mid = x_ref[sl, :].astype(F32) + dot(mixed_ref[sl, :], wproj_ref[...], NN)
        mid_s[sl, :] = mid
        hid_s[sl, :] = mid
        sec_s[sl, :] = (norm_stats(mid)[0] * gain + bias).astype(BF)
        at_row = lax.broadcasted_iota(jnp.int32, (tr, D), 0) + i * tr
        br_s[sl, :] = jnp.where(at_row < len_ref[0], cot_ref[sl, :].astype(F32), 0.0).astype(BF)
        sg_s[sl, :] = jnp.zeros((tr, D), F32)

    enter(0)
    at.meet()
    for group in gathers:
        group[0].spread()
        if group is gathers[0]:
            group[1].spread()
    for i in range(1, n_rows):
        enter(i)
    for cp in loads:
        cp.wait()
    per = n_rows + 2
    plan = {}

    def put(k, i, name, group):
        plan.setdefault((min(k, M - 1), min(i, per - 1)), []).extend(getattr(u, name) for u in group)

    for n, group in enumerate(gathers):
        after = lambda name: (MLP[name + "0"] if n == 0 else (MLP[name + "1"][0] + n - 1, MLP[name + "1"][1]))
        put(*after("relay"), "relay", group)
        if n:
            put(*MLP["spread1"], "spread", group[1:])
        put(*after("last"), "last", group)
        put(half + n, 0, "finish", group)
    put(1, 0, "start", sums[0])
    put(*MLP["pair0"], "pair", sums[0])
    put(2, 0, "start", sums[1])
    put(*MLP["cross0"], "cross", sums[0])
    plan.setdefault(MLP["pair1"], []).extend(functools.partial(u.pair, True) for u in sums[1])
    put(*MLP["join0"], "join", sums[0])

    def block(k, carry):
        def between(i):
            for (at_k, at_i), actions in sorted(plan.items(), key=lambda item: item[0]):
                if at_i == i:

                    @pl.when(k == at_k)
                    def _(actions=actions):
                        for action in actions:
                            action()

        between(0)
        win, wout = (w_s[k, a].reshape(D, Fb) for a in range(2))
        for i in range(n_rows):
            if i:
                between(i)
            sl = rows(i)
            value, slope = gelu_and_slope(dot(sec_s[sl, :], win, NN))
            act = value.astype(BF)
            eg = (dot(br_s[sl, :], wout, NN) * slope).astype(BF)
            act_s[sl, :], eg_s[sl, :] = act, eg
            hid_s[sl, :] += dot(act, wout, NT)
            sg_s[sl, :] += dot(eg, win, NT)
        for a, (left, right) in enumerate(((sec_s, eg_s), (br_s, act_s))):
            between(n_rows + a)
            grad = dot(left[...], right[...], TN)
            for g in range(G):
                for c in range(2):
                    row = (g * 2 + c) * R
                    w_s[k, a, c * G + g] = grad[row : row + R, :].astype(BF)

        @pl.when(k > 1)
        def _():
            for a, ref in enumerate((pin_ref, pout_ref)):
                pltpu.make_async_copy(w_s.at[k, a], ref.at[k - 2], save_sems.at[k - 2, a]).start()

        return carry

    lax.fori_loop(0, M, block, 0)
    sums_ref[...] = jnp.zeros_like(sums_ref)
    n_back = L // 256 if L % 256 == 0 else 1
    tb = L // n_back

    def saves(i):
        sl = pl.ds(pl.multiple_of(i * tb, tb), tb)
        return [pltpu.make_async_copy(src.at[sl], dst.at[sl], out_sems.at[i, j])
                for j, (src, dst) in enumerate(((x_ref, y_hbm), (mid_s, mgrad_hbm), (cot_ref, dmixed_hbm)))]

    def back(i, carry):
        sl = pl.ds(pl.multiple_of(i * tb, tb), tb)
        x_ref[sl, :] = hid_s[sl, :].astype(BF)
        xhat, r = norm_stats(mid_s[sl, :])
        e = sg_s[sl, :]
        sums_ref[1:2, :] += jnp.sum(e * xhat, axis=0, keepdims=True)
        sums_ref[3:4, :] += jnp.sum(e, axis=0, keepdims=True)
        grad = br_s[sl, :].astype(F32) + norm_pull(e, xhat, r, gain)
        mid_s[sl, :] = grad
        low = grad.astype(BF)
        sec_s[sl, :] = low
        cot_ref[sl, :] = dot(low, wproj_ref[...], NT).astype(BF)
        for cp in saves(i):
            cp.start()
        return carry

    lax.fori_loop(0, n_back, back, 0)
    for u in sums[1]:
        u.cross(True)
    save_half = pltpu.make_async_copy(got_s.at[pl.ds(2, 2)], half_ref, load_sems.at[0, 0])
    save_half.start()
    grad = dot(mixed_ref[...], sec_s[...], TN)
    R_p = pproj_ref.shape[3]
    for g in range(G):
        for c in range(2):
            for z in range(M):
                row = ((g * 2 + c) * M + z) * R_p
                pproj_ref[z, c, g] = grad[row : row + R_p, :].astype(BF)
    for k in range(2, M):
        for a, ref in enumerate((pin_ref, pout_ref)):
            pltpu.make_async_copy(w_s.at[k, a], ref.at[k - 2], save_sems.at[k - 2, a]).wait()
    save_half.wait()

    def saved(i, carry):
        for cp in saves(i):
            cp.wait()
        return carry

    lax.fori_loop(0, n_back, saved, 0)
    for k, group in enumerate(sums):
        for u in group:
            u.finish(True, k == 0)


def mlp(lengths, x, mixed, cot, params, wproj, win, wout, land, R_p, tr):
    G, M = lax.axis_size("dp") // 2, lax.axis_size("mp")
    half = M // 2
    L, D = x.shape
    R, Fb = block = land.shape[2:]
    gsems, ssems = (M - half, 2, GatherUnit.count(G)), (4, SumUnit.count(G))
    pieces = jax.ShapeDtypeStruct((M - 2, 2 * G) + block, BF)
    return pl.pallas_call(
        functools.partial(mlp_kernel, tr=tr),
        in_specs=[SMEM, ANY, ANY, ANY, VMEM, ANY, ANY, ANY, ANY],
        out_specs=[ANY] * 3 + [VMEM] * 2 + [ANY, ANY, VMEM, VMEM, ANY],
        out_shape=[
            jax.ShapeDtypeStruct((L, D), BF),
            jax.ShapeDtypeStruct((L, D), F32),
            jax.ShapeDtypeStruct((L, D), BF),
            jax.ShapeDtypeStruct(params.shape, F32),
            jax.ShapeDtypeStruct((M, 2, G, R_p, D), BF),
            pieces, pieces,
            jax.ShapeDtypeStruct(block, F32), jax.ShapeDtypeStruct(block, F32), jax.ShapeDtypeStruct((2, G) + block, BF),
        ],
        scratch_shapes=[
            pltpu.VMEM((L, D), BF), pltpu.VMEM((L, D), BF), pltpu.VMEM((L, D), BF), pltpu.VMEM((D, D), BF),
            DMA((L // tr, 4)), DMA((L // 256 if L % 256 == 0 else 1, 3)),
            pltpu.VMEM((M, 2, 2 * G) + block, BF),
            pltpu.VMEM((L, D), F32), pltpu.VMEM((L, D), F32), pltpu.VMEM((L, D), F32),
            pltpu.VMEM((L, D), BF), pltpu.VMEM((L, D), BF), pltpu.VMEM((L, Fb), BF), pltpu.VMEM((L, Fb), BF),
        ] + sum_buffers(4, G, block, own=False)[:3] + [DMA((half, 2)), DMA((M - 2, 2)), DMA(gsems), DMA(gsems), DMA(ssems), DMA(ssems)],
        compiler_params=params_of(4),
    )(lengths, x, mixed, cot, params, wproj, win, wout, land)


def attend_back_kernel(len_ref, q_ref, k_ref, v_ref, do_ref, wide_ref, lse_ref, normed_hbm, pin_ref, pout_ref, pproj_ref, hin_ref, hout_ref, half_ref,
                       dqkv_ref, din_ref, dout_ref, dproj_ref, sum_ref, rest_ref,
                       own_m, got_m, near_m, diag_m, send_m, far_in, far_out, own_p, got_p, near_p, diag_p, send_p, far_p,
                       parts_s, got_q, near_q, diag_q, send_q, far_q, sends, recvs, far_recvs, far_recvs_q, save_sem, normed_ref, *, tq):
    p, steps = pl.program_id(0), ATTEND_STEPS
    at = Place()
    G, M = at.G, at.M
    parts = q_ref.shape[0] // tq
    R = sum_ref.shape[1]
    units = []

    def add(part, bufs, far, total, n, way, recv, local=True):
        k = len(units)
        units.append(SumUnit(at, part, *bufs, far, total, n, way, sends.at[k], recvs.at[k], recv, local=local))
        return units[-1]

    def block(n):
        made = []
        for a, (ref, far, total) in enumerate(((pin_ref, far_in, din_ref), (pout_ref, far_out, dout_ref))):
            k = 2 * (n - 1) + a
            near, diag, out = [b.at[k] for b in (near_m, diag_m, send_m)]
            own, got = (None, half_ref.at[a]) if n == 1 else (own_m.at[k - 2], got_m.at[k - 2])
            made.append(add(lambda c, ref=ref: ref.at[n - 2, pl.ds(c * G, G)], (own, got, near, diag, out), far, total, n, a, far_recvs.at[a]))
        return made

    main = {n: block(n) for n in range(1, M)}
    for a in range(2):
        link([main[n][a] for n in main])
    proj = {}
    for n in reversed(range(M)):
        proj[n] = add(lambda c, n=n: pproj_ref.at[at.near[n], c], [b.at[n] for b in (own_p, got_p, near_p, diag_p, send_p)],
                      far_p, dproj_ref, n, n % 2, far_recvs.at[2])
    heads = []
    for t in range(steps // 2 - 1):
        heads.append({})
        for n in reversed(range(M)):
            heads[t][n] = add(lambda c, t=t, n=n: parts_s.at[t, at.near[n], c], [None] + [b.at[t * M + n] for b in (got_q, near_q, diag_q, send_q)],
                              far_q.at[pl.ds(t * M, M)], sum_ref.at[t], n, (n + t) % 2, far_recvs_q.at[t], False)
    for group in [proj] + heads:
        link(list(group.values()))
    every = lambda group: list(group.values())
    early = lambda group: [group[n] for n in group if n != 2]
    late = lambda group: [group[n] for n in group if n == 2]
    plan = {}

    def put(step, name, group):
        plan.setdefault(step * parts, []).extend(getattr(u, name) for u in group)

    load = pltpu.make_async_copy(normed_hbm, normed_ref, save_sem.at[1])
    pl.when(p == 0)(load.start)
    pl.when(p == 1)(load.wait)

    def begin():
        din_ref[...], dout_ref[...] = hin_ref[...], hout_ref[...]

    plan[0] = [at.greet, begin, at.meet]
    put(0, "launch", main[1])
    others = [main[n] for n in reversed(range(2, M))]
    for group in others + [every(proj)]:
        put(0, "start", group)
    for n, group in enumerate(others):
        put(BACK["pair0"] if n == 0 else BACK["pair1"], "pair", group)
        if n != 1:
            put(BACK["join0"], "join", group)
    put(BACK["pair_p"], "pair", every(proj))
    for group in others[1:]:
        put(BACK["cross1"], "cross", group)
    put(BACK["pair_h0"], "pair", every(heads[0]))
    put(BACK["cross_p"], "cross", every(proj))
    put(BACK["join_p"], "join", early(proj))
    put(BACK["pair_h1"], "pair", every(heads[1]))
    put(BACK["cross_h1"], "cross", every(heads[1]))
    put(BACK["late_p"], "join", late(proj))
    put(BACK["join_h0"], "join", early(heads[0]))
    grad_to = lambda t: dqkv_ref.at[0, :, pl.ds(pl.multiple_of(t * 256 + lax.rem(p, 2) * 128, 128), 128)]
    attend_back_step(p, len_ref, q_ref, k_ref, v_ref, do_ref, wide_ref, lse_ref, grad_to(0), grad_to(1), grad_to(2), tq, at_slots(p, parts, plan))

    @pl.when(p == 1)
    def _():
        for u in others[0]:
            u.cross()
        for u in main[1]:
            u.join()

    @pl.when(p == 3)
    def _():
        for u in every(heads[0]):
            u.cross()

    @pl.when(p == steps - 1)
    def _():
        for u in late(heads[0]) + early(heads[1]):
            u.join()

    @pl.when(lax.rem(p, 2) == 1)
    def _():
        t = p // 2
        grad = dot(normed_ref[...], dqkv_ref[0], TN)
        for g in range(G):
            for c in range(2):
                for z in range(M):
                    k = ((g * 2 + c) * M + z) * R
                    parts_s[t, z, c, g] = grad[k : k + R, :].astype(BF)

    save = pltpu.make_async_copy(parts_s.at[steps // 2 - 1], rest_ref, save_sem.at[0])
    for t, group in enumerate(heads):

        @pl.when(p == 2 * t + 1)
        def _(group=group):
            for u in every(group):
                u.start()

    @pl.when(p == 3)
    def _():
        for u in others[1] if len(others) > 1 else []:
            u.join()

    @pl.when(p == steps - 1)
    def _():
        save.start()
        for u in late(heads[1]):
            u.join()
        for u in units:
            u.close()
        for u in units:
            u.finish(u not in main[1], True)
        save.wait()


def attend_back(lengths, packed, do, wide, lse, normed, p_in, p_out, p_proj, h_in, h_out, halfway, tq):
    G, M = lax.axis_size("dp") // 2, lax.axis_size("mp")
    L, D = do.shape
    pairs = D // 128
    column = lambda off: pl.BlockSpec((L, 128), lambda p, off=off: (0, off + p))
    whole = lambda shape: pl.BlockSpec(shape, lambda p: (0,) * len(shape), pipeline_mode=pl.Buffered(1))
    out = lambda shape: pl.BlockSpec(shape, lambda p: (0,) * len(shape))
    mshape, pshape = h_in.shape, p_proj.shape[3:]
    groups = pairs // 2
    rest = 2 * (M - 1)
    sems = (rest + groups * M, SumUnit.count(G))
    return pl.pallas_call(
        functools.partial(attend_back_kernel, tq=tq),
        grid=(pairs,),
        in_specs=[SMEM, column(0), column(pairs), column(2 * pairs), column(0), column(0), whole((L, 128)), ANY, ANY, ANY, ANY,
                  whole(mshape), whole(mshape), whole(halfway.shape)],
        out_specs=[pl.BlockSpec((1, L, 768), lambda p: (p // 2, 0, 0)), out(mshape), out(mshape), out(pshape), out((groups - 1,) + pshape), ANY],
        out_shape=[jax.ShapeDtypeStruct((groups, L, 768), BF)]
        + [jax.ShapeDtypeStruct(mshape, F32)] * 2
        + [jax.ShapeDtypeStruct(pshape, F32), jax.ShapeDtypeStruct((groups - 1,) + pshape, F32), jax.ShapeDtypeStruct((M, 2, G) + pshape, BF)],
        scratch_shapes=sum_buffers(rest - 2, G, mshape)[:2] + sum_buffers(rest, G, mshape, far=M)[2:] + [pltpu.VMEM((M,) + mshape, BF)] + sum_buffers(M, G, pshape, far=M)
        + [pltpu.VMEM((groups, M, 2, G) + pshape, BF)] + sum_buffers((groups - 1) * M, G, pshape, own=False, far=(groups - 1) * M)
        + [DMA(sems), DMA(sems), DMA((3, M)), DMA((groups - 1, M)), DMA((2,)), pltpu.VMEM((L, D), BF)],
        compiler_params=params_of(2, grid=1),
    )(lengths, packed, packed, packed, do, wide, lse, normed, p_in, p_out, p_proj, h_in, h_out, halfway)


def exit_kernel(x_hbm, dqkv_hbm, w_hbm, mid_hbm, second_ref, params_ref, parts_hbm, sums_ref, grad_hbm, qkv_ref, norms_ref,
                x_ref, dqkv_ref, w_ref, mid_ref, parts_ref, load_sems, save_sems,
                got_s, near_s, diag_s, send_s, far_s, sum_s, norm_s, e_s, small_parts, small_got,
                sends, recvs, far_recvs, small_sends, small_recvs, *, rows):
    at = Place(everyone=True)
    M = at.M
    L, D = x_ref.shape
    R = qkv_ref.shape[0]
    groups = dqkv_ref.shape[0]
    loads = [
        [pltpu.make_async_copy(dqkv_hbm.at[g], dqkv_ref.at[g], load_sems.at[g, 0]),
         pltpu.make_async_copy(w_hbm.at[:, :, pl.ds(g * 256, 256)], w_ref.at[g], load_sems.at[g, 1])]
        for g in range(groups)
    ]
    later = [pltpu.make_async_copy(parts_hbm, parts_ref, load_sems.at[0, 2]), pltpu.make_async_copy(x_hbm, x_ref, load_sems.at[1, 2]),
             pltpu.make_async_copy(mid_hbm, mid_ref, load_sems.at[2, 2])]
    for cp in loads[0] + later[:1] + [cp for group in loads[1:] for cp in group] + later[1:]:
        cp.start()
    small = SmallScatter(at, small_parts, small_got, small_sends, small_recvs)
    units = [
        SumUnit(at, lambda c, n=n: parts_ref.at[at.near[n], c], None, *[b.at[n] for b in (got_s, near_s, diag_s, send_s)], far_s, sum_s, n, n % 2,
                sends.at[n], recvs.at[n], far_recvs)
        for n in reversed(range(M))
    ]

    def run(name):
        for u in units:
            getattr(u, name)()

    gain = params_ref[0:1, :]
    plan = {0: "start", 2: "pair", 5: "cross"}

    def matmul(step, carry):
        g, i = step // 2, lax.rem(step, 2)
        for j, group in enumerate(loads):

            @pl.when(step == 2 * j)
            def _(group=group):
                for cp in group:
                    cp.wait()

        sl = pl.ds(pl.multiple_of(i * (L // 2), L // 2), L // 2)
        e = sum(dot(dqkv_ref[g, sl, t * 256 : t * 256 + 256], w_ref[g, t], NT) for t in range(3))
        e_s[sl, :] = e_s[sl, :] + e
        for j, name in plan.items():

            @pl.when(step == j)
            def _(j=j, name=name):
                if j == 0:
                    later[0].wait()
                    at.meet()
                run(name)

        return carry

    def saves(i):
        sl = pl.ds(pl.multiple_of(i * rows, rows), rows)
        return pltpu.make_async_copy(mid_ref.at[sl], grad_hbm.at[sl], save_sems.at[i])

    def norm(i, carry):
        sl = pl.ds(pl.multiple_of(i * rows, rows), rows)
        e = e_s[sl, :]
        xhat, r = norm_stats(x_ref[sl, :].astype(F32))
        mid_ref[sl, :] = mid_ref[sl, :] + norm_pull(e, xhat, r, gain)
        saves(i).start()
        norm_s[0:1, :] += jnp.sum(e * xhat, axis=0, keepdims=True)
        norm_s[2:3, :] += jnp.sum(e, axis=0, keepdims=True)
        return carry

    at.greet()
    norm_s[...] = second_ref[...]
    e_s[...] = jnp.zeros_like(e_s)
    lax.fori_loop(0, 2 * groups, matmul, 0)
    for cp in later[1:]:
        cp.wait()
    lax.fori_loop(0, L // rows, norm, 0)
    small.start(norm_s[...], R)
    run("join")
    for g in range(groups - 1):
        for t in range(3):
            qkv_ref[:, pl.ds(t * D + g * 256, 256)] = sums_ref[g, :, pl.ds(t * 256, 256)]
    norms_ref[...] = small.collect()
    run("close")
    for t in range(3):
        qkv_ref[:, pl.ds(t * D + (groups - 1) * 256, 256)] = sum_s[:, pl.ds(t * 256, 256)]
    run("finish")
    small.finish()

    def saved(i, carry):
        saves(i).wait()
        return carry

    lax.fori_loop(0, L // rows, saved, 0)


def leave(x, dqkv, w, middle_grad, second_sums, params, parts, sums):
    G, M = lax.axis_size("dp") // 2, lax.axis_size("mp")
    L, D = x.shape
    R = parts.shape[3]
    n = 2 * G * M
    sems = (M, SumUnit.count(G))
    return pl.pallas_call(
        functools.partial(exit_kernel, rows=min(256, L)),
        in_specs=[ANY] * 4 + [VMEM, VMEM, ANY, VMEM],
        out_specs=[ANY, VMEM, VMEM],
        out_shape=[
            jax.ShapeDtypeStruct((L, D), F32),
            jax.ShapeDtypeStruct((R, 3 * D), F32),
            jax.ShapeDtypeStruct((8, 128), F32),
        ],
        scratch_shapes=[
            pltpu.VMEM((L, D), BF), pltpu.VMEM(dqkv.shape, BF), pltpu.VMEM((dqkv.shape[0], 3, D, 256), BF), pltpu.VMEM((L, D), F32),
            pltpu.VMEM(parts.shape, BF), DMA((3, 3)), DMA((L // min(256, L),)),
        ] + sum_buffers(M, G, (R, D), own=False, far=M)
        + [pltpu.VMEM((R, D), F32), pltpu.VMEM((8, D), F32), pltpu.VMEM((L, D), F32), pltpu.VMEM((n, 8, 128), F32), pltpu.VMEM((n, 8, 128), F32),
           DMA(sems), DMA(sems), DMA((M,)), DMA((n,)), DMA((n,))],
        compiler_params=params_of(3),
    )(x, dqkv, w, middle_grad, second_sums, params, parts, sums)


def per_device(inputs, lengths, attn_qkv, attn_proj, mlp_in, mlp_out, norm_gain, norm_bias, cotangent):
    n_dp, n_mp = lax.axis_size("dp"), lax.axis_size("mp")
    G = n_dp // 2
    L, D = inputs.shape
    R = attn_qkv.shape[1]
    wqkv, normed, params = entry(inputs, attn_qkv[0], norm_gain[0], norm_bias[0])
    wqkv = wqkv.reshape(3, D, D)
    mixed, wide, lse, packed, wproj, land, win, wout = attend(lengths, normed, wqkv, attn_proj[0], mlp_in[0], mlp_out[0].T, min(512, L))
    pieces = lambda w: w.reshape((w.shape[0], n_dp) + w.shape[3:])
    outputs, middle_grad, mixed_grad, second_sums, p_proj, p_in, p_out, h_in, h_out, halfway = mlp(
        lengths, inputs, mixed, cotangent, params, wproj.reshape(D, D), pieces(win), pieces(wout), land, R, min(512, L))
    dqkv, d_in, d_out, d_proj, sums, parts = attend_back(
        lengths, packed, mixed_grad, wide, lse, normed, p_in, p_out, p_proj, h_in, h_out, halfway, min(256, L))
    input_grad, d_qkv, norms = leave(inputs, dqkv, wqkv, middle_grad, second_sums, params, parts, sums)
    return (
        outputs,
        input_grad,
        d_qkv[None],
        d_proj[None],
        d_in[None],
        d_out.T[None],
        norms[None, :2, :R],
        norms[None, 2:4, :R],
    )


def solution(mesh):
    everywhere = ("dp", "mp")
    wide, columns, vector = P(everywhere, None), P(None, everywhere, None), P(None, None, everywhere)
    return jax.shard_map(
        per_device,
        mesh=mesh,
        in_specs=(wide, P(everywhere), columns, columns, P(None, "dp", "mp"), P(None, "mp", "dp"), vector, vector, wide),
        out_specs=(wide, wide, columns, columns, P(None, "dp", "mp"), P(None, "mp", "dp"), vector, vector),
        check_vma=False,
    )
```

```python
import functools

import jax
import jax.numpy as jnp
from jax import lax
from jax.experimental import pallas as pl
from jax.experimental.pallas import tpu as pltpu
from jax.sharding import PartitionSpec as P

F32, BF = jnp.float32, jnp.bfloat16
MESH = pl.DeviceIdType.MESH
HEAD_DIM = 64
SCALE = 0.125
LOG2E = 1.4426950408889634
TO_LOG2 = SCALE * LOG2E
NEG = -1e30
EPS = 1e-06
NN = (((1,), (0,)), ((), ()))
NT = (((1,), (1,)), ((), ()))
TN = (((0,), (0,)), ((), ()))
VMEM_LIMIT = 60 * 2**20
ANY = pl.BlockSpec(memory_space=pl.ANY)
VMEM = pl.BlockSpec(memory_space=pltpu.VMEM)
SMEM = pl.BlockSpec(memory_space=pltpu.SMEM)
DMA = pltpu.SemaphoreType.DMA


def dot(a, b, dims):
    return lax.dot_general(a, b, dims, preferred_element_type=F32)


def params_of(collective_id=None, grid=0):
    extra = {} if collective_id is None else {"collective_id": collective_id, "has_side_effects": True}
    if grid:
        extra["dimension_semantics"] = ("arbitrary",) * grid
    return pltpu.CompilerParams(vmem_limit_bytes=VMEM_LIMIT, **extra)


class Place:
    def __init__(self, everyone=False):
        self.everyone = everyone
        n_dp, self.M = lax.axis_size("dp"), lax.axis_size("mp")
        self.G = n_dp // 2
        dp = lax.axis_index("dp")
        self.g, self.c, self.z = dp // 2, lax.rem(dp, 2), lax.axis_index("mp")
        self.square = self.G == 4
        self.near = [self.z ^ n if self.M & (self.M - 1) == 0 else lax.rem(self.z + n, self.M) for n in range(self.M)]
        if self.square:
            self.chips = [self.g ^ 1, self.g ^ 2]
            self.diag = self.g ^ 3
        else:
            self.chips = [lax.rem(self.g + d, self.G) for d in range(1, self.G)]

    def chip(self, h):
        return (h * 2 + self.c, self.z)

    def core(self):
        return (self.g * 2 + 1 - self.c, self.z)

    def along(self, z):
        return (self.g * 2 + self.c, z)

    def peers(self):
        if self.everyone:
            n = 2 * self.G * self.M
            return [self.device(lax.rem(self.index + d, n)) for d in range(1, n)]
        return [self.along(s) for s in self.near[1:]] + [self.chip(h) for h in self.chips] + [self.core()]

    @property
    def index(self):
        return (self.g * 2 + self.c) * self.M + self.z

    def device(self, i):
        return (i // self.M, lax.rem(i, self.M))

    def greet(self):
        for dev in self.peers():
            pl.semaphore_signal(pltpu.get_barrier_semaphore(), inc=1, device_id=dev, device_id_type=MESH)

    def meet(self):
        pl.semaphore_wait(pltpu.get_barrier_semaphore(), len(self.peers()))


def remote(src, dst, send, recv, dev):
    return pltpu.make_async_remote_copy(src_ref=src, dst_ref=dst, send_sem=send, recv_sem=recv, device_id=dev, device_id_type=MESH)


class Along:
    def __init__(self, at, own, land, sends, recvs):
        self.at, self.own, self.land, self.sends, self.recvs = at, own, land, sends, recvs

    def _copy(self, n, source):
        return remote(self.own, self.land(source), self.sends.at[n], self.recvs.at[source], self.at.along(self.at.near[n]))

    def start(self, *ns):
        for n in ns:
            self._copy(n, self.at.z).start()

    def pass_on(self):
        block = self.land(self.at.near[2])
        remote(block, block, self.sends.at[3], self.recvs.at[self.at.near[2]], self.at.along(self.at.near[1])).start()

    def arrive(self, n):
        self._copy(n, self.at.near[n]).wait_recv()

    def finish(self, ns=None):
        for n in range(1, self.at.M) if ns is None else ns:
            self._copy(n, self.at.z).wait_send()


class GatherUnit:
    def __init__(self, at, src, slot, way, sends, recvs, local=True):
        self.at, self.src, self.slot, self.way, self.local = at, src, slot, way, local
        self.sends, self.recvs = sends, recvs

    @staticmethod
    def count(G):
        return 1 + (3 if G == 4 else G - 1) + G

    def _local(self):
        return pltpu.make_async_copy(self.src, self.slot(self.at.g, self.at.c), self.sends.at[0])

    def _to_chip(self, i):
        at = self.at
        return remote(self.src, self.slot(at.g, at.c), self.sends.at[1 + i], self.recvs.at[1 + i], at.chip(at.chips[i]))

    def _relay(self):
        at = self.at
        block = self.slot(at.chips[self.way], at.c)
        return remote(block, block, self.sends.at[3], self.recvs.at[3], at.chip(at.chips[1 - self.way]))

    def _to_core(self, i):
        at = self.at
        h = ([at.g] + at.chips + ([at.diag] if at.square else []))[i]
        k = self.count(at.G) - at.G + i
        block = self.slot(h, at.c)
        return remote(block if i else self.src, block, self.sends.at[k], self.recvs.at[k], at.core())

    def spread(self):
        for i in range(len(self.at.chips)):
            self._to_chip(i).start()
        self._to_core(0).start()
        if self.local:
            self._local().start()

    def relay(self):
        n = len(self.at.chips)
        for i in range(n):
            self._to_chip(i).wait_recv()
        if self.at.square:
            self._relay().start()
        for i in range(n):
            self._to_core(1 + i).start()

    def last(self):
        if self.at.square:
            self._relay().wait_recv()
            self._to_core(3).start()

    def finish(self):
        if self.local:
            self._local().wait()
        for i in range(len(self.at.chips)):
            self._to_chip(i).wait_send()
        if self.at.square:
            self._relay().wait_send()
        for i in range(self.at.G):
            self._to_core(i).wait()


class SumUnit:
    def __init__(self, at, part, own, got, near, diag, out, far, total, n, way, sends, recvs, far_recvs, local=False):
        self.at, self.part, self.own, self.got, self.near, self.diagonal = at, part, own, got, near, diag
        self.out, self.far, self.total, self.n, self.way = out, far, total, n, way
        self.sends, self.recvs, self.far_recvs, self.local = sends, recvs, far_recvs, local
        self.place = at.near[n]
        self.passed = False
        self.opposite = None

    @staticmethod
    def count(G):
        return 3 + (3 if G == 4 else G)

    def _core(self):
        at = self.at
        return remote(self.part(1 - at.c), self.got, self.sends.at[0], self.recvs.at[0], at.core())

    def _local(self):
        return pltpu.make_async_copy(self.part(self.at.c), self.own, self.sends.at[2])

    def _diag(self):
        at = self.at
        return remote(self.got.at[at.diag], self.diagonal, self.sends.at[5], self.recvs.at[5], at.chip(at.chips[1 - self.way]))

    def _chip(self, i):
        at = self.at
        k = 3 + i
        return remote(self.got.at[at.chips[i]], self.near.at[i], self.sends.at[k], self.recvs.at[k], at.chip(at.chips[i]))

    def _z(self, slot):
        dev = self.at.along(self.at.near[1] if self.passed else self.place)
        return remote(self.out, self.far.at[slot], self.sends.at[1], self.far_recvs.at[slot], dev)

    def send_z(self):
        self._z(self.at.near[2] if self.passed else self.at.z).start()

    def start(self):
        self._core().start()
        if self.local:
            self._local().start()

    def launch(self):
        for i in range(len(self.at.chips)):
            self._chip(i).start()

    def pair(self, hold=False):
        at = self.at
        self._core().wait_recv()
        if self.local:
            self._local().wait()
            own = self.own
        else:
            own = self.part(at.c)

        def add(h, carry):
            self.got[h] = (self.got[h].astype(F32) + own[h].astype(F32)).astype(BF)
            return carry

        lax.fori_loop(0, at.G, add, 0)
        if at.square:
            self._diag().start()
        elif not hold:
            self.launch()

    def cross(self, hold=False):
        at = self.at
        if at.square:
            self._diag().wait_recv()
            h = at.chips[self.way]
            self.got[h] = (self.got[h].astype(F32) + self.diagonal[...].astype(F32)).astype(BF)
            if not hold:
                self.launch()

    def join(self):
        at = self.at
        value = self.got[at.g].astype(F32)
        for i in range(len(at.chips)):
            self._chip(i).wait_recv()
            value = value + self.near[i].astype(F32)
        if self.opposite is not None:
            self._z(at.near[3]).wait_recv()
            value = value + self.far[at.near[3]].astype(F32)
        if self.n:
            self.out[...] = value.astype(BF)
            self.send_z()
        else:
            self.total[...] = value

    def close(self):
        if self.n and not self.passed:
            self._z(self.place).wait_recv()
            self.total[...] += self.far[self.place].astype(F32)

    def finish(self, core=True, rest=True):
        at = self.at
        if core:
            self._core().wait_send()
            if at.square:
                self._diag().wait_send()
        if rest:
            if self.n:
                self._z(at.near[2] if self.passed else at.z).wait_send()
            for i in range(len(at.chips)):
                self._chip(i).wait_send()


def link(units):
    by_n = {u.n: u for u in units}
    if units[0].at.M == 4 and 3 in by_n:
        by_n[2].opposite = by_n[3]
        by_n[3].passed = True
    return units


def sum_buffers(n, G, shape, own=True, far=0):
    chips = 2 if G == 4 else G - 1
    block = lambda *lead: pltpu.VMEM(lead + shape, BF)
    return ([block(n, G)] if own else []) + [block(n, G), block(n, chips), block(n), block(n), block(max(far, 1))]


class SmallGather:
    def __init__(self, at, got, sends, recvs):
        self.at, self.got, self.sends, self.recvs = at, got, sends, recvs
        self.count = 2 * at.G * at.M

    def _copy(self, own, d, back):
        at = self.at
        to, other = lax.rem(at.index + d, self.count), lax.rem(at.index + self.count - d, self.count)
        return remote(own, self.got.at[other if back else at.index], self.sends.at[d], self.recvs.at[d], at.device(to))

    def start(self, own):
        def send(d, carry):
            self._copy(own, d, False).start()
            return carry

        lax.fori_loop(1, self.count, send, 0)

    def collect(self, own, R, width):
        def wait(d, carry):
            self._copy(own, d, True).wait_recv()
            return carry

        lax.fori_loop(1, self.count, wait, 0)
        self.got[self.at.index] = own[...]
        lane = lanes((own.shape[0], width))
        total = jnp.zeros((own.shape[0], width), F32)
        for i in range(self.count):
            wide = jnp.concatenate([self.got[i]] * (width // 128), axis=1)
            total = jnp.where(lane // R == i, pltpu.roll(wide, i * R % width, 1) if i else wide, total)
        return total

    def finish(self, own):
        def wait(d, carry):
            self._copy(own, d, False).wait_send()
            return carry

        lax.fori_loop(1, self.count, wait, 0)


class SmallScatter:
    def __init__(self, at, parts, got, sends, recvs):
        self.at, self.parts, self.got, self.sends, self.recvs = at, parts, got, sends, recvs
        self.count = 2 * at.G * at.M

    def _copy(self, d, back):
        at = self.at
        to, other = lax.rem(at.index + d, self.count), lax.rem(at.index + self.count - d, self.count)
        return remote(self.parts.at[to], self.got.at[other if back else at.index], self.sends.at[d], self.recvs.at[d], at.device(to))

    def start(self, value, R):
        for i in range(self.count):
            self.parts[i] = (pltpu.roll(value, value.shape[1] - i * R, 1) if i else value)[:, :128]

        def send(d, carry):
            self._copy(d, False).start()
            return carry

        lax.fori_loop(1, self.count, send, 0)

    def collect(self):
        def add(d, value):
            self._copy(d, True).wait_recv()
            return value + self.got[lax.rem(self.at.index + self.count - d, self.count)]

        return lax.fori_loop(1, self.count, add, self.parts[self.at.index])

    def finish(self):
        def wait(d, carry):
            self._copy(d, False).wait_send()
            return carry

        lax.fori_loop(1, self.count, wait, 0)


def norm_stats(v):
    centre = v - jnp.mean(v, axis=-1, keepdims=True)
    r = lax.rsqrt(jnp.mean(centre * centre, axis=-1, keepdims=True) + EPS)
    return centre * r, r


def norm_pull(e, xhat, r, g):
    y = e * g
    return r * (y - jnp.mean(y, axis=-1, keepdims=True) - xhat * jnp.mean(y * xhat, axis=-1, keepdims=True))


def entry_kernel(x_ref, block_ref, gain_ref, bias_ref, w_ref, normed_ref, params_ref, shard_ref, own_ref, got, chain_sends, chain_recvs, sends, recvs,
                 small_sends, small_recvs, *, rows):
    at = Place(everyone=True)
    at.greet()
    land = lambda s: w_ref.at[:, at.g, at.c, s]
    chain = Along(at, shard_ref, land, chain_sends, chain_recvs)
    units = [
        GatherUnit(at, land(at.near[n]) if n else shard_ref, lambda g, c, n=n: w_ref.at[:, g, c, at.near[n]], n % 2, sends.at[n], recvs.at[n], n == 0)
        for n in range(at.M)
    ]
    small = SmallGather(at, got, small_sends, small_recvs)
    L, D = x_ref.shape
    R = block_ref.shape[0]
    for t in range(3):
        shard_ref[t] = block_ref[:, pl.ds(t * D, D)]
    own_ref[...] = jnp.zeros_like(own_ref)
    own_ref[0:2, 0:R] = gain_ref[...].astype(F32)
    own_ref[2:4, 0:R] = bias_ref[...].astype(F32)
    at.meet()
    chain.start(1)
    units[0].spread()
    chain.start(*range(2, 3 if at.M == 4 else at.M))
    small.start(own_ref)

    def norm(i, carry):
        sl = pl.ds(pl.multiple_of(i * rows, rows), rows)
        xhat, _ = norm_stats(x_ref[sl, :].astype(F32))
        normed_ref[sl, :] = (xhat * params_ref[0:1, :] + params_ref[2:3, :]).astype(BF)
        return carry

    steps = L // rows
    for n in range(1, at.M):
        chain.arrive(n)
        if at.M == 4 and n == 2:
            chain.pass_on()
        units[n].spread()
        units[n - 1].relay()
        if n > 1:
            units[n - 2].last()
    params_ref[...] = small.collect(own_ref, R, D)
    lax.fori_loop(0, steps // 2, norm, 0)
    units[-1].relay()
    if at.M > 1:
        units[-2].last()
    lax.fori_loop(steps // 2, steps, norm, 0)
    units[-1].last()
    for u in units:
        u.finish()
    chain.finish()
    small.finish(own_ref)


def entry(x, block, gain, bias):
    G, M = lax.axis_size("dp") // 2, lax.axis_size("mp")
    L, D = x.shape
    R = block.shape[0]
    n = 2 * G * M
    sems = (M, GatherUnit.count(G))
    return pl.pallas_call(
        functools.partial(entry_kernel, rows=min(256, L)),
        in_specs=[VMEM] * 4,
        out_specs=[ANY, VMEM, VMEM],
        out_shape=[
            jax.ShapeDtypeStruct((3, G, 2, M, R, D), BF),
            jax.ShapeDtypeStruct((L, D), BF),
            jax.ShapeDtypeStruct((8, D), F32),
        ],
        scratch_shapes=[pltpu.VMEM((3, R, D), BF), pltpu.VMEM((8, 128), F32), pltpu.VMEM((n, 8, 128), F32), DMA((M + 1,)), DMA((M,)), DMA(sems), DMA(sems), DMA((n,)), DMA((n,))],
        compiler_params=params_of(0),
    )(x, block, gain, bias)


def lanes(shape):
    return lax.broadcasted_iota(jnp.int32, shape, len(shape) - 1)


def three_parts(x):
    hi = x.astype(BF)
    rest = x - hi.astype(F32)
    mid = rest.astype(BF)
    return hi, mid, (rest - mid.astype(F32)).astype(BF)


def mask_bias(shape, length):
    return jnp.where(lax.broadcasted_iota(jnp.int32, shape, 0) < length, 0.0, NEG).astype(BF)


def attend_step(p, len_ref, q_ref, k_ref, v_ref, o_ref, wide_ref, lse_ref, tq, between):
    L = q_ref.shape[0]
    lane = lanes((L, 128))
    k, v = k_ref[...], v_ref[...]
    bias = mask_bias((L, 128), len_ref[0])
    zero, one = jnp.zeros((L, 128), BF), jnp.ones((L, 128), BF)

    @pl.when(p == 0)
    def _():
        lse_ref[...] = jnp.zeros_like(lse_ref)

    keys, values = [], []
    for h in range(2):
        mine = (lane < 64) if h == 0 else (lane >= 64)
        spare = 64 * (1 - h)
        keys.append(jnp.where(mine, k, jnp.where(lane == spare, bias, zero)))
        values.append(jnp.where(mine, v, jnp.where(lane == spare, one, zero)))
    lq = lanes((tq, 128))
    for i in range(L // tq):
        between(i)
        sl = pl.ds(i * tq, tq)
        q = q_ref[sl, :]
        outs, sums = [], []
        for h in range(2):
            mine = (lq < 64) if h == 0 else (lq >= 64)
            spare = 64 * (1 - h)
            q_h = jnp.where(mine, q, jnp.where(lq == spare, jnp.ones((tq, 128), BF), jnp.zeros((tq, 128), BF)))
            s = dot(q_h, keys[h], NT)
            top = jnp.max(s, axis=1, keepdims=True) * TO_LOG2
            e = jnp.exp2(s * TO_LOG2 - top)
            o = dot(e.astype(BF), values[h], NN)
            total = o[:, spare : spare + 1]
            outs.append(o / total)
            sums.append(top + jnp.log2(total))
        out = jnp.where(lq < 64, outs[0], outs[1])
        wide_ref[sl, :] = out
        o_ref[sl, :] = out.astype(BF)
        lse = lse_ref[sl, :]
        lse = jnp.where(lq == 2 * p, sums[0], lse)
        lse_ref[sl, :] = jnp.where(lq == 2 * p + 1, sums[1], lse)


def attend_back_step(p, len_ref, q_ref, k_ref, v_ref, do_ref, wide_ref, lse_ref, dq_ref, dk_ref, dv_ref, tq, between):
    L = q_ref.shape[0]
    lane = lanes((L, 128))
    k, v = k_ref[...], v_ref[...]
    bias = mask_bias((L, 128), len_ref[0])
    zero, one = jnp.zeros((L, 128), BF), jnp.ones((L, 128), BF)
    keys, values = [], []
    for h in range(2):
        mine = (lane < 64) if h == 0 else (lane >= 64)
        b = 64 * (1 - h)
        ones = jnp.where((lane > b) & (lane < b + 4), one, zero)
        keys.append(jnp.where(mine, k, jnp.where(lane == b, bias, ones)))
        values.append(jnp.where(mine, v, ones))
    lq = lanes((tq, 128))
    dk, dv = [jnp.zeros((L, 128), F32)] * 2, [jnp.zeros((L, 128), F32)] * 2
    for i in range(L // tq):
        between(i)
        sl = pl.ds(i * tq, tq)
        q, do, lse = q_ref[sl, :], do_ref[sl, :], lse_ref[sl, :]
        product = wide_ref[sl, :] * do.astype(F32)
        dq = []
        for h in range(2):
            mine = (lq < 64) if h == 0 else (lq >= 64)
            b = 64 * (1 - h)
            minus_delta = -jnp.sum(jnp.where(mine, product, 0.0), axis=1, keepdims=True)
            minus_lse = -jnp.sum(jnp.where(lq == 2 * p + h, lse, 0.0), axis=1, keepdims=True) * (1.0 / TO_LOG2)

            def with_spare(x, term, first):
                hi, mid, lo = three_parts(jnp.broadcast_to(term, (tq, 128)))
                low = jnp.where(lq == b + 2, mid, jnp.where(lq == b + 3, lo, jnp.zeros((tq, 128), BF)))
                low = jnp.where(lq == b, jnp.full((tq, 128), first, BF), jnp.where(lq == b + 1, hi, low))
                return jnp.where(mine, x, low)

            st = dot(keys[h], with_spare(q, minus_lse, 1.0), NT)
            pt = jnp.exp2(st * TO_LOG2)
            dpt = dot(values[h], with_spare(do, minus_delta, 0.0), NT)
            ds = (pt * dpt).astype(BF)
            dv[h] = dv[h] + dot(pt.astype(BF), do, NN)
            dk[h] = dk[h] + dot(ds, q, NN)
            dq.append(dot(ds, k, TN))
        dq_ref[sl, :] = (jnp.where(lq < 64, dq[0], dq[1]) * SCALE).astype(BF)
    dk_ref[...] = (jnp.where(lane < 64, dk[0], dk[1]) * SCALE).astype(BF)
    dv_ref[...] = jnp.where(lane < 64, dv[0], dv[1]).astype(BF)


def at_slots(p, per_step, plan):
    def between(i):
        for slot, actions in sorted(plan.items()):
            if slot % per_step == i:

                @pl.when(p == slot // per_step)
                def _(actions=actions):
                    for action in actions:
                        action()

    return between


def attend_kernel(len_ref, x_ref, w_ref, proj_ref, in_ref, out_ref, o_ref, wide_ref, lse_ref, packed_ref, wproj_ref, land_ref, win_ref, wout_ref,
                  w_s, w_sem, packed_s, save_sem, pchain_sends, pchain_recvs, chain_sends, chain_recvs, sends, recvs, *, tq):
    p, steps = pl.program_id(0), pl.num_programs(0)
    at = Place()
    M = at.M
    half = M // 2
    D = x_ref.shape[1]
    parts = x_ref.shape[0] // tq
    land = [lambda s, a=a: land_ref.at[s, a] for a in range(2)]
    own = (in_ref, out_ref)
    direct = [n for n in range(1, M) if M != 4 or n < 3]
    pland = lambda s: wproj_ref.at[at.g, at.c, s]
    pchain = Along(at, proj_ref, pland, pchain_sends, pchain_recvs)
    chains = [Along(at, own[a], land[a], chain_sends.at[a], chain_recvs.at[a]) for a in range(2)]
    main = [
        [GatherUnit(at, land[a](at.near[n]) if n else own[a], lambda g, c, n=n, ref=ref: ref.at[n, g, c], a, sends.at[2 * n + a], recvs.at[2 * n + a])
         for a, ref in enumerate((win_ref, wout_ref))]
        for n in range(half)
    ]
    proj = [
        GatherUnit(at, pland(at.near[n]) if n else proj_ref, lambda g, c, n=n: wproj_ref.at[g, c, at.near[n]], n % 2,
                   sends.at[2 * half + n], recvs.at[2 * half + n], n == 0)
        for n in range(M)
    ]
    own_land = [pltpu.make_async_copy(own[a], land_ref.at[at.z, a], save_sem.at[1 + a]) for a in range(2)]
    save = pltpu.make_async_copy(packed_s, packed_ref, save_sem.at[0])

    loads = [pltpu.make_async_copy(w_ref.at[t], w_s.at[t], w_sem.at[t]) for t in range(3)]

    def third(t):
        loads[t].wait()
        packed_s[:, pl.ds(t * D, D)] = dot(x_ref[...], w_s[t], NN).astype(BF)

    @pl.when(p == 0)
    def _():
        for cp in loads:
            cp.start()
        at.greet()
        third(0)
        at.meet()
        pchain.start(*range(1, M))
        for n in direct:
            for chain in chains:
                chain.start(n)
        proj[0].spread()
        for u in main[0]:
            u.spread()
        for cp in own_land:
            cp.start()
        third(1)
        third(2)
        save.start()

    plan = {}

    def put(slot, *actions):
        plan.setdefault(min(slot, ATTEND_STEPS * parts - 1), []).extend(actions)

    def arrive(chain, n, unit=None):
        def act():
            chain.arrive(n)
            if unit is not None:
                unit.spread()

        return act

    for n in range(M):
        arrives, relays, lasts = ATTEND_PROJ[min(n, 3)]
        put(relays, proj[n].relay)
        put(lasts, proj[n].last)
        if n:
            put(arrives, arrive(pchain, n, proj[n]))
    for n in range(half):
        for a in range(2):
            arrives, relays, lasts = ATTEND_MAIN[min(n, 1)][a]
            if n:
                put(arrives, arrive(chains[a], n, main[n][a]))
            put(relays, main[n][a].relay)
            put(lasts, main[n][a].last)
    lane = pl.multiple_of(p * 128, 128)
    column = lambda t: packed_s.at[:, pl.ds(t * D + lane, 128)]
    attend_step(p, len_ref, column(0), column(1), column(2), o_ref, wide_ref, lse_ref, tq, at_slots(p, parts, plan))

    @pl.when(p == steps - 1)
    def _():
        for n in direct[half - 1 :]:
            for chain in chains:
                chain.arrive(n)
        for group in main + [proj, [pchain]]:
            for u in group:
                u.finish()
        for chain in chains:
            chain.finish(direct)
        save.wait()
        for cp in own_land:
            cp.wait()


ATTEND_STEPS = 6
ATTEND_PROJ = [[0, 0, 4], [0, 4, 6], [4, 6, 8], [6, 8, 10]]
ATTEND_MAIN = [[[0, 4, 8], [0, 4, 8]], [[2, 8, 10], [4, 8, 10]]]
BACK = {"pair0": 1, "pair1": 1, "pair_p": 1, "cross1": 2, "pair_h0": 3, "cross_p": 3, "join0": 3, "pair_h1": 4, "join_p": 4, "cross_h1": 5, "late_p": 5, "join_h0": 5}
MLP = {"relay0": (0, 2), "spread1": (0, 2), "relay1": (2, 0), "last0": (1, 2), "last1": (2, 2), "pair0": (1, 2), "cross0": (2, 2), "pair1": (3, 0), "join0": (3, 2)}


def attend(lengths, x, w, proj, w_in, w_out, tq):
    G, M = lax.axis_size("dp") // 2, lax.axis_size("mp")
    L, D = x.shape
    half = M // 2
    column = pl.BlockSpec((L, 128), lambda p: (0, p))
    whole = lambda shape: pl.BlockSpec(shape, lambda p: (0,) * len(shape), pipeline_mode=pl.Buffered(1))
    sems = (2 * half + M, GatherUnit.count(G))
    weights = jax.ShapeDtypeStruct((half, G, 2) + w_in.shape, BF)
    return pl.pallas_call(
        functools.partial(attend_kernel, tq=tq),
        grid=(D // 128,),
        in_specs=[SMEM, whole(x.shape), ANY, ANY, ANY, ANY],
        out_specs=[column, column, pl.BlockSpec((L, 128), lambda p: (0, 0)), ANY, ANY, ANY, ANY, ANY],
        out_shape=[
            jax.ShapeDtypeStruct((L, D), BF),
            jax.ShapeDtypeStruct((L, D), F32),
            jax.ShapeDtypeStruct((L, 128), F32),
            jax.ShapeDtypeStruct((L, 3 * D), BF),
            jax.ShapeDtypeStruct((G, 2, M) + proj.shape, BF),
            jax.ShapeDtypeStruct((M, 2) + w_in.shape, BF),
            weights, weights,
        ],
        scratch_shapes=[pltpu.VMEM(w.shape, BF), DMA((3,)), pltpu.VMEM((L, 3 * D), BF), DMA((3,)), DMA((M + 1,)), DMA((M,)), DMA((2, M + 1)), DMA((2, M)), DMA(sems), DMA(sems)],
        compiler_params=params_of(1, grid=1),
    )(lengths, x, w, proj, w_in, w_out)


def gelu_and_slope(x):
    phi = 0.5 + 0.5 * lax.erf(x * 0.7071067811865476)
    return x * phi, phi + x * (jnp.exp2((x * x) * (-0.5 * LOG2E)) * 0.3989422804014327)


def mlp_kernel(len_ref, x_hbm, mixed_hbm, cot_hbm, params_ref, wproj_hbm, win_ref, wout_ref, land_ref,
               y_hbm, mgrad_hbm, dmixed_hbm, sums_ref, pproj_ref, pin_ref, pout_ref, din_ref, dout_ref, half_ref,
               x_ref, mixed_ref, cot_ref, wproj_ref, in_sems, out_sems, w_s, mid_s, hid_s, sg_s, sec_s, br_s, act_s, eg_s, got_s, near_s, diag_s, last_s, hand_sems,
               load_sems, save_sems, gsends, grecvs, ssends, srecvs, *, tr):
    at = Place()
    G, M = at.G, at.M
    L, D = x_ref.shape
    n_rows = L // tr
    enter_loads = [
        [pltpu.make_async_copy(src.at[pl.ds(i * tr, tr)], dst.at[pl.ds(i * tr, tr)], in_sems.at[i, j])
         for j, (src, dst) in enumerate(((mixed_hbm, mixed_ref), (x_hbm, x_ref), (cot_hbm, cot_ref)))]
        for i in range(n_rows)
    ]
    proj_load = pltpu.make_async_copy(wproj_hbm, wproj_ref, in_sems.at[0, 3])
    proj_load.start()
    for group in enter_loads:
        for cp in group:
            cp.start()
    R, Fb = land_ref.shape[2:]
    half = M // 2
    gain, bias = params_ref[1:2, :], params_ref[3:4, :]
    loads = [pltpu.make_async_copy((win_ref, wout_ref)[a].at[k], w_s.at[k, a], load_sems.at[k, a]) for k in range(half) for a in range(2)]
    for cp in loads:
        cp.start()
    at.greet()
    gathers = [
        [GatherUnit(at, last_s.at[a] if M == 4 and k == 3 else land_ref.at[at.near[k], a], lambda g, c, k=k, a=a: w_s.at[k, a, g * 2 + c], a, gsends.at[k - half, a], grecvs.at[k - half, a])
         for a in range(2)]
        for k in range(half, M)
    ]
    sums = [
        [SumUnit(at, lambda c, k=k, a=a: w_s.at[k, a, pl.ds(c * G, G)], None, *[b.at[2 * k + a] for b in (got_s, near_s, diag_s)], None,
                 None, total, k, a, ssends.at[2 * k + a], srecvs.at[2 * k + a], None)
         for a, total in enumerate((din_ref, dout_ref))]
        for k in range(2)
    ]

    hand = [remote(land_ref.at[at.near[2], a], last_s.at[a], hand_sems.at[0, a], hand_sems.at[1, a], at.along(at.near[1])) for a in range(2)] if M == 4 else []

    def rows(i):
        return pl.ds(i * tr, tr)

    def enter(i):
        if i == 0:
            proj_load.wait()
        for cp in enter_loads[i]:
            cp.wait()
        sl = rows(i)
        mid = x_ref[sl, :].astype(F32) + dot(mixed_ref[sl, :], wproj_ref[...], NN)
        mid_s[sl, :] = mid
        hid_s[sl, :] = mid
        sec_s[sl, :] = (norm_stats(mid)[0] * gain + bias).astype(BF)
        at_row = lax.broadcasted_iota(jnp.int32, (tr, D), 0) + i * tr
        br_s[sl, :] = jnp.where(at_row < len_ref[0], cot_ref[sl, :].astype(F32), 0.0).astype(BF)
        sg_s[sl, :] = jnp.zeros((tr, D), F32)

    enter(0)
    at.meet()
    for cp in hand:
        cp.start()
    for n, group in enumerate(gathers):
        for u in group:
            if n == 0 or not hand:
                u.spread()
    for i in range(1, n_rows):
        enter(i)
    for cp in loads:
        cp.wait()
    per = n_rows + 2
    plan = {}

    def put(k, i, name, group):
        plan.setdefault((min(k, M - 1), min(i, per - 1)), []).extend(getattr(u, name) for u in group)

    for n, group in enumerate(gathers):
        after = lambda name: (MLP[name + "0"] if n == 0 else (MLP[name + "1"][0] + n - 1, MLP[name + "1"][1]))
        put(*after("relay"), "relay", group)
        if n and hand:
            plan.setdefault(MLP["spread1"], []).extend([cp.wait_recv for cp in hand])
            put(*MLP["spread1"], "spread", group)
        put(*after("last"), "last", group)
        put(half + n, 0, "finish", group)
    put(1, 0, "start", sums[0])
    put(*MLP["pair0"], "pair", sums[0])
    put(2, 0, "start", sums[1])
    put(*MLP["cross0"], "cross", sums[0])
    plan.setdefault(MLP["pair1"], []).extend(functools.partial(u.pair, True) for u in sums[1])
    put(*MLP["join0"], "join", sums[0])

    def block(k, carry):
        def between(i):
            for (at_k, at_i), actions in sorted(plan.items(), key=lambda item: item[0]):
                if at_i == i:

                    @pl.when(k == at_k)
                    def _(actions=actions):
                        for action in actions:
                            action()

        between(0)
        win, wout = (w_s[k, a].reshape(D, Fb) for a in range(2))
        for i in range(n_rows):
            if i:
                between(i)
            sl = rows(i)
            value, slope = gelu_and_slope(dot(sec_s[sl, :], win, NN))
            act = value.astype(BF)
            eg = (dot(br_s[sl, :], wout, NN) * slope).astype(BF)
            act_s[sl, :], eg_s[sl, :] = act, eg
            hid_s[sl, :] += dot(act, wout, NT)
            sg_s[sl, :] += dot(eg, win, NT)
        for a, (left, right) in enumerate(((sec_s, eg_s), (br_s, act_s))):
            between(n_rows + a)
            grad = dot(left[...], right[...], TN)
            for g in range(G):
                for c in range(2):
                    row = (g * 2 + c) * R
                    w_s[k, a, c * G + g] = grad[row : row + R, :].astype(BF)

        @pl.when(k > 1)
        def _():
            for a, ref in enumerate((pin_ref, pout_ref)):
                pltpu.make_async_copy(w_s.at[k, a], ref.at[k - 2], save_sems.at[k - 2, a]).start()

        return carry

    lax.fori_loop(0, M, block, 0)
    sums_ref[...] = jnp.zeros_like(sums_ref)
    n_back = L // 256 if L % 256 == 0 else 1
    tb = L // n_back

    def saves(i):
        sl = pl.ds(pl.multiple_of(i * tb, tb), tb)
        return [pltpu.make_async_copy(src.at[sl], dst.at[sl], out_sems.at[i, j])
                for j, (src, dst) in enumerate(((x_ref, y_hbm), (mid_s, mgrad_hbm), (cot_ref, dmixed_hbm)))]

    def back(i, carry):
        sl = pl.ds(pl.multiple_of(i * tb, tb), tb)
        x_ref[sl, :] = hid_s[sl, :].astype(BF)
        xhat, r = norm_stats(mid_s[sl, :])
        e = sg_s[sl, :]
        sums_ref[1:2, :] += jnp.sum(e * xhat, axis=0, keepdims=True)
        sums_ref[3:4, :] += jnp.sum(e, axis=0, keepdims=True)
        grad = br_s[sl, :].astype(F32) + norm_pull(e, xhat, r, gain)
        mid_s[sl, :] = grad
        low = grad.astype(BF)
        sec_s[sl, :] = low
        cot_ref[sl, :] = dot(low, wproj_ref[...], NT).astype(BF)
        for cp in saves(i):
            cp.start()
        return carry

    lax.fori_loop(0, n_back, back, 0)
    for u in sums[1]:
        u.cross(True)
    save_half = pltpu.make_async_copy(got_s.at[pl.ds(2, 2)], half_ref, load_sems.at[0, 0])
    save_half.start()
    grad = dot(mixed_ref[...], sec_s[...], TN)
    R_p = pproj_ref.shape[3]
    for g in range(G):
        for c in range(2):
            for z in range(M):
                row = ((g * 2 + c) * M + z) * R_p
                pproj_ref[z, c, g] = grad[row : row + R_p, :].astype(BF)
    for k in range(2, M):
        for a, ref in enumerate((pin_ref, pout_ref)):
            pltpu.make_async_copy(w_s.at[k, a], ref.at[k - 2], save_sems.at[k - 2, a]).wait()
    save_half.wait()

    def saved(i, carry):
        for cp in saves(i):
            cp.wait()
        return carry

    lax.fori_loop(0, n_back, saved, 0)
    for k, group in enumerate(sums):
        for u in group:
            u.finish(True, k == 0)
    for cp in hand:
        cp.wait_send()


def mlp(lengths, x, mixed, cot, params, wproj, win, wout, land, R_p, tr):
    G, M = lax.axis_size("dp") // 2, lax.axis_size("mp")
    half = M // 2
    L, D = x.shape
    R, Fb = block = land.shape[2:]
    gsems, ssems = (M - half, 2, GatherUnit.count(G)), (4, SumUnit.count(G))
    pieces = jax.ShapeDtypeStruct((M - 2, 2 * G) + block, BF)
    return pl.pallas_call(
        functools.partial(mlp_kernel, tr=tr),
        in_specs=[SMEM, ANY, ANY, ANY, VMEM, ANY, ANY, ANY, ANY],
        out_specs=[ANY] * 3 + [VMEM] * 2 + [ANY, ANY, VMEM, VMEM, ANY],
        out_shape=[
            jax.ShapeDtypeStruct((L, D), BF),
            jax.ShapeDtypeStruct((L, D), F32),
            jax.ShapeDtypeStruct((L, D), BF),
            jax.ShapeDtypeStruct(params.shape, F32),
            jax.ShapeDtypeStruct((M, 2, G, R_p, D), BF),
            pieces, pieces,
            jax.ShapeDtypeStruct(block, F32), jax.ShapeDtypeStruct(block, F32), jax.ShapeDtypeStruct((2, G) + block, BF),
        ],
        scratch_shapes=[
            pltpu.VMEM((L, D), BF), pltpu.VMEM((L, D), BF), pltpu.VMEM((L, D), BF), pltpu.VMEM((D, D), BF),
            DMA((L // tr, 4)), DMA((L // 256 if L % 256 == 0 else 1, 3)),
            pltpu.VMEM((M, 2, 2 * G) + block, BF),
            pltpu.VMEM((L, D), F32), pltpu.VMEM((L, D), F32), pltpu.VMEM((L, D), F32),
            pltpu.VMEM((L, D), BF), pltpu.VMEM((L, D), BF), pltpu.VMEM((L, Fb), BF), pltpu.VMEM((L, Fb), BF),
        ] + sum_buffers(4, G, block, own=False)[:3] + [pltpu.VMEM((2,) + block, BF), DMA((2, 2)), DMA((half, 2)), DMA((M - 2, 2)), DMA(gsems), DMA(gsems), DMA(ssems), DMA(ssems)],
        compiler_params=params_of(4),
    )(lengths, x, mixed, cot, params, wproj, win, wout, land)


def attend_back_kernel(len_ref, q_ref, k_ref, v_ref, do_ref, wide_ref, lse_ref, normed_hbm, pin_ref, pout_ref, pproj_ref, hin_ref, hout_ref, half_ref,
                       dqkv_ref, din_ref, dout_ref, dproj_ref, sum_ref, rest_ref,
                       own_m, got_m, near_m, diag_m, send_m, far_in, far_out, own_p, got_p, near_p, diag_p, send_p, far_p,
                       parts_s, got_q, near_q, diag_q, send_q, far_q, sends, recvs, far_recvs, far_recvs_q, save_sem, normed_ref, *, tq):
    p, steps = pl.program_id(0), ATTEND_STEPS
    at = Place()
    G, M = at.G, at.M
    parts = q_ref.shape[0] // tq
    R = sum_ref.shape[1]
    units = []

    def add(part, bufs, far, total, n, way, recv, local=True):
        k = len(units)
        units.append(SumUnit(at, part, *bufs, far, total, n, way, sends.at[k], recvs.at[k], recv, local=local))
        return units[-1]

    def block(n):
        made = []
        for a, (ref, far, total) in enumerate(((pin_ref, far_in, din_ref), (pout_ref, far_out, dout_ref))):
            k = 2 * (n - 1) + a
            near, diag, out = [b.at[k] for b in (near_m, diag_m, send_m)]
            own, got = (None, half_ref.at[a]) if n == 1 else (own_m.at[k - 2], got_m.at[k - 2])
            made.append(add(lambda c, ref=ref: ref.at[n - 2, pl.ds(c * G, G)], (own, got, near, diag, out), far, total, n, a, far_recvs.at[a]))
        return made

    main = {n: block(n) for n in range(1, M)}
    for a in range(2):
        link([main[n][a] for n in main])
    proj = {}
    for n in reversed(range(M)):
        proj[n] = add(lambda c, n=n: pproj_ref.at[at.near[n], c], [b.at[n] for b in (own_p, got_p, near_p, diag_p, send_p)],
                      far_p, dproj_ref, n, n % 2, far_recvs.at[2])
    heads = []
    for t in range(steps // 2 - 1):
        heads.append({})
        for n in reversed(range(M)):
            heads[t][n] = add(lambda c, t=t, n=n: parts_s.at[t, at.near[n], c], [None] + [b.at[t * M + n] for b in (got_q, near_q, diag_q, send_q)],
                              far_q.at[pl.ds(t * M, M)], sum_ref.at[t], n, (n + t) % 2, far_recvs_q.at[t], False)
    for group in [proj] + heads:
        link(list(group.values()))
    every = lambda group: list(group.values())
    early = lambda group: [group[n] for n in group if n != 2]
    late = lambda group: [group[n] for n in group if n == 2]
    plan = {}

    def put(step, name, group):
        plan.setdefault(step * parts, []).extend(getattr(u, name) for u in group)

    load = pltpu.make_async_copy(normed_hbm, normed_ref, save_sem.at[1])
    pl.when(p == 0)(load.start)
    pl.when(p == 1)(load.wait)

    def begin():
        din_ref[...], dout_ref[...] = hin_ref[...], hout_ref[...]

    plan[0] = [at.greet, begin, at.meet]
    put(0, "launch", main[1])
    others = [main[n] for n in reversed(range(2, M))]
    for group in others + [every(proj)]:
        put(0, "start", group)
    for n, group in enumerate(others):
        put(BACK["pair0"] if n == 0 else BACK["pair1"], "pair", group)
        if n != 1:
            put(BACK["join0"], "join", group)
    put(BACK["pair_p"], "pair", every(proj))
    for group in others[1:]:
        put(BACK["cross1"], "cross", group)
    put(BACK["pair_h0"], "pair", every(heads[0]))
    put(BACK["cross_p"], "cross", every(proj))
    put(BACK["join_p"], "join", early(proj))
    put(BACK["pair_h1"], "pair", every(heads[1]))
    put(BACK["cross_h1"], "cross", every(heads[1]))
    put(BACK["late_p"], "join", late(proj))
    put(BACK["join_h0"], "join", early(heads[0]))
    grad_to = lambda t: dqkv_ref.at[0, :, pl.ds(pl.multiple_of(t * 256 + lax.rem(p, 2) * 128, 128), 128)]
    attend_back_step(p, len_ref, q_ref, k_ref, v_ref, do_ref, wide_ref, lse_ref, grad_to(0), grad_to(1), grad_to(2), tq, at_slots(p, parts, plan))

    @pl.when(p == 1)
    def _():
        for u in others[0]:
            u.cross()
        for u in main[1]:
            u.join()

    @pl.when(p == 3)
    def _():
        for u in every(heads[0]):
            u.cross()

    @pl.when(p == steps - 1)
    def _():
        for u in late(heads[0]) + early(heads[1]):
            u.join()

    @pl.when(lax.rem(p, 2) == 1)
    def _():
        t = p // 2
        grad = dot(normed_ref[...], dqkv_ref[0], TN)
        for g in range(G):
            for c in range(2):
                for z in range(M):
                    k = ((g * 2 + c) * M + z) * R
                    parts_s[t, z, c, g] = grad[k : k + R, :].astype(BF)

    save = pltpu.make_async_copy(parts_s.at[steps // 2 - 1], rest_ref, save_sem.at[0])
    for t, group in enumerate(heads):

        @pl.when(p == 2 * t + 1)
        def _(group=group):
            for u in every(group):
                u.start()

    @pl.when(p == 3)
    def _():
        for u in others[1] if len(others) > 1 else []:
            u.join()

    @pl.when(p == steps - 1)
    def _():
        save.start()
        for u in late(heads[1]):
            u.join()
        for u in units:
            u.close()
        for u in units:
            u.finish(u not in main[1], True)
        save.wait()


def attend_back(lengths, packed, do, wide, lse, normed, p_in, p_out, p_proj, h_in, h_out, halfway, tq):
    G, M = lax.axis_size("dp") // 2, lax.axis_size("mp")
    L, D = do.shape
    pairs = D // 128
    column = lambda off: pl.BlockSpec((L, 128), lambda p, off=off: (0, off + p))
    whole = lambda shape: pl.BlockSpec(shape, lambda p: (0,) * len(shape), pipeline_mode=pl.Buffered(1))
    out = lambda shape: pl.BlockSpec(shape, lambda p: (0,) * len(shape))
    mshape, pshape = h_in.shape, p_proj.shape[3:]
    groups = pairs // 2
    rest = 2 * (M - 1)
    sems = (rest + groups * M, SumUnit.count(G))
    return pl.pallas_call(
        functools.partial(attend_back_kernel, tq=tq),
        grid=(pairs,),
        in_specs=[SMEM, column(0), column(pairs), column(2 * pairs), column(0), column(0), whole((L, 128)), ANY, ANY, ANY, ANY,
                  whole(mshape), whole(mshape), whole(halfway.shape)],
        out_specs=[pl.BlockSpec((1, L, 768), lambda p: (p // 2, 0, 0)), out(mshape), out(mshape), out(pshape), out((groups - 1,) + pshape), ANY],
        out_shape=[jax.ShapeDtypeStruct((groups, L, 768), BF)]
        + [jax.ShapeDtypeStruct(mshape, F32)] * 2
        + [jax.ShapeDtypeStruct(pshape, F32), jax.ShapeDtypeStruct((groups - 1,) + pshape, F32), jax.ShapeDtypeStruct((M, 2, G) + pshape, BF)],
        scratch_shapes=sum_buffers(rest - 2, G, mshape)[:2] + sum_buffers(rest, G, mshape, far=M)[2:] + [pltpu.VMEM((M,) + mshape, BF)] + sum_buffers(M, G, pshape, far=M)
        + [pltpu.VMEM((groups, M, 2, G) + pshape, BF)] + sum_buffers((groups - 1) * M, G, pshape, own=False, far=(groups - 1) * M)
        + [DMA(sems), DMA(sems), DMA((3, M)), DMA((groups - 1, M)), DMA((2,)), pltpu.VMEM((L, D), BF)],
        compiler_params=params_of(2, grid=1),
    )(lengths, packed, packed, packed, do, wide, lse, normed, p_in, p_out, p_proj, h_in, h_out, halfway)


def exit_kernel(x_hbm, dqkv_hbm, w_hbm, mid_hbm, second_ref, params_ref, parts_hbm, sums_ref, grad_hbm, qkv_ref, norms_ref,
                x_ref, dqkv_ref, w_ref, mid_ref, parts_ref, load_sems, save_sems,
                got_s, near_s, diag_s, send_s, far_s, sum_s, norm_s, e_s, small_parts, small_got,
                sends, recvs, far_recvs, small_sends, small_recvs, *, rows):
    at = Place(everyone=True)
    M = at.M
    L, D = x_ref.shape
    R = qkv_ref.shape[0]
    groups = dqkv_ref.shape[0]
    loads = [
        [pltpu.make_async_copy(dqkv_hbm.at[g], dqkv_ref.at[g], load_sems.at[g, 0]),
         pltpu.make_async_copy(w_hbm.at[:, :, pl.ds(g * 256, 256)], w_ref.at[g], load_sems.at[g, 1])]
        for g in range(groups)
    ]
    later = [pltpu.make_async_copy(parts_hbm, parts_ref, load_sems.at[0, 2]), pltpu.make_async_copy(x_hbm, x_ref, load_sems.at[1, 2]),
             pltpu.make_async_copy(mid_hbm, mid_ref, load_sems.at[2, 2])]
    for cp in loads[0] + later[:1] + [cp for group in loads[1:] for cp in group] + later[1:]:
        cp.start()
    small = SmallScatter(at, small_parts, small_got, small_sends, small_recvs)
    units = [
        SumUnit(at, lambda c, n=n: parts_ref.at[at.near[n], c], None, *[b.at[n] for b in (got_s, near_s, diag_s, send_s)], far_s, sum_s, n, n % 2,
                sends.at[n], recvs.at[n], far_recvs)
        for n in reversed(range(M))
    ]

    def run(name):
        for u in units:
            getattr(u, name)()

    gain = params_ref[0:1, :]
    plan = {0: "start", 2: "pair", 5: "cross"}

    def matmul(step, carry):
        g, i = step // 2, lax.rem(step, 2)
        for j, group in enumerate(loads):

            @pl.when(step == 2 * j)
            def _(group=group):
                for cp in group:
                    cp.wait()

        sl = pl.ds(pl.multiple_of(i * (L // 2), L // 2), L // 2)
        e = sum(dot(dqkv_ref[g, sl, t * 256 : t * 256 + 256], w_ref[g, t], NT) for t in range(3))
        e_s[sl, :] = e_s[sl, :] + e
        for j, name in plan.items():

            @pl.when(step == j)
            def _(j=j, name=name):
                if j == 0:
                    later[0].wait()
                    at.meet()
                run(name)

        return carry

    def saves(i):
        sl = pl.ds(pl.multiple_of(i * rows, rows), rows)
        return pltpu.make_async_copy(mid_ref.at[sl], grad_hbm.at[sl], save_sems.at[i])

    def norm(i, carry):
        sl = pl.ds(pl.multiple_of(i * rows, rows), rows)
        e = e_s[sl, :]
        xhat, r = norm_stats(x_ref[sl, :].astype(F32))
        mid_ref[sl, :] = mid_ref[sl, :] + norm_pull(e, xhat, r, gain)
        saves(i).start()
        norm_s[0:1, :] += jnp.sum(e * xhat, axis=0, keepdims=True)
        norm_s[2:3, :] += jnp.sum(e, axis=0, keepdims=True)
        return carry

    at.greet()
    norm_s[...] = second_ref[...]
    e_s[...] = jnp.zeros_like(e_s)
    lax.fori_loop(0, 2 * groups, matmul, 0)
    for cp in later[1:]:
        cp.wait()
    lax.fori_loop(0, L // rows, norm, 0)
    small.start(norm_s[...], R)
    run("join")
    for g in range(groups - 1):
        for t in range(3):
            qkv_ref[:, pl.ds(t * D + g * 256, 256)] = sums_ref[g, :, pl.ds(t * 256, 256)]
    norms_ref[...] = small.collect()
    run("close")
    for t in range(3):
        qkv_ref[:, pl.ds(t * D + (groups - 1) * 256, 256)] = sum_s[:, pl.ds(t * 256, 256)]
    run("finish")
    small.finish()

    def saved(i, carry):
        saves(i).wait()
        return carry

    lax.fori_loop(0, L // rows, saved, 0)


def leave(x, dqkv, w, middle_grad, second_sums, params, parts, sums):
    G, M = lax.axis_size("dp") // 2, lax.axis_size("mp")
    L, D = x.shape
    R = parts.shape[3]
    n = 2 * G * M
    sems = (M, SumUnit.count(G))
    return pl.pallas_call(
        functools.partial(exit_kernel, rows=min(256, L)),
        in_specs=[ANY] * 4 + [VMEM, VMEM, ANY, VMEM],
        out_specs=[ANY, VMEM, VMEM],
        out_shape=[
            jax.ShapeDtypeStruct((L, D), F32),
            jax.ShapeDtypeStruct((R, 3 * D), F32),
            jax.ShapeDtypeStruct((8, 128), F32),
        ],
        scratch_shapes=[
            pltpu.VMEM((L, D), BF), pltpu.VMEM(dqkv.shape, BF), pltpu.VMEM((dqkv.shape[0], 3, D, 256), BF), pltpu.VMEM((L, D), F32),
            pltpu.VMEM(parts.shape, BF), DMA((3, 3)), DMA((L // min(256, L),)),
        ] + sum_buffers(M, G, (R, D), own=False, far=M)
        + [pltpu.VMEM((R, D), F32), pltpu.VMEM((8, D), F32), pltpu.VMEM((L, D), F32), pltpu.VMEM((n, 8, 128), F32), pltpu.VMEM((n, 8, 128), F32),
           DMA(sems), DMA(sems), DMA((M,)), DMA((n,)), DMA((n,))],
        compiler_params=params_of(3),
    )(x, dqkv, w, middle_grad, second_sums, params, parts, sums)


def per_device(inputs, lengths, attn_qkv, attn_proj, mlp_in, mlp_out, norm_gain, norm_bias, cotangent):
    n_dp, n_mp = lax.axis_size("dp"), lax.axis_size("mp")
    G = n_dp // 2
    L, D = inputs.shape
    R = attn_qkv.shape[1]
    wqkv, normed, params = entry(inputs, attn_qkv[0], norm_gain[0], norm_bias[0])
    wqkv = wqkv.reshape(3, D, D)
    mixed, wide, lse, packed, wproj, land, win, wout = attend(lengths, normed, wqkv, attn_proj[0], mlp_in[0], mlp_out[0].T, min(512, L))
    pieces = lambda w: w.reshape((w.shape[0], n_dp) + w.shape[3:])
    outputs, middle_grad, mixed_grad, second_sums, p_proj, p_in, p_out, h_in, h_out, halfway = mlp(
        lengths, inputs, mixed, cotangent, params, wproj.reshape(D, D), pieces(win), pieces(wout), land, R, min(512, L))
    dqkv, d_in, d_out, d_proj, sums, parts = attend_back(
        lengths, packed, mixed_grad, wide, lse, normed, p_in, p_out, p_proj, h_in, h_out, halfway, min(256, L))
    input_grad, d_qkv, norms = leave(inputs, dqkv, wqkv, middle_grad, second_sums, params, parts, sums)
    return (
        outputs,
        input_grad,
        d_qkv[None],
        d_proj[None],
        d_in[None],
        d_out.T[None],
        norms[None, :2, :R],
        norms[None, 2:4, :R],
    )


def solution(mesh):
    everywhere = ("dp", "mp")
    wide, columns, vector = P(everywhere, None), P(None, everywhere, None), P(None, None, everywhere)
    return jax.shard_map(
        per_device,
        mesh=mesh,
        in_specs=(wide, P(everywhere), columns, columns, P(None, "dp", "mp"), P(None, "mp", "dp"), vector, vector, wide),
        out_specs=(wide, wide, columns, columns, P(None, "dp", "mp"), P(None, "mp", "dp"), vector, vector),
        check_vma=False,
    )
```

```python
import functools

import jax
import jax.numpy as jnp
from jax import lax
from jax.experimental import pallas as pl
from jax.experimental.pallas import tpu as pltpu
from jax.sharding import PartitionSpec as P

F32, BF = jnp.float32, jnp.bfloat16
MESH = pl.DeviceIdType.MESH
HEAD_DIM = 64
SCALE = 0.125
LOG2E = 1.4426950408889634
TO_LOG2 = SCALE * LOG2E
NEG = -1e30
EPS = 1e-06
NN = (((1,), (0,)), ((), ()))
NT = (((1,), (1,)), ((), ()))
TN = (((0,), (0,)), ((), ()))
VMEM_LIMIT = 60 * 2**20
ANY = pl.BlockSpec(memory_space=pl.ANY)
VMEM = pl.BlockSpec(memory_space=pltpu.VMEM)
SMEM = pl.BlockSpec(memory_space=pltpu.SMEM)
DMA = pltpu.SemaphoreType.DMA


def dot(a, b, dims):
    return lax.dot_general(a, b, dims, preferred_element_type=F32)


def params_of(collective_id=None, grid=0):
    extra = {} if collective_id is None else {"collective_id": collective_id, "has_side_effects": True}
    if grid:
        extra["dimension_semantics"] = ("arbitrary",) * grid
    return pltpu.CompilerParams(vmem_limit_bytes=VMEM_LIMIT, **extra)


class Place:
    def __init__(self, everyone=False):
        self.everyone = everyone
        n_dp, self.M = lax.axis_size("dp"), lax.axis_size("mp")
        self.G = n_dp // 2
        dp = lax.axis_index("dp")
        self.g, self.c, self.z = dp // 2, lax.rem(dp, 2), lax.axis_index("mp")
        self.square = self.G == 4
        self.near = [self.z ^ n if self.M & (self.M - 1) == 0 else lax.rem(self.z + n, self.M) for n in range(self.M)]
        if self.square:
            self.chips = [self.g ^ 1, self.g ^ 2]
            self.diag = self.g ^ 3
        else:
            self.chips = [lax.rem(self.g + d, self.G) for d in range(1, self.G)]

    def chip(self, h):
        return (h * 2 + self.c, self.z)

    def core(self):
        return (self.g * 2 + 1 - self.c, self.z)

    def along(self, z):
        return (self.g * 2 + self.c, z)

    def peers(self):
        if self.everyone:
            n = 2 * self.G * self.M
            return [self.device(lax.rem(self.index + d, n)) for d in range(1, n)]
        return [self.along(s) for s in self.near[1:]] + [self.chip(h) for h in self.chips] + [self.core()]

    @property
    def index(self):
        return (self.g * 2 + self.c) * self.M + self.z

    def device(self, i):
        return (i // self.M, lax.rem(i, self.M))

    def greet(self):
        for dev in self.peers():
            pl.semaphore_signal(pltpu.get_barrier_semaphore(), inc=1, device_id=dev, device_id_type=MESH)

    def meet(self):
        pl.semaphore_wait(pltpu.get_barrier_semaphore(), len(self.peers()))


def remote(src, dst, send, recv, dev):
    return pltpu.make_async_remote_copy(src_ref=src, dst_ref=dst, send_sem=send, recv_sem=recv, device_id=dev, device_id_type=MESH)


class Along:
    def __init__(self, at, own, land, sends, recvs):
        self.at, self.own, self.land, self.sends, self.recvs = at, own, land, sends, recvs

    def _copy(self, n, source):
        return remote(self.own, self.land(source), self.sends.at[n], self.recvs.at[source], self.at.along(self.at.near[n]))

    def start(self, *ns):
        for n in ns:
            self._copy(n, self.at.z).start()

    def pass_on(self):
        block = self.land(self.at.near[2])
        remote(block, block, self.sends.at[3], self.recvs.at[self.at.near[2]], self.at.along(self.at.near[1])).start()

    def arrive(self, n):
        self._copy(n, self.at.near[n]).wait_recv()

    def finish(self, ns=None):
        for n in range(1, self.at.M) if ns is None else ns:
            self._copy(n, self.at.z).wait_send()


class GatherUnit:
    def __init__(self, at, src, slot, way, sends, recvs, local=True):
        self.at, self.src, self.slot, self.way, self.local = at, src, slot, way, local
        self.sends, self.recvs = sends, recvs

    @staticmethod
    def count(G):
        return 1 + (3 if G == 4 else G - 1) + G

    def _local(self):
        return pltpu.make_async_copy(self.src, self.slot(self.at.g, self.at.c), self.sends.at[0])

    def _to_chip(self, i):
        at = self.at
        return remote(self.src, self.slot(at.g, at.c), self.sends.at[1 + i], self.recvs.at[1 + i], at.chip(at.chips[i]))

    def _relay(self):
        at = self.at
        block = self.slot(at.chips[self.way], at.c)
        return remote(block, block, self.sends.at[3], self.recvs.at[3], at.chip(at.chips[1 - self.way]))

    def _to_core(self, i):
        at = self.at
        h = ([at.g] + at.chips + ([at.diag] if at.square else []))[i]
        k = self.count(at.G) - at.G + i
        block = self.slot(h, at.c)
        return remote(block if i else self.src, block, self.sends.at[k], self.recvs.at[k], at.core())

    def spread(self):
        for i in range(len(self.at.chips)):
            self._to_chip(i).start()
        self._to_core(0).start()
        if self.local:
            self._local().start()

    def relay(self):
        n = len(self.at.chips)
        for i in range(n):
            self._to_chip(i).wait_recv()
        if self.at.square:
            self._relay().start()
        for i in range(n):
            self._to_core(1 + i).start()

    def last(self):
        if self.at.square:
            self._relay().wait_recv()
            self._to_core(3).start()

    def finish(self):
        if self.local:
            self._local().wait()
        for i in range(len(self.at.chips)):
            self._to_chip(i).wait_send()
        if self.at.square:
            self._relay().wait_send()
        for i in range(self.at.G):
            self._to_core(i).wait()


class SumUnit:
    def __init__(self, at, part, own, got, near, diag, out, far, total, n, way, sends, recvs, far_recvs, local=False):
        self.at, self.part, self.own, self.got, self.near, self.diagonal = at, part, own, got, near, diag
        self.out, self.far, self.total, self.n, self.way = out, far, total, n, way
        self.sends, self.recvs, self.far_recvs, self.local = sends, recvs, far_recvs, local
        self.place = at.near[n]
        self.passed = False
        self.opposite = None

    @staticmethod
    def count(G):
        return 3 + (3 if G == 4 else G)

    def _core(self):
        at = self.at
        return remote(self.part(1 - at.c), self.got, self.sends.at[0], self.recvs.at[0], at.core())

    def _local(self):
        return pltpu.make_async_copy(self.part(self.at.c), self.own, self.sends.at[2])

    def _diag(self):
        at = self.at
        return remote(self.got.at[at.diag], self.diagonal, self.sends.at[5], self.recvs.at[5], at.chip(at.chips[1 - self.way]))

    def _chip(self, i):
        at = self.at
        k = 3 + i
        return remote(self.got.at[at.chips[i]], self.near.at[i], self.sends.at[k], self.recvs.at[k], at.chip(at.chips[i]))

    def _z(self, slot):
        dev = self.at.along(self.at.near[1] if self.passed else self.place)
        return remote(self.out, self.far.at[slot], self.sends.at[1], self.far_recvs.at[slot], dev)

    def send_z(self):
        self._z(self.at.near[2] if self.passed else self.at.z).start()

    def start(self):
        self._core().start()
        if self.local:
            self._local().start()

    def launch(self):
        for i in range(len(self.at.chips)):
            self._chip(i).start()

    def pair(self, hold=False):
        at = self.at
        self._core().wait_recv()
        if self.local:
            self._local().wait()
            own = self.own
        else:
            own = self.part(at.c)

        def add(h, carry):
            self.got[h] = (self.got[h].astype(F32) + own[h].astype(F32)).astype(BF)
            return carry

        lax.fori_loop(0, at.G, add, 0)
        if at.square:
            self._diag().start()
        elif not hold:
            self.launch()

    def cross(self, hold=False):
        at = self.at
        if at.square:
            self._diag().wait_recv()
            h = at.chips[self.way]
            self.got[h] = (self.got[h].astype(F32) + self.diagonal[...].astype(F32)).astype(BF)
            if not hold:
                self.launch()

    def join(self):
        at = self.at
        value = self.got[at.g].astype(F32)
        for i in range(len(at.chips)):
            self._chip(i).wait_recv()
            value = value + self.near[i].astype(F32)
        if self.opposite is not None:
            self._z(at.near[3]).wait_recv()
            value = value + self.far[at.near[3]].astype(F32)
        if self.n:
            self.out[...] = value.astype(BF)
            self.send_z()
        else:
            self.total[...] = value

    def close(self):
        if self.n and not self.passed:
            self._z(self.place).wait_recv()
            self.total[...] += self.far[self.place].astype(F32)

    def finish(self, core=True, rest=True):
        at = self.at
        if core:
            self._core().wait_send()
            if at.square:
                self._diag().wait_send()
        if rest:
            if self.n:
                self._z(at.near[2] if self.passed else at.z).wait_send()
            for i in range(len(at.chips)):
                self._chip(i).wait_send()


def link(units):
    by_n = {u.n: u for u in units}
    if units[0].at.M == 4 and 3 in by_n:
        by_n[2].opposite = by_n[3]
        by_n[3].passed = True
    return units


def sum_buffers(n, G, shape, own=True, far=0):
    chips = 2 if G == 4 else G - 1
    block = lambda *lead: pltpu.VMEM(lead + shape, BF)
    return ([block(n, G)] if own else []) + [block(n, G), block(n, chips), block(n), block(n), block(max(far, 1))]


class SmallGather:
    def __init__(self, at, got, sends, recvs):
        self.at, self.got, self.sends, self.recvs = at, got, sends, recvs
        self.count = 2 * at.G * at.M

    def _copy(self, own, d, back):
        at = self.at
        to, other = lax.rem(at.index + d, self.count), lax.rem(at.index + self.count - d, self.count)
        return remote(own, self.got.at[other if back else at.index], self.sends.at[d], self.recvs.at[d], at.device(to))

    def start(self, own):
        def send(d, carry):
            self._copy(own, d, False).start()
            return carry

        lax.fori_loop(1, self.count, send, 0)

    def collect(self, own, R, width):
        def wait(d, carry):
            self._copy(own, d, True).wait_recv()
            return carry

        lax.fori_loop(1, self.count, wait, 0)
        self.got[self.at.index] = own[...]
        lane = lanes((own.shape[0], width))
        total = jnp.zeros((own.shape[0], width), F32)
        for i in range(self.count):
            wide = jnp.concatenate([self.got[i]] * (width // 128), axis=1)
            total = jnp.where(lane // R == i, pltpu.roll(wide, i * R % width, 1) if i else wide, total)
        return total

    def finish(self, own):
        def wait(d, carry):
            self._copy(own, d, False).wait_send()
            return carry

        lax.fori_loop(1, self.count, wait, 0)


class SmallScatter:
    def __init__(self, at, parts, got, sends, recvs):
        self.at, self.parts, self.got, self.sends, self.recvs = at, parts, got, sends, recvs
        self.count = 2 * at.G * at.M

    def _copy(self, d, back):
        at = self.at
        to, other = lax.rem(at.index + d, self.count), lax.rem(at.index + self.count - d, self.count)
        return remote(self.parts.at[to], self.got.at[other if back else at.index], self.sends.at[d], self.recvs.at[d], at.device(to))

    def start(self, value, R):
        for i in range(self.count):
            self.parts[i] = (pltpu.roll(value, value.shape[1] - i * R, 1) if i else value)[:, :128]

        def send(d, carry):
            self._copy(d, False).start()
            return carry

        lax.fori_loop(1, self.count, send, 0)

    def collect(self):
        def add(d, value):
            self._copy(d, True).wait_recv()
            return value + self.got[lax.rem(self.at.index + self.count - d, self.count)]

        return lax.fori_loop(1, self.count, add, self.parts[self.at.index])

    def finish(self):
        def wait(d, carry):
            self._copy(d, False).wait_send()
            return carry

        lax.fori_loop(1, self.count, wait, 0)


def norm_stats(v):
    centre = v - jnp.mean(v, axis=-1, keepdims=True)
    r = lax.rsqrt(jnp.mean(centre * centre, axis=-1, keepdims=True) + EPS)
    return centre * r, r


def norm_pull(e, xhat, r, g):
    y = e * g
    return r * (y - jnp.mean(y, axis=-1, keepdims=True) - xhat * jnp.mean(y * xhat, axis=-1, keepdims=True))


def entry_kernel(x_hbm, block_ref, gain_ref, bias_ref, w_ref, normed_ref, params_ref, x_ref, load_sem, shard_ref, own_ref, got, chain_sends, chain_recvs, sends, recvs,
                 small_sends, small_recvs, *, rows):
    at = Place(everyone=True)
    at.greet()
    load = pltpu.make_async_copy(x_hbm, x_ref, load_sem.at[0])
    load.start()
    land = lambda s: w_ref.at[:, at.g, at.c, s]
    chain = Along(at, shard_ref, land, chain_sends, chain_recvs)
    units = [
        GatherUnit(at, land(at.near[n]) if n else shard_ref, lambda g, c, n=n: w_ref.at[:, g, c, at.near[n]], n % 2, sends.at[n], recvs.at[n], n == 0)
        for n in range(at.M)
    ]
    small = SmallGather(at, got, small_sends, small_recvs)
    L, D = x_ref.shape
    R = block_ref.shape[0]
    for t in range(3):
        shard_ref[t] = block_ref[:, pl.ds(t * D, D)]
    own_ref[...] = jnp.zeros_like(own_ref)
    own_ref[0:2, 0:R] = gain_ref[...].astype(F32)
    own_ref[2:4, 0:R] = bias_ref[...].astype(F32)
    at.meet()
    chain.start(1)
    units[0].spread()
    chain.start(*range(2, 3 if at.M == 4 else at.M))
    small.start(own_ref)

    def norm(i, carry):
        sl = pl.ds(pl.multiple_of(i * rows, rows), rows)
        xhat, _ = norm_stats(x_ref[sl, :].astype(F32))
        normed_ref[sl, :] = (xhat * params_ref[0:1, :] + params_ref[2:3, :]).astype(BF)
        return carry

    steps = L // rows
    for n in range(1, at.M):
        chain.arrive(n)
        if at.M == 4 and n == 2:
            chain.pass_on()
        units[n].spread()
        units[n - 1].relay()
        if n > 1:
            units[n - 2].last()
    params_ref[...] = small.collect(own_ref, R, D)
    load.wait()
    lax.fori_loop(0, steps // 2, norm, 0)
    units[-1].relay()
    if at.M > 1:
        units[-2].last()
    lax.fori_loop(steps // 2, steps, norm, 0)
    units[-1].last()
    for u in units:
        u.finish()
    chain.finish()
    small.finish(own_ref)


def entry(x, block, gain, bias):
    G, M = lax.axis_size("dp") // 2, lax.axis_size("mp")
    L, D = x.shape
    R = block.shape[0]
    n = 2 * G * M
    sems = (M, GatherUnit.count(G))
    return pl.pallas_call(
        functools.partial(entry_kernel, rows=min(256, L)),
        in_specs=[ANY, VMEM, VMEM, VMEM],
        out_specs=[ANY, VMEM, VMEM],
        out_shape=[
            jax.ShapeDtypeStruct((3, G, 2, M, R, D), BF),
            jax.ShapeDtypeStruct((L, D), BF),
            jax.ShapeDtypeStruct((8, D), F32),
        ],
        scratch_shapes=[pltpu.VMEM((L, D), BF), DMA((1,)), pltpu.VMEM((3, R, D), BF), pltpu.VMEM((8, 128), F32), pltpu.VMEM((n, 8, 128), F32), DMA((M + 1,)), DMA((M,)), DMA(sems), DMA(sems), DMA((n,)), DMA((n,))],
        compiler_params=params_of(0),
    )(x, block, gain, bias)


def lanes(shape):
    return lax.broadcasted_iota(jnp.int32, shape, len(shape) - 1)


def three_parts(x):
    hi = x.astype(BF)
    rest = x - hi.astype(F32)
    mid = rest.astype(BF)
    return hi, mid, (rest - mid.astype(F32)).astype(BF)


def mask_bias(shape, length):
    return jnp.where(lax.broadcasted_iota(jnp.int32, shape, 0) < length, 0.0, NEG).astype(BF)


def attend_step(p, len_ref, q_ref, k_ref, v_ref, o_ref, wide_ref, lse_ref, tq, between):
    L = q_ref.shape[0]
    lane = lanes((L, 128))
    k, v = k_ref[...], v_ref[...]
    bias = mask_bias((L, 128), len_ref[0])
    zero, one = jnp.zeros((L, 128), BF), jnp.ones((L, 128), BF)

    @pl.when(p == 0)
    def _():
        lse_ref[...] = jnp.zeros_like(lse_ref)

    keys, values = [], []
    for h in range(2):
        mine = (lane < 64) if h == 0 else (lane >= 64)
        spare = 64 * (1 - h)
        keys.append(jnp.where(mine, k, jnp.where(lane == spare, bias, zero)))
        values.append(jnp.where(mine, v, jnp.where(lane == spare, one, zero)))
    lq = lanes((tq, 128))
    for i in range(L // tq):
        between(i)
        sl = pl.ds(i * tq, tq)
        q = q_ref[sl, :]
        outs, sums = [], []
        for h in range(2):
            mine = (lq < 64) if h == 0 else (lq >= 64)
            spare = 64 * (1 - h)
            q_h = jnp.where(mine, q, jnp.where(lq == spare, jnp.ones((tq, 128), BF), jnp.zeros((tq, 128), BF)))
            s = dot(q_h, keys[h], NT)
            top = jnp.max(s, axis=1, keepdims=True) * TO_LOG2
            e = jnp.exp2(s * TO_LOG2 - top)
            o = dot(e.astype(BF), values[h], NN)
            total = o[:, spare : spare + 1]
            outs.append(o / total)
            sums.append(top + jnp.log2(total))
        out = jnp.where(lq < 64, outs[0], outs[1])
        wide_ref[sl, :] = out
        o_ref[sl, :] = out.astype(BF)
        lse = lse_ref[sl, :]
        lse = jnp.where(lq == 2 * p, sums[0], lse)
        lse_ref[sl, :] = jnp.where(lq == 2 * p + 1, sums[1], lse)


def attend_back_step(p, len_ref, q_ref, k_ref, v_ref, do_ref, wide_ref, lse_ref, dq_ref, dk_ref, dv_ref, tq, between):
    L = q_ref.shape[0]
    lane = lanes((L, 128))
    k, v = k_ref[...], v_ref[...]
    bias = mask_bias((L, 128), len_ref[0])
    zero, one = jnp.zeros((L, 128), BF), jnp.ones((L, 128), BF)
    keys, values = [], []
    for h in range(2):
        mine = (lane < 64) if h == 0 else (lane >= 64)
        b = 64 * (1 - h)
        ones = jnp.where((lane > b) & (lane < b + 4), one, zero)
        keys.append(jnp.where(mine, k, jnp.where(lane == b, bias, ones)))
        values.append(jnp.where(mine, v, ones))
    lq = lanes((tq, 128))
    dk, dv = [jnp.zeros((L, 128), F32)] * 2, [jnp.zeros((L, 128), F32)] * 2
    for i in range(L // tq):
        between(i)
        sl = pl.ds(i * tq, tq)
        q, do, lse = q_ref[sl, :], do_ref[sl, :], lse_ref[sl, :]
        product = wide_ref[sl, :] * do.astype(F32)
        dq = []
        for h in range(2):
            mine = (lq < 64) if h == 0 else (lq >= 64)
            b = 64 * (1 - h)
            minus_delta = -jnp.sum(jnp.where(mine, product, 0.0), axis=1, keepdims=True)
            minus_lse = -jnp.sum(jnp.where(lq == 2 * p + h, lse, 0.0), axis=1, keepdims=True) * (1.0 / TO_LOG2)

            def with_spare(x, term, first):
                hi, mid, lo = three_parts(jnp.broadcast_to(term, (tq, 128)))
                low = jnp.where(lq == b + 2, mid, jnp.where(lq == b + 3, lo, jnp.zeros((tq, 128), BF)))
                low = jnp.where(lq == b, jnp.full((tq, 128), first, BF), jnp.where(lq == b + 1, hi, low))
                return jnp.where(mine, x, low)

            st = dot(keys[h], with_spare(q, minus_lse, 1.0), NT)
            pt = jnp.exp2(st * TO_LOG2)
            dpt = dot(values[h], with_spare(do, minus_delta, 0.0), NT)
            ds = (pt * dpt).astype(BF)
            dv[h] = dv[h] + dot(pt.astype(BF), do, NN)
            dk[h] = dk[h] + dot(ds, q, NN)
            dq.append(dot(ds, k, TN))
        dq_ref[sl, :] = (jnp.where(lq < 64, dq[0], dq[1]) * SCALE).astype(BF)
    dk_ref[...] = (jnp.where(lane < 64, dk[0], dk[1]) * SCALE).astype(BF)
    dv_ref[...] = jnp.where(lane < 64, dv[0], dv[1]).astype(BF)


def at_slots(p, per_step, plan):
    def between(i):
        for slot, actions in sorted(plan.items()):
            if slot % per_step == i:

                @pl.when(p == slot // per_step)
                def _(actions=actions):
                    for action in actions:
                        action()

    return between


def attend_kernel(len_ref, x_ref, w_ref, proj_ref, in_ref, out_ref, o_ref, wide_ref, lse_ref, packed_ref, wproj_ref, land_ref, win_ref, wout_ref,
                  w_s, w_sem, packed_s, save_sem, pchain_sends, pchain_recvs, chain_sends, chain_recvs, sends, recvs, *, tq):
    p, steps = pl.program_id(0), pl.num_programs(0)
    at = Place()
    M = at.M
    half = M // 2
    D = x_ref.shape[1]
    parts = x_ref.shape[0] // tq
    land = [lambda s, a=a: land_ref.at[s, a] for a in range(2)]
    own = (in_ref, out_ref)
    direct = [n for n in range(1, M) if M != 4 or n < 3]
    pland = lambda s: wproj_ref.at[at.g, at.c, s]
    pchain = Along(at, proj_ref, pland, pchain_sends, pchain_recvs)
    chains = [Along(at, own[a], land[a], chain_sends.at[a], chain_recvs.at[a]) for a in range(2)]
    main = [
        [GatherUnit(at, land[a](at.near[n]) if n else own[a], lambda g, c, n=n, ref=ref: ref.at[n, g, c], a, sends.at[2 * n + a], recvs.at[2 * n + a])
         for a, ref in enumerate((win_ref, wout_ref))]
        for n in range(half)
    ]
    proj = [
        GatherUnit(at, pland(at.near[n]) if n else proj_ref, lambda g, c, n=n: wproj_ref.at[g, c, at.near[n]], n % 2,
                   sends.at[2 * half + n], recvs.at[2 * half + n], n == 0)
        for n in range(M)
    ]
    own_land = [pltpu.make_async_copy(own[a], land_ref.at[at.z, a], save_sem.at[1 + a]) for a in range(2)]
    save = pltpu.make_async_copy(packed_s, packed_ref, save_sem.at[0])

    loads = [pltpu.make_async_copy(w_ref.at[t], w_s.at[t], w_sem.at[t]) for t in range(3)]

    def third(t):
        loads[t].wait()
        packed_s[:, pl.ds(t * D, D)] = dot(x_ref[...], w_s[t], NN).astype(BF)

    @pl.when(p == 0)
    def _():
        for cp in loads:
            cp.start()
        at.greet()
        third(0)
        at.meet()
        pchain.start(*range(1, M))
        for n in direct:
            for chain in chains:
                chain.start(n)
        proj[0].spread()
        for u in main[0]:
            u.spread()
        for cp in own_land:
            cp.start()
        third(1)
        third(2)
        save.start()

    plan = {}

    def put(slot, *actions):
        plan.setdefault(min(slot, ATTEND_STEPS * parts - 1), []).extend(actions)

    def arrive(chain, n, unit=None):
        def act():
            chain.arrive(n)
            if unit is not None:
                unit.spread()

        return act

    for n in range(M):
        arrives, relays, lasts = ATTEND_PROJ[min(n, 3)]
        put(relays, proj[n].relay)
        put(lasts, proj[n].last)
        if n:
            put(arrives, arrive(pchain, n, proj[n]))
    for n in range(half):
        for a in range(2):
            arrives, relays, lasts = ATTEND_MAIN[min(n, 1)][a]
            if n:
                put(arrives, arrive(chains[a], n, main[n][a]))
            put(relays, main[n][a].relay)
            put(lasts, main[n][a].last)
    lane = pl.multiple_of(p * 128, 128)
    column = lambda t: packed_s.at[:, pl.ds(t * D + lane, 128)]
    attend_step(p, len_ref, column(0), column(1), column(2), o_ref, wide_ref, lse_ref, tq, at_slots(p, parts, plan))

    @pl.when(p == steps - 1)
    def _():
        for n in direct[half - 1 :]:
            for chain in chains:
                chain.arrive(n)
        for group in main + [proj, [pchain]]:
            for u in group:
                u.finish()
        for chain in chains:
            chain.finish(direct)
        save.wait()
        for cp in own_land:
            cp.wait()


ATTEND_STEPS = 6
ATTEND_PROJ = [[0, 0, 4], [0, 4, 6], [4, 6, 8], [6, 8, 10]]
ATTEND_MAIN = [[[0, 4, 8], [0, 4, 8]], [[2, 8, 10], [4, 8, 10]]]
BACK = {"pair0": 1, "pair1": 1, "pair_p": 1, "cross1": 2, "pair_h0": 3, "cross_p": 3, "join0": 3, "pair_h1": 4, "join_p": 4, "cross_h1": 5, "late_p": 5, "join_h0": 5}
MLP = {"relay0": (0, 2), "spread1": (0, 2), "relay1": (2, 0), "last0": (1, 2), "last1": (2, 2), "pair0": (1, 2), "cross0": (2, 2), "pair1": (3, 0), "join0": (3, 2)}


def attend(lengths, x, w, proj, w_in, w_out, tq):
    G, M = lax.axis_size("dp") // 2, lax.axis_size("mp")
    L, D = x.shape
    half = M // 2
    column = pl.BlockSpec((L, 128), lambda p: (0, p))
    whole = lambda shape: pl.BlockSpec(shape, lambda p: (0,) * len(shape), pipeline_mode=pl.Buffered(1))
    sems = (2 * half + M, GatherUnit.count(G))
    weights = jax.ShapeDtypeStruct((half, G, 2) + w_in.shape, BF)
    return pl.pallas_call(
        functools.partial(attend_kernel, tq=tq),
        grid=(D // 128,),
        in_specs=[SMEM, whole(x.shape), ANY, ANY, ANY, ANY],
        out_specs=[column, column, pl.BlockSpec((L, 128), lambda p: (0, 0)), ANY, ANY, ANY, ANY, ANY],
        out_shape=[
            jax.ShapeDtypeStruct((L, D), BF),
            jax.ShapeDtypeStruct((L, D), F32),
            jax.ShapeDtypeStruct((L, 128), F32),
            jax.ShapeDtypeStruct((L, 3 * D), BF),
            jax.ShapeDtypeStruct((G, 2, M) + proj.shape, BF),
            jax.ShapeDtypeStruct((M, 2) + w_in.shape, BF),
            weights, weights,
        ],
        scratch_shapes=[pltpu.VMEM(w.shape, BF), DMA((3,)), pltpu.VMEM((L, 3 * D), BF), DMA((3,)), DMA((M + 1,)), DMA((M,)), DMA((2, M + 1)), DMA((2, M)), DMA(sems), DMA(sems)],
        compiler_params=params_of(1, grid=1),
    )(lengths, x, w, proj, w_in, w_out)


def gelu_and_slope(x):
    phi = 0.5 + 0.5 * lax.erf(x * 0.7071067811865476)
    return x * phi, phi + x * (jnp.exp2((x * x) * (-0.5 * LOG2E)) * 0.3989422804014327)


def mlp_kernel(len_ref, x_hbm, mixed_hbm, cot_hbm, params_ref, wproj_hbm, win_ref, wout_ref, land_ref,
               y_hbm, mgrad_hbm, dmixed_hbm, sums_ref, pproj_ref, pin_ref, pout_ref, din_ref, dout_ref, half_ref,
               x_ref, mixed_ref, cot_ref, wproj_ref, in_sems, out_sems, w_s, mid_s, hid_s, sg_s, sec_s, br_s, act_s, eg_s, got_s, near_s, diag_s, last_s, hand_sems,
               load_sems, save_sems, gsends, grecvs, ssends, srecvs, *, tr):
    at = Place()
    G, M = at.G, at.M
    L, D = x_ref.shape
    n_rows = L // tr
    enter_loads = [
        [pltpu.make_async_copy(src.at[pl.ds(i * tr, tr)], dst.at[pl.ds(i * tr, tr)], in_sems.at[i, j])
         for j, (src, dst) in enumerate(((mixed_hbm, mixed_ref), (x_hbm, x_ref), (cot_hbm, cot_ref)))]
        for i in range(n_rows)
    ]
    proj_load = pltpu.make_async_copy(wproj_hbm, wproj_ref, in_sems.at[0, 3])
    proj_load.start()
    for group in enter_loads:
        for cp in group:
            cp.start()
    R, Fb = land_ref.shape[2:]
    half = M // 2
    gain, bias = params_ref[1:2, :], params_ref[3:4, :]
    loads = [pltpu.make_async_copy((win_ref, wout_ref)[a].at[k], w_s.at[k, a], load_sems.at[k, a]) for k in range(half) for a in range(2)]
    for cp in loads:
        cp.start()
    at.greet()
    gathers = [
        [GatherUnit(at, last_s.at[a] if M == 4 and k == 3 else land_ref.at[at.near[k], a], lambda g, c, k=k, a=a: w_s.at[k, a, g * 2 + c], a, gsends.at[k - half, a], grecvs.at[k - half, a])
         for a in range(2)]
        for k in range(half, M)
    ]
    sums = [
        [SumUnit(at, lambda c, k=k, a=a: w_s.at[k, a, pl.ds(c * G, G)], None, *[b.at[2 * k + a] for b in (got_s, near_s, diag_s)], None,
                 None, total, k, a, ssends.at[2 * k + a], srecvs.at[2 * k + a], None)
         for a, total in enumerate((din_ref, dout_ref))]
        for k in range(2)
    ]

    hand = [remote(land_ref.at[at.near[2], a], last_s.at[a], hand_sems.at[0, a], hand_sems.at[1, a], at.along(at.near[1])) for a in range(2)] if M == 4 else []

    def rows(i):
        return pl.ds(i * tr, tr)

    def enter(i):
        if i == 0:
            proj_load.wait()
        for cp in enter_loads[i]:
            cp.wait()
        sl = rows(i)
        mid = x_ref[sl, :].astype(F32) + dot(mixed_ref[sl, :], wproj_ref[...], NN)
        mid_s[sl, :] = mid
        hid_s[sl, :] = mid
        sec_s[sl, :] = (norm_stats(mid)[0] * gain + bias).astype(BF)
        at_row = lax.broadcasted_iota(jnp.int32, (tr, D), 0) + i * tr
        br_s[sl, :] = jnp.where(at_row < len_ref[0], cot_ref[sl, :].astype(F32), 0.0).astype(BF)
        sg_s[sl, :] = jnp.zeros((tr, D), F32)

    enter(0)
    at.meet()
    for cp in hand:
        cp.start()
    for n, group in enumerate(gathers):
        for u in group:
            if n == 0 or not hand:
                u.spread()
    for i in range(1, n_rows):
        enter(i)
    for cp in loads:
        cp.wait()
    per = n_rows + 2
    plan = {}

    def put(k, i, name, group):
        plan.setdefault((min(k, M - 1), min(i, per - 1)), []).extend(getattr(u, name) for u in group)

    for n, group in enumerate(gathers):
        after = lambda name: (MLP[name + "0"] if n == 0 else (MLP[name + "1"][0] + n - 1, MLP[name + "1"][1]))
        put(*after("relay"), "relay", group)
        if n and hand:
            plan.setdefault(MLP["spread1"], []).extend([cp.wait_recv for cp in hand])
            put(*MLP["spread1"], "spread", group)
        put(*after("last"), "last", group)
        put(half + n, 0, "finish", group)
    put(1, 0, "start", sums[0])
    put(*MLP["pair0"], "pair", sums[0])
    put(2, 0, "start", sums[1])
    put(*MLP["cross0"], "cross", sums[0])
    plan.setdefault(MLP["pair1"], []).extend(functools.partial(u.pair, True) for u in sums[1])
    put(*MLP["join0"], "join", sums[0])

    def block(k, carry):
        def between(i):
            for (at_k, at_i), actions in sorted(plan.items(), key=lambda item: item[0]):
                if at_i == i:

                    @pl.when(k == at_k)
                    def _(actions=actions):
                        for action in actions:
                            action()

        between(0)
        win, wout = (w_s[k, a].reshape(D, Fb) for a in range(2))
        for i in range(n_rows):
            if i:
                between(i)
            sl = rows(i)
            value, slope = gelu_and_slope(dot(sec_s[sl, :], win, NN))
            act = value.astype(BF)
            eg = (dot(br_s[sl, :], wout, NN) * slope).astype(BF)
            act_s[sl, :], eg_s[sl, :] = act, eg
            hid_s[sl, :] += dot(act, wout, NT)
            sg_s[sl, :] += dot(eg, win, NT)
        for a, (left, right) in enumerate(((sec_s, eg_s), (br_s, act_s))):
            between(n_rows + a)
            grad = dot(left[...], right[...], TN)
            for g in range(G):
                for c in range(2):
                    row = (g * 2 + c) * R
                    w_s[k, a, c * G + g] = grad[row : row + R, :].astype(BF)

        @pl.when(k > 1)
        def _():
            for a, ref in enumerate((pin_ref, pout_ref)):
                pltpu.make_async_copy(w_s.at[k, a], ref.at[k - 2], save_sems.at[k - 2, a]).start()

        return carry

    lax.fori_loop(0, M, block, 0)
    sums_ref[...] = jnp.zeros_like(sums_ref)
    n_back = L // 256 if L % 256 == 0 else 1
    tb = L // n_back

    def saves(i):
        sl = pl.ds(pl.multiple_of(i * tb, tb), tb)
        return [pltpu.make_async_copy(src.at[sl], dst.at[sl], out_sems.at[i, j])
                for j, (src, dst) in enumerate(((x_ref, y_hbm), (mid_s, mgrad_hbm), (cot_ref, dmixed_hbm)))]

    def back(i, carry):
        sl = pl.ds(pl.multiple_of(i * tb, tb), tb)
        x_ref[sl, :] = hid_s[sl, :].astype(BF)
        xhat, r = norm_stats(mid_s[sl, :])
        e = sg_s[sl, :]
        sums_ref[1:2, :] += jnp.sum(e * xhat, axis=0, keepdims=True)
        sums_ref[3:4, :] += jnp.sum(e, axis=0, keepdims=True)
        grad = br_s[sl, :].astype(F32) + norm_pull(e, xhat, r, gain)
        mid_s[sl, :] = grad
        low = grad.astype(BF)
        sec_s[sl, :] = low
        cot_ref[sl, :] = dot(low, wproj_ref[...], NT).astype(BF)
        for cp in saves(i):
            cp.start()
        return carry

    lax.fori_loop(0, n_back, back, 0)
    for u in sums[1]:
        u.cross(True)
    save_half = pltpu.make_async_copy(got_s.at[pl.ds(2, 2)], half_ref, load_sems.at[0, 0])
    save_half.start()
    grad = dot(mixed_ref[...], sec_s[...], TN)
    R_p = pproj_ref.shape[3]
    for g in range(G):
        for c in range(2):
            for z in range(M):
                row = ((g * 2 + c) * M + z) * R_p
                pproj_ref[z, c, g] = grad[row : row + R_p, :].astype(BF)
    for k in range(2, M):
        for a, ref in enumerate((pin_ref, pout_ref)):
            pltpu.make_async_copy(w_s.at[k, a], ref.at[k - 2], save_sems.at[k - 2, a]).wait()
    save_half.wait()

    def saved(i, carry):
        for cp in saves(i):
            cp.wait()
        return carry

    lax.fori_loop(0, n_back, saved, 0)
    for k, group in enumerate(sums):
        for u in group:
            u.finish(True, k == 0)
    for cp in hand:
        cp.wait_send()


def mlp(lengths, x, mixed, cot, params, wproj, win, wout, land, R_p, tr):
    G, M = lax.axis_size("dp") // 2, lax.axis_size("mp")
    half = M // 2
    L, D = x.shape
    R, Fb = block = land.shape[2:]
    gsems, ssems = (M - half, 2, GatherUnit.count(G)), (4, SumUnit.count(G))
    pieces = jax.ShapeDtypeStruct((M - 2, 2 * G) + block, BF)
    return pl.pallas_call(
        functools.partial(mlp_kernel, tr=tr),
        in_specs=[SMEM, ANY, ANY, ANY, VMEM, ANY, ANY, ANY, ANY],
        out_specs=[ANY] * 3 + [VMEM] * 2 + [ANY, ANY, VMEM, VMEM, ANY],
        out_shape=[
            jax.ShapeDtypeStruct((L, D), BF),
            jax.ShapeDtypeStruct((L, D), F32),
            jax.ShapeDtypeStruct((L, D), BF),
            jax.ShapeDtypeStruct(params.shape, F32),
            jax.ShapeDtypeStruct((M, 2, G, R_p, D), BF),
            pieces, pieces,
            jax.ShapeDtypeStruct(block, F32), jax.ShapeDtypeStruct(block, F32), jax.ShapeDtypeStruct((2, G) + block, BF),
        ],
        scratch_shapes=[
            pltpu.VMEM((L, D), BF), pltpu.VMEM((L, D), BF), pltpu.VMEM((L, D), BF), pltpu.VMEM((D, D), BF),
            DMA((L // tr, 4)), DMA((L // 256 if L % 256 == 0 else 1, 3)),
            pltpu.VMEM((M, 2, 2 * G) + block, BF),
            pltpu.VMEM((L, D), F32), pltpu.VMEM((L, D), F32), pltpu.VMEM((L, D), F32),
            pltpu.VMEM((L, D), BF), pltpu.VMEM((L, D), BF), pltpu.VMEM((L, Fb), BF), pltpu.VMEM((L, Fb), BF),
        ] + sum_buffers(4, G, block, own=False)[:3] + [pltpu.VMEM((2,) + block, BF), DMA((2, 2)), DMA((half, 2)), DMA((M - 2, 2)), DMA(gsems), DMA(gsems), DMA(ssems), DMA(ssems)],
        compiler_params=params_of(4),
    )(lengths, x, mixed, cot, params, wproj, win, wout, land)


def attend_back_kernel(len_ref, q_ref, k_ref, v_ref, do_ref, wide_ref, lse_ref, normed_hbm, pin_ref, pout_ref, pproj_ref, hin_ref, hout_ref, half_ref,
                       dqkv_ref, din_ref, dout_ref, dproj_ref, sum_ref, rest_ref,
                       own_m, got_m, near_m, diag_m, send_m, far_in, far_out, own_p, got_p, near_p, diag_p, send_p, far_p,
                       parts_s, got_q, near_q, diag_q, send_q, far_q, sends, recvs, far_recvs, far_recvs_q, save_sem, normed_ref, *, tq):
    p, steps = pl.program_id(0), ATTEND_STEPS
    at = Place()
    G, M = at.G, at.M
    parts = q_ref.shape[0] // tq
    R = sum_ref.shape[1]
    units = []

    def add(part, bufs, far, total, n, way, recv, local=True):
        k = len(units)
        units.append(SumUnit(at, part, *bufs, far, total, n, way, sends.at[k], recvs.at[k], recv, local=local))
        return units[-1]

    def block(n):
        made = []
        for a, (ref, far, total) in enumerate(((pin_ref, far_in, din_ref), (pout_ref, far_out, dout_ref))):
            k = 2 * (n - 1) + a
            near, diag, out = [b.at[k] for b in (near_m, diag_m, send_m)]
            own, got = (None, half_ref.at[a]) if n == 1 else (own_m.at[k - 2], got_m.at[k - 2])
            made.append(add(lambda c, ref=ref: ref.at[n - 2, pl.ds(c * G, G)], (own, got, near, diag, out), far, total, n, a, far_recvs.at[a]))
        return made

    main = {n: block(n) for n in range(1, M)}
    for a in range(2):
        link([main[n][a] for n in main])
    proj = {}
    for n in reversed(range(M)):
        proj[n] = add(lambda c, n=n: pproj_ref.at[at.near[n], c], [b.at[n] for b in (own_p, got_p, near_p, diag_p, send_p)],
                      far_p, dproj_ref, n, n % 2, far_recvs.at[2])
    heads = []
    for t in range(steps // 2 - 1):
        heads.append({})
        for n in reversed(range(M)):
            heads[t][n] = add(lambda c, t=t, n=n: parts_s.at[t, at.near[n], c], [None] + [b.at[t * M + n] for b in (got_q, near_q, diag_q, send_q)],
                              far_q.at[pl.ds(t * M, M)], sum_ref.at[t], n, (n + t) % 2, far_recvs_q.at[t], False)
    for group in [proj] + heads:
        link(list(group.values()))
    every = lambda group: list(group.values())
    early = lambda group: [group[n] for n in group if n != 2]
    late = lambda group: [group[n] for n in group if n == 2]
    plan = {}

    def put(step, name, group):
        plan.setdefault(step * parts, []).extend(getattr(u, name) for u in group)

    load = pltpu.make_async_copy(normed_hbm, normed_ref, save_sem.at[1])
    pl.when(p == 0)(load.start)
    pl.when(p == 1)(load.wait)

    def begin():
        din_ref[...], dout_ref[...] = hin_ref[...], hout_ref[...]

    plan[0] = [at.greet, begin, at.meet]
    put(0, "launch", main[1])
    others = [main[n] for n in reversed(range(2, M))]
    for group in others + [every(proj)]:
        put(0, "start", group)
    for n, group in enumerate(others):
        put(BACK["pair0"] if n == 0 else BACK["pair1"], "pair", group)
        if n != 1:
            put(BACK["join0"], "join", group)
    put(BACK["pair_p"], "pair", every(proj))
    for group in others[1:]:
        put(BACK["cross1"], "cross", group)
    put(BACK["pair_h0"], "pair", every(heads[0]))
    put(BACK["cross_p"], "cross", every(proj))
    put(BACK["join_p"], "join", early(proj))
    put(BACK["pair_h1"], "pair", every(heads[1]))
    put(BACK["cross_h1"], "cross", every(heads[1]))
    put(BACK["late_p"], "join", late(proj))
    put(BACK["join_h0"], "join", early(heads[0]))
    grad_to = lambda t: dqkv_ref.at[0, :, pl.ds(pl.multiple_of(t * 256 + lax.rem(p, 2) * 128, 128), 128)]
    attend_back_step(p, len_ref, q_ref, k_ref, v_ref, do_ref, wide_ref, lse_ref, grad_to(0), grad_to(1), grad_to(2), tq, at_slots(p, parts, plan))

    @pl.when(p == 1)
    def _():
        for u in others[0]:
            u.cross()
        for u in main[1]:
            u.join()

    @pl.when(p == 3)
    def _():
        for u in every(heads[0]):
            u.cross()

    @pl.when(p == steps - 1)
    def _():
        for u in late(heads[0]) + early(heads[1]):
            u.join()

    @pl.when(lax.rem(p, 2) == 1)
    def _():
        t = p // 2
        grad = dot(normed_ref[...], dqkv_ref[0], TN)
        for g in range(G):
            for c in range(2):
                for z in range(M):
                    k = ((g * 2 + c) * M + z) * R
                    parts_s[t, z, c, g] = grad[k : k + R, :].astype(BF)

    save = pltpu.make_async_copy(parts_s.at[steps // 2 - 1], rest_ref, save_sem.at[0])
    for t, group in enumerate(heads):

        @pl.when(p == 2 * t + 1)
        def _(group=group):
            for u in every(group):
                u.start()

    @pl.when(p == 3)
    def _():
        for u in others[1] if len(others) > 1 else []:
            u.join()

    @pl.when(p == steps - 1)
    def _():
        save.start()
        for u in late(heads[1]):
            u.join()
        for u in units:
            u.close()
        for u in units:
            u.finish(u not in main[1], True)
        save.wait()


def attend_back(lengths, packed, do, wide, lse, normed, p_in, p_out, p_proj, h_in, h_out, halfway, tq):
    G, M = lax.axis_size("dp") // 2, lax.axis_size("mp")
    L, D = do.shape
    pairs = D // 128
    column = lambda off: pl.BlockSpec((L, 128), lambda p, off=off: (0, off + p))
    whole = lambda shape: pl.BlockSpec(shape, lambda p: (0,) * len(shape), pipeline_mode=pl.Buffered(1))
    out = lambda shape: pl.BlockSpec(shape, lambda p: (0,) * len(shape))
    mshape, pshape = h_in.shape, p_proj.shape[3:]
    groups = pairs // 2
    rest = 2 * (M - 1)
    sems = (rest + groups * M, SumUnit.count(G))
    return pl.pallas_call(
        functools.partial(attend_back_kernel, tq=tq),
        grid=(pairs,),
        in_specs=[SMEM, column(0), column(pairs), column(2 * pairs), column(0), column(0), whole((L, 128)), ANY, ANY, ANY, ANY,
                  whole(mshape), whole(mshape), whole(halfway.shape)],
        out_specs=[pl.BlockSpec((1, L, 768), lambda p: (p // 2, 0, 0)), out(mshape), out(mshape), out(pshape), out((groups - 1,) + pshape), ANY],
        out_shape=[jax.ShapeDtypeStruct((groups, L, 768), BF)]
        + [jax.ShapeDtypeStruct(mshape, F32)] * 2
        + [jax.ShapeDtypeStruct(pshape, F32), jax.ShapeDtypeStruct((groups - 1,) + pshape, F32), jax.ShapeDtypeStruct((M, 2, G) + pshape, BF)],
        scratch_shapes=sum_buffers(rest - 2, G, mshape)[:2] + sum_buffers(rest, G, mshape, far=M)[2:] + [pltpu.VMEM((M,) + mshape, BF)] + sum_buffers(M, G, pshape, far=M)
        + [pltpu.VMEM((groups, M, 2, G) + pshape, BF)] + sum_buffers((groups - 1) * M, G, pshape, own=False, far=(groups - 1) * M)
        + [DMA(sems), DMA(sems), DMA((3, M)), DMA((groups - 1, M)), DMA((2,)), pltpu.VMEM((L, D), BF)],
        compiler_params=params_of(2, grid=1),
    )(lengths, packed, packed, packed, do, wide, lse, normed, p_in, p_out, p_proj, h_in, h_out, halfway)


def exit_kernel(x_hbm, dqkv_hbm, w_hbm, mid_hbm, second_ref, params_ref, parts_hbm, sums_ref, grad_hbm, qkv_ref, norms_ref,
                x_ref, dqkv_ref, w_ref, mid_ref, parts_ref, load_sems, save_sems,
                got_s, near_s, diag_s, send_s, far_s, sum_s, norm_s, e_s, small_parts, small_got,
                sends, recvs, far_recvs, small_sends, small_recvs, *, rows):
    at = Place(everyone=True)
    M = at.M
    L, D = x_ref.shape
    R = qkv_ref.shape[0]
    groups = dqkv_ref.shape[0]
    loads = [
        [pltpu.make_async_copy(dqkv_hbm.at[g], dqkv_ref.at[g], load_sems.at[g, 0]),
         pltpu.make_async_copy(w_hbm.at[:, :, pl.ds(g * 256, 256)], w_ref.at[g], load_sems.at[g, 1])]
        for g in range(groups)
    ]
    later = [pltpu.make_async_copy(parts_hbm, parts_ref, load_sems.at[0, 2]), pltpu.make_async_copy(x_hbm, x_ref, load_sems.at[1, 2]),
             pltpu.make_async_copy(mid_hbm, mid_ref, load_sems.at[2, 2])]
    for cp in loads[0] + later[:1] + [cp for group in loads[1:] for cp in group] + later[1:]:
        cp.start()
    small = SmallScatter(at, small_parts, small_got, small_sends, small_recvs)
    units = [
        SumUnit(at, lambda c, n=n: parts_ref.at[at.near[n], c], None, *[b.at[n] for b in (got_s, near_s, diag_s, send_s)], far_s, sum_s, n, n % 2,
                sends.at[n], recvs.at[n], far_recvs)
        for n in reversed(range(M))
    ]

    def run(name):
        for u in units:
            getattr(u, name)()

    gain = params_ref[0:1, :]
    plan = {0: "start", 2: "pair", 5: "cross"}

    def matmul(step, carry):
        g, i = step // 2, lax.rem(step, 2)
        for j, group in enumerate(loads):

            @pl.when(step == 2 * j)
            def _(group=group):
                for cp in group:
                    cp.wait()

        sl = pl.ds(pl.multiple_of(i * (L // 2), L // 2), L // 2)
        e = sum(dot(dqkv_ref[g, sl, t * 256 : t * 256 + 256], w_ref[g, t], NT) for t in range(3))
        e_s[sl, :] = e_s[sl, :] + e
        for j, name in plan.items():

            @pl.when(step == j)
            def _(j=j, name=name):
                if j == 0:
                    later[0].wait()
                    at.meet()
                run(name)

        return carry

    def saves(i):
        sl = pl.ds(pl.multiple_of(i * rows, rows), rows)
        return pltpu.make_async_copy(mid_ref.at[sl], grad_hbm.at[sl], save_sems.at[i])

    def norm(i, carry):
        sl = pl.ds(pl.multiple_of(i * rows, rows), rows)
        e = e_s[sl, :]
        xhat, r = norm_stats(x_ref[sl, :].astype(F32))
        mid_ref[sl, :] = mid_ref[sl, :] + norm_pull(e, xhat, r, gain)
        saves(i).start()
        norm_s[0:1, :] += jnp.sum(e * xhat, axis=0, keepdims=True)
        norm_s[2:3, :] += jnp.sum(e, axis=0, keepdims=True)
        return carry

    at.greet()
    norm_s[...] = second_ref[...]
    e_s[...] = jnp.zeros_like(e_s)
    lax.fori_loop(0, 2 * groups, matmul, 0)
    for cp in later[1:]:
        cp.wait()
    lax.fori_loop(0, L // rows, norm, 0)
    small.start(norm_s[...], R)
    run("join")
    for g in range(groups - 1):
        for t in range(3):
            qkv_ref[:, pl.ds(t * D + g * 256, 256)] = sums_ref[g, :, pl.ds(t * 256, 256)]
    norms_ref[...] = small.collect()
    run("close")
    for t in range(3):
        qkv_ref[:, pl.ds(t * D + (groups - 1) * 256, 256)] = sum_s[:, pl.ds(t * 256, 256)]
    run("finish")
    small.finish()

    def saved(i, carry):
        saves(i).wait()
        return carry

    lax.fori_loop(0, L // rows, saved, 0)


def leave(x, dqkv, w, middle_grad, second_sums, params, parts, sums):
    G, M = lax.axis_size("dp") // 2, lax.axis_size("mp")
    L, D = x.shape
    R = parts.shape[3]
    n = 2 * G * M
    sems = (M, SumUnit.count(G))
    return pl.pallas_call(
        functools.partial(exit_kernel, rows=min(256, L)),
        in_specs=[ANY] * 4 + [VMEM, VMEM, ANY, VMEM],
        out_specs=[ANY, VMEM, VMEM],
        out_shape=[
            jax.ShapeDtypeStruct((L, D), F32),
            jax.ShapeDtypeStruct((R, 3 * D), F32),
            jax.ShapeDtypeStruct((8, 128), F32),
        ],
        scratch_shapes=[
            pltpu.VMEM((L, D), BF), pltpu.VMEM(dqkv.shape, BF), pltpu.VMEM((dqkv.shape[0], 3, D, 256), BF), pltpu.VMEM((L, D), F32),
            pltpu.VMEM(parts.shape, BF), DMA((3, 3)), DMA((L // min(256, L),)),
        ] + sum_buffers(M, G, (R, D), own=False, far=M)
        + [pltpu.VMEM((R, D), F32), pltpu.VMEM((8, D), F32), pltpu.VMEM((L, D), F32), pltpu.VMEM((n, 8, 128), F32), pltpu.VMEM((n, 8, 128), F32),
           DMA(sems), DMA(sems), DMA((M,)), DMA((n,)), DMA((n,))],
        compiler_params=params_of(3),
    )(x, dqkv, w, middle_grad, second_sums, params, parts, sums)


def per_device(inputs, lengths, attn_qkv, attn_proj, mlp_in, mlp_out, norm_gain, norm_bias, cotangent):
    n_dp, n_mp = lax.axis_size("dp"), lax.axis_size("mp")
    G = n_dp // 2
    L, D = inputs.shape
    R = attn_qkv.shape[1]
    wqkv, normed, params = entry(inputs, attn_qkv[0], norm_gain[0], norm_bias[0])
    wqkv = wqkv.reshape(3, D, D)
    mixed, wide, lse, packed, wproj, land, win, wout = attend(lengths, normed, wqkv, attn_proj[0], mlp_in[0], mlp_out[0].T, min(512, L))
    pieces = lambda w: w.reshape((w.shape[0], n_dp) + w.shape[3:])
    outputs, middle_grad, mixed_grad, second_sums, p_proj, p_in, p_out, h_in, h_out, halfway = mlp(
        lengths, inputs, mixed, cotangent, params, wproj.reshape(D, D), pieces(win), pieces(wout), land, R, min(512, L))
    dqkv, d_in, d_out, d_proj, sums, parts = attend_back(
        lengths, packed, mixed_grad, wide, lse, normed, p_in, p_out, p_proj, h_in, h_out, halfway, min(256, L))
    input_grad, d_qkv, norms = leave(inputs, dqkv, wqkv, middle_grad, second_sums, params, parts, sums)
    return (
        outputs,
        input_grad,
        d_qkv[None],
        d_proj[None],
        d_in[None],
        d_out.T[None],
        norms[None, :2, :R],
        norms[None, 2:4, :R],
    )


def solution(mesh):
    everywhere = ("dp", "mp")
    wide, columns, vector = P(everywhere, None), P(None, everywhere, None), P(None, None, everywhere)
    return jax.shard_map(
        per_device,
        mesh=mesh,
        in_specs=(wide, P(everywhere), columns, columns, P(None, "dp", "mp"), P(None, "mp", "dp"), vector, vector, wide),
        out_specs=(wide, wide, columns, columns, P(None, "dp", "mp"), P(None, "mp", "dp"), vector, vector),
        check_vma=False,
    )
```
